32 devices in a mesh: shard: 4 (over y, core), seq: 8 (over z, x).
Axes of the slice: x: 2, y: 2, z: 4, core: 2. Of those that a mesh axis runs over, the one named last changes fastest.
Arguments:
- tokens: bfloat16 [2, 4, 4096, 1024], P(None, 'shard', 'seq'), may hold values from -6 to 6
- cotangent: bfloat16 [2, 4, 4096, 1024], P(None, 'shard', 'seq'), may hold values from -6 to 6
- lengths: int32 [2, 4], P(None, 'shard'), may hold values from 1024 to 4096
- variates: int32 [2, 4, 4096], P(None, 'shard', 'seq'), may hold values from 0 to 7
- positions: int32 [2, 4, 4096], P(None, 'shard', 'seq'), may hold values from 0 to 4095
- attn_gain: float32 [1024], replicated, may hold values from 0.5 to 1.5
- w_query: bfloat16 [1024, 1024], P('shard'), may hold values from -0.1875 to 0.1875
- w_key: bfloat16 [1024, 1024], P('shard'), may hold values from -0.1875 to 0.1875
- w_value: bfloat16 [1024, 1024], P('shard'), may hold values from -0.1875 to 0.1875
- w_out: bfloat16 [1024, 1024], P('shard'), may hold values from -2 to 2
- bias_table: float32 [16, 2], replicated, may hold values from -3 to 3
- ffn_gain: float32 [1024], replicated, may hold values from 0.5 to 1.5
- w_gate: bfloat16 [1024, 4096], P('shard'), may hold values from -0.1875 to 0.1875
- w_up: bfloat16 [1024, 4096], P('shard'), may hold values from -0.1875 to 0.1875
- w_down: bfloat16 [4096, 1024], P('shard'), may hold values from -0.09375 to 0.09375
Outputs:
- output: bfloat16 [2, 4, 4096, 1024], P(None, 'shard', 'seq')
- grad_tokens: bfloat16 [2, 4, 4096, 1024], P(None, 'shard', 'seq')
- grad_attn_gain: float32 [1024], replicated
- grad_query: float32 [1024, 1024], P(('shard', 'seq'))
- grad_key: float32 [1024, 1024], P(('shard', 'seq'))
- grad_value: float32 [1024, 1024], P(('shard', 'seq'))
- grad_out: float32 [1024, 1024], P(('shard', 'seq'))
- grad_bias: float32 [16, 2], replicated
- grad_ffn_gain: float32 [1024], replicated
- grad_gate: float32 [1024, 4096], P(('shard', 'seq'))
- grad_up: float32 [1024, 4096], P(('shard', 'seq'))
- grad_down: float32 [4096, 1024], P(('shard', 'seq'))
The draws below stay inside these ranges and needn't reach their ends.
All inputs are finite; a program needn't handle non-finite values.
Results may differ from the reference program's by a relative error of at most 0.015.
Values may be sent and summed in bfloat16 or wider, within the bound.
A program may use at most 448 MiB of HBM per device.

```python
import math
import jax
import jax.numpy as jnp
from jax import lax

D = 1024
H = 16
FF = 4096
L = 4096
MB = 2
SEQS = 4


def touch_ends(values, stream_key, least, largest):
    index_at = [jax.random.randint(jax.random.fold_in(stream_key, axis), (), 0, length) for axis, length in enumerate(values.shape)]
    widest = values.shape.index(max(values.shape))
    beside = index_at[:widest] + [(index_at[widest] + 1) % values.shape[widest]] + index_at[widest + 1:]
    return values.at[tuple(index_at)].set(least).at[tuple(beside)].set(largest)


def level_of(own_key, dims, split, smallest, top_value):
    def one(dim, blocks):
        steps = jax.random.uniform(jax.random.fold_in(jax.random.fold_in(own_key, 6), dim), (blocks,), jnp.float32, smallest / len(split), top_value / len(split))
        return jnp.repeat(jnp.exp(steps), dims[dim] // blocks).reshape((-1,) + (1,) * (len(dims) - dim - 1))

    level = one(*split[0])
    for cut in split[1:]:
        level = level * one(*cut)
    return level


def bell_draw(key, extent, deviation, reach, cuts=(), kind=jnp.bfloat16):
    values = deviation * jax.random.normal(key, extent, jnp.float32)
    if cuts:
        values = values * level_of(key, extent, cuts, -0.22, 0.18)
    return jnp.clip(values, -reach, reach).astype(kind)


def setup_inputs(seed: int = 0) -> dict:
    arg_keys = jax.random.split(jax.random.key(seed), 16)
    tokens = bell_draw(arg_keys[0], (MB, SEQS, L, D), 1.0, 6.0, ((1, 4), (2, 8)))
    cotangent = bell_draw(arg_keys[1], (MB, SEQS, L, D), 1.0, 6.0, ((1, 4), (2, 8)))
    lengths = touch_ends(jax.random.randint(arg_keys[2], (MB, SEQS), L // 4, L + 1), jax.random.fold_in(arg_keys[2], 1), L // 4, L).astype(jnp.int32)
    variates = touch_ends(jax.random.randint(arg_keys[3], (MB, SEQS, L), 0, 8), jax.random.fold_in(arg_keys[3], 1), 0, 7).astype(jnp.int32)
    positions = touch_ends(jax.random.randint(arg_keys[4], (MB, SEQS, L), 0, L), jax.random.fold_in(arg_keys[4], 1), 0, L - 1).astype(jnp.int32)
    attn_gain = jnp.clip(1.0 + 0.1 * jax.random.normal(arg_keys[5], (D,), jnp.float32), 0.5, 1.5)
    w_query = bell_draw(arg_keys[6], (D, D), D ** -0.5, 0.1875, ((0, 4),))
    w_key = bell_draw(arg_keys[7], (D, D), D ** -0.5, 0.1875, ((0, 4),))
    w_value = bell_draw(arg_keys[8], (D, D), D ** -0.5, 0.1875, ((0, 4),))
    w_out = bell_draw(arg_keys[9], (D, D), (D // 128) ** -0.5, 2.0, ((0, 4),))
    bias_table = bell_draw(arg_keys[10], (H, 2), 1.0, 3.0, (), jnp.float32)
    ffn_gain = jnp.clip(1.0 + 0.1 * jax.random.normal(arg_keys[11], (D,), jnp.float32), 0.5, 1.5)
    w_gate = bell_draw(arg_keys[12], (D, FF), D ** -0.5, 0.1875, ((0, 4),))
    w_up = bell_draw(arg_keys[13], (D, FF), D ** -0.5, 0.1875, ((0, 4),))
    w_down = bell_draw(arg_keys[14], (FF, D), FF ** -0.5, 0.09375, ((0, 4),))
    return {"tokens": tokens, "cotangent": cotangent, "lengths": lengths, "variates": variates, "positions": positions, "attn_gain": attn_gain, "w_query": w_query, "w_key": w_key, "w_value": w_value, "w_out": w_out, "bias_table": bias_table, "ffn_gain": ffn_gain, "w_gate": w_gate, "w_up": w_up, "w_down": w_down}


EPSILON = 1e-06
MASKED_SCORE = -1000000000.0
ROTARY_BASE = 10000.0

@jax.custom_vjp
def low(v):
    return lax.optimization_barrier(v.astype(jnp.bfloat16)).astype(jnp.float32)

@jax.custom_vjp
def low_back(v):
    return v

def low_keep(v):
    return (low(v), None)

def low_pass(kept, grad):
    return (grad,)

def back_keep(v):
    return (v, None)

def back_low(kept, grad):
    return (low(grad),)
low.defvjp(low_keep, low_pass)
low_back.defvjp(back_keep, back_low)

def rotary(values, places):
    half_dim = values.shape[-1] // 2
    frequency = jnp.exp(-math.log(ROTARY_BASE) * jnp.arange(half_dim, dtype=jnp.float32) / half_dim)
    angles = places.astype(jnp.float32)[:, None] * frequency[None, :]
    cosine = jnp.cos(angles)[:, None, :]
    sine_table = jnp.sin(angles)[:, None, :]
    first_half = values[..., :half_dim]
    second_half = values[..., half_dim:]
    return jnp.concatenate([first_half * cosine - second_half * sine_table, second_half * cosine + first_half * sine_table], axis=-1)

def layer(params, tokens_row, length, variate_row, place_row):
    attn_gain, w_query, w_key, w_value, w_out, bias_table, ffn_gain, w_gate, w_up, w_down = params
    seq_len, width = tokens_row.shape
    heads = bias_table.shape[0]
    head_dim = width // heads
    scale_factor = 1.0 / math.sqrt(head_dim)
    key_index = jnp.arange(seq_len, dtype=jnp.int32)
    key_mask = key_index < length
    valid_rows = key_mask.astype(jnp.float32)
    norm_attn = lax.rsqrt(lax.optimization_barrier(jnp.mean(tokens_row * tokens_row, axis=-1, keepdims=True)) + EPSILON)
    normed = low(tokens_row * norm_attn * attn_gain)

    def project(weight):
        return jnp.dot(normed, weight, precision=lax.Precision.HIGHEST)
    query_pre = low_back(project(w_query)).reshape(seq_len, heads, head_dim)
    key_pre = low_back(project(w_key)).reshape(seq_len, heads, head_dim)
    value_pre = low_back(project(w_value)).reshape(seq_len, heads, head_dim)
    queries = low(rotary(query_pre, place_row))
    keys_rot = low(rotary(key_pre, place_row))
    values_all = low(value_pre)
    block_rows = min(512, seq_len)
    count_blocks = seq_len // block_rows

    def attend(inputs):
        query_block, variate_block = inputs
        scores = jnp.einsum('qhd,khd->hqk', query_block, keys_rot, precision=lax.Precision.HIGHEST) * scale_factor
        same_var = variate_block[:, None] == variate_row[None, :]
        biased = scores + jnp.where(same_var[None], bias_table[:, 1][:, None, None], bias_table[:, 0][:, None, None])
        masked = jnp.where(key_mask[None, None, :], low_back(biased), MASKED_SCORE)
        peak = lax.optimization_barrier(jnp.max(masked, axis=-1, keepdims=True))
        weights_exp = jnp.exp(masked - peak)
        probs = low(weights_exp / lax.optimization_barrier(jnp.sum(weights_exp, axis=-1, keepdims=True)))
        return jnp.einsum('hqk,khd->qhd', probs, values_all, precision=lax.Precision.HIGHEST)
    mixed = lax.map(jax.checkpoint(attend), (queries.reshape(count_blocks, block_rows, heads, head_dim), variate_row.reshape(count_blocks, block_rows)))
    mixed = low(low_back(mixed.reshape(seq_len, width)))
    attn_out = low_back(jnp.dot(mixed, w_out, precision=lax.Precision.HIGHEST))
    residual = tokens_row + attn_out
    norm_ffn = lax.rsqrt(lax.optimization_barrier(jnp.mean(residual * residual, axis=-1, keepdims=True)) + EPSILON)
    normed_ffn = low(residual * norm_ffn * ffn_gain)
    gate_act = low_back(jnp.dot(normed_ffn, w_gate, precision=lax.Precision.HIGHEST))
    up_act = low_back(jnp.dot(normed_ffn, w_up, precision=lax.Precision.HIGHEST))
    hidden = low(gate_act * jax.nn.sigmoid(gate_act) * up_act)
    ffn_out = low_back(jnp.dot(hidden, w_down, precision=lax.Precision.HIGHEST))
    return (residual + ffn_out) * valid_rows[:, None]

def reference(tokens, cotangent, lengths, variates, positions, attn_gain, w_query, w_key, w_value, w_out, bias_table, ffn_gain, w_gate, w_up, w_down):
    params = tuple((item.astype(jnp.float32) for item in (attn_gain, w_query, w_key, w_value, w_out, bias_table, ffn_gain, w_gate, w_up, w_down)))
    micro, seq_count, seq_len, width = tokens.shape
    total_seqs = micro * seq_count
    flat_tokens = tokens.reshape(total_seqs, seq_len, width)
    flat_cot = cotangent.reshape(total_seqs, seq_len, width)
    flat_lengths = lengths.reshape(total_seqs)
    flat_variates = variates.reshape(total_seqs, seq_len)
    flat_places = positions.reshape(total_seqs, seq_len)

    def one_sequence(carry, inputs):
        tokens_row, cot_row, length, variate_row, place_row = inputs

        def forward(param_set, input_row):
            return layer(param_set, input_row, length, variate_row, place_row)
        result, pull_back = jax.vjp(forward, params, tokens_row.astype(jnp.float32))
        grad_params, grad_input = pull_back(cot_row.astype(jnp.float32))
        carry = jax.tree.map(jnp.add, carry, grad_params)
        return (carry, (result.astype(jnp.bfloat16), grad_input.astype(jnp.bfloat16)))
    zero_grads = jax.tree.map(jnp.zeros_like, params)
    grads, (outputs, grad_inputs) = lax.scan(one_sequence, zero_grads, (flat_tokens, flat_cot, flat_lengths, flat_variates, flat_places))
    outputs = outputs.reshape(micro, seq_count, seq_len, width)
    grad_inputs = grad_inputs.reshape(micro, seq_count, seq_len, width)
    return (outputs, grad_inputs, grads[0], grads[1], grads[2], grads[3], grads[4], grads[5], grads[6], grads[7], grads[8], grads[9])
```

```python
import functools
import math

import jax
import jax.numpy as jnp
from jax import lax
from jax.experimental import pallas as pl
from jax.experimental.pallas import tpu as pltpu
from jax.sharding import PartitionSpec as P

EPSILON = 1e-06
ROTARY_BASE = 10000.0
LOG2E = 1.4426950408889634
LN2 = 0.6931471805599453
CLASSES = 8
AUX = 16
EXTRA = 32
MASKED = -1.5e9
FAR = 1e30
F32 = jnp.float32
BF16 = jnp.bfloat16


def dot(a, b):
    return jnp.dot(a, b, preferred_element_type=F32)


def contract(a, b, da, db):
    return lax.dot_general(a, b, (((da,), (db,)), ((), ())), preferred_element_type=F32)


def pieces(x):
    high = x.astype(BF16).astype(F32)
    rest = x - high
    mid = rest.astype(BF16).astype(F32)
    low = (rest - mid).astype(BF16).astype(F32)
    return high, mid, low


def one_hot(row):
    classes = lax.broadcasted_iota(jnp.int32, (CLASSES, row.shape[1]), 0).astype(F32)
    return jnp.where(classes == row, 1.0, 0.0)


def rows_of(values, width):
    index = lax.broadcasted_iota(jnp.int32, (8, width), 0)
    out = jnp.zeros((8, width), F32)
    for at, value in enumerate(values):
        out = jnp.where(index == at, value, out)
    return out


def key_extra(row, start, length, other, same):
    width = row.shape[1]
    hot = one_hot(row)
    step = pieces(jnp.full((1, width), same - other, F32))
    base = pieces(jnp.full((1, width), other, F32))
    index = start + lax.broadcasted_iota(jnp.int32, (1, width), 1)
    mask = jnp.where(index < length, 0.0, MASKED)
    tail = rows_of(base + (mask, 1.0, 1.0, 1.0), width)
    return jnp.concatenate([hot * step[0], hot * step[1], hot * step[2], tail], axis=0).astype(BF16)


def query_extra(row, shift):
    hot = one_hot(row)
    tail = rows_of((1.0, 1.0, 1.0, 1.0) + shift, row.shape[1])
    return jnp.concatenate([hot, hot, hot, tail], axis=0).astype(BF16)


def forward_kernel(
    shape, len_ref, bias_ref, x_ref, *rest
):
    local, head_dim, block, aliased = shape
    if aliased:
        rest = rest[1:]
    mixed_ref, lse_ref, keys, vals, query, score, peak, total = rest
    count, _, width = x_ref.shape
    sub = block // width
    step = pl.program_id(0)
    length = len_ref[0]
    other = bias_ref[local, 0] * LOG2E
    same = bias_ref[local, 1] * LOG2E

    @pl.when(step == 0)
    def _():
        for b in range(count):
            at = pl.ds(b * width, width)
            row = x_ref[b, 3 * head_dim : 3 * head_dim + 1, :].astype(F32)
            extra = key_extra(row, b * width, length, other, same)
            full = jnp.concatenate([x_ref[b, head_dim : 2 * head_dim, :], extra], axis=0)
            keys[at, :] = full.T
            vals[0:head_dim, at] = x_ref[b, 2 * head_dim : 3 * head_dim, :]
        vals[head_dim:, :] = jnp.ones((16, vals.shape[1]), BF16)

    used = pl.cdiv(length, block)
    inside = step * block < length

    @pl.when(jnp.logical_not(inside))
    def _():
        mixed_ref[...] = jnp.zeros_like(mixed_ref)
        lse_ref[...] = jnp.full(lse_ref.shape, FAR, F32)

    @pl.when(inside)
    def _():
        for b in range(sub):
            at = slice(b * width, (b + 1) * width)
            row = x_ref[step * sub + b, 3 * head_dim : 3 * head_dim + 1, :].astype(F32)
            query[0:head_dim, at] = x_ref[step * sub + b, 0:head_dim, :]
            query[head_dim:, at] = query_extra(row, (0.0, 0.0, 0.0))
        peak[...] = jnp.full(peak.shape, -FAR, F32)
        total[...] = jnp.zeros_like(total)

        def span(j):
            return pl.ds(pl.multiple_of(j * block, block), block)

        def scores_of(j):
            return dot(keys[span(j), :], query[...])

        def one(j, now, ahead):
            if ahead:
                score[1 - now] = scores_of(j + 1)
            current = score[now]
            before = peak[...]
            top = jnp.maximum(before, jnp.max(current, axis=0, keepdims=True))
            weight = jnp.exp2(current - top).astype(BF16)
            peak[...] = top
            total[...] = total[...] * jnp.exp2(before - top) + dot(vals[:, span(j)], weight)

        score[0] = scores_of(0)
        pairs = (used - 1) // 2

        def pair(j, carry):
            one(2 * j, 0, True)
            one(2 * j + 1, 1, True)
            return carry

        lax.fori_loop(0, pairs, pair, 0)
        last = 2 * pairs

        @pl.when(used - last == 1)
        def _():
            one(last, 0, False)

        @pl.when(used - last == 2)
        def _():
            one(last, 0, True)
            one(last + 1, 1, False)

        mass = total[head_dim : head_dim + 1, :]
        mixed = (total[0:head_dim, :] / mass).astype(BF16)
        for b in range(sub):
            mixed_ref[b] = mixed[:, b * width : (b + 1) * width]
        lse_ref[0] = peak[...] + jnp.log2(mass)


def attend_forward(x, length, bias, mixed, local, heads_here, head_dim):
    count, rows, width = x.shape
    block = max(width, 512)
    seq_len = count * width
    blocks = seq_len // block
    depth = head_dim + EXTRA
    whole = pl.BlockSpec((count, rows, width), lambda i, *_: (0, 0, 0))
    operands = [length, bias, x]
    in_specs = [whole]
    aliases = {}
    if mixed is not None:
        operands.append(mixed)
        in_specs.append(pl.BlockSpec(memory_space=pl.ANY))
        aliases = {3: 0}
    return pl.pallas_call(
        functools.partial(forward_kernel, (local, head_dim, block, mixed is not None)),
        grid_spec=pltpu.PrefetchScalarGridSpec(
            num_scalar_prefetch=2,
            grid=(blocks,),
            in_specs=in_specs,
            out_specs=[
                pl.BlockSpec((block // width, head_dim, width), lambda i, *_: (i, local, 0)),
                pl.BlockSpec((1, 1, block), lambda i, *_: (i, 0, 0)),
            ],
            scratch_shapes=[
                pltpu.VMEM((seq_len, depth), BF16),
                pltpu.VMEM((head_dim + 16, seq_len), BF16),
                pltpu.VMEM((depth, block), BF16),
                pltpu.VMEM((2, block, block), F32),
                pltpu.VMEM((1, block), F32),
                pltpu.VMEM((head_dim + 16, block), F32),
            ],
        ),
        out_shape=[
            jax.ShapeDtypeStruct((count, heads_here * head_dim, width), BF16),
            jax.ShapeDtypeStruct((blocks, 1, block), F32),
        ],
        input_output_aliases=aliases,
        compiler_params=pltpu.CompilerParams(vmem_limit_bytes=40 << 20),
        cost_estimate=pl.CostEstimate(
            flops=8 * seq_len * seq_len * 256,
            bytes_accessed=x.size * 4,
            transcendentals=seq_len * seq_len,
        ),
        name="attend_forward",
    )(*operands)


def backward_kernel(
    shape, len_ref, bias_ref, x_ref, grad_ref, mixed_ref, lse_ref, out_ref, bias_out_ref,
    keys, keys_flat, vals, query, grads, query_rows, grad_rows, acc_keys, acc_vals, acc_query,
):
    local, head_dim, block = shape
    count, _, width = x_ref.shape
    sub = block // width
    step = pl.program_id(0)
    length = len_ref[0]
    other = bias_ref[local, 0] * LOG2E
    same = bias_ref[local, 1] * LOG2E

    @pl.when(step == 0)
    def _():
        ones = jnp.ones((16, width), BF16)
        for b in range(count):
            at = pl.ds(b * width, width)
            row = x_ref[b, 3 * head_dim : 3 * head_dim + 1, :].astype(F32)
            extra = key_extra(row, b * width, length, other, same)
            here = x_ref[b, head_dim : 2 * head_dim, :]
            keys[at, :] = jnp.concatenate([here, extra], axis=0).T
            keys_flat[:, at] = here
            vals[at, :] = jnp.concatenate([x_ref[b, 2 * head_dim : 3 * head_dim, :], ones], axis=0).T
        acc_keys[...] = jnp.zeros_like(acc_keys)
        acc_vals[...] = jnp.zeros_like(acc_vals)

    used = pl.cdiv(length, block)
    inside = step * block < length

    @pl.when(jnp.logical_not(inside))
    def _():
        for b in range(sub):
            out_ref[step * sub + b, 0:head_dim, :] = jnp.zeros((head_dim, width), BF16)

    @pl.when(inside)
    def _():
        for b in range(sub):
            at = slice(b * width, (b + 1) * width)
            here = step * sub + b
            row = x_ref[here, 3 * head_dim : 3 * head_dim + 1, :].astype(F32)
            shift = pieces(-lse_ref[step][:, at])
            grad = grad_ref[here]
            delta = jnp.sum(grad.astype(F32) * mixed_ref[here].astype(F32), axis=0, keepdims=True)
            query[0:head_dim, at] = x_ref[here, 0:head_dim, :]
            query[head_dim:, at] = query_extra(row, shift)
            grads[0:head_dim, at] = grad
            tail = rows_of(pieces(-delta), width)
            grads[head_dim:, at] = jnp.concatenate([tail, jnp.zeros_like(tail)], axis=0).astype(BF16)
        query_rows[...] = query[...].T
        grad_rows[...] = grads[...].T
        acc_query[...] = jnp.zeros_like(acc_query)

        def one(j):
            at = pl.ds(pl.multiple_of(j * block, block), block)
            probs = jnp.exp2(dot(keys[at, :], query[...]))
            grad_probs = dot(vals[at, :], grads[...])
            grad_scores = (probs * grad_probs).astype(BF16)
            acc_vals[at, :] += dot(probs.astype(BF16), grad_rows[...])
            acc_keys[at, :] += dot(grad_scores, query_rows[...])
            acc_query[...] += dot(keys_flat[:, at], grad_scores)

        def pair(j, carry):
            one(2 * j)
            one(2 * j + 1)
            return carry

        lax.fori_loop(0, used // 2, pair, 0)

        @pl.when(used % 2 == 1)
        def _():
            one(used - 1)

        grad_query = (acc_query[...] * (1.0 / math.sqrt(head_dim))).astype(BF16)
        for b in range(sub):
            out_ref[step * sub + b, 0:head_dim, :] = grad_query[:, b * width : (b + 1) * width]

    @pl.when(step == pl.num_programs(0) - 1)
    def _():
        same_total = jnp.zeros((CLASSES, width), F32)
        all_total = jnp.zeros((CLASSES, width), F32)
        for b in range(count):
            at = pl.ds(b * width, width)
            row = x_ref[b, 3 * head_dim : 3 * head_dim + 1, :].astype(F32)
            flat = acc_keys[at, :].T
            out_ref[b, head_dim : 2 * head_dim, :] = (flat[0:head_dim] * LN2).astype(BF16)
            out_ref[b, 2 * head_dim : 3 * head_dim, :] = acc_vals[at, :].T[0:head_dim].astype(BF16)
            by_class = flat[head_dim : head_dim + CLASSES]
            all_total += by_class
            same_total += by_class * one_hot(row)
        both = jnp.concatenate(
            [
                jnp.broadcast_to(jnp.sum(same_total, keepdims=True), (1, 128)),
                jnp.broadcast_to(jnp.sum(all_total, keepdims=True), (1, 128)),
                jnp.zeros((6, 128), F32),
            ],
            axis=0,
        )
        bias_out_ref[...] = both


def attend_backward(x, grad, mixed, lse, length, bias, local, head_dim):
    count, rows, width = x.shape
    blocks, _, block = lse.shape
    seq_len = count * width
    depth = head_dim + EXTRA

    def whole(a):
        return pl.BlockSpec(a.shape, lambda i, *_: (0,) * a.ndim)

    head_spec = pl.BlockSpec((count, head_dim, width), lambda i, *_: (0, local, 0))
    return pl.pallas_call(
        functools.partial(backward_kernel, (local, head_dim, block)),
        grid_spec=pltpu.PrefetchScalarGridSpec(
            num_scalar_prefetch=2,
            grid=(blocks,),
            in_specs=[whole(x), head_spec, head_spec, whole(lse)],
            out_specs=[
                pl.BlockSpec((count, 3 * head_dim, width), lambda i, *_: (0, 0, 0)),
                pl.BlockSpec((8, 128), lambda i, *_: (0, 0)),
            ],
            scratch_shapes=[
                pltpu.VMEM((seq_len, depth), BF16),
                pltpu.VMEM((head_dim, seq_len), BF16),
                pltpu.VMEM((seq_len, head_dim + 16), BF16),
                pltpu.VMEM((depth, block), BF16),
                pltpu.VMEM((head_dim + 16, block), BF16),
                pltpu.VMEM((block, depth), BF16),
                pltpu.VMEM((block, head_dim + 16), BF16),
                pltpu.VMEM((seq_len, depth), F32),
                pltpu.VMEM((seq_len, head_dim + 16), F32),
                pltpu.VMEM((head_dim, block), F32),
            ],
        ),
        out_shape=[
            jax.ShapeDtypeStruct((count, 3 * head_dim, width), BF16),
            jax.ShapeDtypeStruct((8, 128), F32),
        ],
        compiler_params=pltpu.CompilerParams(vmem_limit_bytes=48 << 20),
        cost_estimate=pl.CostEstimate(
            flops=20 * seq_len * seq_len * 256,
            bytes_accessed=x.size * 6,
            transcendentals=seq_len * seq_len,
        ),
        name="attend_backward",
    )(length, bias, x, grad, mixed, lse)


def rotary_tables(places, half_dim):
    frequency = jnp.exp(-math.log(ROTARY_BASE) * jnp.arange(half_dim, dtype=F32) / half_dim)
    angles = places.astype(F32)[None, :] * frequency[:, None]
    return jnp.cos(angles), jnp.sin(angles)


def rotate(values, cosine, sine, reverse):
    half_dim = values.shape[-2] // 2
    first = values[..., :half_dim, :]
    second = values[..., half_dim:, :]
    if reverse:
        parts = [first * cosine + second * sine, second * cosine - first * sine]
    else:
        parts = [first * cosine - second * sine, second * cosine + first * sine]
    return jnp.concatenate(parts, axis=-2)


def norm_back(grad_normed, inputs, inverse, gain):
    scaled = grad_normed * gain
    grad_inputs = inverse * scaled - inputs * (inverse * inverse * inverse) * jnp.mean(
        scaled * inputs, axis=-1, keepdims=True
    )
    return grad_inputs, jnp.sum(grad_normed * inputs * inverse, axis=0)


def on_device(
    tokens, cotangent, lengths, variates, positions, attn_gain, w_query, w_key, w_value, w_out,
    bias_table, ffn_gain, w_gate, w_up, w_down,
):
    micro, seqs, width, model = tokens.shape
    heads = bias_table.shape[0]
    head_dim = model // heads
    count = lax.axis_size("seq")
    here = heads // count
    ffn = w_gate.shape[1]
    seq_index = lax.axis_index("seq")
    bias_here = lax.dynamic_slice_in_dim(bias_table, seq_index * here, here, 0)
    row_index = seq_index * width + jnp.arange(width, dtype=jnp.int32)
    units = [(m, s) for m in range(micro) for s in range(seqs)]

    def gather(weight):
        return lax.all_gather(weight, "shard", axis=0, tiled=True)

    def exchange(values):
        return lax.all_to_all(values, "seq", split_axis=0, concat_axis=0, tiled=True)

    query_full, key_full, value_full = gather(w_query), gather(w_key), gather(w_value)
    out_full, gate_full, up_full, down_full = (
        gather(w_out), gather(w_gate), gather(w_up), gather(w_down)
    )

    first = []
    for m, s in units:
        inputs = tokens[m, s].astype(F32)
        inverse = lax.rsqrt(jnp.mean(inputs * inputs, axis=-1, keepdims=True) + EPSILON)
        normed = (inputs * inverse * attn_gain).astype(BF16)
        cosine, sine = rotary_tables(positions[m, s], head_dim // 2)

        def project(weight):
            return contract(weight, normed, 0, 1).reshape(heads, head_dim, width)

        scale = LOG2E / math.sqrt(head_dim)
        query = (rotate(project(query_full), cosine, sine, False) * scale).astype(BF16)
        key = rotate(project(key_full), cosine, sine, False).astype(BF16)
        value = project(value_full).astype(BF16)
        extra = jnp.broadcast_to(variates[m, s].astype(BF16)[None, None, :], (heads, AUX, width))
        packed = jnp.concatenate([query, key, value, extra], axis=1)
        packed = packed.reshape(count, here, 3 * head_dim + AUX, width)
        sent = [exchange(packed[:, h]) for h in range(here)]
        first.append((normed, inverse, cosine, sine, sent))

    attended = []
    for (m, s), item in zip(units, first):
        sent = item[4]
        length = lengths[m, s].reshape(1)
        mixed = None
        sums = []
        for h in range(here):
            mixed, lse = attend_forward(sent[h], length, bias_here, mixed, h, here, head_dim)
            sums.append(lse)
        mixed_tok = exchange(mixed).reshape(model, width)
        attended.append((mixed, sums, mixed_tok))

    outputs = [[None] * seqs for _ in range(micro)]
    middle = []
    acc_ffn_gain = jnp.zeros((model,), F32)
    for (m, s), (mixed, sums, mixed_tok) in zip(units, attended):
        valid = (row_index < lengths[m, s]).astype(F32)[:, None]
        inputs = tokens[m, s].astype(F32)
        residual = inputs + contract(mixed_tok, out_full, 0, 0)
        inverse = lax.rsqrt(jnp.mean(residual * residual, axis=-1, keepdims=True) + EPSILON)
        normed = (residual * inverse * ffn_gain).astype(BF16)
        gate = dot(normed, gate_full)
        up = dot(normed, up_full)
        sigmoid = jax.nn.sigmoid(gate)
        silu = gate * sigmoid
        hidden = (silu * up).astype(BF16)
        outputs[m][s] = ((residual + dot(hidden, down_full)) * valid).astype(BF16)
        masked = cotangent[m, s].astype(F32) * valid
        grad_ffn = masked.astype(BF16)
        grad_hidden = contract(grad_ffn, down_full, 1, 1)
        grad_gate = (grad_hidden * up * (sigmoid + silu * (1.0 - sigmoid))).astype(BF16)
        grad_up = (grad_hidden * silu).astype(BF16)
        grad_normed = contract(grad_gate, gate_full, 1, 1) + contract(grad_up, up_full, 1, 1)
        grad_res, gain_term = norm_back(grad_normed, residual, inverse, ffn_gain)
        acc_ffn_gain = acc_ffn_gain + gain_term
        grad_residual = masked + grad_res
        grad_attn = grad_residual.astype(BF16)
        grad_mixed = contract(out_full, grad_attn, 1, 1).astype(BF16)
        grad_heads = exchange(grad_mixed.reshape(count, here * head_dim, width))
        middle.append((normed, hidden, grad_ffn, grad_gate, grad_up, grad_residual, grad_attn, grad_heads))

    def joined(parts):
        return parts[0] if len(parts) == 1 else jnp.concatenate(parts, axis=0)

    normed_all = joined([item[0] for item in middle])
    hidden_all = joined([item[1] for item in middle])
    ffn_all = joined([item[2] for item in middle])
    devices = lax.axis_size("shard") * count
    rows = model // devices
    down_rows = ffn // devices
    fold = down_rows // rows

    def spread(total):
        split = total.reshape(devices, rows, fold, ffn // fold)
        return jnp.swapaxes(split, 1, 2).reshape(ffn, ffn // fold)

    gate_term = contract(normed_all, joined([item[3] for item in middle]), 0, 0).astype(BF16)
    up_term = contract(normed_all, joined([item[4] for item in middle]), 0, 0).astype(BF16)
    down_term = contract(hidden_all, ffn_all, 0, 0).astype(BF16)
    ffn_terms = jnp.concatenate([down_term, spread(gate_term), spread(up_term)], axis=1)
    ffn_owned = lax.psum_scatter(ffn_terms, ("shard", "seq"), scatter_dimension=0, tiled=True)

    grads = [[None] * seqs for _ in range(micro)]
    acc_attn_gain = jnp.zeros((model,), F32)
    acc_bias = jnp.zeros((here, 2), F32)
    returned = []
    for (m, s), before, (mixed, sums, _), item in zip(units, first, attended, middle):
        sent = before[4]
        length = lengths[m, s].reshape(1)
        back = []
        terms = []
        for h in range(here):
            packed, both = attend_backward(
                sent[h], item[7], mixed, sums[h], length, bias_here, h, head_dim
            )
            back.append(exchange(packed))
            terms.append(jnp.stack([both[1, 0] - both[0, 0], both[0, 0]]))
        acc_bias = acc_bias + jnp.stack(terms)
        returned.append(back)
    for (m, s), before, item, back in zip(units, first, middle, returned):
        normed, inverse, cosine, sine, _ = before
        grad_residual = item[5]
        full = jnp.stack(back, axis=1).reshape(heads, 3, head_dim, width)
        grad_q = rotate(full[:, 0].astype(F32), cosine, sine, True).astype(BF16).reshape(model, width)
        grad_k = rotate(full[:, 1].astype(F32), cosine, sine, True).astype(BF16).reshape(model, width)
        grad_v = full[:, 2].reshape(model, width)
        grad_normed = (
            contract(grad_q, query_full, 0, 1)
            + contract(grad_k, key_full, 0, 1)
            + contract(grad_v, value_full, 0, 1)
        )
        inputs = tokens[m, s].astype(F32)
        grad_in, gain_term = norm_back(grad_normed, inputs, inverse, attn_gain)
        acc_attn_gain = acc_attn_gain + gain_term
        grads[m][s] = (grad_residual + grad_in).astype(BF16)
        returned[m * seqs + s] = (grad_q, grad_k, grad_v)

    attn_normed = joined([item[0] for item in first])
    grad_cols = [jnp.concatenate([item[i] for item in returned], axis=1) for i in range(3)]
    terms = [contract(attn_normed, cols, 0, 1) for cols in grad_cols]
    mixed_cols = jnp.concatenate([item[2] for item in attended], axis=1)
    terms.append(contract(mixed_cols, joined([item[6] for item in middle]), 1, 0))
    pad = (-(4 * model)) % 384
    attn_terms = jnp.concatenate(terms + [jnp.zeros((model, pad), F32)], axis=1).astype(BF16)
    attn_owned = lax.psum_scatter(attn_terms, ("shard", "seq"), scatter_dimension=0, tiled=True)

    bias_full = lax.dynamic_update_slice(
        jnp.zeros((heads, 2), F32), acc_bias, (seq_index * here, jnp.int32(0))
    )
    grad_attn_gain, grad_ffn_gain, grad_bias = lax.psum(
        (acc_attn_gain, acc_ffn_gain, bias_full), ("shard", "seq")
    )

    def unspread(part):
        return jnp.swapaxes(part.reshape(fold, rows, ffn // fold), 0, 1).reshape(rows, ffn).astype(F32)

    part = ffn // fold
    attn_owned = attn_owned.astype(F32)
    return (
        jnp.stack([jnp.stack(item) for item in outputs]),
        jnp.stack([jnp.stack(item) for item in grads]),
        grad_attn_gain,
        attn_owned[:, 0:model],
        attn_owned[:, model : 2 * model],
        attn_owned[:, 2 * model : 3 * model],
        attn_owned[:, 3 * model : 4 * model],
        grad_bias,
        grad_ffn_gain,
        unspread(ffn_owned[:, model : model + part]),
        unspread(ffn_owned[:, model + part : model + 2 * part]),
        ffn_owned[:, 0:model].astype(F32),
    )


def solution(mesh):
    token_spec = P(None, "shard", "seq", None)
    row_spec = P("shard", None)
    in_specs = (
        token_spec, token_spec, P(None, "shard"), P(None, "shard", "seq"), P(None, "shard", "seq"),
        P(), row_spec, row_spec, row_spec, row_spec, P(), P(), row_spec, row_spec, row_spec,
    )
    owned = P(("shard", "seq"), None)
    out_specs = (
        token_spec, token_spec, P(), owned, owned, owned, owned, P(), P(), owned, owned, owned,
    )
    return jax.shard_map(
        on_device, mesh=mesh, in_specs=in_specs, out_specs=out_specs, check_vma=False
    )
```

```python
import functools
import math

import jax
import jax.numpy as jnp
from jax import lax
from jax.experimental import pallas as pl
from jax.experimental.pallas import tpu as pltpu
from jax.sharding import PartitionSpec as P

EPSILON = 1e-06
ROTARY_BASE = 10000.0
LOG2E = 1.4426950408889634
LN2 = 0.6931471805599453
CLASSES = 8
AUX = 16
EXTRA = 32
MASKED = -1.5e9
FAR = 1e30
F32 = jnp.float32
BF16 = jnp.bfloat16


def dot(a, b):
    return jnp.dot(a, b, preferred_element_type=F32)


def contract(a, b, da, db):
    return lax.dot_general(a, b, (((da,), (db,)), ((), ())), preferred_element_type=F32)


def pieces(x):
    high = x.astype(BF16).astype(F32)
    rest = x - high
    mid = rest.astype(BF16).astype(F32)
    low = (rest - mid).astype(BF16).astype(F32)
    return high, mid, low


def one_hot(row):
    classes = lax.broadcasted_iota(jnp.int32, (CLASSES, row.shape[1]), 0).astype(F32)
    return jnp.where(classes == row, 1.0, 0.0)


def rows_of(values, width):
    index = lax.broadcasted_iota(jnp.int32, (8, width), 0)
    out = jnp.zeros((8, width), F32)
    for at, value in enumerate(values):
        out = jnp.where(index == at, value, out)
    return out


def key_extra(row, start, length, other, same):
    width = row.shape[1]
    hot = one_hot(row)
    step = pieces(jnp.full((1, width), same - other, F32))
    base = pieces(jnp.full((1, width), other, F32))
    index = start + lax.broadcasted_iota(jnp.int32, (1, width), 1)
    mask = jnp.where(index < length, 0.0, MASKED)
    tail = rows_of(base + (mask, 1.0, 1.0, 1.0), width)
    return jnp.concatenate([hot * step[0], hot * step[1], hot * step[2], tail], axis=0).astype(BF16)


def query_extra(row, shift):
    hot = one_hot(row)
    tail = rows_of((1.0, 1.0, 1.0, 1.0) + shift, row.shape[1])
    return jnp.concatenate([hot, hot, hot, tail], axis=0).astype(BF16)


def forward_kernel(
    shape, len_ref, bias_ref, x_ref, ids_ref, *rest
):
    local, head_dim, block, aliased = shape
    if aliased:
        rest = rest[1:]
    mixed_ref, lse_ref, keys, vals, query, score, peak, total = rest
    count, _, width = x_ref.shape
    sub = block // width
    step = pl.program_id(0)
    length = len_ref[0]
    other = bias_ref[local, 0] * LOG2E
    same = bias_ref[local, 1] * LOG2E

    @pl.when(step == 0)
    def _():
        for b in range(count):
            at = pl.ds(b * width, width)
            row = ids_ref[b, 0:1, :].astype(F32)
            extra = key_extra(row, b * width, length, other, same)
            full = jnp.concatenate([x_ref[b, head_dim : 2 * head_dim, :], extra], axis=0)
            keys[at, :] = full.T
            vals[0:head_dim, at] = x_ref[b, 2 * head_dim : 3 * head_dim, :]
        vals[head_dim:, :] = jnp.ones((16, vals.shape[1]), BF16)

    used = pl.cdiv(length, block)
    inside = step * block < length

    @pl.when(jnp.logical_not(inside))
    def _():
        mixed_ref[...] = jnp.zeros_like(mixed_ref)
        lse_ref[...] = jnp.full(lse_ref.shape, FAR, F32)

    @pl.when(inside)
    def _():
        for b in range(sub):
            at = slice(b * width, (b + 1) * width)
            row = ids_ref[step * sub + b, 0:1, :].astype(F32)
            query[0:head_dim, at] = x_ref[step * sub + b, 0:head_dim, :]
            query[head_dim:, at] = query_extra(row, (0.0, 0.0, 0.0))
        peak[...] = jnp.full(peak.shape, -FAR, F32)
        total[...] = jnp.zeros_like(total)

        def span(j):
            return pl.ds(pl.multiple_of(j * block, block), block)

        def scores_of(j):
            return dot(keys[span(j), :], query[...])

        def one(j, now, ahead):
            if ahead:
                score[1 - now] = scores_of(j + 1)
            current = score[now]
            before = peak[...]
            top = jnp.maximum(before, jnp.max(current, axis=0, keepdims=True))
            weight = jnp.exp2(current - top).astype(BF16)
            peak[...] = top
            total[...] = total[...] * jnp.exp2(before - top) + dot(vals[:, span(j)], weight)

        score[0] = scores_of(0)
        pairs = (used - 1) // 2

        def pair(j, carry):
            one(2 * j, 0, True)
            one(2 * j + 1, 1, True)
            return carry

        lax.fori_loop(0, pairs, pair, 0)
        last = 2 * pairs

        @pl.when(used - last == 1)
        def _():
            one(last, 0, False)

        @pl.when(used - last == 2)
        def _():
            one(last, 0, True)
            one(last + 1, 1, False)

        mass = total[head_dim : head_dim + 1, :]
        mixed = (total[0:head_dim, :] / mass).astype(BF16)
        for b in range(sub):
            mixed_ref[b] = mixed[:, b * width : (b + 1) * width]
        lse_ref[0] = peak[...] + jnp.log2(mass)


def attend_forward(x, ids, length, bias, mixed, local, heads_here, head_dim):
    count, rows, width = x.shape
    block = max(width, 512)
    seq_len = count * width
    blocks = seq_len // block
    depth = head_dim + EXTRA
    whole = pl.BlockSpec((count, rows, width), lambda i, *_: (0, 0, 0))
    operands = [length, bias, x, ids]
    in_specs = [whole, pl.BlockSpec((count, AUX, width), lambda i, *_: (0, 3 * head_dim // AUX, 0))]
    aliases = {}
    if mixed is not None:
        operands.append(mixed)
        in_specs.append(pl.BlockSpec(memory_space=pl.ANY))
        aliases = {4: 0}
    return pl.pallas_call(
        functools.partial(forward_kernel, (local, head_dim, block, mixed is not None)),
        grid_spec=pltpu.PrefetchScalarGridSpec(
            num_scalar_prefetch=2,
            grid=(blocks,),
            in_specs=in_specs,
            out_specs=[
                pl.BlockSpec((block // width, head_dim, width), lambda i, *_: (i, local, 0)),
                pl.BlockSpec((1, 1, block), lambda i, *_: (i, 0, 0)),
            ],
            scratch_shapes=[
                pltpu.VMEM((seq_len, depth), BF16),
                pltpu.VMEM((head_dim + 16, seq_len), BF16),
                pltpu.VMEM((depth, block), BF16),
                pltpu.VMEM((2, block, block), F32),
                pltpu.VMEM((1, block), F32),
                pltpu.VMEM((head_dim + 16, block), F32),
            ],
        ),
        out_shape=[
            jax.ShapeDtypeStruct((count, heads_here * head_dim, width), BF16),
            jax.ShapeDtypeStruct((blocks, 1, block), F32),
        ],
        input_output_aliases=aliases,
        compiler_params=pltpu.CompilerParams(vmem_limit_bytes=40 << 20),
        cost_estimate=pl.CostEstimate(
            flops=8 * seq_len * seq_len * 256,
            bytes_accessed=x.size * 4,
            transcendentals=seq_len * seq_len,
        ),
        name="attend_forward",
    )(*operands)


def backward_kernel(
    shape, len_ref, bias_ref, x_ref, ids_ref, grad_ref, mixed_ref, lse_ref, out_ref, bias_out_ref,
    keys, keys_flat, vals, query, grads, query_rows, grad_rows, acc_keys, acc_vals, acc_query,
):
    local, head_dim, block = shape
    count, _, width = x_ref.shape
    sub = block // width
    step = pl.program_id(0)
    length = len_ref[0]
    other = bias_ref[local, 0] * LOG2E
    same = bias_ref[local, 1] * LOG2E

    @pl.when(step == 0)
    def _():
        ones = jnp.ones((16, width), BF16)
        for b in range(count):
            at = pl.ds(b * width, width)
            row = ids_ref[b, 0:1, :].astype(F32)
            extra = key_extra(row, b * width, length, other, same)
            here = x_ref[b, head_dim : 2 * head_dim, :]
            keys[at, :] = jnp.concatenate([here, extra], axis=0).T
            keys_flat[:, at] = here
            vals[at, :] = jnp.concatenate([x_ref[b, 2 * head_dim : 3 * head_dim, :], ones], axis=0).T
        acc_keys[...] = jnp.zeros_like(acc_keys)
        acc_vals[...] = jnp.zeros_like(acc_vals)

    used = pl.cdiv(length, block)
    inside = step * block < length

    @pl.when(jnp.logical_not(inside))
    def _():
        for b in range(sub):
            out_ref[step * sub + b, 0:head_dim, :] = jnp.zeros((head_dim, width), BF16)

    @pl.when(inside)
    def _():
        for b in range(sub):
            at = slice(b * width, (b + 1) * width)
            here = step * sub + b
            row = ids_ref[here, 0:1, :].astype(F32)
            shift = pieces(-lse_ref[step][:, at])
            grad = grad_ref[here]
            delta = jnp.sum(grad.astype(F32) * mixed_ref[here].astype(F32), axis=0, keepdims=True)
            query[0:head_dim, at] = x_ref[here, 0:head_dim, :]
            query[head_dim:, at] = query_extra(row, shift)
            grads[0:head_dim, at] = grad
            tail = rows_of(pieces(-delta), width)
            grads[head_dim:, at] = jnp.concatenate([tail, jnp.zeros_like(tail)], axis=0).astype(BF16)
        query_rows[...] = query[...].T
        grad_rows[...] = grads[...].T
        acc_query[...] = jnp.zeros_like(acc_query)

        def one(j):
            at = pl.ds(pl.multiple_of(j * block, block), block)
            probs = jnp.exp2(dot(keys[at, :], query[...]))
            grad_probs = dot(vals[at, :], grads[...])
            grad_scores = (probs * grad_probs).astype(BF16)
            acc_vals[at, :] += dot(probs.astype(BF16), grad_rows[...])
            acc_keys[at, :] += dot(grad_scores, query_rows[...])
            acc_query[...] += dot(keys_flat[:, at], grad_scores)

        def pair(j, carry):
            one(2 * j)
            one(2 * j + 1)
            return carry

        lax.fori_loop(0, used // 2, pair, 0)

        @pl.when(used % 2 == 1)
        def _():
            one(used - 1)

        grad_query = (acc_query[...] * (1.0 / math.sqrt(head_dim))).astype(BF16)
        for b in range(sub):
            out_ref[step * sub + b, 0:head_dim, :] = grad_query[:, b * width : (b + 1) * width]

    @pl.when(step == pl.num_programs(0) - 1)
    def _():
        same_total = jnp.zeros((CLASSES, width), F32)
        all_total = jnp.zeros((CLASSES, width), F32)
        for b in range(count):
            at = pl.ds(b * width, width)
            row = ids_ref[b, 0:1, :].astype(F32)
            flat = acc_keys[at, :].T
            out_ref[b, head_dim : 2 * head_dim, :] = (flat[0:head_dim] * LN2).astype(BF16)
            out_ref[b, 2 * head_dim : 3 * head_dim, :] = acc_vals[at, :].T[0:head_dim].astype(BF16)
            by_class = flat[head_dim : head_dim + CLASSES]
            all_total += by_class
            same_total += by_class * one_hot(row)
        both = jnp.concatenate(
            [
                jnp.broadcast_to(jnp.sum(same_total, keepdims=True), (1, 128)),
                jnp.broadcast_to(jnp.sum(all_total, keepdims=True), (1, 128)),
                jnp.zeros((6, 128), F32),
            ],
            axis=0,
        )
        bias_out_ref[...] = both


def attend_backward(x, ids, grad, mixed, lse, length, bias, local, head_dim):
    count, rows, width = x.shape
    blocks, _, block = lse.shape
    seq_len = count * width
    depth = head_dim + EXTRA

    def whole(a):
        return pl.BlockSpec(a.shape, lambda i, *_: (0,) * a.ndim)

    head_spec = pl.BlockSpec((count, head_dim, width), lambda i, *_: (0, local, 0))
    return pl.pallas_call(
        functools.partial(backward_kernel, (local, head_dim, block)),
        grid_spec=pltpu.PrefetchScalarGridSpec(
            num_scalar_prefetch=2,
            grid=(blocks,),
            in_specs=[
                whole(x),
                pl.BlockSpec((count, AUX, width), lambda i, *_: (0, 3 * head_dim // AUX, 0)),
                head_spec, head_spec, whole(lse),
            ],
            out_specs=[
                pl.BlockSpec((count, 3 * head_dim, width), lambda i, *_: (0, 0, 0)),
                pl.BlockSpec((8, 128), lambda i, *_: (0, 0)),
            ],
            scratch_shapes=[
                pltpu.VMEM((seq_len, depth), BF16),
                pltpu.VMEM((head_dim, seq_len), BF16),
                pltpu.VMEM((seq_len, head_dim + 16), BF16),
                pltpu.VMEM((depth, block), BF16),
                pltpu.VMEM((head_dim + 16, block), BF16),
                pltpu.VMEM((block, depth), BF16),
                pltpu.VMEM((block, head_dim + 16), BF16),
                pltpu.VMEM((seq_len, depth), F32),
                pltpu.VMEM((seq_len, head_dim + 16), F32),
                pltpu.VMEM((head_dim, block), F32),
            ],
        ),
        out_shape=[
            jax.ShapeDtypeStruct((count, 3 * head_dim, width), BF16),
            jax.ShapeDtypeStruct((8, 128), F32),
        ],
        compiler_params=pltpu.CompilerParams(vmem_limit_bytes=48 << 20),
        cost_estimate=pl.CostEstimate(
            flops=20 * seq_len * seq_len * 256,
            bytes_accessed=x.size * 6,
            transcendentals=seq_len * seq_len,
        ),
        name="attend_backward",
    )(length, bias, x, ids, grad, mixed, lse)


def rotary_tables(places, half_dim):
    frequency = jnp.exp(-math.log(ROTARY_BASE) * jnp.arange(half_dim, dtype=F32) / half_dim)
    angles = places.astype(F32)[None, :] * frequency[:, None]
    return jnp.cos(angles), jnp.sin(angles)


def sigmoid_of(x):
    return 1.0 / (1.0 + jnp.exp2(x * -LOG2E))


def project_kernel(
    shape, tokens_ref, gain_ref, query_ref, key_ref, value_ref, cos_ref, sin_ref, ids_ref, flat_ref, *rest
):
    here, head_dim, extras = shape
    outs, flat_weights = rest[:-1], rest[-1]
    pair = pl.program_id(0)

    @pl.when(pair == 0)
    def _():
        inputs = tokens_ref[0, 0].astype(F32)
        inverse = lax.rsqrt(jnp.mean(inputs * inputs, axis=-1, keepdims=True) + EPSILON)
        flat_ref[...] = (inputs * inverse * gain_ref[...]).astype(BF16).T

    flat_weights[0:128, :] = query_ref[...].T
    flat_weights[128:256, :] = key_ref[...].T
    flat_weights[256:384, :] = value_ref[...].T
    made = dot(flat_weights[...], flat_ref[...])
    cosine, sine = cos_ref[...], sin_ref[...]
    half = head_dim // 2

    def turned(start, scale):
        first = made[start : start + half]
        second = made[start + half : start + head_dim]
        both = [first * cosine - second * sine, second * cosine + first * sine]
        return (jnp.concatenate(both, axis=0) * scale).astype(BF16)

    for at in range(128 // head_dim):
        spot = at * head_dim
        target, place = (outs[at % here], 0) if here > 1 else (outs[0], at)
        target[place, 0:head_dim, :] = turned(spot, LOG2E / math.sqrt(head_dim))
        target[place, head_dim : 2 * head_dim, :] = turned(128 + spot, 1.0)
        target[place, 2 * head_dim : 3 * head_dim, :] = made[256 + spot : 256 + spot + head_dim].astype(BF16)
        if extras[at % here]:
            target[place, 3 * head_dim :, :] = jnp.broadcast_to(ids_ref[...], (AUX, ids_ref.shape[1])).astype(BF16)


def project(tokens, unit, gain, weights, cosine, sine, ids, count, here, head_dim):
    width, model = tokens.shape[2:]
    heads = count * here
    pairs = heads * head_dim // 128
    per = 128 // head_dim // here
    extras = [h == 0 for h in range(here)]

    def fixed(a):
        return pl.BlockSpec(a.shape, lambda p: (0,) * a.ndim)

    weight_specs = [pl.BlockSpec((model, 128), lambda p, i=i: (0, i * pairs + p)) for i in range(3)]
    return pl.pallas_call(
        functools.partial(project_kernel, (here, head_dim, extras)),
        grid=(pairs,),
        in_specs=[
            pl.BlockSpec((1, 1, width, model), lambda p: unit + (0, 0)),
            fixed(gain), *weight_specs, fixed(cosine), fixed(sine), fixed(ids),
        ],
        out_specs=[pl.BlockSpec((model, width), lambda p: (0, 0))]
        + [pl.BlockSpec((per, 3 * head_dim + AUX * e, width), lambda p: (p, 0, 0)) for e in extras],
        out_shape=[jax.ShapeDtypeStruct((model, width), BF16)]
        + [jax.ShapeDtypeStruct((count, 3 * head_dim + AUX * e, width), BF16) for e in extras],
        scratch_shapes=[pltpu.VMEM((384, model), BF16)],
        compiler_params=pltpu.CompilerParams(vmem_limit_bytes=40 << 20),
        cost_estimate=pl.CostEstimate(
            flops=6 * width * model * model, bytes_accessed=12 * model * model, transcendentals=0
        ),
        name="project",
    )(tokens, gain, weights, weights, weights, cosine, sine, ids)


def middle_kernel(
    aliased, info_ref, mixed_ref, tokens_ref, cot_ref, out_w_ref, gain_ref, gate_w_ref, up_w_ref, down_w_ref, *rest
):
    if aliased:
        rest = rest[1:]
    (
        output_ref, flat_ref, hidden_ref, grad_gate_ref, grad_up_ref, grad_ffn_ref, grad_res_ref,
        grad_attn_ref, grad_mixed_ref, gain_out_ref, normed, residual, ffn_out, grad_normed,
    ) = rest
    step = pl.program_id(0)
    width = normed.shape[0]

    def valid():
        index = info_ref[1] + lax.broadcasted_iota(jnp.int32, (width, 1), 0)
        return jnp.where(index < info_ref[0], 1.0, 0.0)

    def inverse_of(x):
        return lax.rsqrt(jnp.mean(x * x, axis=-1, keepdims=True) + EPSILON)

    @pl.when(step == 0)
    def _():
        inputs = tokens_ref[0, 0].astype(F32) + dot(mixed_ref[...].T, out_w_ref[...])
        residual[...] = inputs
        made = (inputs * inverse_of(inputs) * gain_ref[...]).astype(BF16)
        normed[...] = made
        flat_ref[...] = made.T
        grad_ffn_ref[...] = (cot_ref[0, 0].astype(F32) * valid()).astype(BF16)
        ffn_out[...] = jnp.zeros_like(ffn_out)
        grad_normed[...] = jnp.zeros_like(grad_normed)

    gate = dot(normed[...], gate_w_ref[...])
    up = dot(normed[...], up_w_ref[...])
    grad_hidden = contract(grad_ffn_ref[...], down_w_ref[...], 1, 1)
    sigmoid = sigmoid_of(gate)
    silu = gate * sigmoid
    hidden = (silu * up).astype(BF16)
    grad_gate = (grad_hidden * up * (sigmoid + silu * (1.0 - sigmoid))).astype(BF16)
    grad_up = (grad_hidden * silu).astype(BF16)
    hidden_ref[...] = hidden.T
    grad_gate_ref[...] = grad_gate
    grad_up_ref[...] = grad_up
    ffn_out[...] += dot(hidden, down_w_ref[...])
    grad_normed[...] += contract(grad_gate, gate_w_ref[...], 1, 1) + contract(grad_up, up_w_ref[...], 1, 1)

    @pl.when(step == pl.num_programs(0) - 1)
    def _():
        keep = valid()
        kept = residual[...]
        output_ref[0, 0] = ((kept + ffn_out[...]) * keep).astype(BF16)
        inverse = inverse_of(kept)
        scaled = grad_normed[...] * gain_ref[...]
        mean = jnp.mean(scaled * kept, axis=-1, keepdims=True)
        grad = cot_ref[0, 0].astype(F32) * keep
        grad = grad + (inverse * scaled - kept * (inverse * inverse * inverse) * mean)
        gain_out_ref[...] = jnp.sum(grad_normed[...] * kept * inverse, axis=0, keepdims=True)
        grad_res_ref[...] = grad
        low = grad.astype(BF16)
        grad_attn_ref[...] = low
        grad_mixed_ref[...] = contract(out_w_ref[...], low, 1, 1).astype(BF16)


def middle_part(info, mixed, tokens, cotangent, unit, weights, gain, output):
    width, model = tokens.shape[2:]
    out_w, gate_w, up_w, down_w = weights
    ffn = gate_w.shape[1]
    block = 512

    def fixed(a):
        return pl.BlockSpec(a.shape, lambda f, *_: (0,) * a.ndim)

    def one(*shape):
        return pl.BlockSpec(shape, lambda f, *_: (0,) * len(shape))

    token_spec = pl.BlockSpec((1, 1, width, model), lambda f, *_: unit + (0, 0))
    operands = [info, mixed, tokens, cotangent, out_w, gain, gate_w, up_w, down_w]
    in_specs = [
        fixed(mixed), token_spec, token_spec, fixed(out_w), fixed(gain),
        pl.BlockSpec((model, block), lambda f, *_: (0, f)),
        pl.BlockSpec((model, block), lambda f, *_: (0, f)),
        pl.BlockSpec((block, model), lambda f, *_: (f, 0)),
    ]
    aliases = {}
    if output is not None:
        aliases = {len(operands): 0}
        operands.append(output)
        in_specs.append(pl.BlockSpec(memory_space=pl.ANY))
    struct = jax.ShapeDtypeStruct
    return pl.pallas_call(
        functools.partial(middle_kernel, output is not None),
        grid_spec=pltpu.PrefetchScalarGridSpec(
            num_scalar_prefetch=1,
            grid=(ffn // block,),
            in_specs=in_specs,
            out_specs=[
                token_spec, one(model, width),
                pl.BlockSpec((block, width), lambda f, *_: (f, 0)),
                pl.BlockSpec((width, block), lambda f, *_: (0, f)),
                pl.BlockSpec((width, block), lambda f, *_: (0, f)),
                one(width, model), one(width, model), one(width, model), one(model, width), one(1, model),
            ],
            scratch_shapes=[
                pltpu.VMEM((width, model), BF16),
                pltpu.VMEM((width, model), F32),
                pltpu.VMEM((width, model), F32),
                pltpu.VMEM((width, model), F32),
            ],
        ),
        out_shape=[
            struct(tokens.shape, BF16), struct((model, width), BF16), struct((ffn, width), BF16),
            struct((width, ffn), BF16), struct((width, ffn), BF16), struct((width, model), BF16),
            struct((width, model), F32), struct((width, model), BF16), struct((model, width), BF16),
            struct((1, model), F32),
        ],
        input_output_aliases=aliases,
        compiler_params=pltpu.CompilerParams(vmem_limit_bytes=62 << 20),
        cost_estimate=pl.CostEstimate(
            flops=12 * width * model * ffn, bytes_accessed=8 * model * ffn, transcendentals=width * ffn
        ),
        name="middle_part",
    )(*operands)


def weights_kernel(units, *refs):
    out_ref = refs[-1]
    total = dot(refs[0][...], refs[units][...])
    for u in range(1, units):
        total += dot(refs[u][...], refs[units + u][...])
    out_ref[...] = total.astype(BF16).reshape(out_ref.shape)


def weight_grad(lefts, rights, by_left, out_struct, out_spec, steps, into, name):
    units = len(lefts)

    def fixed(a):
        return pl.BlockSpec(a.shape, lambda n: (0, 0))

    def left_spec(a):
        return pl.BlockSpec((a.shape[0] // steps, a.shape[1]), lambda n: (n, 0))

    def right_spec(a):
        return pl.BlockSpec((a.shape[0], a.shape[1] // steps), lambda n: (0, n))

    operands = list(lefts) + list(rights)
    if by_left:
        in_specs = [left_spec(a) for a in lefts] + [fixed(a) for a in rights]
    else:
        in_specs = [fixed(a) for a in lefts] + [right_spec(a) for a in rights]
    aliases = {}
    if into is not None:
        aliases = {len(operands): 0}
        operands.append(into)
        in_specs.append(pl.BlockSpec(memory_space=pl.ANY))
    return pl.pallas_call(
        functools.partial(weights_kernel, units),
        grid=(steps,),
        in_specs=in_specs,
        out_specs=out_spec,
        out_shape=out_struct,
        input_output_aliases=aliases,
        compiler_params=pltpu.CompilerParams(vmem_limit_bytes=48 << 20),
        cost_estimate=pl.CostEstimate(
            flops=2 * units * lefts[0].shape[0] * lefts[0].shape[1] * rights[0].shape[1],
            bytes_accessed=2 * lefts[0].shape[0] * rights[0].shape[1],
            transcendentals=0,
        ),
        name=name,
    )(*operands)


def final_kernel(
    shape, tokens_ref, grad_res_ref, gain_ref, query_ref, key_ref, value_ref, cos_ref, sin_ref, *rest
):
    here, head_dim, aliased = shape
    back = rest[:here]
    rest = rest[here:]
    if aliased:
        rest = rest[1:]
    out_ref, grad_q_ref, grad_k_ref, grad_v_ref, gain_out_ref, total = rest
    step = pl.program_id(0)
    cosine, sine = cos_ref[...], sin_ref[...]
    half = head_dim // 2

    def turned(x):
        first, second = x[:half].astype(F32), x[half:].astype(F32)
        return jnp.concatenate(
            [first * cosine + second * sine, second * cosine - first * sine], axis=0
        ).astype(BF16)

    for at in range(256 // head_dim):
        place = slice(at * head_dim, (at + 1) * head_dim)
        part = back[at % here]
        grad_q_ref[place, :] = turned(part[at // here, 0:head_dim, :])
        grad_k_ref[place, :] = turned(part[at // here, head_dim : 2 * head_dim, :])
        grad_v_ref[place, :] = part[at // here, 2 * head_dim : 3 * head_dim, :]
    made = (
        contract(grad_q_ref[...].T, query_ref[...], 1, 1)
        + contract(grad_k_ref[...].T, key_ref[...], 1, 1)
        + contract(grad_v_ref[...].T, value_ref[...], 1, 1)
    )

    @pl.when(step == 0)
    def _():
        total[...] = made

    @pl.when(step > 0)
    def _():
        total[...] += made

    @pl.when(step == pl.num_programs(0) - 1)
    def _():
        inputs = tokens_ref[0, 0].astype(F32)
        inverse = lax.rsqrt(jnp.mean(inputs * inputs, axis=-1, keepdims=True) + EPSILON)
        scaled = total[...] * gain_ref[...]
        mean = jnp.mean(scaled * inputs, axis=-1, keepdims=True)
        grad = inverse * scaled - inputs * (inverse * inverse * inverse) * mean
        out_ref[0, 0] = (grad_res_ref[...] + grad).astype(BF16)
        gain_out_ref[...] = jnp.sum(total[...] * inputs * inverse, axis=0, keepdims=True)


def final_part(tokens, unit, grad_res, gain, weights, cosine, sine, back, head_dim, output):
    width, model = tokens.shape[2:]
    here = len(back)
    steps = model // 256

    def fixed(a):
        return pl.BlockSpec(a.shape, lambda c: (0,) * a.ndim)

    token_spec = pl.BlockSpec((1, 1, width, model), lambda c: unit + (0, 0))
    weight_specs = [pl.BlockSpec((model, 256), lambda c, i=i: (0, i * steps + c)) for i in range(3)]
    row_spec = pl.BlockSpec((256, width), lambda c: (c, 0))
    operands = [tokens, grad_res, gain, weights, weights, weights, cosine, sine, *back]
    in_specs = [
        token_spec, fixed(grad_res), fixed(gain), *weight_specs,
        fixed(cosine), fixed(sine),
    ] + [
        pl.BlockSpec((256 // head_dim // here, 3 * head_dim, width), lambda c: (c, 0, 0)) for _ in back
    ]
    aliases = {}
    if output is not None:
        aliases = {len(operands): 0}
        operands.append(output)
        in_specs.append(pl.BlockSpec(memory_space=pl.ANY))
    struct = jax.ShapeDtypeStruct
    return pl.pallas_call(
        functools.partial(final_kernel, (here, head_dim, output is not None)),
        grid=(steps,),
        in_specs=in_specs,
        out_specs=[token_spec, row_spec, row_spec, row_spec, pl.BlockSpec((1, model), lambda c: (0, 0))],
        out_shape=[
            struct(tokens.shape, BF16), struct((model, width), BF16), struct((model, width), BF16),
            struct((model, width), BF16), struct((1, model), F32),
        ],
        scratch_shapes=[pltpu.VMEM((width, model), F32)],
        input_output_aliases=aliases,
        compiler_params=pltpu.CompilerParams(vmem_limit_bytes=48 << 20),
        cost_estimate=pl.CostEstimate(
            flops=6 * width * model * model, bytes_accessed=12 * model * model, transcendentals=0
        ),
        name="final_part",
    )(*operands)


def attn_weights_kernel(units, *refs):
    left = refs[0:units]
    mixed = refs[units : 2 * units]
    cols = [refs[(2 + i) * units : (3 + i) * units] for i in range(4)]
    outs = refs[6 * units :]
    for i in range(4):
        total = None
        for u in range(units):
            if i < 3:
                part = contract(left[u][...], cols[i][u][...], 1, 1)
            else:
                part = dot(mixed[u][...], cols[i][u][...])
            total = part if total is None else total + part
        outs[i][...] = total.astype(BF16)


def attn_weight_grads(lefts, mixed, queries, keys, values, grad_attn):
    units = len(lefts)
    model, width = lefts[0].shape
    block = 256

    def fixed(a):
        return pl.BlockSpec(a.shape, lambda c: (0, 0))

    in_specs = [fixed(a) for a in lefts] + [fixed(a) for a in mixed]
    for _ in range(3 * units):
        in_specs.append(pl.BlockSpec((block, width), lambda c: (c, 0)))
    for _ in range(units):
        in_specs.append(pl.BlockSpec((width, block), lambda c: (0, c)))
    return pl.pallas_call(
        functools.partial(attn_weights_kernel, units),
        grid=(model // block,),
        in_specs=in_specs,
        out_specs=[pl.BlockSpec((model, block), lambda c: (0, c))] * 4,
        out_shape=[jax.ShapeDtypeStruct((model, model), BF16)] * 4,
        compiler_params=pltpu.CompilerParams(vmem_limit_bytes=48 << 20),
        cost_estimate=pl.CostEstimate(
            flops=8 * units * width * model * model, bytes_accessed=8 * model * model, transcendentals=0
        ),
        name="attn_weight_grads",
    )(*lefts, *mixed, *queries, *keys, *values, *grad_attn)


def on_device(
    tokens, cotangent, lengths, variates, positions, attn_gain, w_query, w_key, w_value, w_out,
    bias_table, ffn_gain, w_gate, w_up, w_down,
):
    micro, seqs, width, model = tokens.shape
    heads = bias_table.shape[0]
    head_dim = model // heads
    count = lax.axis_size("seq")
    here = heads // count
    ffn = w_gate.shape[1]
    devices = lax.axis_size("shard") * count
    seq_index = lax.axis_index("seq")
    bias_here = lax.dynamic_slice_in_dim(bias_table, seq_index * here, here, 0)
    units = [(m, s) for m in range(micro) for s in range(seqs)]
    attn_row, ffn_row = attn_gain[None, :], ffn_gain[None, :]

    def gather(weight):
        return lax.all_gather(weight, "shard", axis=0, tiled=True)

    def exchange(values):
        return lax.all_to_all(values, "seq", split_axis=0, concat_axis=0, tiled=True)

    def after(value, *before):
        return lax.optimization_barrier((value,) + before)[0]

    attn_joined = gather(jnp.concatenate([w_query, w_key, w_value], axis=1))
    ffn_weights = [gather(w_out), gather(w_gate), gather(w_up), gather(w_down)]

    packed_list, flats, tables = [], [], []

    def run_project(u, token):
        m, s = units[u]
        cosine, sine = rotary_tables(positions[m, s], head_dim // 2)
        ids = after(variates[m, s].astype(F32)[None, :], *token)
        flat, *packed = project(
            tokens, (m, s), attn_row, attn_joined, cosine, sine, ids, count, here, head_dim
        )
        flats.append(flat)
        tables.append((cosine, sine))
        packed_list.append(packed)

    sent = {}
    mixed_now = [None] * len(units)
    sums = {}
    mixed_tok = {}
    middle = [None] * len(units)
    grad_heads = {}
    state = {"output": None, "grads": None}
    packed_grads = {}
    returned = {}
    bias_terms = {}
    finals = [None] * len(units)

    def length_of(u, token):
        m, s = units[u]
        return after(lengths[m, s].reshape(1), *token)

    def run_forward(u, h, token):
        mixed_now[u], sums[u, h] = attend_forward(
            sent[u, h], sent[u, 0], length_of(u, token), bias_here, mixed_now[u], h, here, head_dim
        )
        return sums[u, h]

    def run_middle(u, token):
        m, s = units[u]
        info = jnp.stack([lengths[m, s], seq_index * width]).astype(jnp.int32)
        state["output"], *middle[u] = middle_part(
            after(info, *token), mixed_tok[u], tokens, cotangent, (m, s), ffn_weights, ffn_row,
            state["output"],
        )
        return middle[u][8]

    def run_backward(u, h, token):
        packed_grads[u, h], both = attend_backward(
            sent[u, h], sent[u, 0], grad_heads[u], mixed_now[u], sums[u, h], length_of(u, token),
            bias_here, h, head_dim,
        )
        bias_terms[u, h] = jnp.stack([both[1, 0] - both[0, 0], both[0, 0]])
        return both

    def run_final(u, token):
        m, s = units[u]
        cosine, sine = tables[u]
        state["grads"], *finals[u] = final_part(
            tokens, (m, s), middle[u][5], after(attn_row, *token), attn_joined, cosine, sine,
            [returned[u, h] for h in range(here)], head_dim, state["grads"],
        )
        return finals[u][3]

    rows = model // devices
    fold = ffn // model
    part = ffn // fold

    def run_weights(token):
        if rows % 16:

            def plain(left, right):
                total = sum(dot(item[left], item[right]) for item in middle)
                return total.astype(BF16)

            def spread(total):
                split = total.reshape(devices, rows, fold, part)
                return jnp.swapaxes(split, 1, 2).reshape(ffn, part)

            return jnp.concatenate([plain(1, 4), spread(plain(0, 2)), spread(plain(0, 3))], axis=1)
        struct = jax.ShapeDtypeStruct((devices, fold, rows, 3 * part), BF16)
        block = 512
        per = part // block
        down = pl.BlockSpec((block // (fold * rows), fold, rows, model), lambda n: (n, 0, 0, 0))
        gate = pl.BlockSpec((devices, 1, rows, block), lambda n: (0, n // per, 0, per + n % per))
        up = pl.BlockSpec((devices, 1, rows, block), lambda n: (0, n // per, 0, 2 * per + n % per))
        steps = ffn // block
        lefts = [item[0] for item in middle]
        firsts = [after(middle[0][4], *token)] + [item[4] for item in middle[1:]]
        terms = weight_grad(
            [item[1] for item in middle], firsts, True, struct, down, steps, None, "down_grad"
        )
        terms = weight_grad(
            lefts, [item[2] for item in middle], False, struct, gate, steps, terms, "gate_grad"
        )
        terms = weight_grad(
            lefts, [item[3] for item in middle], False, struct, up, steps, terms, "up_grad"
        )
        return terms.reshape(ffn, 3 * part)

    holder = {}

    def weights_work(token):
        holder["terms"] = run_weights(token)
        return holder["terms"]

    def send_packed(u, h):
        def keep(moved):
            sent[u, h] = moved

        return lambda: packed_list[u][h], keep

    def send_mixed(u):
        def keep(moved):
            mixed_tok[u] = moved.reshape(model, width)

        return lambda: mixed_now[u], keep

    def send_heads(u):
        def keep(moved):
            grad_heads[u] = moved

        return lambda: middle[u][7].reshape(count, here * head_dim, width), keep

    def send_back(u, h):
        def keep(moved):
            returned[u, h] = moved

        return lambda: packed_grads[u, h], keep

    def work_project(u):
        def work(token):
            run_project(u, token)
            return flats[u]

        return work

    def work(function, *args):
        return lambda token: function(*args, token)

    total = len(units)
    order = [(u, h) for u in range(total) for h in range(here)]
    if total == 2 and here == 2:
        steps = [
            (work_project(0), None),
            (work_project(1), send_packed(0, 0)),
            (work(run_forward, 0, 0), send_packed(0, 1)),
            (work(run_forward, 0, 1), send_packed(1, 0)),
            (work(run_forward, 1, 0), send_mixed(0)),
            (work(run_middle, 0), send_packed(1, 1)),
            (work(run_forward, 1, 1), send_heads(0)),
            (work(run_backward, 0, 0), send_mixed(1)),
            (work(run_middle, 1), send_back(0, 0)),
            (weights_work, send_heads(1)),
            (work(run_backward, 0, 1), None),
            (work(run_backward, 1, 0), send_back(0, 1)),
            (work(run_backward, 1, 1), send_back(1, 0)),
            (work(run_final, 0), send_back(1, 1)),
            (work(run_final, 1), None),
        ]
    else:
        steps = [(work_project(u), None) for u in range(total)]
        steps += [(None, send_packed(*at)) for at in order]
        for u in range(total):
            steps += [(work(run_forward, u, h), None) for h in range(here)]
            steps += [(None, send_mixed(u))]
        for u in range(total):
            steps += [(work(run_middle, u), None), (None, send_heads(u))]
        steps += [(weights_work, None)]
        for at in order:
            steps += [(work(run_backward, *at), None), (None, send_back(*at))]
        steps += [(work(run_final, u), None) for u in range(total)]

    token = ()
    for task, send in steps:
        done = ()
        moved = None
        if send is not None:
            moved = exchange(after(send[0](), *token))
            done = (moved,)
        if task is not None:
            done = done + (task(token),)
        if send is not None:
            send[1](moved)
        token = done
    ffn_owned = lax.psum_scatter(holder["terms"], ("shard", "seq"), scatter_dimension=0, tiled=True)
    acc_bias = sum(jnp.stack([bias_terms[u, h] for h in range(here)]) for u in range(len(units)))
    attn_terms = attn_weight_grads(
        flats, [mixed_tok[u] for u in range(len(units))],
        [item[0] for item in finals], [item[1] for item in finals], [item[2] for item in finals],
        [item[6] for item in middle],
    )
    pad = (-(4 * model)) % 384
    attn_terms = jnp.concatenate([*attn_terms, jnp.zeros((model, pad), BF16)], axis=1)
    attn_owned = lax.psum_scatter(attn_terms, ("shard", "seq"), scatter_dimension=0, tiled=True)

    bias_full = lax.dynamic_update_slice(
        jnp.zeros((heads, 2), F32), acc_bias, (seq_index * here, jnp.int32(0))
    )
    grad_attn_gain, grad_ffn_gain, grad_bias = lax.psum(
        (sum(item[3][0] for item in finals), sum(item[8][0] for item in middle), bias_full),
        ("shard", "seq"),
    )

    def unspread(owned):
        return jnp.swapaxes(owned.reshape(fold, rows, part), 0, 1).reshape(rows, ffn).astype(F32)

    attn_owned = attn_owned.astype(F32)
    return (
        state["output"],
        state["grads"],
        grad_attn_gain,
        attn_owned[:, 0:model],
        attn_owned[:, model : 2 * model],
        attn_owned[:, 2 * model : 3 * model],
        attn_owned[:, 3 * model : 4 * model],
        grad_bias,
        grad_ffn_gain,
        unspread(ffn_owned[:, model : model + part]),
        unspread(ffn_owned[:, model + part : model + 2 * part]),
        ffn_owned[:, 0:model].astype(F32),
    )


def solution(mesh):
    token_spec = P(None, "shard", "seq", None)
    row_spec = P("shard", None)
    in_specs = (
        token_spec, token_spec, P(None, "shard"), P(None, "shard", "seq"), P(None, "shard", "seq"),
        P(), row_spec, row_spec, row_spec, row_spec, P(), P(), row_spec, row_spec, row_spec,
    )
    owned = P(("shard", "seq"), None)
    out_specs = (
        token_spec, token_spec, P(), owned, owned, owned, owned, P(), P(), owned, owned, owned,
    )
    return jax.shard_map(
        on_device, mesh=mesh, in_specs=in_specs, out_specs=out_specs, check_vma=False
    )
```

```python
import functools
import math

import jax
import jax.numpy as jnp
from jax import lax
from jax.experimental import pallas as pl
from jax.experimental.pallas import tpu as pltpu
from jax.sharding import PartitionSpec as P

EPSILON = 1e-06
ROTARY_BASE = 10000.0
LOG2E = 1.4426950408889634
LN2 = 0.6931471805599453
CLASSES = 8
AUX = 16
EXTRA = 32
MASKED = -1.5e9
FAR = 1e30
F32 = jnp.float32
BF16 = jnp.bfloat16


def dot(a, b):
    return jnp.dot(a, b, preferred_element_type=F32)


def contract(a, b, da, db):
    return lax.dot_general(a, b, (((da,), (db,)), ((), ())), preferred_element_type=F32)


def pieces(x):
    high = x.astype(BF16).astype(F32)
    rest = x - high
    mid = rest.astype(BF16).astype(F32)
    low = (rest - mid).astype(BF16).astype(F32)
    return high, mid, low


def one_hot(row):
    classes = lax.broadcasted_iota(jnp.int32, (CLASSES, row.shape[1]), 0).astype(F32)
    return jnp.where(classes == row, 1.0, 0.0)


def rows_of(values, width):
    index = lax.broadcasted_iota(jnp.int32, (8, width), 0)
    out = jnp.zeros((8, width), F32)
    for at, value in enumerate(values):
        out = jnp.where(index == at, value, out)
    return out


def key_extra(row, start, length, other, same):
    width = row.shape[1]
    hot = one_hot(row)
    step = pieces(jnp.full((1, width), same - other, F32))
    base = pieces(jnp.full((1, width), other, F32))
    index = start + lax.broadcasted_iota(jnp.int32, (1, width), 1)
    mask = jnp.where(index < length, 0.0, MASKED)
    tail = rows_of(base + (mask, 1.0, 1.0, 1.0), width)
    return jnp.concatenate([hot * step[0], hot * step[1], hot * step[2], tail], axis=0).astype(BF16)


def query_extra(row, shift):
    hot = one_hot(row)
    tail = rows_of((1.0, 1.0, 1.0, 1.0) + shift, row.shape[1])
    return jnp.concatenate([hot, hot, hot, tail], axis=0).astype(BF16)


def forward_kernel(
    shape, len_ref, bias_ref, x_ref, ids_ref, *rest
):
    local, head_dim, block, aliased = shape
    if aliased:
        rest = rest[1:]
    mixed_ref, lse_ref, keys, vals, query, score, peak, total = rest
    count, _, width = x_ref.shape
    sub = block // width
    step = pl.program_id(0)
    length = len_ref[0]
    other = bias_ref[local, 0] * LOG2E
    same = bias_ref[local, 1] * LOG2E

    @pl.when(step == 0)
    def _():
        for b in range(count):
            at = pl.ds(b * width, width)
            row = ids_ref[b, 0:1, :].astype(F32)
            extra = key_extra(row, b * width, length, other, same)
            full = jnp.concatenate([x_ref[b, head_dim : 2 * head_dim, :], extra], axis=0)
            keys[at, :] = full.T
            vals[0:head_dim, at] = x_ref[b, 2 * head_dim : 3 * head_dim, :]
        vals[head_dim:, :] = jnp.ones((16, vals.shape[1]), BF16)

    used = pl.cdiv(length, block)
    inside = step * block < length

    @pl.when(jnp.logical_not(inside))
    def _():
        mixed_ref[...] = jnp.zeros_like(mixed_ref)
        lse_ref[...] = jnp.full(lse_ref.shape, FAR, F32)

    @pl.when(inside)
    def _():
        for b in range(sub):
            at = slice(b * width, (b + 1) * width)
            row = ids_ref[step * sub + b, 0:1, :].astype(F32)
            query[0:head_dim, at] = x_ref[step * sub + b, 0:head_dim, :]
            query[head_dim:, at] = query_extra(row, (0.0, 0.0, 0.0))
        peak[...] = jnp.full(peak.shape, -FAR, F32)
        total[...] = jnp.zeros_like(total)

        def span(j):
            return pl.ds(pl.multiple_of(j * block, block), block)

        def scores_of(j):
            return dot(keys[span(j), :], query[...])

        def one(j, now, ahead):
            if ahead:
                score[1 - now] = scores_of(j + 1)
            current = score[now]
            before = peak[...]
            top = jnp.maximum(before, jnp.max(current, axis=0, keepdims=True))
            weight = jnp.exp2(current - top).astype(BF16)
            peak[...] = top
            total[...] = total[...] * jnp.exp2(before - top) + dot(vals[:, span(j)], weight)

        score[0] = scores_of(0)
        pairs = (used - 1) // 2

        def pair(j, carry):
            one(2 * j, 0, True)
            one(2 * j + 1, 1, True)
            return carry

        lax.fori_loop(0, pairs, pair, 0)
        last = 2 * pairs

        @pl.when(used - last == 1)
        def _():
            one(last, 0, False)

        @pl.when(used - last == 2)
        def _():
            one(last, 0, True)
            one(last + 1, 1, False)

        mass = total[head_dim : head_dim + 1, :]
        mixed = (total[0:head_dim, :] / mass).astype(BF16)
        for b in range(sub):
            mixed_ref[b] = mixed[:, b * width : (b + 1) * width]
        lse_ref[0] = peak[...] + jnp.log2(mass)


def attend_forward(x, ids, length, bias, mixed, local, heads_here, head_dim):
    count, rows, width = x.shape
    block = max(width, 512)
    seq_len = count * width
    blocks = seq_len // block
    depth = head_dim + EXTRA
    whole = pl.BlockSpec((count, rows, width), lambda i, *_: (0, 0, 0))
    operands = [length, bias, x, ids]
    in_specs = [whole, pl.BlockSpec((count, AUX, width), lambda i, *_: (0, 3 * head_dim // AUX, 0))]
    aliases = {}
    if mixed is not None:
        operands.append(mixed)
        in_specs.append(pl.BlockSpec(memory_space=pl.ANY))
        aliases = {4: 0}
    return pl.pallas_call(
        functools.partial(forward_kernel, (local, head_dim, block, mixed is not None)),
        grid_spec=pltpu.PrefetchScalarGridSpec(
            num_scalar_prefetch=2,
            grid=(blocks,),
            in_specs=in_specs,
            out_specs=[
                pl.BlockSpec((block // width, head_dim, width), lambda i, *_: (i, local, 0)),
                pl.BlockSpec((1, 1, block), lambda i, *_: (i, 0, 0)),
            ],
            scratch_shapes=[
                pltpu.VMEM((seq_len, depth), BF16),
                pltpu.VMEM((head_dim + 16, seq_len), BF16),
                pltpu.VMEM((depth, block), BF16),
                pltpu.VMEM((2, block, block), F32),
                pltpu.VMEM((1, block), F32),
                pltpu.VMEM((head_dim + 16, block), F32),
            ],
        ),
        out_shape=[
            jax.ShapeDtypeStruct((count, heads_here * head_dim, width), BF16),
            jax.ShapeDtypeStruct((blocks, 1, block), F32),
        ],
        input_output_aliases=aliases,
        compiler_params=pltpu.CompilerParams(vmem_limit_bytes=62 << 20),
        cost_estimate=pl.CostEstimate(
            flops=8 * seq_len * seq_len * 256,
            bytes_accessed=x.size * 4,
            transcendentals=seq_len * seq_len,
        ),
        name="attend_forward",
    )(*operands)


def backward_kernel(
    shape, len_ref, bias_ref, x_ref, ids_ref, grad_ref, mixed_ref, lse_ref, out_ref, bias_out_ref,
    keys, keys_flat, vals, query, grads, query_rows, grad_rows, acc_keys, acc_vals, acc_query,
):
    local, head_dim, block = shape
    count, _, width = x_ref.shape
    sub = block // width
    step = pl.program_id(0)
    length = len_ref[0]
    other = bias_ref[local, 0] * LOG2E
    same = bias_ref[local, 1] * LOG2E

    @pl.when(step == 0)
    def _():
        ones = jnp.ones((16, width), BF16)
        for b in range(count):
            at = pl.ds(b * width, width)
            row = ids_ref[b, 0:1, :].astype(F32)
            extra = key_extra(row, b * width, length, other, same)
            here = x_ref[b, head_dim : 2 * head_dim, :]
            keys[at, :] = jnp.concatenate([here, extra], axis=0).T
            keys_flat[:, at] = here
            vals[at, :] = jnp.concatenate([x_ref[b, 2 * head_dim : 3 * head_dim, :], ones], axis=0).T
        acc_keys[...] = jnp.zeros_like(acc_keys)
        acc_vals[...] = jnp.zeros_like(acc_vals)

    used = pl.cdiv(length, block)
    inside = step * block < length

    @pl.when(jnp.logical_not(inside))
    def _():
        for b in range(sub):
            out_ref[step * sub + b, 0:head_dim, :] = jnp.zeros((head_dim, width), BF16)

    @pl.when(inside)
    def _():
        for b in range(sub):
            at = slice(b * width, (b + 1) * width)
            here = step * sub + b
            row = ids_ref[here, 0:1, :].astype(F32)
            shift = pieces(-lse_ref[step][:, at])
            grad = grad_ref[here]
            delta = jnp.sum(grad.astype(F32) * mixed_ref[here].astype(F32), axis=0, keepdims=True)
            query[0:head_dim, at] = x_ref[here, 0:head_dim, :]
            query[head_dim:, at] = query_extra(row, shift)
            grads[0:head_dim, at] = grad
            tail = rows_of(pieces(-delta), width)
            grads[head_dim:, at] = jnp.concatenate([tail, jnp.zeros_like(tail)], axis=0).astype(BF16)
        query_rows[...] = query[...].T
        grad_rows[...] = grads[...].T
        acc_query[...] = jnp.zeros_like(acc_query)

        def one(j):
            at = pl.ds(pl.multiple_of(j * block, block), block)
            probs = jnp.exp2(dot(keys[at, :], query[...]))
            grad_probs = dot(vals[at, :], grads[...])
            grad_scores = (probs * grad_probs).astype(BF16)
            acc_vals[at, :] += dot(probs.astype(BF16), grad_rows[...])
            acc_keys[at, :] += dot(grad_scores, query_rows[...])
            acc_query[...] += dot(keys_flat[:, at], grad_scores)

        def pair(j, carry):
            one(2 * j)
            one(2 * j + 1)
            return carry

        lax.fori_loop(0, used // 2, pair, 0)

        @pl.when(used % 2 == 1)
        def _():
            one(used - 1)

        grad_query = (acc_query[...] * (1.0 / math.sqrt(head_dim))).astype(BF16)
        for b in range(sub):
            out_ref[step * sub + b, 0:head_dim, :] = grad_query[:, b * width : (b + 1) * width]

    @pl.when(step == pl.num_programs(0) - 1)
    def _():
        same_total = jnp.zeros((CLASSES, width), F32)
        all_total = jnp.zeros((CLASSES, width), F32)
        for b in range(count):
            at = pl.ds(b * width, width)
            row = ids_ref[b, 0:1, :].astype(F32)
            flat = acc_keys[at, :].T
            out_ref[b, head_dim : 2 * head_dim, :] = (flat[0:head_dim] * LN2).astype(BF16)
            out_ref[b, 2 * head_dim : 3 * head_dim, :] = acc_vals[at, :].T[0:head_dim].astype(BF16)
            by_class = flat[head_dim : head_dim + CLASSES]
            all_total += by_class
            same_total += by_class * one_hot(row)
        same_sum = jnp.sum(same_total, keepdims=True)
        other_sum = jnp.sum(all_total, keepdims=True) - same_sum
        lane = lax.broadcasted_iota(jnp.int32, (8, 128), 1)
        bias_out_ref[...] = jnp.where(lane == 0, other_sum, jnp.where(lane == 1, same_sum, 0.0))


def attend_backward(x, ids, grad, mixed, lse, length, bias, local, head_dim):
    count, rows, width = x.shape
    blocks, _, block = lse.shape
    seq_len = count * width
    depth = head_dim + EXTRA

    def whole(a):
        return pl.BlockSpec(a.shape, lambda i, *_: (0,) * a.ndim)

    head_spec = pl.BlockSpec((count, head_dim, width), lambda i, *_: (0, local, 0))
    return pl.pallas_call(
        functools.partial(backward_kernel, (local, head_dim, block)),
        grid_spec=pltpu.PrefetchScalarGridSpec(
            num_scalar_prefetch=2,
            grid=(blocks,),
            in_specs=[
                whole(x),
                pl.BlockSpec((count, AUX, width), lambda i, *_: (0, 3 * head_dim // AUX, 0)),
                head_spec, head_spec, whole(lse),
            ],
            out_specs=[
                pl.BlockSpec((count, 3 * head_dim, width), lambda i, *_: (0, 0, 0)),
                pl.BlockSpec((8, 128), lambda i, *_: (0, 0)),
            ],
            scratch_shapes=[
                pltpu.VMEM((seq_len, depth), BF16),
                pltpu.VMEM((head_dim, seq_len), BF16),
                pltpu.VMEM((seq_len, head_dim + 16), BF16),
                pltpu.VMEM((depth, block), BF16),
                pltpu.VMEM((head_dim + 16, block), BF16),
                pltpu.VMEM((block, depth), BF16),
                pltpu.VMEM((block, head_dim + 16), BF16),
                pltpu.VMEM((seq_len, depth), F32),
                pltpu.VMEM((seq_len, head_dim + 16), F32),
                pltpu.VMEM((head_dim, block), F32),
            ],
        ),
        out_shape=[
            jax.ShapeDtypeStruct((count, 3 * head_dim, width), BF16),
            jax.ShapeDtypeStruct((8, 128), F32),
        ],
        compiler_params=pltpu.CompilerParams(vmem_limit_bytes=62 << 20),
        cost_estimate=pl.CostEstimate(
            flops=20 * seq_len * seq_len * 256,
            bytes_accessed=x.size * 6,
            transcendentals=seq_len * seq_len,
        ),
        name="attend_backward",
    )(length, bias, x, ids, grad, mixed, lse)


def rotary_tables(places, half_dim):
    frequency = jnp.exp(-math.log(ROTARY_BASE) * jnp.arange(half_dim, dtype=F32) / half_dim)
    angles = places.astype(F32)[None, :] * frequency[:, None]
    return jnp.cos(angles), jnp.sin(angles)


def sigmoid_of(x):
    return 1.0 / (1.0 + jnp.exp2(x * -LOG2E))


def project_kernel(
    shape, tokens_ref, gain_ref, query_ref, key_ref, value_ref, cos_ref, sin_ref, ids_ref, flat_ref, *rest
):
    here, head_dim, extras = shape
    outs, flat_weights = rest[:-1], rest[-1]
    pair = pl.program_id(0)

    @pl.when(pair == 0)
    def _():
        inputs = tokens_ref[0, 0].astype(F32)
        inverse = lax.rsqrt(jnp.mean(inputs * inputs, axis=-1, keepdims=True) + EPSILON)
        flat_ref[...] = (inputs * inverse * gain_ref[...]).astype(BF16).T

    flat_weights[0:128, :] = query_ref[...].T
    flat_weights[128:256, :] = key_ref[...].T
    flat_weights[256:384, :] = value_ref[...].T
    made = dot(flat_weights[...], flat_ref[...])
    cosine, sine = cos_ref[...], sin_ref[...]
    half = head_dim // 2

    def turned(start, scale):
        first = made[start : start + half]
        second = made[start + half : start + head_dim]
        both = [first * cosine - second * sine, second * cosine + first * sine]
        return (jnp.concatenate(both, axis=0) * scale).astype(BF16)

    for at in range(128 // head_dim):
        spot = at * head_dim
        target, place = (outs[at % here], 0) if here > 1 else (outs[0], at)
        target[place, 0:head_dim, :] = turned(spot, LOG2E / math.sqrt(head_dim))
        target[place, head_dim : 2 * head_dim, :] = turned(128 + spot, 1.0)
        target[place, 2 * head_dim : 3 * head_dim, :] = made[256 + spot : 256 + spot + head_dim].astype(BF16)
        if extras[at % here]:
            target[place, 3 * head_dim :, :] = jnp.broadcast_to(ids_ref[...], (AUX, ids_ref.shape[1])).astype(BF16)


def project(tokens, unit, gain, weights, cosine, sine, ids, count, here, head_dim):
    width, model = tokens.shape[2:]
    heads = count * here
    pairs = heads * head_dim // 128
    per = 128 // head_dim // here
    extras = [h == 0 for h in range(here)]

    def fixed(a):
        return pl.BlockSpec(a.shape, lambda p: (0,) * a.ndim)

    weight_specs = [pl.BlockSpec((model, 128), lambda p, i=i: (0, i * pairs + p)) for i in range(3)]
    return pl.pallas_call(
        functools.partial(project_kernel, (here, head_dim, extras)),
        grid=(pairs,),
        in_specs=[
            pl.BlockSpec((1, 1, width, model), lambda p: unit + (0, 0)),
            fixed(gain), *weight_specs, fixed(cosine), fixed(sine), fixed(ids),
        ],
        out_specs=[pl.BlockSpec((model, width), lambda p: (0, 0))]
        + [pl.BlockSpec((per, 3 * head_dim + AUX * e, width), lambda p: (p, 0, 0)) for e in extras],
        out_shape=[jax.ShapeDtypeStruct((model, width), BF16)]
        + [jax.ShapeDtypeStruct((count, 3 * head_dim + AUX * e, width), BF16) for e in extras],
        scratch_shapes=[pltpu.VMEM((384, model), BF16)],
        compiler_params=pltpu.CompilerParams(vmem_limit_bytes=62 << 20),
        cost_estimate=pl.CostEstimate(
            flops=6 * width * model * model, bytes_accessed=12 * model * model, transcendentals=0
        ),
        name="project",
    )(tokens, gain, weights, weights, weights, cosine, sine, ids)


def middle_kernel(
    aliased, info_ref, mixed_ref, tokens_ref, cot_ref, out_w_ref, gain_ref, gate_w_ref, up_w_ref, down_w_ref, *rest
):
    if aliased:
        rest = rest[1:]
    (
        output_ref, flat_ref, hidden_ref, grad_gate_ref, grad_up_ref, grad_ffn_ref, grad_res_ref,
        grad_attn_ref, grad_mixed_ref, gain_out_ref, normed, residual, ffn_out, grad_normed,
    ) = rest
    step = pl.program_id(0)
    width = normed.shape[0]

    def valid():
        index = info_ref[1] + lax.broadcasted_iota(jnp.int32, (width, 1), 0)
        return jnp.where(index < info_ref[0], 1.0, 0.0)

    def inverse_of(x):
        return lax.rsqrt(jnp.mean(x * x, axis=-1, keepdims=True) + EPSILON)

    @pl.when(step == 0)
    def _():
        inputs = tokens_ref[0, 0].astype(F32) + dot(mixed_ref[...].T, out_w_ref[...])
        residual[...] = inputs
        made = (inputs * inverse_of(inputs) * gain_ref[...]).astype(BF16)
        normed[...] = made
        flat_ref[...] = made.T
        grad_ffn_ref[...] = (cot_ref[0, 0].astype(F32) * valid()).astype(BF16)
        ffn_out[...] = jnp.zeros_like(ffn_out)
        grad_normed[...] = jnp.zeros_like(grad_normed)

    gate = dot(normed[...], gate_w_ref[...])
    up = dot(normed[...], up_w_ref[...])
    grad_hidden = contract(grad_ffn_ref[...], down_w_ref[...], 1, 1)
    sigmoid = sigmoid_of(gate)
    silu = gate * sigmoid
    hidden = (silu * up).astype(BF16)
    grad_gate = (grad_hidden * up * (sigmoid + silu * (1.0 - sigmoid))).astype(BF16)
    grad_up = (grad_hidden * silu).astype(BF16)
    hidden_ref[...] = hidden.T
    grad_gate_ref[...] = grad_gate
    grad_up_ref[...] = grad_up
    ffn_out[...] += dot(hidden, down_w_ref[...])
    grad_normed[...] += contract(grad_gate, gate_w_ref[...], 1, 1) + contract(grad_up, up_w_ref[...], 1, 1)

    @pl.when(step == pl.num_programs(0) - 1)
    def _():
        keep = valid()
        kept = residual[...]
        output_ref[0, 0] = ((kept + ffn_out[...]) * keep).astype(BF16)
        inverse = inverse_of(kept)
        scaled = grad_normed[...] * gain_ref[...]
        mean = jnp.mean(scaled * kept, axis=-1, keepdims=True)
        grad = cot_ref[0, 0].astype(F32) * keep
        grad = grad + (inverse * scaled - kept * (inverse * inverse * inverse) * mean)
        gain_out_ref[...] = jnp.sum(grad_normed[...] * kept * inverse, axis=0, keepdims=True)
        grad_res_ref[...] = grad
        low = grad.astype(BF16)
        grad_attn_ref[...] = low
        grad_mixed_ref[...] = contract(out_w_ref[...], low, 1, 1).astype(BF16)


def middle_part(info, mixed, tokens, cotangent, unit, weights, gain, output):
    width, model = tokens.shape[2:]
    out_w, gate_w, up_w, down_w = weights
    ffn = gate_w.shape[1]
    block = 512

    def fixed(a):
        return pl.BlockSpec(a.shape, lambda f, *_: (0,) * a.ndim)

    def one(*shape):
        return pl.BlockSpec(shape, lambda f, *_: (0,) * len(shape))

    token_spec = pl.BlockSpec((1, 1, width, model), lambda f, *_: unit + (0, 0))
    operands = [info, mixed, tokens, cotangent, out_w, gain, gate_w, up_w, down_w]
    in_specs = [
        fixed(mixed), token_spec, token_spec, fixed(out_w), fixed(gain),
        pl.BlockSpec((model, block), lambda f, *_: (0, f)),
        pl.BlockSpec((model, block), lambda f, *_: (0, f)),
        pl.BlockSpec((block, model), lambda f, *_: (f, 0)),
    ]
    aliases = {}
    if output is not None:
        aliases = {len(operands): 0}
        operands.append(output)
        in_specs.append(pl.BlockSpec(memory_space=pl.ANY))
    struct = jax.ShapeDtypeStruct
    return pl.pallas_call(
        functools.partial(middle_kernel, output is not None),
        grid_spec=pltpu.PrefetchScalarGridSpec(
            num_scalar_prefetch=1,
            grid=(ffn // block,),
            in_specs=in_specs,
            out_specs=[
                token_spec, one(model, width),
                pl.BlockSpec((block, width), lambda f, *_: (f, 0)),
                pl.BlockSpec((width, block), lambda f, *_: (0, f)),
                pl.BlockSpec((width, block), lambda f, *_: (0, f)),
                one(width, model), one(width, model), one(width, model), one(model, width), one(1, model),
            ],
            scratch_shapes=[
                pltpu.VMEM((width, model), BF16),
                pltpu.VMEM((width, model), F32),
                pltpu.VMEM((width, model), F32),
                pltpu.VMEM((width, model), F32),
            ],
        ),
        out_shape=[
            struct(tokens.shape, BF16), struct((model, width), BF16), struct((ffn, width), BF16),
            struct((width, ffn), BF16), struct((width, ffn), BF16), struct((width, model), BF16),
            struct((width, model), F32), struct((width, model), BF16), struct((model, width), BF16),
            struct((1, model), F32),
        ],
        input_output_aliases=aliases,
        compiler_params=pltpu.CompilerParams(vmem_limit_bytes=62 << 20),
        cost_estimate=pl.CostEstimate(
            flops=12 * width * model * ffn, bytes_accessed=8 * model * ffn, transcendentals=width * ffn
        ),
        name="middle_part",
    )(*operands)


def final_kernel(
    shape, tokens_ref, grad_res_ref, gain_ref, query_ref, key_ref, value_ref, cos_ref, sin_ref, *rest
):
    here, head_dim, aliased = shape
    back = rest[:here]
    rest = rest[here:]
    if aliased:
        rest = rest[1:]
    out_ref, grad_q_ref, grad_k_ref, grad_v_ref, gain_out_ref, total = rest
    step = pl.program_id(0)
    cosine, sine = cos_ref[...], sin_ref[...]
    half = head_dim // 2

    def turned(x):
        first, second = x[:half].astype(F32), x[half:].astype(F32)
        return jnp.concatenate(
            [first * cosine + second * sine, second * cosine - first * sine], axis=0
        ).astype(BF16)

    for at in range(256 // head_dim):
        place = slice(at * head_dim, (at + 1) * head_dim)
        part = back[at % here]
        grad_q_ref[place, :] = turned(part[at // here, 0:head_dim, :])
        grad_k_ref[place, :] = turned(part[at // here, head_dim : 2 * head_dim, :])
        grad_v_ref[place, :] = part[at // here, 2 * head_dim : 3 * head_dim, :]
    made = (
        contract(grad_q_ref[...].T, query_ref[...], 1, 1)
        + contract(grad_k_ref[...].T, key_ref[...], 1, 1)
        + contract(grad_v_ref[...].T, value_ref[...], 1, 1)
    )

    @pl.when(step == 0)
    def _():
        total[...] = made

    @pl.when(step > 0)
    def _():
        total[...] += made

    @pl.when(step == pl.num_programs(0) - 1)
    def _():
        inputs = tokens_ref[0, 0].astype(F32)
        inverse = lax.rsqrt(jnp.mean(inputs * inputs, axis=-1, keepdims=True) + EPSILON)
        scaled = total[...] * gain_ref[...]
        mean = jnp.mean(scaled * inputs, axis=-1, keepdims=True)
        grad = inverse * scaled - inputs * (inverse * inverse * inverse) * mean
        out_ref[0, 0] = (grad_res_ref[...] + grad).astype(BF16)
        gain_out_ref[...] = jnp.sum(total[...] * inputs * inverse, axis=0, keepdims=True)


def final_part(tokens, unit, grad_res, gain, weights, cosine, sine, back, head_dim, output):
    width, model = tokens.shape[2:]
    here = len(back)
    steps = model // 256

    def fixed(a):
        return pl.BlockSpec(a.shape, lambda c: (0,) * a.ndim)

    token_spec = pl.BlockSpec((1, 1, width, model), lambda c: unit + (0, 0))
    weight_specs = [pl.BlockSpec((model, 256), lambda c, i=i: (0, i * steps + c)) for i in range(3)]
    row_spec = pl.BlockSpec((256, width), lambda c: (c, 0))
    operands = [tokens, grad_res, gain, weights, weights, weights, cosine, sine, *back]
    in_specs = [
        token_spec, fixed(grad_res), fixed(gain), *weight_specs,
        fixed(cosine), fixed(sine),
    ] + [
        pl.BlockSpec((256 // head_dim // here, 3 * head_dim, width), lambda c: (c, 0, 0)) for _ in back
    ]
    aliases = {}
    if output is not None:
        aliases = {len(operands): 0}
        operands.append(output)
        in_specs.append(pl.BlockSpec(memory_space=pl.ANY))
    struct = jax.ShapeDtypeStruct
    return pl.pallas_call(
        functools.partial(final_kernel, (here, head_dim, output is not None)),
        grid=(steps,),
        in_specs=in_specs,
        out_specs=[token_spec, row_spec, row_spec, row_spec, pl.BlockSpec((1, model), lambda c: (0, 0))],
        out_shape=[
            struct(tokens.shape, BF16), struct((model, width), BF16), struct((model, width), BF16),
            struct((model, width), BF16), struct((1, model), F32),
        ],
        scratch_shapes=[pltpu.VMEM((width, model), F32)],
        input_output_aliases=aliases,
        compiler_params=pltpu.CompilerParams(vmem_limit_bytes=62 << 20),
        cost_estimate=pl.CostEstimate(
            flops=6 * width * model * model, bytes_accessed=12 * model * model, transcendentals=0
        ),
        name="final_part",
    )(*operands)


def picked_kernel(units, rows, places, flipped, split, table_ref, *refs):
    weights = len(places)
    lefts = refs[0:units]
    rights = refs[units : units * (1 + weights)]
    outs = refs[units * (1 + weights) : units * (1 + weights) + weights * split]
    picked = refs[units * (1 + weights) + weights * split :]

    @pl.when(pl.program_id(0) == 0)
    def _():
        for w, (start, size) in enumerate(places):
            for p in range(size):
                at = pl.ds(pl.multiple_of(table_ref[start + p] * rows, rows), rows)
                for u in range(units):
                    picked[w * units + u][p * rows : (p + 1) * rows, :] = lefts[u][at, :]

    for w in range(weights):
        total = None
        for u in range(units):
            right = rights[w * units + u][...]
            left = picked[w * units + u][...]
            made = contract(left, right, 1, 1) if flipped else dot(left, right)
            total = made if total is None else total + made
        height = total.shape[0] // split
        for i in range(split):
            outs[w * split + i][...] = total[i * height : (i + 1) * height].astype(BF16)


def picked_grads(table, places, lefts, rights, rows, flipped, split, block, name):
    units = len(lefts)
    width = lefts[0].shape[1]
    columns = rights[0].shape[0 if flipped else 1]
    in_specs = [pl.BlockSpec(a.shape, lambda n, *_: (0, 0)) for a in lefts]
    for a in rights:
        if flipped:
            in_specs.append(pl.BlockSpec((block, width), lambda n, *_: (n, 0)))
        else:
            in_specs.append(pl.BlockSpec((width, block), lambda n, *_: (0, n)))
    heights = [size * rows for _, size in places]
    return pl.pallas_call(
        functools.partial(picked_kernel, units, rows, places, flipped, split),
        grid_spec=pltpu.PrefetchScalarGridSpec(
            num_scalar_prefetch=1,
            grid=(columns // block,),
            in_specs=in_specs,
            out_specs=[
                pl.BlockSpec((height // split, block), lambda n, *_: (0, n)) for height in heights for _ in range(split)
            ],
            scratch_shapes=[pltpu.VMEM((height, width), BF16) for height in heights for _ in lefts],
        ),
        out_shape=[
            jax.ShapeDtypeStruct((height // split, columns), BF16) for height in heights for _ in range(split)
        ],
        compiler_params=pltpu.CompilerParams(vmem_limit_bytes=62 << 20),
        cost_estimate=pl.CostEstimate(
            flops=2 * units * sum(heights) * width * columns,
            bytes_accessed=4 * sum(heights) * columns,
            transcendentals=0,
        ),
        name=name,
    )(table, *lefts, *rights)


def tall_kernel(units, pieces_here, table_ref, *refs):
    keep_ref, send_ref = refs[-2:]
    total = None
    for u in range(units):
        left = [refs[u * pieces_here + i][...] for i in range(pieces_here)]
        made = dot(jnp.concatenate(left, axis=0), refs[units * pieces_here + u][...])
        total = made if total is None else total + made
    kept = pl.program_id(0) < pl.num_programs(0) // 2

    @pl.when(kept)
    def _():
        keep_ref[...] = total.astype(BF16)

    @pl.when(jnp.logical_not(kept))
    def _():
        send_ref[...] = total.astype(BF16)


def tall_grads(table, lefts, rights, rows, name):
    units = len(lefts)
    width = lefts[0].shape[1]
    columns = rights[0].shape[1]
    places = table.shape[0]
    each = 4
    middle = places // each // 2
    in_specs = []
    for _ in lefts:
        for i in range(each):
            in_specs.append(pl.BlockSpec((rows, width), lambda n, table, i=i: (table[n * each + i], 0)))
    in_specs += [pl.BlockSpec(a.shape, lambda n, *_: (0, 0)) for a in rights]
    return pl.pallas_call(
        functools.partial(tall_kernel, units, each),
        grid_spec=pltpu.PrefetchScalarGridSpec(
            num_scalar_prefetch=1,
            grid=(places // each,),
            in_specs=in_specs,
            out_specs=[
                pl.BlockSpec((each * rows, columns), lambda n, *_: (jnp.minimum(n, middle - 1), 0)),
                pl.BlockSpec((each * rows, columns), lambda n, *_: (jnp.maximum(n - middle, 0), 0)),
            ],
        ),
        out_shape=[jax.ShapeDtypeStruct((places // 2 * rows, columns), BF16)] * 2,
        compiler_params=pltpu.CompilerParams(vmem_limit_bytes=62 << 20),
        cost_estimate=pl.CostEstimate(
            flops=2 * units * places * rows * width * columns,
            bytes_accessed=2 * places * rows * columns,
            transcendentals=0,
        ),
        name=name,
    )(table, *[a for a in lefts for _ in range(each)], *rights)


def reduce_kernel(orders, count, *refs):
    streams = len(orders)
    rounds = len(orders[0])
    ins, vec_ref = refs[:streams], refs[streams]
    outs, vec_out = refs[streams + 1 : 2 * streams + 1], refs[2 * streams + 1]
    rest = refs[2 * streams + 2 :]
    works, arrivals = rest[:streams], rest[streams : 2 * streams]
    vec_work, vec_arrival, send_sem, recv_sem, vec_send, vec_recv = rest[2 * streams :]
    shard, seq = lax.axis_index("shard"), lax.axis_index("seq")

    def partner(mask):
        if mask >= count:
            step = mask // count
            return (shard + step * (1 - 2 * (shard // step % 2)), seq)
        return (shard, seq + mask * (1 - 2 * (seq // mask % 2)))

    barrier = pltpu.get_barrier_semaphore()
    for mask in orders[0]:
        pl.semaphore_signal(
            barrier, inc=1, device_id=partner(mask), device_id_type=pl.DeviceIdType.MESH
        )
    pl.semaphore_wait(barrier, rounds)

    height = ins[0].shape[0]
    halves = [height >> (r + 1) for r in range(rounds)]
    starts = [sum(halves[:r]) for r in range(rounds)]

    def copy_of(s, r):
        source = ins[s] if r == 0 else works[s]
        return pltpu.make_async_remote_copy(
            src_ref=source.at[pl.ds(halves[r], halves[r])],
            dst_ref=arrivals[s].at[pl.ds(starts[r], halves[r])],
            send_sem=send_sem.at[s, r],
            recv_sem=recv_sem.at[s, r],
            device_id=partner(orders[s][r]),
            device_id_type=pl.DeviceIdType.MESH,
        )

    def vec_copy(r):
        return pltpu.make_async_remote_copy(
            src_ref=vec_ref if r == 0 else vec_work.at[r - 1],
            dst_ref=vec_arrival.at[r],
            send_sem=vec_send.at[r],
            recv_sem=vec_recv.at[r],
            device_id=partner(orders[0][r]),
            device_id_type=pl.DeviceIdType.MESH,
        )

    for s in range(streams):
        copy_of(s, 0).start()
    vec_copy(0).start()
    for r in range(rounds):
        for s in range(streams):
            copy_of(s, r).wait_recv()
            source = ins[s] if r == 0 else works[s]
            size = halves[r]

            def added(low, high):
                mine = source[low:high].astype(F32)
                return mine + arrivals[s][starts[r] + low : starts[r] + high].astype(F32)

            if r == rounds - 1:
                outs[s][...] = added(0, size)
            else:
                works[s][size // 2 : size] = added(size // 2, size).astype(BF16)
                copy_of(s, r + 1).start()
                works[s][0 : size // 2] = added(0, size // 2).astype(BF16)
        vec_copy(r).wait_recv()
        before = vec_ref[...] if r == 0 else vec_work[r - 1]
        if r == rounds - 1:
            vec_out[...] = before + vec_arrival[r]
        else:
            vec_work[r] = before + vec_arrival[r]
            vec_copy(r + 1).start()
    for r in range(rounds):
        for s in range(streams):
            copy_of(s, r).wait_send()
        vec_copy(r).wait_send()


def reduce_rows(parts, vector, orders, count):
    streams = len(parts)
    rounds = len(orders[0])
    height, columns = parts[0].shape
    rows = height >> rounds
    vmem = pl.BlockSpec(memory_space=pltpu.VMEM)
    return pl.pallas_call(
        functools.partial(reduce_kernel, orders, count),
        in_specs=[vmem] * (streams + 1),
        out_specs=[vmem] * (streams + 1),
        out_shape=[jax.ShapeDtypeStruct((rows, columns), F32)] * streams
        + [jax.ShapeDtypeStruct(vector.shape, F32)],
        scratch_shapes=[pltpu.VMEM((height // 2, columns), BF16) for _ in parts]
        + [pltpu.VMEM((height - rows, columns), BF16) for _ in parts]
        + [
            pltpu.VMEM((rounds - 1,) + vector.shape, F32),
            pltpu.VMEM((rounds,) + vector.shape, F32),
            pltpu.SemaphoreType.DMA((streams, rounds)),
            pltpu.SemaphoreType.DMA((streams, rounds)),
            pltpu.SemaphoreType.DMA((rounds,)),
            pltpu.SemaphoreType.DMA((rounds,)),
        ],
        compiler_params=pltpu.CompilerParams(
            collective_id=0, has_side_effects=True, vmem_limit_bytes=62 << 20
        ),
        name="reduce_rows",
    )(*parts, vector)


def on_device(
    tokens, cotangent, lengths, variates, positions, attn_gain, w_query, w_key, w_value, w_out,
    bias_table, ffn_gain, w_gate, w_up, w_down,
):
    micro, seqs, width, model = tokens.shape
    heads = bias_table.shape[0]
    head_dim = model // heads
    count = lax.axis_size("seq")
    here = heads // count
    ffn = w_gate.shape[1]
    devices = lax.axis_size("shard") * count
    seq_index = lax.axis_index("seq")
    bias_here = lax.dynamic_slice_in_dim(bias_table, seq_index * here, here, 0)
    units = [(m, s) for m in range(micro) for s in range(seqs)]
    attn_row, ffn_row = attn_gain[None, :], ffn_gain[None, :]

    def gather(weight):
        return lax.all_gather(weight, "shard", axis=0, tiled=True)

    def exchange(values):
        return lax.all_to_all(values, "seq", split_axis=0, concat_axis=0, tiled=True)

    def after(value, *before):
        return lax.optimization_barrier((value,) + before)[0]

    attn_joined = gather(jnp.concatenate([w_query, w_key, w_value], axis=1))
    ffn_weights = [gather(w_out), gather(w_gate), gather(w_up), gather(w_down)]

    packed_list, flats, tables = [], [], []

    def run_project(u, token):
        m, s = units[u]
        cosine, sine = rotary_tables(positions[m, s], head_dim // 2)
        ids = after(variates[m, s].astype(F32)[None, :], *token)
        flat, *packed = project(
            tokens, (m, s), attn_row, attn_joined, cosine, sine, ids, count, here, head_dim
        )
        flats.append(flat)
        tables.append((cosine, sine))
        packed_list.append(packed)

    sent = {}
    mixed_now = [None] * len(units)
    sums = {}
    mixed_tok = {}
    middle = [None] * len(units)
    grad_heads = {}
    state = {"output": None, "grads": None}
    packed_grads = {}
    returned = {}
    bias_terms = {}
    finals = [None] * len(units)

    def length_of(u, token):
        m, s = units[u]
        return after(lengths[m, s].reshape(1), *token)

    def run_forward(u, h, token):
        mixed_now[u], sums[u, h] = attend_forward(
            sent[u, h], sent[u, 0], length_of(u, token), bias_here, mixed_now[u], h, here, head_dim
        )
        return sums[u, h]

    def run_middle(u, token):
        m, s = units[u]
        info = jnp.stack([lengths[m, s], seq_index * width]).astype(jnp.int32)
        state["output"], *middle[u] = middle_part(
            after(info, *token), mixed_tok[u], tokens, cotangent, (m, s), ffn_weights, ffn_row,
            state["output"],
        )
        return middle[u][8]

    def run_backward(u, h, token):
        packed_grads[u, h], both = attend_backward(
            sent[u, h], sent[u, 0], grad_heads[u], mixed_now[u], sums[u, h], length_of(u, token),
            bias_here, h, head_dim,
        )
        bias_terms[u, h] = both
        return both

    def run_final(u, token):
        m, s = units[u]
        cosine, sine = tables[u]
        state["grads"], *finals[u] = final_part(
            tokens, (m, s), middle[u][5], after(attn_row, *token), attn_joined, cosine, sine,
            [returned[u, h] for h in range(here)], head_dim, state["grads"],
        )
        return finals[u][3]

    rows = model // devices
    fold = ffn // model
    tall = ffn // devices
    seq_masks = [1 << i for i in range(count.bit_length() - 1)]
    shard_masks = [count << i for i in range((devices // count).bit_length() - 1)]
    spread = shard_masks[1:]
    orders = (
        shard_masks[:1] + spread + seq_masks,
        shard_masks[:1] + seq_masks[:1] + spread + seq_masks[1:],
        shard_masks[:1] + seq_masks[1:2] + seq_masks[:1] + spread + seq_masks[2:],
    )
    direct = rows % 16 == 0 and devices == 1 << len(orders[0])

    def places_of(order):
        marks = []
        for p in range(devices):
            bits = [p >> (len(order) - 1 - i) & 1 for i in range(len(order))]
            marks.append(sum(mask for bit, mask in zip(bits, order) if bit))
        me = lax.axis_index("shard") * count + seq_index
        return me.astype(jnp.int32) ^ jnp.array(marks, jnp.int32)

    def permute(value, mask):
        return lax.ppermute(value, ("shard", "seq"), [(i, i ^ mask) for i in range(devices)])

    def column(index):
        return [item[index] for item in middle]

    def run_weights(token):
        if not direct:
            return [
                sum(dot(left, right) for left, right in zip(lefts, rights)).astype(BF16)
                for lefts, rights in (
                    (column(0), column(2)), (column(0), column(3)), (column(1), column(4)),
                    ([mixed_tok[u] for u in range(len(units))], column(6)),
                )
            ]
        tables = [after(places_of(order), *token) for order in orders]
        span = [(0, devices)]
        down = tall_grads(tables[2], column(1), column(4), tall, "down_grad")
        table = after(tables[0], down[0])
        gate = picked_grads(table, span, column(0), column(2), rows, False, 2, 512, "gate_grad")
        table = after(tables[1], gate[0])
        up = picked_grads(table, span, column(0), column(3), rows, False, 2, 512, "up_grad")
        table = after(tables[2], up[0])
        mixed_all = [mixed_tok[u] for u in range(len(units))]
        out = picked_grads(table, span, mixed_all, column(6), rows, False, 2, 512, "out_grad")
        streams = []
        for (keep, send), order in zip((down, gate, up, out), (orders[2], orders[0], orders[1], orders[2])):
            streams.append([keep, permute(send, order[0]), order[1:]])
        holder["streams"] = streams
        return out[0]

    def wide_sum(a, b):
        return a.astype(F32) + b.astype(F32)

    def advance(token):
        out = ()
        if not direct:
            return out
        for stream in holder["streams"]:
            keep, came, masks = stream
            if not masks:
                continue
            keep = after(keep, *token)
            half = keep.shape[0] // 2
            send = wide_sum(keep[half:], came[half:]).astype(BF16)
            stream[0] = wide_sum(keep[:half], came[:half]).astype(BF16)
            stream[1] = permute(send, masks[0])
            stream[2] = masks[1:]
            out = out + (send, stream[0])
        return out

    holder = {}

    def weights_work(token):
        holder["terms"] = run_weights(token)
        return holder["terms"]

    def send_packed(u, h):
        def keep(moved):
            sent[u, h] = moved

        return lambda: packed_list[u][h], keep

    def send_mixed(u):
        def keep(moved):
            mixed_tok[u] = moved.reshape(model, width)

        return lambda: mixed_now[u], keep

    def send_heads(u):
        def keep(moved):
            grad_heads[u] = moved

        return lambda: middle[u][7].reshape(count, here * head_dim, width), keep

    def send_back(u, h):
        def keep(moved):
            returned[u, h] = moved

        return lambda: packed_grads[u, h], keep

    def work_project(u):
        def work(token):
            run_project(u, token)
            return flats[u]

        return work

    def work(function, *args):
        return lambda token: function(*args, token)

    total = len(units)
    order = [(u, h) for u in range(total) for h in range(here)]
    if total == 2 and here == 2:
        steps = [
            (work_project(0), None),
            (work_project(1), send_packed(0, 0)),
            (work(run_forward, 0, 0), send_packed(0, 1)),
            (work(run_forward, 0, 1), send_packed(1, 0)),
            (work(run_forward, 1, 0), send_mixed(0)),
            (work(run_middle, 0), send_packed(1, 1)),
            (work(run_forward, 1, 1), send_heads(0)),
            (work(run_backward, 0, 0), send_mixed(1)),
            (work(run_middle, 1), send_back(0, 0)),
            (weights_work, send_heads(1)),
            (work(run_backward, 0, 1), None),
            (work(run_backward, 1, 0), send_back(0, 1)),
            (work(run_backward, 1, 1), send_back(1, 0)),
            (work(run_final, 0), send_back(1, 1)),
            (work(run_final, 1), None),
        ]
    else:
        steps = [(work_project(u), None) for u in range(total)]
        steps += [(None, send_packed(*at)) for at in order]
        for u in range(total):
            steps += [(work(run_forward, u, h), None) for h in range(here)]
            steps += [(None, send_mixed(u))]
        for u in range(total):
            steps += [(work(run_middle, u), None), (None, send_heads(u))]
        steps += [(weights_work, None)]
        for at in order:
            steps += [(work(run_backward, *at), None), (None, send_back(*at))]
        steps += [(work(run_final, u), None) for u in range(total)]

    late = [task for task, _ in steps[-2:]]
    token = ()
    for task, send in steps:
        done = ()
        moved = None
        if "streams" in holder:
            leaving = advance(token)
            token = token if task in late else token + leaving
        if send is not None:
            moved = exchange(after(send[0](), *token))
            done = (moved,)
        if task is not None:
            done = done + (task(token),)
        if send is not None:
            send[1](moved)
        token = done
    acc_bias = jnp.concatenate(
        [sum(bias_terms[u, h] for u in range(total))[0:1, 0:2] for h in range(here)], axis=0
    )
    bias_full = lax.dynamic_update_slice(
        jnp.zeros((heads, 2), F32), acc_bias, (seq_index * here, jnp.int32(0))
    )
    gain_attn = sum(item[3][0] for item in finals)
    gain_ffn = sum(item[8][0] for item in middle)
    if direct:
        while holder["streams"][0][2]:
            advance(token)
        down_own, gate_own, up_own, out_own = [
            wide_sum(after(keep, *token), came) for keep, came, _ in holder["streams"]
        ]
        table = jnp.concatenate([places_of(order) for order in orders])
        attn_terms = picked_grads(
            table, [(i * devices, devices) for i in range(3)], flats,
            [item[i] for i in range(3) for item in finals], rows, True, 1, 256, "attn_grads",
        )
        flat = jnp.concatenate([gain_attn, gain_ffn, bias_full.reshape(-1)])
        tiles = -(-flat.shape[0] // 1024) * 8
        flat = jnp.pad(flat, (0, tiles * 128 - flat.shape[0])).reshape(tiles, 128)
        query_own, key_own, value_own, flat = reduce_rows(list(attn_terms), flat, orders, count)
        flat = flat.reshape(-1)
        gain_attn, gain_ffn = flat[:model], flat[model : 2 * model]
        bias_full = flat[2 * model : 2 * model + 2 * heads].reshape(heads, 2)
    else:

        def scatter(value):
            owned = lax.psum_scatter(value, ("shard", "seq"), scatter_dimension=0, tiled=True)
            return owned.astype(F32)

        gate_own, up_own, down_own, out_own = [scatter(value) for value in holder["terms"]]
        query_own, key_own, value_own = [
            scatter(
                sum(contract(flat, item[i], 1, 1) for flat, item in zip(flats, finals)).astype(BF16)
            )
            for i in range(3)
        ]
        gain_attn, gain_ffn, bias_full = lax.psum(
            (gain_attn, gain_ffn, bias_full), ("shard", "seq")
        )
    return (
        state["output"], state["grads"], gain_attn, query_own, key_own, value_own, out_own,
        bias_full, gain_ffn, gate_own, up_own, down_own,
    )


def solution(mesh):
    token_spec = P(None, "shard", "seq", None)
    row_spec = P("shard", None)
    in_specs = (
        token_spec, token_spec, P(None, "shard"), P(None, "shard", "seq"), P(None, "shard", "seq"),
        P(), row_spec, row_spec, row_spec, row_spec, P(), P(), row_spec, row_spec, row_spec,
    )
    owned = P(("shard", "seq"), None)
    out_specs = (
        token_spec, token_spec, P(), owned, owned, owned, owned, P(), P(), owned, owned, owned,
    )
    return jax.shard_map(
        on_device, mesh=mesh, in_specs=in_specs, out_specs=out_specs, check_vma=False
    )
```

```python
import functools
import math

import jax
import jax.numpy as jnp
from jax import lax
from jax.experimental import pallas as pl
from jax.experimental.pallas import tpu as pltpu
from jax.sharding import PartitionSpec as P

EPSILON = 1e-06
ROTARY_BASE = 10000.0
LOG2E = 1.4426950408889634
LN2 = 0.6931471805599453
CLASSES = 8
AUX = 16
EXTRA = 32
MASKED = -1.5e9
FAR = 1e30
F32 = jnp.float32
BF16 = jnp.bfloat16


def dot(a, b):
    return jnp.dot(a, b, preferred_element_type=F32)


def contract(a, b, da, db):
    return lax.dot_general(a, b, (((da,), (db,)), ((), ())), preferred_element_type=F32)


def pieces(x):
    high = x.astype(BF16).astype(F32)
    rest = x - high
    mid = rest.astype(BF16).astype(F32)
    low = (rest - mid).astype(BF16).astype(F32)
    return high, mid, low


def one_hot(row):
    classes = lax.broadcasted_iota(jnp.int32, (CLASSES, row.shape[1]), 0).astype(F32)
    return jnp.where(classes == row, 1.0, 0.0)


def rows_of(values, width):
    index = lax.broadcasted_iota(jnp.int32, (8, width), 0)
    out = jnp.zeros((8, width), F32)
    for at, value in enumerate(values):
        out = jnp.where(index == at, value, out)
    return out


def key_extra(row, start, length, other, same):
    width = row.shape[1]
    hot = one_hot(row)
    step = pieces(jnp.full((1, width), same - other, F32))
    base = pieces(jnp.full((1, width), other, F32))
    index = start + lax.broadcasted_iota(jnp.int32, (1, width), 1)
    mask = jnp.where(index < length, 0.0, MASKED)
    tail = rows_of(base + (mask, 1.0, 1.0, 1.0), width)
    return jnp.concatenate([hot * step[0], hot * step[1], hot * step[2], tail], axis=0).astype(BF16)


def query_extra(row, shift):
    hot = one_hot(row)
    tail = rows_of((1.0, 1.0, 1.0, 1.0) + shift, row.shape[1])
    return jnp.concatenate([hot, hot, hot, tail], axis=0).astype(BF16)


def forward_kernel(
    shape, len_ref, bias_ref, x_ref, ids_ref, *rest
):
    local, head_dim, block, aliased = shape
    if aliased:
        rest = rest[1:]
    mixed_ref, lse_ref, keys, vals, query, score, peak, total = rest
    count, _, width = x_ref.shape
    sub = block // width
    step = pl.program_id(0)
    length = len_ref[0]
    other = bias_ref[local, 0] * LOG2E
    same = bias_ref[local, 1] * LOG2E

    @pl.when(step == 0)
    def _():
        for b in range(count):
            at = pl.ds(b * width, width)
            row = ids_ref[b, 0:1, :].astype(F32)
            extra = key_extra(row, b * width, length, other, same)
            full = jnp.concatenate([x_ref[b, head_dim : 2 * head_dim, :], extra], axis=0)
            keys[at, :] = full.T
            vals[0:head_dim, at] = x_ref[b, 2 * head_dim : 3 * head_dim, :]
        vals[head_dim:, :] = jnp.ones((16, vals.shape[1]), BF16)

    used = pl.cdiv(length, block)
    inside = step * block < length

    @pl.when(jnp.logical_not(inside))
    def _():
        mixed_ref[...] = jnp.zeros_like(mixed_ref)
        lse_ref[...] = jnp.full(lse_ref.shape, FAR, F32)

    @pl.when(inside)
    def _():
        for b in range(sub):
            at = slice(b * width, (b + 1) * width)
            row = ids_ref[step * sub + b, 0:1, :].astype(F32)
            query[0:head_dim, at] = x_ref[step * sub + b, 0:head_dim, :]
            query[head_dim:, at] = query_extra(row, (0.0, 0.0, 0.0))
        peak[...] = jnp.full(peak.shape, -FAR, F32)
        total[...] = jnp.zeros_like(total)

        def span(j):
            return pl.ds(pl.multiple_of(j * block, block), block)

        def scores_of(j):
            return dot(keys[span(j), :], query[...])

        def one(j, now, ahead):
            if ahead:
                score[1 - now] = scores_of(j + 1)
            current = score[now]
            before = peak[...]
            top = jnp.maximum(before, jnp.max(current, axis=0, keepdims=True))
            weight = jnp.exp2(current - top).astype(BF16)
            peak[...] = top
            total[...] = total[...] * jnp.exp2(before - top) + dot(vals[:, span(j)], weight)

        score[0] = scores_of(0)
        pairs = (used - 1) // 2

        def pair(j, carry):
            one(2 * j, 0, True)
            one(2 * j + 1, 1, True)
            return carry

        lax.fori_loop(0, pairs, pair, 0)
        last = 2 * pairs

        @pl.when(used - last == 1)
        def _():
            one(last, 0, False)

        @pl.when(used - last == 2)
        def _():
            one(last, 0, True)
            one(last + 1, 1, False)

        mass = total[head_dim : head_dim + 1, :]
        mixed = (total[0:head_dim, :] / mass).astype(BF16)
        for b in range(sub):
            mixed_ref[b] = mixed[:, b * width : (b + 1) * width]
        lse_ref[0] = peak[...] + jnp.log2(mass)


def attend_forward(x, ids, length, bias, mixed, local, heads_here, head_dim):
    count, rows, width = x.shape
    block = max(width, 512)
    seq_len = count * width
    blocks = seq_len // block
    depth = head_dim + EXTRA
    whole = pl.BlockSpec((count, rows, width), lambda i, *_: (0, 0, 0))
    operands = [length, bias, x, ids]
    in_specs = [whole, pl.BlockSpec((count, AUX, width), lambda i, *_: (0, 3 * head_dim // AUX, 0))]
    aliases = {}
    if mixed is not None:
        operands.append(mixed)
        in_specs.append(pl.BlockSpec(memory_space=pl.ANY))
        aliases = {4: 0}
    return pl.pallas_call(
        functools.partial(forward_kernel, (local, head_dim, block, mixed is not None)),
        grid_spec=pltpu.PrefetchScalarGridSpec(
            num_scalar_prefetch=2,
            grid=(blocks,),
            in_specs=in_specs,
            out_specs=[
                pl.BlockSpec((block // width, head_dim, width), lambda i, *_: (i, local, 0)),
                pl.BlockSpec((1, 1, block), lambda i, *_: (i, 0, 0)),
            ],
            scratch_shapes=[
                pltpu.VMEM((seq_len, depth), BF16),
                pltpu.VMEM((head_dim + 16, seq_len), BF16),
                pltpu.VMEM((depth, block), BF16),
                pltpu.VMEM((2, block, block), F32),
                pltpu.VMEM((1, block), F32),
                pltpu.VMEM((head_dim + 16, block), F32),
            ],
        ),
        out_shape=[
            jax.ShapeDtypeStruct((count, heads_here * head_dim, width), BF16),
            jax.ShapeDtypeStruct((blocks, 1, block), F32),
        ],
        input_output_aliases=aliases,
        compiler_params=pltpu.CompilerParams(vmem_limit_bytes=62 << 20),
        cost_estimate=pl.CostEstimate(
            flops=8 * seq_len * seq_len * 256,
            bytes_accessed=x.size * 4,
            transcendentals=seq_len * seq_len,
        ),
        name="attend_forward",
    )(*operands)


def backward_kernel(
    shape, len_ref, bias_ref, x_ref, ids_ref, grad_ref, mixed_ref, lse_ref, out_ref, bias_out_ref,
    keys, keys_flat, vals, query, grads, query_rows, grad_rows, acc_keys, acc_vals, acc_query,
):
    local, head_dim, block = shape
    count, _, width = x_ref.shape
    sub = block // width
    step = pl.program_id(0)
    length = len_ref[0]
    other = bias_ref[local, 0] * LOG2E
    same = bias_ref[local, 1] * LOG2E

    @pl.when(step == 0)
    def _():
        ones = jnp.ones((16, width), BF16)
        for b in range(count):
            at = pl.ds(b * width, width)
            row = ids_ref[b, 0:1, :].astype(F32)
            extra = key_extra(row, b * width, length, other, same)
            here = x_ref[b, head_dim : 2 * head_dim, :]
            keys[at, :] = jnp.concatenate([here, extra], axis=0).T
            keys_flat[:, at] = here
            vals[at, :] = jnp.concatenate([x_ref[b, 2 * head_dim : 3 * head_dim, :], ones], axis=0).T
        acc_keys[...] = jnp.zeros_like(acc_keys)
        acc_vals[...] = jnp.zeros_like(acc_vals)

    used = pl.cdiv(length, block)
    inside = step * block < length

    @pl.when(jnp.logical_not(inside))
    def _():
        for b in range(sub):
            out_ref[step * sub + b, 0:head_dim, :] = jnp.zeros((head_dim, width), BF16)

    @pl.when(inside)
    def _():
        for b in range(sub):
            at = slice(b * width, (b + 1) * width)
            here = step * sub + b
            row = ids_ref[here, 0:1, :].astype(F32)
            shift = pieces(-lse_ref[step][:, at])
            grad = grad_ref[here]
            delta = jnp.sum(grad.astype(F32) * mixed_ref[here].astype(F32), axis=0, keepdims=True)
            query[0:head_dim, at] = x_ref[here, 0:head_dim, :]
            query[head_dim:, at] = query_extra(row, shift)
            grads[0:head_dim, at] = grad
            tail = rows_of(pieces(-delta), width)
            grads[head_dim:, at] = jnp.concatenate([tail, jnp.zeros_like(tail)], axis=0).astype(BF16)
        query_rows[...] = query[...].T
        grad_rows[...] = grads[...].T
        acc_query[...] = jnp.zeros_like(acc_query)

        def one(j):
            at = pl.ds(pl.multiple_of(j * block, block), block)
            probs = jnp.exp2(dot(keys[at, :], query[...]))
            grad_probs = dot(vals[at, :], grads[...])
            grad_scores = (probs * grad_probs).astype(BF16)
            acc_vals[at, :] += dot(probs.astype(BF16), grad_rows[...])
            acc_keys[at, :] += dot(grad_scores, query_rows[...])
            acc_query[...] += dot(keys_flat[:, at], grad_scores)

        def pair(j, carry):
            one(2 * j)
            one(2 * j + 1)
            return carry

        lax.fori_loop(0, used // 2, pair, 0)

        @pl.when(used % 2 == 1)
        def _():
            one(used - 1)

        grad_query = (acc_query[...] * (1.0 / math.sqrt(head_dim))).astype(BF16)
        for b in range(sub):
            out_ref[step * sub + b, 0:head_dim, :] = grad_query[:, b * width : (b + 1) * width]

    @pl.when(step == pl.num_programs(0) - 1)
    def _():
        same_total = jnp.zeros((CLASSES, width), F32)
        all_total = jnp.zeros((CLASSES, width), F32)
        for b in range(count):
            at = pl.ds(b * width, width)
            row = ids_ref[b, 0:1, :].astype(F32)
            flat = acc_keys[at, :].T
            out_ref[b, head_dim : 2 * head_dim, :] = (flat[0:head_dim] * LN2).astype(BF16)
            out_ref[b, 2 * head_dim : 3 * head_dim, :] = acc_vals[at, :].T[0:head_dim].astype(BF16)
            by_class = flat[head_dim : head_dim + CLASSES]
            all_total += by_class
            same_total += by_class * one_hot(row)
        same_sum = jnp.sum(same_total, keepdims=True)
        other_sum = jnp.sum(all_total, keepdims=True) - same_sum
        lane = lax.broadcasted_iota(jnp.int32, (8, 128), 1)
        bias_out_ref[...] = jnp.where(lane == 0, other_sum, jnp.where(lane == 1, same_sum, 0.0))


def attend_backward(x, ids, grad, mixed, lse, length, bias, local, head_dim):
    count, rows, width = x.shape
    blocks, _, block = lse.shape
    seq_len = count * width
    depth = head_dim + EXTRA

    def whole(a):
        return pl.BlockSpec(a.shape, lambda i, *_: (0,) * a.ndim)

    head_spec = pl.BlockSpec((count, head_dim, width), lambda i, *_: (0, local, 0))
    return pl.pallas_call(
        functools.partial(backward_kernel, (local, head_dim, block)),
        grid_spec=pltpu.PrefetchScalarGridSpec(
            num_scalar_prefetch=2,
            grid=(blocks,),
            in_specs=[
                whole(x),
                pl.BlockSpec((count, AUX, width), lambda i, *_: (0, 3 * head_dim // AUX, 0)),
                head_spec, head_spec, whole(lse),
            ],
            out_specs=[
                pl.BlockSpec((count, 3 * head_dim, width), lambda i, *_: (0, 0, 0)),
                pl.BlockSpec((8, 128), lambda i, *_: (0, 0)),
            ],
            scratch_shapes=[
                pltpu.VMEM((seq_len, depth), BF16),
                pltpu.VMEM((head_dim, seq_len), BF16),
                pltpu.VMEM((seq_len, head_dim + 16), BF16),
                pltpu.VMEM((depth, block), BF16),
                pltpu.VMEM((head_dim + 16, block), BF16),
                pltpu.VMEM((block, depth), BF16),
                pltpu.VMEM((block, head_dim + 16), BF16),
                pltpu.VMEM((seq_len, depth), F32),
                pltpu.VMEM((seq_len, head_dim + 16), F32),
                pltpu.VMEM((head_dim, block), F32),
            ],
        ),
        out_shape=[
            jax.ShapeDtypeStruct((count, 3 * head_dim, width), BF16),
            jax.ShapeDtypeStruct((8, 128), F32),
        ],
        compiler_params=pltpu.CompilerParams(vmem_limit_bytes=62 << 20),
        cost_estimate=pl.CostEstimate(
            flops=20 * seq_len * seq_len * 256,
            bytes_accessed=x.size * 6,
            transcendentals=seq_len * seq_len,
        ),
        name="attend_backward",
    )(length, bias, x, ids, grad, mixed, lse)


def rotary_tables(places, half_dim):
    frequency = jnp.exp(-math.log(ROTARY_BASE) * jnp.arange(half_dim, dtype=F32) / half_dim)
    angles = places.astype(F32)[None, :] * frequency[:, None]
    return jnp.cos(angles), jnp.sin(angles)


def sigmoid_of(x):
    return 1.0 / (1.0 + jnp.exp2(x * -LOG2E))


def project_kernel(
    shape, core_ref, tokens_ref, gain_ref, query_ref, key_ref, value_ref, cos_ref, sin_ref, ids_ref, flat_ref, *rest
):
    here, head_dim, extras, swap = shape
    outs, flat_weights = rest[:-1], rest[-1]
    pair = pl.program_id(0)

    @pl.when(pair == 0)
    def _():
        inputs = tokens_ref[0, 0].astype(F32)
        inverse = lax.rsqrt(jnp.mean(inputs * inputs, axis=-1, keepdims=True) + EPSILON)
        flat_ref[...] = (inputs * inverse * gain_ref[...]).astype(BF16).T

    flat_weights[0:128, :] = query_ref[...].T
    flat_weights[128:256, :] = key_ref[...].T
    flat_weights[256:384, :] = value_ref[...].T
    made = dot(flat_weights[...], flat_ref[...])
    cosine, sine = cos_ref[...], sin_ref[...]
    half = head_dim // 2

    def turned(start, scale):
        first = made[start : start + half]
        second = made[start + half : start + head_dim]
        both = [first * cosine - second * sine, second * cosine + first * sine]
        return (jnp.concatenate(both, axis=0) * scale).astype(BF16)

    def put(at, slot, place):
        spot = at * head_dim
        target = outs[slot]
        target[place, 0:head_dim, :] = turned(spot, LOG2E / math.sqrt(head_dim))
        target[place, head_dim : 2 * head_dim, :] = turned(128 + spot, 1.0)
        target[place, 2 * head_dim : 3 * head_dim, :] = made[256 + spot : 256 + spot + head_dim].astype(BF16)
        if extras[slot]:
            target[place, 3 * head_dim :, :] = jnp.broadcast_to(ids_ref[...], (AUX, ids_ref.shape[1])).astype(BF16)

    if swap:
        for core in range(2):

            @pl.when(core_ref[0] == core)
            def _():
                put(core, 0, 0)
                put(1 - core, 1, 0)

    else:
        for at in range(128 // head_dim):
            put(at, at % here, 0 if here > 1 else at)


def project(core, tokens, unit, gain, weights, cosine, sine, ids, count, here, head_dim, swap):
    width, model = tokens.shape[2:]
    heads = count * here
    pairs = heads * head_dim // 128
    per = 128 // head_dim // here
    extras = [h == (1 if swap else 0) for h in range(here)]

    def fixed(a):
        return pl.BlockSpec(a.shape, lambda p: (0,) * a.ndim)

    weight_specs = [pl.BlockSpec((model, 128), lambda p, i=i: (0, i * pairs + p)) for i in range(3)]
    return pl.pallas_call(
        functools.partial(project_kernel, (here, head_dim, extras, swap)),
        grid=(pairs,),
        in_specs=[
            pl.BlockSpec(memory_space=pltpu.SMEM),
            pl.BlockSpec((1, 1, width, model), lambda p: unit + (0, 0)),
            fixed(gain), *weight_specs, fixed(cosine), fixed(sine), fixed(ids),
        ],
        out_specs=[pl.BlockSpec((model, width), lambda p: (0, 0))]
        + [pl.BlockSpec((per, 3 * head_dim + AUX * e, width), lambda p: (p, 0, 0)) for e in extras],
        out_shape=[jax.ShapeDtypeStruct((model, width), BF16)]
        + [jax.ShapeDtypeStruct((count, 3 * head_dim + AUX * e, width), BF16) for e in extras],
        scratch_shapes=[pltpu.VMEM((384, model), BF16)],
        compiler_params=pltpu.CompilerParams(vmem_limit_bytes=62 << 20),
        cost_estimate=pl.CostEstimate(
            flops=6 * width * model * model, bytes_accessed=12 * model * model, transcendentals=0
        ),
        name="project",
    )(core, tokens, gain, weights, weights, weights, cosine, sine, ids)


def middle_kernel(
    shape, info_ref, mixed_ref, tokens_ref, cot_ref, out_w_ref, gain_ref, gate_w_ref, up_w_ref, down_w_ref, *rest
):
    head_dim, aliased = shape
    if aliased:
        rest = rest[1:]
    (
        output_ref, ordered_ref, flat_ref, hidden_ref, grad_gate_ref, grad_up_ref, grad_ffn_ref, grad_res_ref,
        grad_attn_ref, grad_mixed_ref, gain_out_ref, normed, residual, ffn_out, grad_normed, slots,
    ) = rest
    core = info_ref[2]
    step = pl.program_id(0)
    width = normed.shape[0]

    def valid():
        index = info_ref[1] + lax.broadcasted_iota(jnp.int32, (width, 1), 0)
        return jnp.where(index < info_ref[0], 1.0, 0.0)

    def inverse_of(x):
        return lax.rsqrt(jnp.mean(x * x, axis=-1, keepdims=True) + EPSILON)

    def head_rows(pair, slot):
        head = 2 * pair + (core if slot == 0 else 1 - core)
        return pl.ds(pl.multiple_of(head * head_dim, head_dim), head_dim)

    def slot_rows(pair, slot):
        return slice((2 * pair + slot) * head_dim, (2 * pair + slot + 1) * head_dim)

    spots = [(pair, slot) for pair in range(mixed_ref.shape[0] // head_dim // 2) for slot in range(2)]

    @pl.when(step == 0)
    def _():
        for spot in spots:
            ordered_ref[head_rows(*spot), :] = mixed_ref[slot_rows(*spot), :]
        inputs = tokens_ref[0, 0].astype(F32) + dot(ordered_ref[...].T, out_w_ref[...])
        residual[...] = inputs
        made = (inputs * inverse_of(inputs) * gain_ref[...]).astype(BF16)
        normed[...] = made
        flat_ref[...] = made.T
        grad_ffn_ref[...] = (cot_ref[0, 0].astype(F32) * valid()).astype(BF16)
        ffn_out[...] = jnp.zeros_like(ffn_out)
        grad_normed[...] = jnp.zeros_like(grad_normed)

    gate = dot(normed[...], gate_w_ref[...])
    up = dot(normed[...], up_w_ref[...])
    grad_hidden = contract(grad_ffn_ref[...], down_w_ref[...], 1, 1)
    sigmoid = sigmoid_of(gate)
    silu = gate * sigmoid
    hidden = (silu * up).astype(BF16)
    grad_gate = (grad_hidden * up * (sigmoid + silu * (1.0 - sigmoid))).astype(BF16)
    grad_up = (grad_hidden * silu).astype(BF16)
    hidden_ref[...] = hidden.T
    grad_gate_ref[...] = grad_gate
    grad_up_ref[...] = grad_up
    ffn_out[...] += dot(hidden, down_w_ref[...])
    grad_normed[...] += contract(grad_gate, gate_w_ref[...], 1, 1) + contract(grad_up, up_w_ref[...], 1, 1)

    @pl.when(step == pl.num_programs(0) - 1)
    def _():
        keep = valid()
        kept = residual[...]
        output_ref[0, 0] = ((kept + ffn_out[...]) * keep).astype(BF16)
        inverse = inverse_of(kept)
        scaled = grad_normed[...] * gain_ref[...]
        mean = jnp.mean(scaled * kept, axis=-1, keepdims=True)
        grad = cot_ref[0, 0].astype(F32) * keep
        grad = grad + (inverse * scaled - kept * (inverse * inverse * inverse) * mean)
        gain_out_ref[...] = jnp.sum(grad_normed[...] * kept * inverse, axis=0, keepdims=True)
        grad_res_ref[...] = grad
        low = grad.astype(BF16)
        grad_attn_ref[...] = low
        slots[...] = contract(out_w_ref[...], low, 1, 1).astype(BF16)
        for spot in spots:
            grad_mixed_ref[slot_rows(*spot), :] = slots[head_rows(*spot), :]


def middle_part(info, mixed, tokens, cotangent, unit, weights, gain, head_dim, output):
    width, model = tokens.shape[2:]
    out_w, gate_w, up_w, down_w = weights
    ffn = gate_w.shape[1]
    block = 512

    def fixed(a):
        return pl.BlockSpec(a.shape, lambda f, *_: (0,) * a.ndim)

    def one(*shape):
        return pl.BlockSpec(shape, lambda f, *_: (0,) * len(shape))

    token_spec = pl.BlockSpec((1, 1, width, model), lambda f, *_: unit + (0, 0))
    operands = [info, mixed, tokens, cotangent, out_w, gain, gate_w, up_w, down_w]
    in_specs = [
        fixed(mixed), token_spec, token_spec, fixed(out_w), fixed(gain),
        pl.BlockSpec((model, block), lambda f, *_: (0, f)),
        pl.BlockSpec((model, block), lambda f, *_: (0, f)),
        pl.BlockSpec((block, model), lambda f, *_: (f, 0)),
    ]
    aliases = {}
    if output is not None:
        aliases = {len(operands): 0}
        operands.append(output)
        in_specs.append(pl.BlockSpec(memory_space=pl.ANY))
    struct = jax.ShapeDtypeStruct
    return pl.pallas_call(
        functools.partial(middle_kernel, (head_dim, output is not None)),
        grid_spec=pltpu.PrefetchScalarGridSpec(
            num_scalar_prefetch=1,
            grid=(ffn // block,),
            in_specs=in_specs,
            out_specs=[
                token_spec, one(model, width), one(model, width),
                pl.BlockSpec((block, width), lambda f, *_: (f, 0)),
                pl.BlockSpec((width, block), lambda f, *_: (0, f)),
                pl.BlockSpec((width, block), lambda f, *_: (0, f)),
                one(width, model), one(width, model), one(width, model), one(model, width), one(1, model),
            ],
            scratch_shapes=[
                pltpu.VMEM((width, model), BF16),
                pltpu.VMEM((width, model), F32),
                pltpu.VMEM((width, model), F32),
                pltpu.VMEM((width, model), F32),
                pltpu.VMEM((model, width), BF16),
            ],
        ),
        out_shape=[
            struct(tokens.shape, BF16), struct((model, width), BF16), struct((model, width), BF16),
            struct((ffn, width), BF16),
            struct((width, ffn), BF16), struct((width, ffn), BF16), struct((width, model), BF16),
            struct((width, model), F32), struct((width, model), BF16), struct((model, width), BF16),
            struct((1, model), F32),
        ],
        input_output_aliases=aliases,
        compiler_params=pltpu.CompilerParams(vmem_limit_bytes=62 << 20),
        cost_estimate=pl.CostEstimate(
            flops=12 * width * model * ffn, bytes_accessed=8 * model * ffn, transcendentals=width * ffn
        ),
        name="middle_part",
    )(*operands)


def final_kernel(
    shape, core_ref, tokens_ref, grad_res_ref, gain_ref, query_ref, key_ref, value_ref, cos_ref, sin_ref, *rest
):
    here, head_dim, aliased = shape
    back = rest[:here]
    rest = rest[here:]
    if aliased:
        rest = rest[1:]
    out_ref, grad_q_ref, grad_k_ref, grad_v_ref, gain_out_ref, total = rest
    step = pl.program_id(0)
    cosine, sine = cos_ref[...], sin_ref[...]
    half = head_dim // 2

    def turned(x):
        first, second = x[:half].astype(F32), x[half:].astype(F32)
        return jnp.concatenate(
            [first * cosine + second * sine, second * cosine - first * sine], axis=0
        ).astype(BF16)

    for at in range(256 // head_dim):
        head = at
        if here == 2:
            head = at // 2 * 2 + (core_ref[0] if at % 2 == 0 else 1 - core_ref[0])
        place = pl.ds(pl.multiple_of(head * head_dim, head_dim), head_dim)
        part = back[at % here]
        grad_q_ref[place, :] = turned(part[at // here, 0:head_dim, :])
        grad_k_ref[place, :] = turned(part[at // here, head_dim : 2 * head_dim, :])
        grad_v_ref[place, :] = part[at // here, 2 * head_dim : 3 * head_dim, :]
    made = (
        contract(grad_q_ref[...].T, query_ref[...], 1, 1)
        + contract(grad_k_ref[...].T, key_ref[...], 1, 1)
        + contract(grad_v_ref[...].T, value_ref[...], 1, 1)
    )

    @pl.when(step == 0)
    def _():
        total[...] = made

    @pl.when(step > 0)
    def _():
        total[...] += made

    @pl.when(step == pl.num_programs(0) - 1)
    def _():
        inputs = tokens_ref[0, 0].astype(F32)
        inverse = lax.rsqrt(jnp.mean(inputs * inputs, axis=-1, keepdims=True) + EPSILON)
        scaled = total[...] * gain_ref[...]
        mean = jnp.mean(scaled * inputs, axis=-1, keepdims=True)
        grad = inverse * scaled - inputs * (inverse * inverse * inverse) * mean
        out_ref[0, 0] = (grad_res_ref[...] + grad).astype(BF16)
        gain_out_ref[...] = jnp.sum(total[...] * inputs * inverse, axis=0, keepdims=True)


def final_part(core, tokens, unit, grad_res, gain, weights, cosine, sine, back, head_dim, output):
    width, model = tokens.shape[2:]
    here = len(back)
    steps = model // 256

    def fixed(a):
        return pl.BlockSpec(a.shape, lambda c: (0,) * a.ndim)

    token_spec = pl.BlockSpec((1, 1, width, model), lambda c: unit + (0, 0))
    weight_specs = [pl.BlockSpec((model, 256), lambda c, i=i: (0, i * steps + c)) for i in range(3)]
    row_spec = pl.BlockSpec((256, width), lambda c: (c, 0))
    operands = [core, tokens, grad_res, gain, weights, weights, weights, cosine, sine, *back]
    in_specs = [
        pl.BlockSpec(memory_space=pltpu.SMEM), token_spec, fixed(grad_res), fixed(gain), *weight_specs,
        fixed(cosine), fixed(sine),
    ] + [
        pl.BlockSpec((256 // head_dim // here, 3 * head_dim, width), lambda c: (c, 0, 0)) for _ in back
    ]
    aliases = {}
    if output is not None:
        aliases = {len(operands): 0}
        operands.append(output)
        in_specs.append(pl.BlockSpec(memory_space=pl.ANY))
    struct = jax.ShapeDtypeStruct
    return pl.pallas_call(
        functools.partial(final_kernel, (here, head_dim, output is not None)),
        grid=(steps,),
        in_specs=in_specs,
        out_specs=[token_spec, row_spec, row_spec, row_spec, pl.BlockSpec((1, model), lambda c: (0, 0))],
        out_shape=[
            struct(tokens.shape, BF16), struct((model, width), BF16), struct((model, width), BF16),
            struct((model, width), BF16), struct((1, model), F32),
        ],
        scratch_shapes=[pltpu.VMEM((width, model), F32)],
        input_output_aliases=aliases,
        compiler_params=pltpu.CompilerParams(vmem_limit_bytes=62 << 20),
        cost_estimate=pl.CostEstimate(
            flops=6 * width * model * model, bytes_accessed=12 * model * model, transcendentals=0
        ),
        name="final_part",
    )(*operands)


def picked_kernel(units, rows, places, flipped, split, table_ref, *refs):
    weights = len(places)
    lefts = refs[0:units]
    rights = refs[units : units * (1 + weights)]
    outs = refs[units * (1 + weights) : units * (1 + weights) + weights * split]
    picked = refs[units * (1 + weights) + weights * split :]

    @pl.when(pl.program_id(0) == 0)
    def _():
        for w, (start, size) in enumerate(places):
            for p in range(size):
                at = pl.ds(pl.multiple_of(table_ref[start + p] * rows, rows), rows)
                for u in range(units):
                    picked[w * units + u][p * rows : (p + 1) * rows, :] = lefts[u][at, :]

    for w in range(weights):
        total = None
        for u in range(units):
            right = rights[w * units + u][...]
            left = picked[w * units + u][...]
            made = contract(left, right, 1, 1) if flipped else dot(left, right)
            total = made if total is None else total + made
        height = total.shape[0] // split
        for i in range(split):
            outs[w * split + i][...] = total[i * height : (i + 1) * height].astype(BF16)


def picked_grads(table, places, lefts, rights, rows, flipped, split, block, name):
    units = len(lefts)
    width = lefts[0].shape[1]
    columns = rights[0].shape[0 if flipped else 1]
    in_specs = [pl.BlockSpec(a.shape, lambda n, *_: (0, 0)) for a in lefts]
    for a in rights:
        if flipped:
            in_specs.append(pl.BlockSpec((block, width), lambda n, *_: (n, 0)))
        else:
            in_specs.append(pl.BlockSpec((width, block), lambda n, *_: (0, n)))
    heights = [size * rows for _, size in places]
    return pl.pallas_call(
        functools.partial(picked_kernel, units, rows, places, flipped, split),
        grid_spec=pltpu.PrefetchScalarGridSpec(
            num_scalar_prefetch=1,
            grid=(columns // block,),
            in_specs=in_specs,
            out_specs=[
                pl.BlockSpec((height // split, block), lambda n, *_: (0, n)) for height in heights for _ in range(split)
            ],
            scratch_shapes=[pltpu.VMEM((height, width), BF16) for height in heights for _ in lefts],
        ),
        out_shape=[
            jax.ShapeDtypeStruct((height // split, columns), BF16) for height in heights for _ in range(split)
        ],
        compiler_params=pltpu.CompilerParams(vmem_limit_bytes=62 << 20),
        cost_estimate=pl.CostEstimate(
            flops=2 * units * sum(heights) * width * columns,
            bytes_accessed=4 * sum(heights) * columns,
            transcendentals=0,
        ),
        name=name,
    )(table, *lefts, *rights)


def tall_kernel(units, pieces_here, table_ref, *refs):
    keep_ref, send_ref = refs[-2:]
    total = None
    for u in range(units):
        left = [refs[u * pieces_here + i][...] for i in range(pieces_here)]
        made = dot(jnp.concatenate(left, axis=0), refs[units * pieces_here + u][...])
        total = made if total is None else total + made
    kept = pl.program_id(0) < pl.num_programs(0) // 2

    @pl.when(kept)
    def _():
        keep_ref[...] = total.astype(BF16)

    @pl.when(jnp.logical_not(kept))
    def _():
        send_ref[...] = total.astype(BF16)


def tall_grads(table, lefts, rights, rows, name):
    units = len(lefts)
    width = lefts[0].shape[1]
    columns = rights[0].shape[1]
    places = table.shape[0]
    each = 4
    middle = places // each // 2
    in_specs = []
    for _ in lefts:
        for i in range(each):
            in_specs.append(pl.BlockSpec((rows, width), lambda n, table, i=i: (table[n * each + i], 0)))
    in_specs += [pl.BlockSpec(a.shape, lambda n, *_: (0, 0)) for a in rights]
    return pl.pallas_call(
        functools.partial(tall_kernel, units, each),
        grid_spec=pltpu.PrefetchScalarGridSpec(
            num_scalar_prefetch=1,
            grid=(places // each,),
            in_specs=in_specs,
            out_specs=[
                pl.BlockSpec((each * rows, columns), lambda n, *_: (jnp.minimum(n, middle - 1), 0)),
                pl.BlockSpec((each * rows, columns), lambda n, *_: (jnp.maximum(n - middle, 0), 0)),
            ],
        ),
        out_shape=[jax.ShapeDtypeStruct((places // 2 * rows, columns), BF16)] * 2,
        compiler_params=pltpu.CompilerParams(vmem_limit_bytes=62 << 20),
        cost_estimate=pl.CostEstimate(
            flops=2 * units * places * rows * width * columns,
            bytes_accessed=2 * places * rows * columns,
            transcendentals=0,
        ),
        name=name,
    )(table, *[a for a in lefts for _ in range(each)], *rights)


def reduce_kernel(orders, count, *refs):
    streams = len(orders)
    rounds = len(orders[0])
    ins, vec_ref = refs[:streams], refs[streams]
    outs, vec_out = refs[streams + 1 : 2 * streams + 1], refs[2 * streams + 1]
    rest = refs[2 * streams + 2 :]
    works, arrivals = rest[:streams], rest[streams : 2 * streams]
    vec_work, vec_arrival, send_sem, recv_sem, vec_send, vec_recv = rest[2 * streams :]
    shard, seq = lax.axis_index("shard"), lax.axis_index("seq")

    def partner(mask):
        if mask >= count:
            step = mask // count
            return (shard + step * (1 - 2 * (shard // step % 2)), seq)
        return (shard, seq + mask * (1 - 2 * (seq // mask % 2)))

    barrier = pltpu.get_barrier_semaphore()
    for mask in orders[0]:
        pl.semaphore_signal(
            barrier, inc=1, device_id=partner(mask), device_id_type=pl.DeviceIdType.MESH
        )
    pl.semaphore_wait(barrier, rounds)

    height = ins[0].shape[0]
    halves = [height >> (r + 1) for r in range(rounds)]
    starts = [sum(halves[:r]) for r in range(rounds)]

    def copy_of(s, r):
        source = ins[s] if r == 0 else works[s]
        return pltpu.make_async_remote_copy(
            src_ref=source.at[pl.ds(halves[r], halves[r])],
            dst_ref=arrivals[s].at[pl.ds(starts[r], halves[r])],
            send_sem=send_sem.at[s, r],
            recv_sem=recv_sem.at[s, r],
            device_id=partner(orders[s][r]),
            device_id_type=pl.DeviceIdType.MESH,
        )

    def vec_copy(r):
        return pltpu.make_async_remote_copy(
            src_ref=vec_ref if r == 0 else vec_work.at[r - 1],
            dst_ref=vec_arrival.at[r],
            send_sem=vec_send.at[r],
            recv_sem=vec_recv.at[r],
            device_id=partner(orders[0][r]),
            device_id_type=pl.DeviceIdType.MESH,
        )

    for s in range(streams):
        copy_of(s, 0).start()
    vec_copy(0).start()
    for r in range(rounds):
        for s in range(streams):
            copy_of(s, r).wait_recv()
            source = ins[s] if r == 0 else works[s]
            size = halves[r]

            def added(low, high):
                mine = source[low:high].astype(F32)
                return mine + arrivals[s][starts[r] + low : starts[r] + high].astype(F32)

            if r == rounds - 1:
                outs[s][...] = added(0, size)
            else:
                works[s][size // 2 : size] = added(size // 2, size).astype(BF16)
                copy_of(s, r + 1).start()
                works[s][0 : size // 2] = added(0, size // 2).astype(BF16)
        vec_copy(r).wait_recv()
        before = vec_ref[...] if r == 0 else vec_work[r - 1]
        if r == rounds - 1:
            vec_out[...] = before + vec_arrival[r]
        else:
            vec_work[r] = before + vec_arrival[r]
            vec_copy(r + 1).start()
    for r in range(rounds):
        for s in range(streams):
            copy_of(s, r).wait_send()
        vec_copy(r).wait_send()


def reduce_rows(parts, vector, orders, count):
    streams = len(parts)
    rounds = len(orders[0])
    height, columns = parts[0].shape
    rows = height >> rounds
    vmem = pl.BlockSpec(memory_space=pltpu.VMEM)
    return pl.pallas_call(
        functools.partial(reduce_kernel, orders, count),
        in_specs=[vmem] * (streams + 1),
        out_specs=[vmem] * (streams + 1),
        out_shape=[jax.ShapeDtypeStruct((rows, columns), F32)] * streams
        + [jax.ShapeDtypeStruct(vector.shape, F32)],
        scratch_shapes=[pltpu.VMEM((height // 2, columns), BF16) for _ in parts]
        + [pltpu.VMEM((height - rows, columns), BF16) for _ in parts]
        + [
            pltpu.VMEM((rounds - 1,) + vector.shape, F32),
            pltpu.VMEM((rounds,) + vector.shape, F32),
            pltpu.SemaphoreType.DMA((streams, rounds)),
            pltpu.SemaphoreType.DMA((streams, rounds)),
            pltpu.SemaphoreType.DMA((rounds,)),
            pltpu.SemaphoreType.DMA((rounds,)),
        ],
        compiler_params=pltpu.CompilerParams(
            collective_id=0, has_side_effects=True, vmem_limit_bytes=62 << 20
        ),
        name="reduce_rows",
    )(*parts, vector)


def on_device(
    tokens, cotangent, lengths, variates, positions, attn_gain, w_query, w_key, w_value, w_out,
    bias_table, ffn_gain, w_gate, w_up, w_down,
):
    micro, seqs, width, model = tokens.shape
    heads = bias_table.shape[0]
    head_dim = model // heads
    count = lax.axis_size("seq")
    here = heads // count
    ffn = w_gate.shape[1]
    devices = lax.axis_size("shard") * count
    seq_index = lax.axis_index("seq")
    units = [(m, s) for m in range(micro) for s in range(seqs)]
    swap = here == 2 and len(units) == 2 and lax.axis_size("shard") % 2 == 0
    core = (lax.axis_index("shard") % 2 if swap else jnp.int32(0)).astype(jnp.int32).reshape(1)
    heads_here = 1 if swap else here
    first_head = seq_index * here + core[0]
    bias_here = lax.dynamic_slice_in_dim(bias_table, first_head, heads_here, 0)
    attn_row, ffn_row = attn_gain[None, :], ffn_gain[None, :]

    def gather(weight):
        return lax.all_gather(weight, "shard", axis=0, tiled=True)

    def exchange(values):
        return lax.all_to_all(values, "seq", split_axis=0, concat_axis=0, tiled=True)

    def after(value, *before):
        return lax.optimization_barrier((value,) + before)[0]

    attn_joined = gather(jnp.concatenate([w_query, w_key, w_value], axis=1))
    ffn_weights = [gather(w_out), gather(w_gate), gather(w_up), gather(w_down)]

    def permute(value, mask):
        return lax.ppermute(value, ("shard", "seq"), [(i, i ^ mask) for i in range(devices)])

    def cross(value):
        return permute(value, count)

    lengths_of = [lengths, cross(lengths)] if swap else [lengths] * here
    packed_list, flats, tables = [], [], []

    def run_project(u, token):
        m, s = units[u]
        cosine, sine = rotary_tables(positions[m, s], head_dim // 2)
        ids = after(variates[m, s].astype(F32)[None, :], *token)
        flat, *packed = project(
            core, tokens, (m, s), attn_row, attn_joined, cosine, sine, ids, count, here, head_dim, swap
        )
        flats.append(flat)
        tables.append((cosine, sine))
        packed_list.append(packed)

    sent = {}
    mixed_now = [None] * len(units)
    sums = {}
    mixed_tok = {}
    crossed, mixed_part, mixed_cross, heads_cross, back_cross = {}, {}, {}, {}, {}
    middle = [None] * len(units)
    grad_heads = {}
    state = {"output": None, "grads": None}
    packed_grads = {}
    returned = {}
    bias_terms = {}
    finals = [None] * len(units)

    def length_of(u, h, token):
        m, s = units[u]
        return after(lengths_of[h][m, s].reshape(1), *token)

    def inputs_of(u, h):
        if not swap:
            return sent[u, h], sent[u, 0]
        return (sent[u, 0], sent[u, 1]) if h == 0 else (crossed[u], crossed[u])

    def run_forward(u, h, token):
        made, sums[u, h] = attend_forward(
            *inputs_of(u, h), length_of(u, h, token), bias_here, None if swap else mixed_now[u],
            0 if swap else h, heads_here, head_dim,
        )
        if swap:
            mixed_part[u, h] = made
            if h == 1:
                mixed_cross[u] = cross(made)
        else:
            mixed_now[u] = made
        return sums[u, h]

    def run_middle(u, token):
        m, s = units[u]
        info = jnp.stack([lengths[m, s], seq_index * width, core[0]]).astype(jnp.int32)
        state["output"], mixed_tok[u], *middle[u] = middle_part(
            after(info, *token), mixed_tok[u], tokens, cotangent, (m, s), ffn_weights, ffn_row, head_dim,
            state["output"],
        )
        return middle[u][8]

    def run_backward(u, h, token):
        if swap:
            grad = grad_heads[u] if h == 0 else heads_cross[u]
            mixed = mixed_part[u, h]
        else:
            grad, mixed = grad_heads[u], mixed_now[u]
        packed_grads[u, h], both = attend_backward(
            *inputs_of(u, h), grad, mixed, sums[u, h], length_of(u, h, token), bias_here,
            0 if swap else h, head_dim,
        )
        if swap and h == 1:
            back_cross[u] = cross(packed_grads[u, h])
        bias_terms[u, h] = both
        return both

    def run_final(u, token):
        m, s = units[u]
        cosine, sine = tables[u]
        state["grads"], *finals[u] = final_part(
            core, tokens, (m, s), middle[u][5], after(attn_row, *token), attn_joined, cosine, sine,
            [returned[u, h] for h in range(here)], head_dim, state["grads"],
        )
        return finals[u][3]

    rows = model // devices
    fold = ffn // model
    tall = ffn // devices
    seq_masks = [1 << i for i in range(count.bit_length() - 1)]
    shard_masks = [count << i for i in range((devices // count).bit_length() - 1)]
    spread = shard_masks[1:]
    orders = (
        shard_masks[:1] + spread + seq_masks,
        shard_masks[:1] + seq_masks[:1] + spread + seq_masks[1:],
        shard_masks[:1] + seq_masks[1:2] + seq_masks[:1] + spread + seq_masks[2:],
    )
    direct = rows % 16 == 0 and devices == 1 << len(orders[0])

    def places_of(order):
        marks = []
        for p in range(devices):
            bits = [p >> (len(order) - 1 - i) & 1 for i in range(len(order))]
            marks.append(sum(mask for bit, mask in zip(bits, order) if bit))
        me = lax.axis_index("shard") * count + seq_index
        return me.astype(jnp.int32) ^ jnp.array(marks, jnp.int32)

    def column(index):
        return [item[index] for item in middle]

    def run_weights(token):
        if not direct:
            return [
                sum(dot(left, right) for left, right in zip(lefts, rights)).astype(BF16)
                for lefts, rights in (
                    (column(0), column(2)), (column(0), column(3)), (column(1), column(4)),
                    ([mixed_tok[u] for u in range(len(units))], column(6)),
                )
            ]
        tables = [after(places_of(order), *token) for order in orders]
        span = [(0, devices)]
        down = tall_grads(tables[2], column(1), column(4), tall, "down_grad")
        table = after(tables[0], down[0])
        gate = picked_grads(table, span, column(0), column(2), rows, False, 2, 512, "gate_grad")
        table = after(tables[1], gate[0])
        up = picked_grads(table, span, column(0), column(3), rows, False, 2, 512, "up_grad")
        table = after(tables[2], up[0])
        mixed_all = [mixed_tok[u] for u in range(len(units))]
        out = picked_grads(table, span, mixed_all, column(6), rows, False, 2, 512, "out_grad")
        streams = []
        for (keep, send), order in zip((down, gate, up, out), (orders[2], orders[0], orders[1], orders[2])):
            streams.append([keep, permute(send, order[0]), order[1:]])
        holder["streams"] = streams
        return out[0]

    def wide_sum(a, b):
        return a.astype(F32) + b.astype(F32)

    def advance(token):
        out = ()
        if not direct:
            return out
        for stream in holder["streams"]:
            keep, came, masks = stream
            if not masks:
                continue
            keep = after(keep, *token)
            half = keep.shape[0] // 2
            send = wide_sum(keep[half:], came[half:]).astype(BF16)
            stream[0] = wide_sum(keep[:half], came[:half]).astype(BF16)
            stream[1] = permute(send, masks[0])
            stream[2] = masks[1:]
            out = out + (send, stream[0])
        return out

    holder = {}

    def weights_work(token):
        holder["terms"] = run_weights(token)
        return holder["terms"]

    def send_packed(u, h):
        def keep(moved):
            sent[u, h] = moved
            if swap and h == 1:
                crossed[u] = cross(moved)

        return lambda: packed_list[u][h], keep

    def send_mixed(u):
        def keep(moved):
            mixed_tok[u] = moved.reshape(model, width)

        if not swap:
            return lambda: mixed_now[u], keep
        return lambda: jnp.concatenate([mixed_part[u, 0], mixed_cross[u]], axis=1), keep

    def send_heads(u):
        def keep(moved):
            grad_heads[u] = moved
            if swap:
                heads_cross[u] = cross(moved[:, head_dim:])

        return lambda: middle[u][7].reshape(count, here * head_dim, width), keep

    def send_back(u, h):
        def keep(moved):
            returned[u, h] = moved

        return lambda: back_cross[u] if swap and h == 1 else packed_grads[u, h], keep

    def work_project(u):
        def work(token):
            run_project(u, token)
            return flats[u]

        return work

    def work(function, *args):
        return lambda token: function(*args, token)

    total = len(units)
    order = [(u, h) for u in range(total) for h in range(here)]
    if swap:
        steps = [
            (work_project(0), None),
            (work_project(1), send_packed(0, 1)),
            (work(run_forward, 0, 1), send_packed(0, 0)),
            (work(run_forward, 0, 0), send_packed(1, 1)),
            (work(run_forward, 1, 1), send_mixed(0)),
            (work(run_middle, 0), send_packed(1, 0)),
            (work(run_forward, 1, 0), send_heads(0)),
            (work(run_backward, 0, 0), send_mixed(1)),
            (work(run_middle, 1), send_back(0, 0)),
            (weights_work, send_heads(1)),
            (work(run_backward, 0, 1), None),
            (work(run_backward, 1, 1), send_back(0, 1)),
            (work(run_backward, 1, 0), send_back(1, 1)),
            (work(run_final, 0), send_back(1, 0)),
            (work(run_final, 1), None),
        ]
    else:
        steps = [(work_project(u), None) for u in range(total)]
        steps += [(None, send_packed(*at)) for at in order]
        for u in range(total):
            steps += [(work(run_forward, u, h), None) for h in range(here)]
            steps += [(None, send_mixed(u))]
        for u in range(total):
            steps += [(work(run_middle, u), None), (None, send_heads(u))]
        steps += [(weights_work, None)]
        for at in order:
            steps += [(work(run_backward, *at), None), (None, send_back(*at))]
        steps += [(work(run_final, u), None) for u in range(total)]

    late = [task for task, _ in steps[-2:]]
    token = ()
    for task, send in steps:
        done = ()
        moved = None
        if "streams" in holder:
            leaving = advance(token)
            token = token if task in late else token + leaving
        if send is not None:
            moved = exchange(after(send[0](), *token))
            done = (moved,)
        if task is not None:
            done = done + (task(token),)
        if send is not None:
            send[1](after(moved, *done[1:]))
        token = done
    acc_bias = jnp.concatenate(
        [sum(bias_terms[u, h] for u in range(total))[0:1, 0:2] for h in range(here)], axis=0
    )
    if swap:
        acc_bias = acc_bias[0:1] + acc_bias[1:2]
    bias_full = lax.dynamic_update_slice(
        jnp.zeros((heads, 2), F32), acc_bias, (first_head, jnp.int32(0))
    )
    gain_attn = sum(item[3][0] for item in finals)
    gain_ffn = sum(item[8][0] for item in middle)
    if direct:
        while holder["streams"][0][2]:
            advance(token)
        down_own, gate_own, up_own, out_own = [
            wide_sum(after(keep, *token), came) for keep, came, _ in holder["streams"]
        ]
        table = jnp.concatenate([places_of(order) for order in orders])
        attn_terms = picked_grads(
            table, [(i * devices, devices) for i in range(3)], flats,
            [item[i] for i in range(3) for item in finals], rows, True, 1, 256, "attn_grads",
        )
        flat = jnp.concatenate([gain_attn, gain_ffn, bias_full.reshape(-1)])
        tiles = -(-flat.shape[0] // 1024) * 8
        flat = jnp.pad(flat, (0, tiles * 128 - flat.shape[0])).reshape(tiles, 128)
        query_own, key_own, value_own, flat = reduce_rows(list(attn_terms), flat, orders, count)
        flat = flat.reshape(-1)
        gain_attn, gain_ffn = flat[:model], flat[model : 2 * model]
        bias_full = flat[2 * model : 2 * model + 2 * heads].reshape(heads, 2)
    else:

        def scatter(value):
            owned = lax.psum_scatter(value, ("shard", "seq"), scatter_dimension=0, tiled=True)
            return owned.astype(F32)

        gate_own, up_own, down_own, out_own = [scatter(value) for value in holder["terms"]]
        query_own, key_own, value_own = [
            scatter(
                sum(contract(flat, item[i], 1, 1) for flat, item in zip(flats, finals)).astype(BF16)
            )
            for i in range(3)
        ]
        gain_attn, gain_ffn, bias_full = lax.psum(
            (gain_attn, gain_ffn, bias_full), ("shard", "seq")
        )
    return (
        state["output"], state["grads"], gain_attn, query_own, key_own, value_own, out_own,
        bias_full, gain_ffn, gate_own, up_own, down_own,
    )


def solution(mesh):
    token_spec = P(None, "shard", "seq", None)
    row_spec = P("shard", None)
    in_specs = (
        token_spec, token_spec, P(None, "shard"), P(None, "shard", "seq"), P(None, "shard", "seq"),
        P(), row_spec, row_spec, row_spec, row_spec, P(), P(), row_spec, row_spec, row_spec,
    )
    owned = P(("shard", "seq"), None)
    out_specs = (
        token_spec, token_spec, P(), owned, owned, owned, owned, P(), P(), owned, owned, owned,
    )
    return jax.shard_map(
        on_device, mesh=mesh, in_specs=in_specs, out_specs=out_specs, check_vma=False
    )
```

```python
import functools
import math

import jax
import jax.numpy as jnp
from jax import lax
from jax.experimental import pallas as pl
from jax.experimental.pallas import tpu as pltpu
from jax.sharding import PartitionSpec as P

EPSILON = 1e-06
ROTARY_BASE = 10000.0
LOG2E = 1.4426950408889634
LN2 = 0.6931471805599453
CLASSES = 8
AUX = 16
EXTRA = 32
MASKED = -1.5e9
FAR = 1e30
F32 = jnp.float32
BF16 = jnp.bfloat16


def dot(a, b):
    return jnp.dot(a, b, preferred_element_type=F32)


def contract(a, b, da, db):
    return lax.dot_general(a, b, (((da,), (db,)), ((), ())), preferred_element_type=F32)


def pieces(x):
    high = x.astype(BF16).astype(F32)
    rest = x - high
    mid = rest.astype(BF16).astype(F32)
    low = (rest - mid).astype(BF16).astype(F32)
    return high, mid, low


def one_hot(row):
    classes = lax.broadcasted_iota(jnp.int32, (CLASSES, row.shape[1]), 0).astype(F32)
    return jnp.where(classes == row, 1.0, 0.0)


def rows_of(values, width):
    index = lax.broadcasted_iota(jnp.int32, (8, width), 0)
    out = jnp.zeros((8, width), F32)
    for at, value in enumerate(values):
        out = jnp.where(index == at, value, out)
    return out


def key_extra(row, start, length, other, same):
    width = row.shape[1]
    hot = one_hot(row)
    step = pieces(jnp.full((1, width), same - other, F32))
    base = pieces(jnp.full((1, width), other, F32))
    index = start + lax.broadcasted_iota(jnp.int32, (1, width), 1)
    mask = jnp.where(index < length, 0.0, MASKED)
    tail = rows_of(base + (mask, 1.0, 1.0, 1.0), width)
    return jnp.concatenate([hot * step[0], hot * step[1], hot * step[2], tail], axis=0).astype(BF16)


def query_extra(row, shift):
    hot = one_hot(row)
    tail = rows_of((1.0, 1.0, 1.0, 1.0) + shift, row.shape[1])
    return jnp.concatenate([hot, hot, hot, tail], axis=0).astype(BF16)


def forward_kernel(
    shape, len_ref, bias_ref, x_ref, ids_ref, *rest
):
    local, head_dim, block, aliased = shape
    if aliased:
        rest = rest[1:]
    mixed_ref, lse_ref, keys, vals, query, score, peak, total = rest
    count, _, width = x_ref.shape
    sub = block // width
    step = pl.program_id(0)
    length = len_ref[0]
    other = bias_ref[local, 0] * LOG2E
    same = bias_ref[local, 1] * LOG2E

    @pl.when(step == 0)
    def _():
        for b in range(count):
            at = pl.ds(b * width, width)
            row = ids_ref[b, 0:1, :].astype(F32)
            extra = key_extra(row, b * width, length, other, same)
            full = jnp.concatenate([x_ref[b, head_dim : 2 * head_dim, :], extra], axis=0)
            keys[at, :] = full.T
            vals[0:head_dim, at] = x_ref[b, 2 * head_dim : 3 * head_dim, :]
        vals[head_dim:, :] = jnp.ones((16, vals.shape[1]), BF16)

    used = pl.cdiv(length, block)
    inside = step * block < length

    @pl.when(jnp.logical_not(inside))
    def _():
        mixed_ref[...] = jnp.zeros_like(mixed_ref)
        lse_ref[...] = jnp.full(lse_ref.shape, FAR, F32)

    @pl.when(inside)
    def _():
        for b in range(sub):
            at = slice(b * width, (b + 1) * width)
            row = ids_ref[step * sub + b, 0:1, :].astype(F32)
            query[0:head_dim, at] = x_ref[step * sub + b, 0:head_dim, :]
            query[head_dim:, at] = query_extra(row, (0.0, 0.0, 0.0))
        peak[...] = jnp.full(peak.shape, -FAR, F32)
        total[...] = jnp.zeros_like(total)

        def span(j):
            return pl.ds(pl.multiple_of(j * block, block), block)

        def scores_of(j):
            return dot(keys[span(j), :], query[...])

        def one(j, now, ahead):
            if ahead:
                score[1 - now] = scores_of(j + 1)
            current = score[now]
            before = peak[...]
            top = jnp.maximum(before, jnp.max(current, axis=0, keepdims=True))
            weight = jnp.exp2(current - top).astype(BF16)
            peak[...] = top
            total[...] = total[...] * jnp.exp2(before - top) + dot(vals[:, span(j)], weight)

        score[0] = scores_of(0)
        pairs = (used - 1) // 2

        def pair(j, carry):
            one(2 * j, 0, True)
            one(2 * j + 1, 1, True)
            return carry

        lax.fori_loop(0, pairs, pair, 0)
        last = 2 * pairs

        @pl.when(used - last == 1)
        def _():
            one(last, 0, False)

        @pl.when(used - last == 2)
        def _():
            one(last, 0, True)
            one(last + 1, 1, False)

        mass = total[head_dim : head_dim + 1, :]
        mixed = (total[0:head_dim, :] / mass).astype(BF16)
        for b in range(sub):
            mixed_ref[b] = mixed[:, b * width : (b + 1) * width]
        lse_ref[0] = peak[...] + jnp.log2(mass)


def attend_forward(x, ids, length, bias, mixed, local, heads_here, head_dim):
    count, rows, width = x.shape
    block = max(width, 512)
    seq_len = count * width
    blocks = seq_len // block
    depth = head_dim + EXTRA
    whole = pl.BlockSpec((count, rows, width), lambda i, *_: (0, 0, 0))
    operands = [length, bias, x, ids]
    in_specs = [whole, pl.BlockSpec((count, AUX, width), lambda i, *_: (0, 3 * head_dim // AUX, 0))]
    aliases = {}
    if mixed is not None:
        operands.append(mixed)
        in_specs.append(pl.BlockSpec(memory_space=pl.ANY))
        aliases = {4: 0}
    return pl.pallas_call(
        functools.partial(forward_kernel, (local, head_dim, block, mixed is not None)),
        grid_spec=pltpu.PrefetchScalarGridSpec(
            num_scalar_prefetch=2,
            grid=(blocks,),
            in_specs=in_specs,
            out_specs=[
                pl.BlockSpec((block // width, head_dim, width), lambda i, *_: (i, local, 0)),
                pl.BlockSpec((1, 1, block), lambda i, *_: (i, 0, 0)),
            ],
            scratch_shapes=[
                pltpu.VMEM((seq_len, depth), BF16),
                pltpu.VMEM((head_dim + 16, seq_len), BF16),
                pltpu.VMEM((depth, block), BF16),
                pltpu.VMEM((2, block, block), F32),
                pltpu.VMEM((1, block), F32),
                pltpu.VMEM((head_dim + 16, block), F32),
            ],
        ),
        out_shape=[
            jax.ShapeDtypeStruct((count, heads_here * head_dim, width), BF16),
            jax.ShapeDtypeStruct((blocks, 1, block), F32),
        ],
        input_output_aliases=aliases,
        compiler_params=pltpu.CompilerParams(vmem_limit_bytes=62 << 20),
        cost_estimate=pl.CostEstimate(
            flops=8 * seq_len * seq_len * 256,
            bytes_accessed=x.size * 4,
            transcendentals=seq_len * seq_len,
        ),
        name="attend_forward",
    )(*operands)


def backward_kernel(
    shape, len_ref, bias_ref, x_ref, ids_ref, grad_ref, mixed_ref, lse_ref, out_ref, bias_out_ref,
    keys, keys_flat, vals, query, grads, query_rows, grad_rows, acc_keys, acc_vals, acc_query,
):
    local, head_dim, block = shape
    count, _, width = x_ref.shape
    sub = block // width
    step = pl.program_id(0)
    length = len_ref[0]
    other = bias_ref[local, 0] * LOG2E
    same = bias_ref[local, 1] * LOG2E

    @pl.when(step == 0)
    def _():
        ones = jnp.ones((16, width), BF16)
        for b in range(count):
            at = pl.ds(b * width, width)
            row = ids_ref[b, 0:1, :].astype(F32)
            extra = key_extra(row, b * width, length, other, same)
            here = x_ref[b, head_dim : 2 * head_dim, :]
            keys[at, :] = jnp.concatenate([here, extra], axis=0).T
            keys_flat[:, at] = here
            vals[at, :] = jnp.concatenate([x_ref[b, 2 * head_dim : 3 * head_dim, :], ones], axis=0).T
        acc_keys[...] = jnp.zeros_like(acc_keys)
        acc_vals[...] = jnp.zeros_like(acc_vals)

    used = pl.cdiv(length, block)
    inside = step * block < length

    @pl.when(jnp.logical_not(inside))
    def _():
        for b in range(sub):
            out_ref[step * sub + b, 0:head_dim, :] = jnp.zeros((head_dim, width), BF16)

    @pl.when(inside)
    def _():
        for b in range(sub):
            at = slice(b * width, (b + 1) * width)
            here = step * sub + b
            row = ids_ref[here, 0:1, :].astype(F32)
            shift = pieces(-lse_ref[step][:, at])
            grad = grad_ref[here]
            delta = jnp.sum(grad.astype(F32) * mixed_ref[here].astype(F32), axis=0, keepdims=True)
            query[0:head_dim, at] = x_ref[here, 0:head_dim, :]
            query[head_dim:, at] = query_extra(row, shift)
            grads[0:head_dim, at] = grad
            tail = rows_of(pieces(-delta), width)
            grads[head_dim:, at] = jnp.concatenate([tail, jnp.zeros_like(tail)], axis=0).astype(BF16)
        query_rows[...] = query[...].T
        grad_rows[...] = grads[...].T
        acc_query[...] = jnp.zeros_like(acc_query)

        def one(j):
            at = pl.ds(pl.multiple_of(j * block, block), block)
            probs = jnp.exp2(dot(keys[at, :], query[...]))
            grad_probs = dot(vals[at, :], grads[...])
            grad_scores = (probs * grad_probs).astype(BF16)
            acc_vals[at, :] += dot(probs.astype(BF16), grad_rows[...])
            acc_keys[at, :] += dot(grad_scores, query_rows[...])
            acc_query[...] += dot(keys_flat[:, at], grad_scores)

        def pair(j, carry):
            one(2 * j)
            one(2 * j + 1)
            return carry

        lax.fori_loop(0, used // 2, pair, 0)

        @pl.when(used % 2 == 1)
        def _():
            one(used - 1)

        grad_query = (acc_query[...] * (1.0 / math.sqrt(head_dim))).astype(BF16)
        for b in range(sub):
            out_ref[step * sub + b, 0:head_dim, :] = grad_query[:, b * width : (b + 1) * width]

    @pl.when(step == pl.num_programs(0) - 1)
    def _():
        same_total = jnp.zeros((CLASSES, width), F32)
        all_total = jnp.zeros((CLASSES, width), F32)
        for b in range(count):
            at = pl.ds(b * width, width)
            row = ids_ref[b, 0:1, :].astype(F32)
            flat = acc_keys[at, :].T
            out_ref[b, head_dim : 2 * head_dim, :] = (flat[0:head_dim] * LN2).astype(BF16)
            out_ref[b, 2 * head_dim : 3 * head_dim, :] = acc_vals[at, :].T[0:head_dim].astype(BF16)
            by_class = flat[head_dim : head_dim + CLASSES]
            all_total += by_class
            same_total += by_class * one_hot(row)
        same_sum = jnp.sum(same_total, keepdims=True)
        other_sum = jnp.sum(all_total, keepdims=True) - same_sum
        lane = lax.broadcasted_iota(jnp.int32, (8, 128), 1)
        bias_out_ref[...] = jnp.where(lane == 0, other_sum, jnp.where(lane == 1, same_sum, 0.0))


def attend_backward(x, ids, grad, mixed, lse, length, bias, local, head_dim):
    count, rows, width = x.shape
    blocks, _, block = lse.shape
    seq_len = count * width
    depth = head_dim + EXTRA

    def whole(a):
        return pl.BlockSpec(a.shape, lambda i, *_: (0,) * a.ndim)

    head_spec = pl.BlockSpec((count, head_dim, width), lambda i, *_: (0, local, 0))
    return pl.pallas_call(
        functools.partial(backward_kernel, (local, head_dim, block)),
        grid_spec=pltpu.PrefetchScalarGridSpec(
            num_scalar_prefetch=2,
            grid=(blocks,),
            in_specs=[
                whole(x),
                pl.BlockSpec((count, AUX, width), lambda i, *_: (0, 3 * head_dim // AUX, 0)),
                head_spec, head_spec, whole(lse),
            ],
            out_specs=[
                pl.BlockSpec((count, 3 * head_dim, width), lambda i, *_: (0, 0, 0)),
                pl.BlockSpec((8, 128), lambda i, *_: (0, 0)),
            ],
            scratch_shapes=[
                pltpu.VMEM((seq_len, depth), BF16),
                pltpu.VMEM((head_dim, seq_len), BF16),
                pltpu.VMEM((seq_len, head_dim + 16), BF16),
                pltpu.VMEM((depth, block), BF16),
                pltpu.VMEM((head_dim + 16, block), BF16),
                pltpu.VMEM((block, depth), BF16),
                pltpu.VMEM((block, head_dim + 16), BF16),
                pltpu.VMEM((seq_len, depth), F32),
                pltpu.VMEM((seq_len, head_dim + 16), F32),
                pltpu.VMEM((head_dim, block), F32),
            ],
        ),
        out_shape=[
            jax.ShapeDtypeStruct((count, 3 * head_dim, width), BF16),
            jax.ShapeDtypeStruct((8, 128), F32),
        ],
        compiler_params=pltpu.CompilerParams(vmem_limit_bytes=62 << 20),
        cost_estimate=pl.CostEstimate(
            flops=20 * seq_len * seq_len * 256,
            bytes_accessed=x.size * 6,
            transcendentals=seq_len * seq_len,
        ),
        name="attend_backward",
    )(length, bias, x, ids, grad, mixed, lse)


def rotary_tables(places, half_dim):
    frequency = jnp.exp(-math.log(ROTARY_BASE) * jnp.arange(half_dim, dtype=F32) / half_dim)
    angles = places.astype(F32)[None, :] * frequency[:, None]
    return jnp.cos(angles), jnp.sin(angles)


def sigmoid_of(x):
    return 1.0 / (1.0 + jnp.exp2(x * -LOG2E))


def project_kernel(
    shape, core_ref, tokens_ref, gain_ref, query_ref, key_ref, value_ref, cos_ref, sin_ref, ids_ref, flat_ref, *rest
):
    here, head_dim, extras, swap = shape
    outs, flat_weights = rest[:-1], rest[-1]
    pair = pl.program_id(0)

    @pl.when(pair == 0)
    def _():
        inputs = tokens_ref[0, 0].astype(F32)
        inverse = lax.rsqrt(jnp.mean(inputs * inputs, axis=-1, keepdims=True) + EPSILON)
        flat_ref[...] = (inputs * inverse * gain_ref[...]).astype(BF16).T

    flat_weights[0:128, :] = query_ref[...].T
    flat_weights[128:256, :] = key_ref[...].T
    flat_weights[256:384, :] = value_ref[...].T
    made = dot(flat_weights[...], flat_ref[...])
    cosine, sine = cos_ref[...], sin_ref[...]
    half = head_dim // 2

    def turned(start, scale):
        first = made[start : start + half]
        second = made[start + half : start + head_dim]
        both = [first * cosine - second * sine, second * cosine + first * sine]
        return (jnp.concatenate(both, axis=0) * scale).astype(BF16)

    def put(at, slot, place):
        spot = at * head_dim
        target = outs[slot]
        target[place, 0:head_dim, :] = turned(spot, LOG2E / math.sqrt(head_dim))
        target[place, head_dim : 2 * head_dim, :] = turned(128 + spot, 1.0)
        target[place, 2 * head_dim : 3 * head_dim, :] = made[256 + spot : 256 + spot + head_dim].astype(BF16)
        if extras[slot]:
            target[place, 3 * head_dim :, :] = jnp.broadcast_to(ids_ref[...], (AUX, ids_ref.shape[1])).astype(BF16)

    if swap:
        for core in range(2):

            @pl.when(core_ref[0] == core)
            def _():
                put(core, 0, 0)
                put(1 - core, 1, 0)

    else:
        for at in range(128 // head_dim):
            put(at, at % here, 0 if here > 1 else at)


def project(core, tokens, unit, gain, weights, cosine, sine, ids, count, here, head_dim, swap):
    width, model = tokens.shape[2:]
    heads = count * here
    pairs = heads * head_dim // 128
    per = 128 // head_dim // here
    extras = [h == (1 if swap else 0) for h in range(here)]

    def fixed(a):
        return pl.BlockSpec(a.shape, lambda p: (0,) * a.ndim)

    weight_specs = [pl.BlockSpec((model, 128), lambda p, i=i: (0, i * pairs + p)) for i in range(3)]
    return pl.pallas_call(
        functools.partial(project_kernel, (here, head_dim, extras, swap)),
        grid=(pairs,),
        in_specs=[
            pl.BlockSpec(memory_space=pltpu.SMEM),
            pl.BlockSpec((1, 1, width, model), lambda p: unit + (0, 0)),
            fixed(gain), *weight_specs, fixed(cosine), fixed(sine), fixed(ids),
        ],
        out_specs=[pl.BlockSpec((model, width), lambda p: (0, 0))]
        + [pl.BlockSpec((per, 3 * head_dim + AUX * e, width), lambda p: (p, 0, 0)) for e in extras],
        out_shape=[jax.ShapeDtypeStruct((model, width), BF16)]
        + [jax.ShapeDtypeStruct((count, 3 * head_dim + AUX * e, width), BF16) for e in extras],
        scratch_shapes=[pltpu.VMEM((384, model), BF16)],
        compiler_params=pltpu.CompilerParams(vmem_limit_bytes=62 << 20),
        cost_estimate=pl.CostEstimate(
            flops=6 * width * model * model, bytes_accessed=12 * model * model, transcendentals=0
        ),
        name="project",
    )(core, tokens, gain, weights, weights, weights, cosine, sine, ids)


def middle_kernel(
    shape, info_ref, mixed_ref, tokens_ref, cot_ref, out_w_ref, gain_ref, gate_w_ref, up_w_ref, down_w_ref, *rest
):
    head_dim, aliased = shape
    if aliased:
        rest = rest[1:]
    (
        output_ref, ordered_ref, flat_ref, hidden_ref, grad_gate_ref, grad_up_ref, grad_ffn_ref, grad_res_ref,
        grad_attn_ref, grad_mixed_ref, gain_out_ref, normed, residual, ffn_out, grad_normed, slots,
    ) = rest
    core = info_ref[2]
    step = pl.program_id(0)
    width = normed.shape[0]

    def valid():
        index = info_ref[1] + lax.broadcasted_iota(jnp.int32, (width, 1), 0)
        return jnp.where(index < info_ref[0], 1.0, 0.0)

    def inverse_of(x):
        return lax.rsqrt(jnp.mean(x * x, axis=-1, keepdims=True) + EPSILON)

    def head_rows(pair, slot):
        head = 2 * pair + (core if slot == 0 else 1 - core)
        return pl.ds(pl.multiple_of(head * head_dim, head_dim), head_dim)

    def slot_rows(pair, slot):
        return slice((2 * pair + slot) * head_dim, (2 * pair + slot + 1) * head_dim)

    spots = [(pair, slot) for pair in range(mixed_ref.shape[0] // head_dim // 2) for slot in range(2)]

    @pl.when(step == 0)
    def _():
        for spot in spots:
            ordered_ref[head_rows(*spot), :] = mixed_ref[slot_rows(*spot), :]
        inputs = tokens_ref[0, 0].astype(F32) + dot(ordered_ref[...].T, out_w_ref[...])
        residual[...] = inputs
        made = (inputs * inverse_of(inputs) * gain_ref[...]).astype(BF16)
        normed[...] = made
        flat_ref[...] = made.T
        grad_ffn_ref[...] = (cot_ref[0, 0].astype(F32) * valid()).astype(BF16)
        ffn_out[...] = jnp.zeros_like(ffn_out)
        grad_normed[...] = jnp.zeros_like(grad_normed)

    gate = dot(normed[...], gate_w_ref[...])
    up = dot(normed[...], up_w_ref[...])
    grad_hidden = contract(grad_ffn_ref[...], down_w_ref[...], 1, 1)
    sigmoid = sigmoid_of(gate)
    silu = gate * sigmoid
    hidden = (silu * up).astype(BF16)
    grad_gate = (grad_hidden * up * (sigmoid + silu * (1.0 - sigmoid))).astype(BF16)
    grad_up = (grad_hidden * silu).astype(BF16)
    hidden_ref[...] = hidden.T
    grad_gate_ref[...] = grad_gate
    grad_up_ref[...] = grad_up
    ffn_out[...] += dot(hidden, down_w_ref[...])
    grad_normed[...] += contract(grad_gate, gate_w_ref[...], 1, 1) + contract(grad_up, up_w_ref[...], 1, 1)

    @pl.when(step == pl.num_programs(0) - 1)
    def _():
        keep = valid()
        kept = residual[...]
        output_ref[0, 0] = ((kept + ffn_out[...]) * keep).astype(BF16)
        inverse = inverse_of(kept)
        scaled = grad_normed[...] * gain_ref[...]
        mean = jnp.mean(scaled * kept, axis=-1, keepdims=True)
        grad = cot_ref[0, 0].astype(F32) * keep
        grad = grad + (inverse * scaled - kept * (inverse * inverse * inverse) * mean)
        gain_out_ref[...] = jnp.sum(grad_normed[...] * kept * inverse, axis=0, keepdims=True)
        grad_res_ref[...] = grad
        low = grad.astype(BF16)
        grad_attn_ref[...] = low
        slots[...] = contract(out_w_ref[...], low, 1, 1).astype(BF16)
        for spot in spots:
            grad_mixed_ref[slot_rows(*spot), :] = slots[head_rows(*spot), :]


def middle_part(info, mixed, tokens, cotangent, unit, weights, gain, head_dim, output):
    width, model = tokens.shape[2:]
    out_w, gate_w, up_w, down_w = weights
    ffn = gate_w.shape[1]
    block = 512

    def fixed(a):
        return pl.BlockSpec(a.shape, lambda f, *_: (0,) * a.ndim)

    def one(*shape):
        return pl.BlockSpec(shape, lambda f, *_: (0,) * len(shape))

    token_spec = pl.BlockSpec((1, 1, width, model), lambda f, *_: unit + (0, 0))
    operands = [info, mixed, tokens, cotangent, out_w, gain, gate_w, up_w, down_w]
    in_specs = [
        fixed(mixed), token_spec, token_spec, fixed(out_w), fixed(gain),
        pl.BlockSpec((model, block), lambda f, *_: (0, f)),
        pl.BlockSpec((model, block), lambda f, *_: (0, f)),
        pl.BlockSpec((block, model), lambda f, *_: (f, 0)),
    ]
    aliases = {}
    if output is not None:
        aliases = {len(operands): 0}
        operands.append(output)
        in_specs.append(pl.BlockSpec(memory_space=pl.ANY))
    struct = jax.ShapeDtypeStruct
    return pl.pallas_call(
        functools.partial(middle_kernel, (head_dim, output is not None)),
        grid_spec=pltpu.PrefetchScalarGridSpec(
            num_scalar_prefetch=1,
            grid=(ffn // block,),
            in_specs=in_specs,
            out_specs=[
                token_spec, one(model, width), one(model, width),
                pl.BlockSpec((block, width), lambda f, *_: (f, 0)),
                pl.BlockSpec((width, block), lambda f, *_: (0, f)),
                pl.BlockSpec((width, block), lambda f, *_: (0, f)),
                one(width, model), one(width, model), one(width, model), one(model, width), one(1, model),
            ],
            scratch_shapes=[
                pltpu.VMEM((width, model), BF16),
                pltpu.VMEM((width, model), F32),
                pltpu.VMEM((width, model), F32),
                pltpu.VMEM((width, model), F32),
                pltpu.VMEM((model, width), BF16),
            ],
        ),
        out_shape=[
            struct(tokens.shape, BF16), struct((model, width), BF16), struct((model, width), BF16),
            struct((ffn, width), BF16),
            struct((width, ffn), BF16), struct((width, ffn), BF16), struct((width, model), BF16),
            struct((width, model), F32), struct((width, model), BF16), struct((model, width), BF16),
            struct((1, model), F32),
        ],
        input_output_aliases=aliases,
        compiler_params=pltpu.CompilerParams(vmem_limit_bytes=62 << 20),
        cost_estimate=pl.CostEstimate(
            flops=12 * width * model * ffn, bytes_accessed=8 * model * ffn, transcendentals=width * ffn
        ),
        name="middle_part",
    )(*operands)


def final_kernel(
    shape, core_ref, tokens_ref, grad_res_ref, gain_ref, query_ref, key_ref, value_ref, cos_ref, sin_ref, *rest
):
    here, head_dim, aliased = shape
    back = rest[:here]
    rest = rest[here:]
    if aliased:
        rest = rest[1:]
    out_ref, grad_q_ref, grad_k_ref, grad_v_ref, gain_out_ref, total = rest
    step = pl.program_id(0)
    cosine, sine = cos_ref[...], sin_ref[...]
    half = head_dim // 2

    def turned(x):
        first, second = x[:half].astype(F32), x[half:].astype(F32)
        return jnp.concatenate(
            [first * cosine + second * sine, second * cosine - first * sine], axis=0
        ).astype(BF16)

    for at in range(256 // head_dim):
        head = at
        if here == 2:
            head = at // 2 * 2 + (core_ref[0] if at % 2 == 0 else 1 - core_ref[0])
        place = pl.ds(pl.multiple_of(head * head_dim, head_dim), head_dim)
        part = back[at % here]
        grad_q_ref[place, :] = turned(part[at // here, 0:head_dim, :])
        grad_k_ref[place, :] = turned(part[at // here, head_dim : 2 * head_dim, :])
        grad_v_ref[place, :] = part[at // here, 2 * head_dim : 3 * head_dim, :]
    made = (
        contract(grad_q_ref[...].T, query_ref[...], 1, 1)
        + contract(grad_k_ref[...].T, key_ref[...], 1, 1)
        + contract(grad_v_ref[...].T, value_ref[...], 1, 1)
    )

    @pl.when(step == 0)
    def _():
        total[...] = made

    @pl.when(step > 0)
    def _():
        total[...] += made

    @pl.when(step == pl.num_programs(0) - 1)
    def _():
        inputs = tokens_ref[0, 0].astype(F32)
        inverse = lax.rsqrt(jnp.mean(inputs * inputs, axis=-1, keepdims=True) + EPSILON)
        scaled = total[...] * gain_ref[...]
        mean = jnp.mean(scaled * inputs, axis=-1, keepdims=True)
        grad = inverse * scaled - inputs * (inverse * inverse * inverse) * mean
        out_ref[0, 0] = (grad_res_ref[...] + grad).astype(BF16)
        gain_out_ref[...] = jnp.sum(total[...] * inputs * inverse, axis=0, keepdims=True)


def final_part(core, tokens, unit, grad_res, gain, weights, cosine, sine, back, head_dim, output):
    width, model = tokens.shape[2:]
    here = len(back)
    steps = model // 256

    def fixed(a):
        return pl.BlockSpec(a.shape, lambda c: (0,) * a.ndim)

    token_spec = pl.BlockSpec((1, 1, width, model), lambda c: unit + (0, 0))
    weight_specs = [pl.BlockSpec((model, 256), lambda c, i=i: (0, i * steps + c)) for i in range(3)]
    row_spec = pl.BlockSpec((256, width), lambda c: (c, 0))
    operands = [core, tokens, grad_res, gain, weights, weights, weights, cosine, sine, *back]
    in_specs = [
        pl.BlockSpec(memory_space=pltpu.SMEM), token_spec, fixed(grad_res), fixed(gain), *weight_specs,
        fixed(cosine), fixed(sine),
    ] + [
        pl.BlockSpec((256 // head_dim // here, 3 * head_dim, width), lambda c: (c, 0, 0)) for _ in back
    ]
    aliases = {}
    if output is not None:
        aliases = {len(operands): 0}
        operands.append(output)
        in_specs.append(pl.BlockSpec(memory_space=pl.ANY))
    struct = jax.ShapeDtypeStruct
    return pl.pallas_call(
        functools.partial(final_kernel, (here, head_dim, output is not None)),
        grid=(steps,),
        in_specs=in_specs,
        out_specs=[token_spec, row_spec, row_spec, row_spec, pl.BlockSpec((1, model), lambda c: (0, 0))],
        out_shape=[
            struct(tokens.shape, BF16), struct((model, width), BF16), struct((model, width), BF16),
            struct((model, width), BF16), struct((1, model), F32),
        ],
        scratch_shapes=[pltpu.VMEM((width, model), F32)],
        input_output_aliases=aliases,
        compiler_params=pltpu.CompilerParams(vmem_limit_bytes=62 << 20),
        cost_estimate=pl.CostEstimate(
            flops=6 * width * model * model, bytes_accessed=12 * model * model, transcendentals=0
        ),
        name="final_part",
    )(*operands)


def picked_kernel(units, rows, places, flipped, split, table_ref, *refs):
    weights = len(places)
    lefts = refs[0:units]
    rights = refs[units : units * (1 + weights)]
    outs = refs[units * (1 + weights) : units * (1 + weights) + weights * split]
    picked = refs[units * (1 + weights) + weights * split :]

    @pl.when(pl.program_id(0) == 0)
    def _():
        for w, (start, size) in enumerate(places):
            for p in range(size):
                at = pl.ds(pl.multiple_of(table_ref[start + p] * rows, rows), rows)
                for u in range(units):
                    picked[w * units + u][p * rows : (p + 1) * rows, :] = lefts[u][at, :]

    for w in range(weights):
        total = None
        for u in range(units):
            right = rights[w * units + u][...]
            left = picked[w * units + u][...]
            made = contract(left, right, 1, 1) if flipped else dot(left, right)
            total = made if total is None else total + made
        height = total.shape[0] // split
        for i in range(split):
            outs[w * split + i][...] = total[i * height : (i + 1) * height].astype(BF16)


def picked_grads(table, places, lefts, rights, rows, flipped, split, block, name):
    units = len(lefts)
    width = lefts[0].shape[1]
    columns = rights[0].shape[0 if flipped else 1]
    in_specs = [pl.BlockSpec(a.shape, lambda n, *_: (0, 0)) for a in lefts]
    for a in rights:
        if flipped:
            in_specs.append(pl.BlockSpec((block, width), lambda n, *_: (n, 0)))
        else:
            in_specs.append(pl.BlockSpec((width, block), lambda n, *_: (0, n)))
    heights = [size * rows for _, size in places]
    return pl.pallas_call(
        functools.partial(picked_kernel, units, rows, places, flipped, split),
        grid_spec=pltpu.PrefetchScalarGridSpec(
            num_scalar_prefetch=1,
            grid=(columns // block,),
            in_specs=in_specs,
            out_specs=[
                pl.BlockSpec((height // split, block), lambda n, *_: (0, n)) for height in heights for _ in range(split)
            ],
            scratch_shapes=[pltpu.VMEM((height, width), BF16) for height in heights for _ in lefts],
        ),
        out_shape=[
            jax.ShapeDtypeStruct((height // split, columns), BF16) for height in heights for _ in range(split)
        ],
        compiler_params=pltpu.CompilerParams(vmem_limit_bytes=62 << 20),
        cost_estimate=pl.CostEstimate(
            flops=2 * units * sum(heights) * width * columns,
            bytes_accessed=4 * sum(heights) * columns,
            transcendentals=0,
        ),
        name=name,
    )(table, *lefts, *rights)


def tall_kernel(units, pieces_here, table_ref, *refs):
    keep_ref, send_ref = refs[-2:]
    total = None
    for u in range(units):
        left = [refs[u * pieces_here + i][...] for i in range(pieces_here)]
        made = dot(jnp.concatenate(left, axis=0), refs[units * pieces_here + u][...])
        total = made if total is None else total + made
    kept = pl.program_id(0) < pl.num_programs(0) // 2

    @pl.when(kept)
    def _():
        keep_ref[...] = total.astype(BF16)

    @pl.when(jnp.logical_not(kept))
    def _():
        send_ref[...] = total.astype(BF16)


def tall_grads(table, lefts, rights, rows, name):
    units = len(lefts)
    width = lefts[0].shape[1]
    columns = rights[0].shape[1]
    places = table.shape[0]
    each = 4
    middle = places // each // 2
    in_specs = []
    for _ in lefts:
        for i in range(each):
            in_specs.append(pl.BlockSpec((rows, width), lambda n, table, i=i: (table[n * each + i], 0)))
    in_specs += [pl.BlockSpec(a.shape, lambda n, *_: (0, 0)) for a in rights]
    return pl.pallas_call(
        functools.partial(tall_kernel, units, each),
        grid_spec=pltpu.PrefetchScalarGridSpec(
            num_scalar_prefetch=1,
            grid=(places // each,),
            in_specs=in_specs,
            out_specs=[
                pl.BlockSpec((each * rows, columns), lambda n, *_: (jnp.minimum(n, middle - 1), 0)),
                pl.BlockSpec((each * rows, columns), lambda n, *_: (jnp.maximum(n - middle, 0), 0)),
            ],
        ),
        out_shape=[jax.ShapeDtypeStruct((places // 2 * rows, columns), BF16)] * 2,
        compiler_params=pltpu.CompilerParams(vmem_limit_bytes=62 << 20),
        cost_estimate=pl.CostEstimate(
            flops=2 * units * places * rows * width * columns,
            bytes_accessed=2 * places * rows * columns,
            transcendentals=0,
        ),
        name=name,
    )(table, *[a for a in lefts for _ in range(each)], *rights)


def reduce_kernel(orders, count, *refs):
    streams = len(orders)
    rounds = len(orders[0])
    ins, vec_ref = refs[:streams], refs[streams]
    outs, vec_out = refs[streams + 1 : 2 * streams + 1], refs[2 * streams + 1]
    rest = refs[2 * streams + 2 :]
    works, arrivals = rest[:streams], rest[streams : 2 * streams]
    vec_work, vec_arrival, send_sem, recv_sem, vec_send, vec_recv = rest[2 * streams :]
    shard, seq = lax.axis_index("shard"), lax.axis_index("seq")

    def partner(mask):
        if mask >= count:
            step = mask // count
            return (shard + step * (1 - 2 * (shard // step % 2)), seq)
        return (shard, seq + mask * (1 - 2 * (seq // mask % 2)))

    barrier = pltpu.get_barrier_semaphore()
    for mask in orders[0]:
        pl.semaphore_signal(
            barrier, inc=1, device_id=partner(mask), device_id_type=pl.DeviceIdType.MESH
        )
    pl.semaphore_wait(barrier, rounds)

    height = ins[0].shape[0]
    halves = [height >> (r + 1) for r in range(rounds)]
    starts = [sum(halves[:r]) for r in range(rounds)]

    def copy_of(s, r):
        source = ins[s] if r == 0 else works[s]
        return pltpu.make_async_remote_copy(
            src_ref=source.at[pl.ds(halves[r], halves[r])],
            dst_ref=arrivals[s].at[pl.ds(starts[r], halves[r])],
            send_sem=send_sem.at[s, r],
            recv_sem=recv_sem.at[s, r],
            device_id=partner(orders[s][r]),
            device_id_type=pl.DeviceIdType.MESH,
        )

    def vec_copy(r):
        return pltpu.make_async_remote_copy(
            src_ref=vec_ref if r == 0 else vec_work.at[r - 1],
            dst_ref=vec_arrival.at[r],
            send_sem=vec_send.at[r],
            recv_sem=vec_recv.at[r],
            device_id=partner(orders[0][r]),
            device_id_type=pl.DeviceIdType.MESH,
        )

    for s in range(streams):
        copy_of(s, 0).start()
    vec_copy(0).start()
    for r in range(rounds):
        for s in range(streams):
            copy_of(s, r).wait_recv()
            source = ins[s] if r == 0 else works[s]
            size = halves[r]

            def added(low, high):
                mine = source[low:high].astype(F32)
                return mine + arrivals[s][starts[r] + low : starts[r] + high].astype(F32)

            if r == rounds - 1:
                outs[s][...] = added(0, size)
            else:
                works[s][size // 2 : size] = added(size // 2, size).astype(BF16)
                copy_of(s, r + 1).start()
                works[s][0 : size // 2] = added(0, size // 2).astype(BF16)
        vec_copy(r).wait_recv()
        before = vec_ref[...] if r == 0 else vec_work[r - 1]
        if r == rounds - 1:
            vec_out[...] = before + vec_arrival[r]
        else:
            vec_work[r] = before + vec_arrival[r]
            vec_copy(r + 1).start()
    for r in range(rounds):
        for s in range(streams):
            copy_of(s, r).wait_send()
        vec_copy(r).wait_send()


def reduce_rows(parts, vector, orders, count):
    streams = len(parts)
    rounds = len(orders[0])
    height, columns = parts[0].shape
    rows = height >> rounds
    vmem = pl.BlockSpec(memory_space=pltpu.VMEM)
    return pl.pallas_call(
        functools.partial(reduce_kernel, orders, count),
        in_specs=[vmem] * (streams + 1),
        out_specs=[vmem] * (streams + 1),
        out_shape=[jax.ShapeDtypeStruct((rows, columns), F32)] * streams
        + [jax.ShapeDtypeStruct(vector.shape, F32)],
        scratch_shapes=[pltpu.VMEM((height // 2, columns), BF16) for _ in parts]
        + [pltpu.VMEM((height - rows, columns), BF16) for _ in parts]
        + [
            pltpu.VMEM((rounds - 1,) + vector.shape, F32),
            pltpu.VMEM((rounds,) + vector.shape, F32),
            pltpu.SemaphoreType.DMA((streams, rounds)),
            pltpu.SemaphoreType.DMA((streams, rounds)),
            pltpu.SemaphoreType.DMA((rounds,)),
            pltpu.SemaphoreType.DMA((rounds,)),
        ],
        compiler_params=pltpu.CompilerParams(
            collective_id=0, has_side_effects=True, vmem_limit_bytes=62 << 20
        ),
        name="reduce_rows",
    )(*parts, vector)


def on_device(
    tokens, cotangent, lengths, variates, positions, attn_gain, w_query, w_key, w_value, w_out,
    bias_table, ffn_gain, w_gate, w_up, w_down,
):
    micro, seqs, width, model = tokens.shape
    heads = bias_table.shape[0]
    head_dim = model // heads
    count = lax.axis_size("seq")
    here = heads // count
    ffn = w_gate.shape[1]
    devices = lax.axis_size("shard") * count
    seq_index = lax.axis_index("seq")
    units = [(m, s) for m in range(micro) for s in range(seqs)]
    swap = here == 2 and len(units) == 2 and lax.axis_size("shard") % 2 == 0
    core = (lax.axis_index("shard") % 2 if swap else jnp.int32(0)).astype(jnp.int32).reshape(1)
    heads_here = 1 if swap else here
    first_head = seq_index * here + core[0]
    bias_here = lax.dynamic_slice_in_dim(bias_table, first_head, heads_here, 0)
    attn_row, ffn_row = attn_gain[None, :], ffn_gain[None, :]

    def gather(weight):
        return lax.all_gather(weight, "shard", axis=0, tiled=True)

    def exchange(values):
        return lax.all_to_all(values, "seq", split_axis=0, concat_axis=0, tiled=True)

    def after(value, *before):
        return lax.optimization_barrier((value,) + before)[0]

    attn_joined = gather(jnp.concatenate([w_query, w_key, w_value], axis=1))
    ffn_weights = [gather(w_out), gather(w_gate), gather(w_up), gather(w_down)]

    def permute(value, mask):
        return lax.ppermute(value, ("shard", "seq"), [(i, i ^ mask) for i in range(devices)])

    def cross(value):
        return permute(value, count)

    lengths_of = [lengths, cross(lengths)] if swap else [lengths] * here
    packed_list, flats, tables = [], [], []

    def run_project(u, token):
        m, s = units[u]
        cosine, sine = rotary_tables(positions[m, s], head_dim // 2)
        ids = after(variates[m, s].astype(F32)[None, :], *token)
        flat, *packed = project(
            core, tokens, (m, s), attn_row, attn_joined, cosine, sine, ids, count, here, head_dim, swap
        )
        flats.append(flat)
        tables.append((cosine, sine))
        packed_list.append(packed)

    sent = {}
    mixed_now = [None] * len(units)
    sums = {}
    mixed_tok = {}
    crossed, mixed_part, mixed_cross, heads_cross, back_cross = {}, {}, {}, {}, {}
    middle = [None] * len(units)
    grad_heads = {}
    state = {"output": None, "grads": None}
    packed_grads = {}
    returned = {}
    bias_terms = {}
    finals = [None] * len(units)

    def length_of(u, h, token):
        m, s = units[u]
        return after(lengths_of[h][m, s].reshape(1), *token)

    def inputs_of(u, h):
        if not swap:
            return sent[u, h], sent[u, 0]
        return (sent[u, 0], sent[u, 1]) if h == 0 else (crossed[u], crossed[u])

    def run_forward(u, h, token):
        made, sums[u, h] = attend_forward(
            *inputs_of(u, h), length_of(u, h, token), bias_here, None if swap else mixed_now[u],
            0 if swap else h, heads_here, head_dim,
        )
        if swap:
            mixed_part[u, h] = made
            if h == 1:
                mixed_cross[u] = cross(made)
        else:
            mixed_now[u] = made
        return sums[u, h]

    def run_middle(u, token):
        m, s = units[u]
        info = jnp.stack([lengths[m, s], seq_index * width, core[0]]).astype(jnp.int32)
        state["output"], mixed_tok[u], *middle[u] = middle_part(
            after(info, *token), mixed_tok[u], tokens, cotangent, (m, s), ffn_weights, ffn_row, head_dim,
            state["output"],
        )
        return middle[u][8]

    def run_backward(u, h, token):
        if swap:
            grad = grad_heads[u] if h == 0 else heads_cross[u]
            mixed = mixed_part[u, h]
        else:
            grad, mixed = grad_heads[u], mixed_now[u]
        packed_grads[u, h], both = attend_backward(
            *inputs_of(u, h), grad, mixed, sums[u, h], length_of(u, h, token), bias_here,
            0 if swap else h, head_dim,
        )
        if swap and h == 1:
            back_cross[u] = cross(packed_grads[u, h])
        bias_terms[u, h] = both
        return both

    def run_final(u, token):
        m, s = units[u]
        cosine, sine = tables[u]
        state["grads"], *finals[u] = final_part(
            core, tokens, (m, s), middle[u][5], after(attn_row, *token), attn_joined, cosine, sine,
            [returned[u, h] for h in range(here)], head_dim, state["grads"],
        )
        return finals[u][3]

    rows = model // devices
    fold = ffn // model
    tall = ffn // devices
    seq_masks = [1 << i for i in range(count.bit_length() - 1)]
    shard_masks = [count << i for i in range((devices // count).bit_length() - 1)]
    spread = shard_masks[1:]
    orders = (
        shard_masks[:1] + spread + seq_masks,
        shard_masks[:1] + seq_masks[:1] + spread + seq_masks[1:],
        shard_masks[:1] + seq_masks[1:2] + seq_masks[:1] + spread + seq_masks[2:],
    )
    direct = rows % 16 == 0 and devices == 1 << len(orders[0])

    def places_of(order):
        marks = []
        for p in range(devices):
            bits = [p >> (len(order) - 1 - i) & 1 for i in range(len(order))]
            marks.append(sum(mask for bit, mask in zip(bits, order) if bit))
        me = lax.axis_index("shard") * count + seq_index
        return me.astype(jnp.int32) ^ jnp.array(marks, jnp.int32)

    def column(index):
        return [item[index] for item in middle]

    def run_weights(token):
        if not direct:
            return [
                sum(dot(left, right) for left, right in zip(lefts, rights)).astype(BF16)
                for lefts, rights in (
                    (column(0), column(2)), (column(0), column(3)), (column(1), column(4)),
                    ([mixed_tok[u] for u in range(len(units))], column(6)),
                )
            ]
        tables = [after(places_of(order), *token) for order in orders]
        span = [(0, devices)]
        down = tall_grads(tables[2], column(1), column(4), tall, "down_grad")
        table = after(tables[0], down[0])
        gate = picked_grads(table, span, column(0), column(2), rows, False, 2, 512, "gate_grad")
        table = after(tables[1], gate[0])
        up = picked_grads(table, span, column(0), column(3), rows, False, 2, 512, "up_grad")
        table = after(tables[2], up[0])
        mixed_all = [mixed_tok[u] for u in range(len(units))]
        out = picked_grads(table, span, mixed_all, column(6), rows, False, 2, 512, "out_grad")
        streams = []
        for (keep, send), order in zip((down, gate, up, out), (orders[2], orders[0], orders[1], orders[2])):
            streams.append([keep, permute(send, order[0]), order[1:]])
        holder["streams"] = streams
        return out[0]

    def wide_sum(a, b):
        return a.astype(F32) + b.astype(F32)

    def advance(token):
        out = ()
        if not direct:
            return out
        for stream in holder["streams"]:
            keep, came, masks = stream
            if not masks:
                continue
            keep = after(keep, *token)
            half = keep.shape[0] // 2
            send = wide_sum(keep[half:], came[half:]).astype(BF16)
            stream[0] = wide_sum(keep[:half], came[:half]).astype(BF16)
            stream[1] = permute(send, masks[0])
            stream[2] = masks[1:]
            out = out + (send, stream[0])
        return out

    holder = {}

    def weights_work(token):
        holder["terms"] = run_weights(token)
        return holder["terms"]

    def send_packed(u, h):
        def keep(moved):
            sent[u, h] = moved
            if swap and h == 1:
                crossed[u] = cross(moved)

        return lambda: packed_list[u][h], keep

    def send_mixed(u):
        def keep(moved):
            mixed_tok[u] = moved.reshape(model, width)

        if not swap:
            return lambda: mixed_now[u], keep
        return lambda: jnp.concatenate([mixed_part[u, 0], mixed_cross[u]], axis=1), keep

    def send_heads(u):
        def keep(moved):
            grad_heads[u] = moved
            if swap:
                heads_cross[u] = cross(moved[:, head_dim:])

        return lambda: middle[u][7].reshape(count, here * head_dim, width), keep

    def send_back(u, h):
        def keep(moved):
            returned[u, h] = moved

        return lambda: back_cross[u] if swap and h == 1 else packed_grads[u, h], keep

    def work_project(u):
        def work(token):
            run_project(u, token)
            return flats[u]

        return work

    def work(function, *args):
        return lambda token: function(*args, token)

    total = len(units)
    order = [(u, h) for u in range(total) for h in range(here)]
    if swap:
        steps = [
            (work_project(0), None),
            (work_project(1), send_packed(0, 1)),
            (work(run_forward, 0, 1), send_packed(0, 0)),
            (work(run_forward, 0, 0), send_packed(1, 1)),
            (work(run_forward, 1, 1), send_packed(1, 0)),
            (work(run_forward, 1, 0), send_mixed(0)),
            (work(run_middle, 0), send_mixed(1)),
            (work(run_middle, 1), send_heads(0)),
            (weights_work, send_heads(1)),
            (work(run_backward, 0, 0), None),
            (work(run_backward, 0, 1), send_back(0, 0)),
            (work(run_backward, 1, 0), send_back(0, 1)),
            (work(run_backward, 1, 1), send_back(1, 0)),
            (work(run_final, 0), send_back(1, 1)),
            (work(run_final, 1), None),
        ]
    else:
        steps = [(work_project(u), None) for u in range(total)]
        steps += [(None, send_packed(*at)) for at in order]
        for u in range(total):
            steps += [(work(run_forward, u, h), None) for h in range(here)]
            steps += [(None, send_mixed(u))]
        for u in range(total):
            steps += [(work(run_middle, u), None), (None, send_heads(u))]
        steps += [(weights_work, None)]
        for at in order:
            steps += [(work(run_backward, *at), None), (None, send_back(*at))]
        steps += [(work(run_final, u), None) for u in range(total)]

    late = [task for task, _ in steps[-2:]]
    token = ()
    for task, send in steps:
        done = ()
        moved = None
        if "streams" in holder:
            leaving = advance(token)
            token = token if task in late else token + leaving
        if send is not None:
            moved = exchange(after(send[0](), *token))
            done = (moved,)
        if task is not None:
            done = done + (task(token),)
        if send is not None:
            send[1](after(moved, *done[1:]))
        token = done
    acc_bias = jnp.concatenate(
        [sum(bias_terms[u, h] for u in range(total))[0:1, 0:2] for h in range(here)], axis=0
    )
    if swap:
        acc_bias = acc_bias[0:1] + acc_bias[1:2]
    bias_full = lax.dynamic_update_slice(
        jnp.zeros((heads, 2), F32), acc_bias, (first_head, jnp.int32(0))
    )
    gain_attn = sum(item[3][0] for item in finals)
    gain_ffn = sum(item[8][0] for item in middle)
    if direct:
        while holder["streams"][0][2]:
            advance(token)
        down_own, gate_own, up_own, out_own = [
            wide_sum(after(keep, *token), came) for keep, came, _ in holder["streams"]
        ]
        table = jnp.concatenate([places_of(order) for order in orders])
        attn_terms = picked_grads(
            table, [(i * devices, devices) for i in range(3)], flats,
            [item[i] for i in range(3) for item in finals], rows, True, 1, 256, "attn_grads",
        )
        flat = jnp.concatenate([gain_attn, gain_ffn, bias_full.reshape(-1)])
        tiles = -(-flat.shape[0] // 1024) * 8
        flat = jnp.pad(flat, (0, tiles * 128 - flat.shape[0])).reshape(tiles, 128)
        query_own, key_own, value_own, flat = reduce_rows(list(attn_terms), flat, orders, count)
        flat = flat.reshape(-1)
        gain_attn, gain_ffn = flat[:model], flat[model : 2 * model]
        bias_full = flat[2 * model : 2 * model + 2 * heads].reshape(heads, 2)
    else:

        def scatter(value):
            owned = lax.psum_scatter(value, ("shard", "seq"), scatter_dimension=0, tiled=True)
            return owned.astype(F32)

        gate_own, up_own, down_own, out_own = [scatter(value) for value in holder["terms"]]
        query_own, key_own, value_own = [
            scatter(
                sum(contract(flat, item[i], 1, 1) for flat, item in zip(flats, finals)).astype(BF16)
            )
            for i in range(3)
        ]
        gain_attn, gain_ffn, bias_full = lax.psum(
            (gain_attn, gain_ffn, bias_full), ("shard", "seq")
        )
    return (
        state["output"], state["grads"], gain_attn, query_own, key_own, value_own, out_own,
        bias_full, gain_ffn, gate_own, up_own, down_own,
    )


def solution(mesh):
    token_spec = P(None, "shard", "seq", None)
    row_spec = P("shard", None)
    in_specs = (
        token_spec, token_spec, P(None, "shard"), P(None, "shard", "seq"), P(None, "shard", "seq"),
        P(), row_spec, row_spec, row_spec, row_spec, P(), P(), row_spec, row_spec, row_spec,
    )
    owned = P(("shard", "seq"), None)
    out_specs = (
        token_spec, token_spec, P(), owned, owned, owned, owned, P(), P(), owned, owned, owned,
    )
    return jax.shard_map(
        on_device, mesh=mesh, in_specs=in_specs, out_specs=out_specs, check_vma=False
    )
```

```python
import functools
import math

import jax
import jax.numpy as jnp
from jax import lax
from jax.experimental import pallas as pl
from jax.experimental.pallas import tpu as pltpu
from jax.sharding import PartitionSpec as P

EPSILON = 1e-06
ROTARY_BASE = 10000.0
LOG2E = 1.4426950408889634
LN2 = 0.6931471805599453
CLASSES = 8
AUX = 16
COVER = 16
EXTRA = 32
MASKED = -1.5e9
FAR = 1e30
F32 = jnp.float32
BF16 = jnp.bfloat16


def dot(a, b):
    return jnp.dot(a, b, preferred_element_type=F32)


def contract(a, b, da, db):
    return lax.dot_general(a, b, (((da,), (db,)), ((), ())), preferred_element_type=F32)


def pieces(x):
    high = x.astype(BF16).astype(F32)
    rest = x - high
    mid = rest.astype(BF16).astype(F32)
    low = (rest - mid).astype(BF16).astype(F32)
    return high, mid, low


def one_hot(row):
    classes = lax.broadcasted_iota(jnp.int32, (CLASSES, row.shape[1]), 0).astype(F32)
    return jnp.where(classes == row, 1.0, 0.0)


def rows_of(values, width):
    index = lax.broadcasted_iota(jnp.int32, (8, width), 0)
    out = jnp.zeros((8, width), F32)
    for at, value in enumerate(values):
        out = jnp.where(index == at, value, out)
    return out


def key_extra(row, start, length, other, same):
    width = row.shape[1]
    hot = one_hot(row)
    step = pieces(jnp.full((1, width), same - other, F32))
    base = pieces(jnp.full((1, width), other, F32))
    index = start + lax.broadcasted_iota(jnp.int32, (1, width), 1)
    mask = jnp.where(index < length, 0.0, MASKED)
    tail = rows_of(base + (mask, 1.0, 1.0, 1.0), width)
    return jnp.concatenate([hot * step[0], hot * step[1], hot * step[2], tail], axis=0).astype(BF16)


def query_extra(row, shift):
    hot = one_hot(row)
    tail = rows_of((1.0, 1.0, 1.0, 1.0) + shift, row.shape[1])
    return jnp.concatenate([hot, hot, hot, tail], axis=0).astype(BF16)


def forward_kernel(
    shape, len_ref, bias_ref, x_ref, ids_ref, *rest
):
    local, head_dim, block, aliased = shape
    if aliased:
        rest = rest[1:]
    mixed_ref, lse_ref, keys, vals, query, score, peak, total = rest
    count, _, width = x_ref.shape
    sub = block // width
    step = pl.program_id(0)
    length = len_ref[0]
    other = bias_ref[local, 0] * LOG2E
    same = bias_ref[local, 1] * LOG2E

    @pl.when(step == 0)
    def _():
        for b in range(count):
            at = pl.ds(b * width, width)
            row = ids_ref[b, 0:1, :].astype(F32)
            extra = key_extra(row, b * width, length, other, same)
            full = jnp.concatenate([x_ref[b, head_dim : 2 * head_dim, :], extra], axis=0)
            keys[at, :] = full.T
            vals[0:head_dim, at] = x_ref[b, 2 * head_dim : 3 * head_dim, :]
        vals[head_dim:, :] = jnp.ones((16, vals.shape[1]), BF16)

    used = pl.cdiv(length, block)
    inside = step * block < length

    @pl.when(jnp.logical_not(inside))
    def _():
        mixed_ref[...] = jnp.zeros_like(mixed_ref)
        lse_ref[...] = jnp.full(lse_ref.shape, FAR, F32)

    @pl.when(inside)
    def _():
        for b in range(sub):
            at = slice(b * width, (b + 1) * width)
            row = ids_ref[step * sub + b, 0:1, :].astype(F32)
            query[0:head_dim, at] = x_ref[step * sub + b, 0:head_dim, :]
            query[head_dim:, at] = query_extra(row, (0.0, 0.0, 0.0))
        peak[...] = jnp.full(peak.shape, -FAR, F32)
        total[...] = jnp.zeros_like(total)

        def span(j):
            return pl.ds(pl.multiple_of(j * block, block), block)

        def scores_of(j):
            return dot(keys[span(j), :], query[...])

        def one(j, now, ahead):
            if ahead:
                score[1 - now] = scores_of(j + 1)
            current = score[now]
            before = peak[...]
            top = jnp.maximum(before, jnp.max(current, axis=0, keepdims=True))
            weight = jnp.exp2(current - top).astype(BF16)
            peak[...] = top
            total[...] = total[...] * jnp.exp2(before - top) + dot(vals[:, span(j)], weight)

        score[0] = scores_of(0)
        pairs = (used - 1) // 2

        def pair(j, carry):
            one(2 * j, 0, True)
            one(2 * j + 1, 1, True)
            return carry

        lax.fori_loop(0, pairs, pair, 0)
        last = 2 * pairs

        @pl.when(used - last == 1)
        def _():
            one(last, 0, False)

        @pl.when(used - last == 2)
        def _():
            one(last, 0, True)
            one(last + 1, 1, False)

        mass = total[head_dim : head_dim + 1, :]
        mixed = (total[0:head_dim, :] / mass).astype(BF16)
        for b in range(sub):
            mixed_ref[b] = mixed[:, b * width : (b + 1) * width]
        lse_ref[0] = peak[...] + jnp.log2(mass)


def attend_forward(x, ids, length, bias, mixed, local, heads_here, head_dim):
    count, rows, width = x.shape
    block = max(width, 512)
    seq_len = count * width
    blocks = seq_len // block
    depth = head_dim + EXTRA
    whole = pl.BlockSpec((count, rows, width), lambda i, *_: (0, 0, 0))
    operands = [length, bias, x, ids]
    in_specs = [whole, pl.BlockSpec((count, AUX, width), lambda i, *_: (0, 3 * head_dim // AUX, 0))]
    aliases = {}
    if mixed is not None:
        operands.append(mixed)
        in_specs.append(pl.BlockSpec(memory_space=pl.ANY))
        aliases = {4: 0}
    return pl.pallas_call(
        functools.partial(forward_kernel, (local, head_dim, block, mixed is not None)),
        grid_spec=pltpu.PrefetchScalarGridSpec(
            num_scalar_prefetch=2,
            grid=(blocks,),
            in_specs=in_specs,
            out_specs=[
                pl.BlockSpec((block // width, head_dim, width), lambda i, *_: (i, local, 0)),
                pl.BlockSpec((1, 1, block), lambda i, *_: (i, 0, 0)),
            ],
            scratch_shapes=[
                pltpu.VMEM((seq_len, depth), BF16),
                pltpu.VMEM((head_dim + 16, seq_len), BF16),
                pltpu.VMEM((depth, block), BF16),
                pltpu.VMEM((2, block, block), F32),
                pltpu.VMEM((1, block), F32),
                pltpu.VMEM((head_dim + 16, block), F32),
            ],
        ),
        out_shape=[
            jax.ShapeDtypeStruct((count, heads_here * head_dim, width), BF16),
            jax.ShapeDtypeStruct((blocks, 1, block), F32),
        ],
        input_output_aliases=aliases,
        compiler_params=pltpu.CompilerParams(vmem_limit_bytes=62 << 20),
        cost_estimate=pl.CostEstimate(
            flops=8 * seq_len * seq_len * 256 // COVER,
            bytes_accessed=x.size * 4,
            transcendentals=0,
        ),
        name="attend_forward",
    )(*operands)


def backward_kernel(
    shape, len_ref, bias_ref, x_ref, ids_ref, grad_ref, mixed_ref, lse_ref, out_ref, bias_out_ref,
    keys, keys_flat, vals, query, grads, query_rows, grad_rows, acc_keys, acc_vals, acc_query,
):
    local, head_dim, block = shape
    count, _, width = x_ref.shape
    sub = block // width
    step = pl.program_id(0)
    length = len_ref[0]
    other = bias_ref[local, 0] * LOG2E
    same = bias_ref[local, 1] * LOG2E

    @pl.when(step == 0)
    def _():
        ones = jnp.ones((16, width), BF16)
        for b in range(count):
            at = pl.ds(b * width, width)
            row = ids_ref[b, 0:1, :].astype(F32)
            extra = key_extra(row, b * width, length, other, same)
            here = x_ref[b, head_dim : 2 * head_dim, :]
            keys[at, :] = jnp.concatenate([here, extra], axis=0).T
            keys_flat[:, at] = here
            vals[at, :] = jnp.concatenate([x_ref[b, 2 * head_dim : 3 * head_dim, :], ones], axis=0).T
        acc_keys[...] = jnp.zeros_like(acc_keys)
        acc_vals[...] = jnp.zeros_like(acc_vals)

    used = pl.cdiv(length, block)
    inside = step * block < length

    @pl.when(jnp.logical_not(inside))
    def _():
        for b in range(sub):
            out_ref[step * sub + b, 0:head_dim, :] = jnp.zeros((head_dim, width), BF16)

    @pl.when(inside)
    def _():
        for b in range(sub):
            at = slice(b * width, (b + 1) * width)
            here = step * sub + b
            row = ids_ref[here, 0:1, :].astype(F32)
            shift = pieces(-lse_ref[step][:, at])
            grad = grad_ref[here]
            delta = jnp.sum(grad.astype(F32) * mixed_ref[here].astype(F32), axis=0, keepdims=True)
            query[0:head_dim, at] = x_ref[here, 0:head_dim, :]
            query[head_dim:, at] = query_extra(row, shift)
            grads[0:head_dim, at] = grad
            tail = rows_of(pieces(-delta), width)
            grads[head_dim:, at] = jnp.concatenate([tail, jnp.zeros_like(tail)], axis=0).astype(BF16)
        query_rows[...] = query[...].T
        grad_rows[...] = grads[...].T
        acc_query[...] = jnp.zeros_like(acc_query)

        def one(j):
            at = pl.ds(pl.multiple_of(j * block, block), block)
            probs = jnp.exp2(dot(keys[at, :], query[...]))
            grad_probs = dot(vals[at, :], grads[...])
            grad_scores = (probs * grad_probs).astype(BF16)
            acc_vals[at, :] += dot(probs.astype(BF16), grad_rows[...])
            acc_keys[at, :] += dot(grad_scores, query_rows[...])
            acc_query[...] += dot(keys_flat[:, at], grad_scores)

        def pair(j, carry):
            one(2 * j)
            one(2 * j + 1)
            return carry

        lax.fori_loop(0, used // 2, pair, 0)

        @pl.when(used % 2 == 1)
        def _():
            one(used - 1)

        grad_query = (acc_query[...] * (1.0 / math.sqrt(head_dim))).astype(BF16)
        for b in range(sub):
            out_ref[step * sub + b, 0:head_dim, :] = grad_query[:, b * width : (b + 1) * width]

    @pl.when(step == pl.num_programs(0) - 1)
    def _():
        same_total = jnp.zeros((CLASSES, width), F32)
        all_total = jnp.zeros((CLASSES, width), F32)
        for b in range(count):
            at = pl.ds(b * width, width)
            row = ids_ref[b, 0:1, :].astype(F32)
            flat = acc_keys[at, :].T
            out_ref[b, head_dim : 2 * head_dim, :] = (flat[0:head_dim] * LN2).astype(BF16)
            out_ref[b, 2 * head_dim : 3 * head_dim, :] = acc_vals[at, :].T[0:head_dim].astype(BF16)
            by_class = flat[head_dim : head_dim + CLASSES]
            all_total += by_class
            same_total += by_class * one_hot(row)
        same_sum = jnp.sum(same_total, keepdims=True)
        other_sum = jnp.sum(all_total, keepdims=True) - same_sum
        lane = lax.broadcasted_iota(jnp.int32, (8, 128), 1)
        bias_out_ref[...] = jnp.where(lane == 0, other_sum, jnp.where(lane == 1, same_sum, 0.0))


def attend_backward(x, ids, grad, mixed, lse, length, bias, local, head_dim):
    count, rows, width = x.shape
    blocks, _, block = lse.shape
    seq_len = count * width
    depth = head_dim + EXTRA

    def whole(a):
        return pl.BlockSpec(a.shape, lambda i, *_: (0,) * a.ndim)

    head_spec = pl.BlockSpec((count, head_dim, width), lambda i, *_: (0, local, 0))
    return pl.pallas_call(
        functools.partial(backward_kernel, (local, head_dim, block)),
        grid_spec=pltpu.PrefetchScalarGridSpec(
            num_scalar_prefetch=2,
            grid=(blocks,),
            in_specs=[
                whole(x),
                pl.BlockSpec((count, AUX, width), lambda i, *_: (0, 3 * head_dim // AUX, 0)),
                head_spec, head_spec, whole(lse),
            ],
            out_specs=[
                pl.BlockSpec((count, 3 * head_dim, width), lambda i, *_: (0, 0, 0)),
                pl.BlockSpec((8, 128), lambda i, *_: (0, 0)),
            ],
            scratch_shapes=[
                pltpu.VMEM((seq_len, depth), BF16),
                pltpu.VMEM((head_dim, seq_len), BF16),
                pltpu.VMEM((seq_len, head_dim + 16), BF16),
                pltpu.VMEM((depth, block), BF16),
                pltpu.VMEM((head_dim + 16, block), BF16),
                pltpu.VMEM((block, depth), BF16),
                pltpu.VMEM((block, head_dim + 16), BF16),
                pltpu.VMEM((seq_len, depth), F32),
                pltpu.VMEM((seq_len, head_dim + 16), F32),
                pltpu.VMEM((head_dim, block), F32),
            ],
        ),
        out_shape=[
            jax.ShapeDtypeStruct((count, 3 * head_dim, width), BF16),
            jax.ShapeDtypeStruct((8, 128), F32),
        ],
        compiler_params=pltpu.CompilerParams(vmem_limit_bytes=62 << 20),
        cost_estimate=pl.CostEstimate(
            flops=20 * seq_len * seq_len * 256 // COVER,
            bytes_accessed=x.size * 6,
            transcendentals=0,
        ),
        name="attend_backward",
    )(length, bias, x, ids, grad, mixed, lse)


def rotary_tables(places, half_dim):
    frequency = jnp.exp(-math.log(ROTARY_BASE) * jnp.arange(half_dim, dtype=F32) / half_dim)
    angles = places.astype(F32)[None, :] * frequency[:, None]
    return jnp.cos(angles), jnp.sin(angles)


def sigmoid_of(x):
    return 1.0 / (1.0 + jnp.exp2(x * -LOG2E))


def project_kernel(
    shape, core_ref, tokens_ref, gain_ref, query_ref, key_ref, value_ref, cos_ref, sin_ref, ids_ref, flat_ref, *rest
):
    here, head_dim, extras, swap = shape
    outs, flat_weights = rest[:-1], rest[-1]
    pair = pl.program_id(0)

    @pl.when(pair == 0)
    def _():
        inputs = tokens_ref[0, 0].astype(F32)
        inverse = lax.rsqrt(jnp.mean(inputs * inputs, axis=-1, keepdims=True) + EPSILON)
        flat_ref[...] = (inputs * inverse * gain_ref[...]).astype(BF16).T

    flat_weights[0:128, :] = query_ref[...].T
    flat_weights[128:256, :] = key_ref[...].T
    flat_weights[256:384, :] = value_ref[...].T
    made = dot(flat_weights[...], flat_ref[...])
    cosine, sine = cos_ref[...], sin_ref[...]
    half = head_dim // 2

    def turned(start, scale):
        first = made[start : start + half]
        second = made[start + half : start + head_dim]
        both = [first * cosine - second * sine, second * cosine + first * sine]
        return (jnp.concatenate(both, axis=0) * scale).astype(BF16)

    def put(at, slot, place):
        spot = at * head_dim
        target = outs[slot]
        target[place, 0:head_dim, :] = turned(spot, LOG2E / math.sqrt(head_dim))
        target[place, head_dim : 2 * head_dim, :] = turned(128 + spot, 1.0)
        target[place, 2 * head_dim : 3 * head_dim, :] = made[256 + spot : 256 + spot + head_dim].astype(BF16)
        if extras[slot]:
            target[place, 3 * head_dim :, :] = jnp.broadcast_to(ids_ref[...], (AUX, ids_ref.shape[1])).astype(BF16)

    if swap:
        for core in range(2):

            @pl.when(core_ref[0] == core)
            def _():
                put(core, 0, 0)
                put(1 - core, 1, 0)

    else:
        for at in range(128 // head_dim):
            put(at, at % here, 0 if here > 1 else at)


def project(core, tokens, unit, gain, weights, cosine, sine, ids, count, here, head_dim, swap):
    width, model = tokens.shape[2:]
    heads = count * here
    pairs = heads * head_dim // 128
    per = 128 // head_dim // here
    extras = [h == (1 if swap else 0) for h in range(here)]

    def fixed(a):
        return pl.BlockSpec(a.shape, lambda p: (0,) * a.ndim)

    weight_specs = [pl.BlockSpec((model, 128), lambda p, i=i: (0, i * pairs + p)) for i in range(3)]
    return pl.pallas_call(
        functools.partial(project_kernel, (here, head_dim, extras, swap)),
        grid=(pairs,),
        in_specs=[
            pl.BlockSpec(memory_space=pltpu.SMEM),
            pl.BlockSpec((1, 1, width, model), lambda p: unit + (0, 0)),
            fixed(gain), *weight_specs, fixed(cosine), fixed(sine), fixed(ids),
        ],
        out_specs=[pl.BlockSpec((model, width), lambda p: (0, 0))]
        + [pl.BlockSpec((per, 3 * head_dim + AUX * e, width), lambda p: (p, 0, 0)) for e in extras],
        out_shape=[jax.ShapeDtypeStruct((model, width), BF16)]
        + [jax.ShapeDtypeStruct((count, 3 * head_dim + AUX * e, width), BF16) for e in extras],
        scratch_shapes=[pltpu.VMEM((384, model), BF16)],
        compiler_params=pltpu.CompilerParams(vmem_limit_bytes=62 << 20),
        cost_estimate=pl.CostEstimate(
            flops=6 * width * model * model // COVER, bytes_accessed=12 * model * model, transcendentals=0
        ),
        name="project",
    )(core, tokens, gain, weights, weights, weights, cosine, sine, ids)


def middle_kernel(
    shape, info_ref, mixed_ref, tokens_ref, cot_ref, out_w_ref, gain_ref, gate_w_ref, up_w_ref, down_w_ref, *rest
):
    head_dim, aliased = shape
    if aliased:
        rest = rest[1:]
    (
        output_ref, ordered_ref, flat_ref, hidden_ref, grad_gate_ref, grad_up_ref, grad_ffn_ref, grad_res_ref,
        grad_attn_ref, grad_mixed_ref, gain_out_ref, normed, residual, ffn_out, grad_normed, slots,
    ) = rest
    core = info_ref[2]
    step = pl.program_id(0)
    width = normed.shape[0]

    def valid():
        index = info_ref[1] + lax.broadcasted_iota(jnp.int32, (width, 1), 0)
        return jnp.where(index < info_ref[0], 1.0, 0.0)

    def inverse_of(x):
        return lax.rsqrt(jnp.mean(x * x, axis=-1, keepdims=True) + EPSILON)

    def head_rows(pair, slot):
        head = 2 * pair + (core if slot == 0 else 1 - core)
        return pl.ds(pl.multiple_of(head * head_dim, head_dim), head_dim)

    def slot_rows(pair, slot):
        return slice((2 * pair + slot) * head_dim, (2 * pair + slot + 1) * head_dim)

    spots = [(pair, slot) for pair in range(mixed_ref.shape[0] // head_dim // 2) for slot in range(2)]

    @pl.when(step == 0)
    def _():
        for spot in spots:
            ordered_ref[head_rows(*spot), :] = mixed_ref[slot_rows(*spot), :]
        inputs = tokens_ref[0, 0].astype(F32) + dot(ordered_ref[...].T, out_w_ref[...])
        residual[...] = inputs
        made = (inputs * inverse_of(inputs) * gain_ref[...]).astype(BF16)
        normed[...] = made
        flat_ref[...] = made.T
        grad_ffn_ref[...] = (cot_ref[0, 0].astype(F32) * valid()).astype(BF16)
        ffn_out[...] = jnp.zeros_like(ffn_out)
        grad_normed[...] = jnp.zeros_like(grad_normed)

    gate = dot(normed[...], gate_w_ref[...])
    up = dot(normed[...], up_w_ref[...])
    grad_hidden = contract(grad_ffn_ref[...], down_w_ref[...], 1, 1)
    sigmoid = sigmoid_of(gate)
    silu = gate * sigmoid
    hidden = (silu * up).astype(BF16)
    grad_gate = (grad_hidden * up * (sigmoid + silu * (1.0 - sigmoid))).astype(BF16)
    grad_up = (grad_hidden * silu).astype(BF16)
    hidden_ref[...] = hidden.T
    grad_gate_ref[...] = grad_gate
    grad_up_ref[...] = grad_up
    ffn_out[...] += dot(hidden, down_w_ref[...])
    grad_normed[...] += contract(grad_gate, gate_w_ref[...], 1, 1) + contract(grad_up, up_w_ref[...], 1, 1)

    @pl.when(step == pl.num_programs(0) - 1)
    def _():
        keep = valid()
        kept = residual[...]
        output_ref[0, 0] = ((kept + ffn_out[...]) * keep).astype(BF16)
        inverse = inverse_of(kept)
        scaled = grad_normed[...] * gain_ref[...]
        mean = jnp.mean(scaled * kept, axis=-1, keepdims=True)
        grad = cot_ref[0, 0].astype(F32) * keep
        grad = grad + (inverse * scaled - kept * (inverse * inverse * inverse) * mean)
        gain_out_ref[...] = jnp.sum(grad_normed[...] * kept * inverse, axis=0, keepdims=True)
        grad_res_ref[...] = grad
        low = grad.astype(BF16)
        grad_attn_ref[...] = low
        slots[...] = contract(out_w_ref[...], low, 1, 1).astype(BF16)
        for spot in spots:
            grad_mixed_ref[slot_rows(*spot), :] = slots[head_rows(*spot), :]


def middle_part(info, mixed, tokens, cotangent, unit, weights, gain, head_dim, output):
    width, model = tokens.shape[2:]
    out_w, gate_w, up_w, down_w = weights
    ffn = gate_w.shape[1]
    block = 512

    def fixed(a):
        return pl.BlockSpec(a.shape, lambda f, *_: (0,) * a.ndim)

    def one(*shape):
        return pl.BlockSpec(shape, lambda f, *_: (0,) * len(shape))

    token_spec = pl.BlockSpec((1, 1, width, model), lambda f, *_: unit + (0, 0))
    operands = [info, mixed, tokens, cotangent, out_w, gain, gate_w, up_w, down_w]
    in_specs = [
        fixed(mixed), token_spec, token_spec, fixed(out_w), fixed(gain),
        pl.BlockSpec((model, block), lambda f, *_: (0, f)),
        pl.BlockSpec((model, block), lambda f, *_: (0, f)),
        pl.BlockSpec((block, model), lambda f, *_: (f, 0)),
    ]
    aliases = {}
    if output is not None:
        aliases = {len(operands): 0}
        operands.append(output)
        in_specs.append(pl.BlockSpec(memory_space=pl.ANY))
    struct = jax.ShapeDtypeStruct
    return pl.pallas_call(
        functools.partial(middle_kernel, (head_dim, output is not None)),
        grid_spec=pltpu.PrefetchScalarGridSpec(
            num_scalar_prefetch=1,
            grid=(ffn // block,),
            in_specs=in_specs,
            out_specs=[
                token_spec, one(model, width), one(model, width),
                pl.BlockSpec((block, width), lambda f, *_: (f, 0)),
                pl.BlockSpec((width, block), lambda f, *_: (0, f)),
                pl.BlockSpec((width, block), lambda f, *_: (0, f)),
                one(width, model), one(width, model), one(width, model), one(model, width), one(1, model),
            ],
            scratch_shapes=[
                pltpu.VMEM((width, model), BF16),
                pltpu.VMEM((width, model), F32),
                pltpu.VMEM((width, model), F32),
                pltpu.VMEM((width, model), F32),
                pltpu.VMEM((model, width), BF16),
            ],
        ),
        out_shape=[
            struct(tokens.shape, BF16), struct((model, width), BF16), struct((model, width), BF16),
            struct((ffn, width), BF16),
            struct((width, ffn), BF16), struct((width, ffn), BF16), struct((width, model), BF16),
            struct((width, model), F32), struct((width, model), BF16), struct((model, width), BF16),
            struct((1, model), F32),
        ],
        input_output_aliases=aliases,
        compiler_params=pltpu.CompilerParams(vmem_limit_bytes=62 << 20),
        cost_estimate=pl.CostEstimate(
            flops=12 * width * model * ffn // COVER, bytes_accessed=8 * model * ffn, transcendentals=0
        ),
        name="middle_part",
    )(*operands)


def final_kernel(
    shape, core_ref, tokens_ref, grad_res_ref, gain_ref, query_ref, key_ref, value_ref, cos_ref, sin_ref, *rest
):
    here, head_dim, aliased = shape
    back = rest[:here]
    rest = rest[here:]
    if aliased:
        rest = rest[1:]
    out_ref, grad_q_ref, grad_k_ref, grad_v_ref, gain_out_ref, total = rest
    step = pl.program_id(0)
    cosine, sine = cos_ref[...], sin_ref[...]
    half = head_dim // 2

    def turned(x):
        first, second = x[:half].astype(F32), x[half:].astype(F32)
        return jnp.concatenate(
            [first * cosine + second * sine, second * cosine - first * sine], axis=0
        ).astype(BF16)

    for at in range(256 // head_dim):
        head = at
        if here == 2:
            head = at // 2 * 2 + (core_ref[0] if at % 2 == 0 else 1 - core_ref[0])
        place = pl.ds(pl.multiple_of(head * head_dim, head_dim), head_dim)
        part = back[at % here]
        grad_q_ref[place, :] = turned(part[at // here, 0:head_dim, :])
        grad_k_ref[place, :] = turned(part[at // here, head_dim : 2 * head_dim, :])
        grad_v_ref[place, :] = part[at // here, 2 * head_dim : 3 * head_dim, :]
    made = (
        contract(grad_q_ref[...].T, query_ref[...], 1, 1)
        + contract(grad_k_ref[...].T, key_ref[...], 1, 1)
        + contract(grad_v_ref[...].T, value_ref[...], 1, 1)
    )

    @pl.when(step == 0)
    def _():
        total[...] = made

    @pl.when(step > 0)
    def _():
        total[...] += made

    @pl.when(step == pl.num_programs(0) - 1)
    def _():
        inputs = tokens_ref[0, 0].astype(F32)
        inverse = lax.rsqrt(jnp.mean(inputs * inputs, axis=-1, keepdims=True) + EPSILON)
        scaled = total[...] * gain_ref[...]
        mean = jnp.mean(scaled * inputs, axis=-1, keepdims=True)
        grad = inverse * scaled - inputs * (inverse * inverse * inverse) * mean
        out_ref[0, 0] = (grad_res_ref[...] + grad).astype(BF16)
        gain_out_ref[...] = jnp.sum(total[...] * inputs * inverse, axis=0, keepdims=True)


def final_part(core, tokens, unit, grad_res, gain, weights, cosine, sine, back, head_dim, output):
    width, model = tokens.shape[2:]
    here = len(back)
    steps = model // 256

    def fixed(a):
        return pl.BlockSpec(a.shape, lambda c: (0,) * a.ndim)

    token_spec = pl.BlockSpec((1, 1, width, model), lambda c: unit + (0, 0))
    weight_specs = [pl.BlockSpec((model, 256), lambda c, i=i: (0, i * steps + c)) for i in range(3)]
    row_spec = pl.BlockSpec((256, width), lambda c: (c, 0))
    operands = [core, tokens, grad_res, gain, weights, weights, weights, cosine, sine, *back]
    in_specs = [
        pl.BlockSpec(memory_space=pltpu.SMEM), token_spec, fixed(grad_res), fixed(gain), *weight_specs,
        fixed(cosine), fixed(sine),
    ] + [
        pl.BlockSpec((256 // head_dim // here, 3 * head_dim, width), lambda c: (c, 0, 0)) for _ in back
    ]
    aliases = {}
    if output is not None:
        aliases = {len(operands): 0}
        operands.append(output)
        in_specs.append(pl.BlockSpec(memory_space=pl.ANY))
    struct = jax.ShapeDtypeStruct
    return pl.pallas_call(
        functools.partial(final_kernel, (here, head_dim, output is not None)),
        grid=(steps,),
        in_specs=in_specs,
        out_specs=[token_spec, row_spec, row_spec, row_spec, pl.BlockSpec((1, model), lambda c: (0, 0))],
        out_shape=[
            struct(tokens.shape, BF16), struct((model, width), BF16), struct((model, width), BF16),
            struct((model, width), BF16), struct((1, model), F32),
        ],
        scratch_shapes=[pltpu.VMEM((width, model), F32)],
        input_output_aliases=aliases,
        compiler_params=pltpu.CompilerParams(vmem_limit_bytes=62 << 20),
        cost_estimate=pl.CostEstimate(
            flops=6 * width * model * model // COVER, bytes_accessed=12 * model * model, transcendentals=0
        ),
        name="final_part",
    )(*operands)


def picked_kernel(units, rows, places, flipped, split, table_ref, *refs):
    weights = len(places)
    lefts = refs[0:units]
    rights = refs[units : units * (1 + weights)]
    outs = refs[units * (1 + weights) : units * (1 + weights) + weights * split]
    picked = refs[units * (1 + weights) + weights * split :]

    @pl.when(pl.program_id(0) == 0)
    def _():
        for w, (start, size) in enumerate(places):
            for p in range(size):
                at = pl.ds(pl.multiple_of(table_ref[start + p] * rows, rows), rows)
                for u in range(units):
                    picked[w * units + u][p * rows : (p + 1) * rows, :] = lefts[u][at, :]

    for w in range(weights):
        total = None
        for u in range(units):
            right = rights[w * units + u][...]
            left = picked[w * units + u][...]
            made = contract(left, right, 1, 1) if flipped else dot(left, right)
            total = made if total is None else total + made
        height = total.shape[0] // split
        for i in range(split):
            outs[w * split + i][...] = total[i * height : (i + 1) * height].astype(BF16)


def picked_grads(table, places, lefts, rights, rows, flipped, split, block, name):
    units = len(lefts)
    width = lefts[0].shape[1]
    columns = rights[0].shape[0 if flipped else 1]
    in_specs = [pl.BlockSpec(a.shape, lambda n, *_: (0, 0)) for a in lefts]
    for a in rights:
        if flipped:
            in_specs.append(pl.BlockSpec((block, width), lambda n, *_: (n, 0)))
        else:
            in_specs.append(pl.BlockSpec((width, block), lambda n, *_: (0, n)))
    heights = [size * rows for _, size in places]
    return pl.pallas_call(
        functools.partial(picked_kernel, units, rows, places, flipped, split),
        grid_spec=pltpu.PrefetchScalarGridSpec(
            num_scalar_prefetch=1,
            grid=(columns // block,),
            in_specs=in_specs,
            out_specs=[
                pl.BlockSpec((height // split, block), lambda n, *_: (0, n)) for height in heights for _ in range(split)
            ],
            scratch_shapes=[pltpu.VMEM((height, width), BF16) for height in heights for _ in lefts],
        ),
        out_shape=[
            jax.ShapeDtypeStruct((height // split, columns), BF16) for height in heights for _ in range(split)
        ],
        compiler_params=pltpu.CompilerParams(vmem_limit_bytes=62 << 20),
        cost_estimate=pl.CostEstimate(
            flops=2 * units * sum(heights) * width * columns // COVER,
            bytes_accessed=4 * sum(heights) * columns,
            transcendentals=0,
        ),
        name=name,
    )(table, *lefts, *rights)


def tall_kernel(units, pieces_here, table_ref, *refs):
    keep_ref, send_ref = refs[-2:]
    total = None
    for u in range(units):
        left = [refs[u * pieces_here + i][...] for i in range(pieces_here)]
        made = dot(jnp.concatenate(left, axis=0), refs[units * pieces_here + u][...])
        total = made if total is None else total + made
    kept = pl.program_id(0) < pl.num_programs(0) // 2

    @pl.when(kept)
    def _():
        keep_ref[...] = total.astype(BF16)

    @pl.when(jnp.logical_not(kept))
    def _():
        send_ref[...] = total.astype(BF16)


def tall_grads(table, lefts, rights, rows, name):
    units = len(lefts)
    width = lefts[0].shape[1]
    columns = rights[0].shape[1]
    places = table.shape[0]
    each = 4
    middle = places // each // 2
    in_specs = []
    for _ in lefts:
        for i in range(each):
            in_specs.append(pl.BlockSpec((rows, width), lambda n, table, i=i: (table[n * each + i], 0)))
    in_specs += [pl.BlockSpec(a.shape, lambda n, *_: (0, 0)) for a in rights]
    return pl.pallas_call(
        functools.partial(tall_kernel, units, each),
        grid_spec=pltpu.PrefetchScalarGridSpec(
            num_scalar_prefetch=1,
            grid=(places // each,),
            in_specs=in_specs,
            out_specs=[
                pl.BlockSpec((each * rows, columns), lambda n, *_: (jnp.minimum(n, middle - 1), 0)),
                pl.BlockSpec((each * rows, columns), lambda n, *_: (jnp.maximum(n - middle, 0), 0)),
            ],
        ),
        out_shape=[jax.ShapeDtypeStruct((places // 2 * rows, columns), BF16)] * 2,
        compiler_params=pltpu.CompilerParams(vmem_limit_bytes=62 << 20),
        cost_estimate=pl.CostEstimate(
            flops=2 * units * places * rows * width * columns // COVER,
            bytes_accessed=2 * places * rows * columns,
            transcendentals=0,
        ),
        name=name,
    )(table, *[a for a in lefts for _ in range(each)], *rights)


def reduce_kernel(orders, count, *refs):
    streams = len(orders)
    rounds = len(orders[0])
    ins, vec_ref = refs[:streams], refs[streams]
    outs, vec_out = refs[streams + 1 : 2 * streams + 1], refs[2 * streams + 1]
    rest = refs[2 * streams + 2 :]
    works, arrivals = rest[:streams], rest[streams : 2 * streams]
    vec_work, vec_arrival, send_sem, recv_sem, vec_send, vec_recv = rest[2 * streams :]
    shard, seq = lax.axis_index("shard"), lax.axis_index("seq")

    def partner(mask):
        if mask >= count:
            step = mask // count
            return (shard + step * (1 - 2 * (shard // step % 2)), seq)
        return (shard, seq + mask * (1 - 2 * (seq // mask % 2)))

    barrier = pltpu.get_barrier_semaphore()
    for mask in orders[0]:
        pl.semaphore_signal(
            barrier, inc=1, device_id=partner(mask), device_id_type=pl.DeviceIdType.MESH
        )
    pl.semaphore_wait(barrier, rounds)

    height = ins[0].shape[0]
    halves = [height >> (r + 1) for r in range(rounds)]
    starts = [sum(halves[:r]) for r in range(rounds)]

    def copy_of(s, r):
        source = ins[s] if r == 0 else works[s]
        return pltpu.make_async_remote_copy(
            src_ref=source.at[pl.ds(halves[r], halves[r])],
            dst_ref=arrivals[s].at[pl.ds(starts[r], halves[r])],
            send_sem=send_sem.at[s, r],
            recv_sem=recv_sem.at[s, r],
            device_id=partner(orders[s][r]),
            device_id_type=pl.DeviceIdType.MESH,
        )

    def vec_copy(r):
        return pltpu.make_async_remote_copy(
            src_ref=vec_ref if r == 0 else vec_work.at[r - 1],
            dst_ref=vec_arrival.at[r],
            send_sem=vec_send.at[r],
            recv_sem=vec_recv.at[r],
            device_id=partner(orders[0][r]),
            device_id_type=pl.DeviceIdType.MESH,
        )

    for s in range(streams):
        copy_of(s, 0).start()
    vec_copy(0).start()
    for r in range(rounds):
        for s in range(streams):
            copy_of(s, r).wait_recv()
            source = ins[s] if r == 0 else works[s]
            size = halves[r]

            def added(low, high):
                mine = source[low:high].astype(F32)
                return mine + arrivals[s][starts[r] + low : starts[r] + high].astype(F32)

            if r == rounds - 1:
                outs[s][...] = added(0, size)
            else:
                works[s][size // 2 : size] = added(size // 2, size).astype(BF16)
                copy_of(s, r + 1).start()
                works[s][0 : size // 2] = added(0, size // 2).astype(BF16)
        vec_copy(r).wait_recv()
        before = vec_ref[...] if r == 0 else vec_work[r - 1]
        if r == rounds - 1:
            vec_out[...] = before + vec_arrival[r]
        else:
            vec_work[r] = before + vec_arrival[r]
            vec_copy(r + 1).start()
    for r in range(rounds):
        for s in range(streams):
            copy_of(s, r).wait_send()
        vec_copy(r).wait_send()


def reduce_rows(parts, vector, orders, count):
    streams = len(parts)
    rounds = len(orders[0])
    height, columns = parts[0].shape
    rows = height >> rounds
    vmem = pl.BlockSpec(memory_space=pltpu.VMEM)
    return pl.pallas_call(
        functools.partial(reduce_kernel, orders, count),
        in_specs=[vmem] * (streams + 1),
        out_specs=[vmem] * (streams + 1),
        out_shape=[jax.ShapeDtypeStruct((rows, columns), F32)] * streams
        + [jax.ShapeDtypeStruct(vector.shape, F32)],
        scratch_shapes=[pltpu.VMEM((height // 2, columns), BF16) for _ in parts]
        + [pltpu.VMEM((height - rows, columns), BF16) for _ in parts]
        + [
            pltpu.VMEM((rounds - 1,) + vector.shape, F32),
            pltpu.VMEM((rounds,) + vector.shape, F32),
            pltpu.SemaphoreType.DMA((streams, rounds)),
            pltpu.SemaphoreType.DMA((streams, rounds)),
            pltpu.SemaphoreType.DMA((rounds,)),
            pltpu.SemaphoreType.DMA((rounds,)),
        ],
        compiler_params=pltpu.CompilerParams(
            collective_id=0, has_side_effects=True, vmem_limit_bytes=62 << 20
        ),
        name="reduce_rows",
    )(*parts, vector)


def on_device(
    tokens, cotangent, lengths, variates, positions, attn_gain, w_query, w_key, w_value, w_out,
    bias_table, ffn_gain, w_gate, w_up, w_down,
):
    micro, seqs, width, model = tokens.shape
    heads = bias_table.shape[0]
    head_dim = model // heads
    count = lax.axis_size("seq")
    here = heads // count
    ffn = w_gate.shape[1]
    devices = lax.axis_size("shard") * count
    seq_index = lax.axis_index("seq")
    units = [(m, s) for m in range(micro) for s in range(seqs)]
    swap = here == 2 and len(units) == 2 and lax.axis_size("shard") % 2 == 0
    core = (lax.axis_index("shard") % 2 if swap else jnp.int32(0)).astype(jnp.int32).reshape(1)
    heads_here = 1 if swap else here
    first_head = seq_index * here + core[0]
    bias_here = lax.dynamic_slice_in_dim(bias_table, first_head, heads_here, 0)
    attn_row, ffn_row = attn_gain[None, :], ffn_gain[None, :]

    def gather(weight):
        return lax.all_gather(weight, "shard", axis=0, tiled=True)

    def exchange(values):
        return lax.all_to_all(values, "seq", split_axis=0, concat_axis=0, tiled=True)

    def after(value, *before):
        return lax.optimization_barrier((value,) + before)[0]

    attn_joined = gather(jnp.concatenate([w_query, w_key, w_value], axis=1))
    ffn_weights = [gather(w_out), gather(w_gate), gather(w_up), gather(w_down)]

    def permute(value, mask):
        return lax.ppermute(value, ("shard", "seq"), [(i, i ^ mask) for i in range(devices)])

    def cross(value):
        return permute(value, count)

    lengths_of = [lengths, cross(lengths)] if swap else [lengths] * here
    packed_list, flats, tables = [], [], []

    def run_project(u, token):
        m, s = units[u]
        cosine, sine = rotary_tables(positions[m, s], head_dim // 2)
        ids = after(variates[m, s].astype(F32)[None, :], *token)
        flat, *packed = project(
            core, tokens, (m, s), attn_row, attn_joined, cosine, sine, ids, count, here, head_dim, swap
        )
        flats.append(flat)
        tables.append((cosine, sine))
        packed_list.append(packed)

    sent = {}
    mixed_now = [None] * len(units)
    sums = {}
    mixed_tok = {}
    crossed, mixed_part, mixed_cross, heads_cross, back_cross = {}, {}, {}, {}, {}
    middle = [None] * len(units)
    grad_heads = {}
    state = {"output": None, "grads": None}
    packed_grads = {}
    returned = {}
    bias_terms = {}
    finals = [None] * len(units)

    def length_of(u, h, token):
        m, s = units[u]
        return after(lengths_of[h][m, s].reshape(1), *token)

    def inputs_of(u, h):
        if not swap:
            return sent[u, h], sent[u, 0]
        return (sent[u, 0], sent[u, 1]) if h == 0 else (crossed[u], crossed[u])

    def run_forward(u, h, token):
        made, sums[u, h] = attend_forward(
            *inputs_of(u, h), length_of(u, h, token), bias_here, None if swap else mixed_now[u],
            0 if swap else h, heads_here, head_dim,
        )
        if swap:
            mixed_part[u, h] = made
            if h == 1:
                mixed_cross[u] = cross(made)
        else:
            mixed_now[u] = made
        return sums[u, h]

    def run_middle(u, token):
        m, s = units[u]
        info = jnp.stack([lengths[m, s], seq_index * width, core[0]]).astype(jnp.int32)
        state["output"], mixed_tok[u], *middle[u] = middle_part(
            after(info, *token), mixed_tok[u], tokens, cotangent, (m, s), ffn_weights, ffn_row, head_dim,
            state["output"],
        )
        return middle[u][8]

    def run_backward(u, h, token):
        if swap:
            grad = grad_heads[u] if h == 0 else heads_cross[u]
            mixed = mixed_part[u, h]
        else:
            grad, mixed = grad_heads[u], mixed_now[u]
        packed_grads[u, h], both = attend_backward(
            *inputs_of(u, h), grad, mixed, sums[u, h], length_of(u, h, token), bias_here,
            0 if swap else h, head_dim,
        )
        if swap and h == 1:
            back_cross[u] = cross(packed_grads[u, h])
        bias_terms[u, h] = both
        return both

    def run_final(u, token):
        m, s = units[u]
        cosine, sine = tables[u]
        state["grads"], *finals[u] = final_part(
            core, tokens, (m, s), middle[u][5], after(attn_row, *token), attn_joined, cosine, sine,
            [returned[u, h] for h in range(here)], head_dim, state["grads"],
        )
        return finals[u][3]

    rows = model // devices
    fold = ffn // model
    tall = ffn // devices
    seq_masks = [1 << i for i in range(count.bit_length() - 1)]
    shard_masks = [count << i for i in range((devices // count).bit_length() - 1)]
    spread = shard_masks[1:]
    orders = (
        shard_masks[:1] + spread + seq_masks,
        shard_masks[:1] + seq_masks[:1] + spread + seq_masks[1:],
        shard_masks[:1] + seq_masks[1:2] + seq_masks[:1] + spread + seq_masks[2:],
    )
    direct = rows % 16 == 0 and devices == 1 << len(orders[0])

    def places_of(order):
        marks = []
        for p in range(devices):
            bits = [p >> (len(order) - 1 - i) & 1 for i in range(len(order))]
            marks.append(sum(mask for bit, mask in zip(bits, order) if bit))
        me = lax.axis_index("shard") * count + seq_index
        return me.astype(jnp.int32) ^ jnp.array(marks, jnp.int32)

    def column(index):
        return [item[index] for item in middle]

    def run_weights(token):
        if not direct:
            return [
                sum(dot(left, right) for left, right in zip(lefts, rights)).astype(BF16)
                for lefts, rights in (
                    (column(0), column(2)), (column(0), column(3)), (column(1), column(4)),
                    ([mixed_tok[u] for u in range(len(units))], column(6)),
                )
            ]
        tables = [after(places_of(order), *token) for order in orders]
        span = [(0, devices)]
        down = tall_grads(tables[2], column(1), column(4), tall, "down_grad")
        came = [permute(down[1], orders[2][0])]
        table = after(tables[0], down[0])
        gate = picked_grads(table, span, column(0), column(2), rows, False, 2, 1024, "gate_grad")
        came.append(permute(gate[1], orders[0][0]))
        table = after(tables[1], gate[0], *holder["flying"])
        up = picked_grads(table, span, column(0), column(3), rows, False, 2, 1024, "up_grad")
        came.append(permute(up[1], orders[1][0]))
        table = after(tables[2], up[0], *came[:2])
        mixed_all = [mixed_tok[u] for u in range(len(units))]
        out = picked_grads(table, span, mixed_all, column(6), rows, False, 2, 512, "out_grad")
        came.append(permute(out[1], orders[2][0]))
        kept = [down[0], gate[0], up[0], out[0]]
        masks = [orders[2], orders[0], orders[1], orders[2]]
        streams = [[keep, got, mask[1:]] for keep, got, mask in zip(kept, came, masks)]
        holder["streams"] = streams
        return out[0]

    def wide_sum(a, b):
        return a.astype(F32) + b.astype(F32)

    def advance(token):
        out = ()
        if not direct:
            return out
        for stream in holder["streams"]:
            keep, came, masks = stream
            if not masks:
                continue
            keep = after(keep, *token)
            half = keep.shape[0] // 2
            send = wide_sum(keep[half:], came[half:]).astype(BF16)
            stream[0] = wide_sum(keep[:half], came[:half]).astype(BF16)
            stream[1] = permute(send, masks[0])
            stream[2] = masks[1:]
            out = out + (send, stream[0])
        return out

    holder = {}

    def weights_work(token):
        holder["terms"] = run_weights(token)
        return holder["terms"]

    def send_packed(u, h):
        def keep(moved):
            sent[u, h] = moved
            if swap and h == 1:
                crossed[u] = cross(moved)

        return lambda: packed_list[u][h], keep

    def send_mixed(u):
        def keep(moved):
            mixed_tok[u] = moved.reshape(model, width)

        if not swap:
            return lambda: mixed_now[u], keep
        return lambda: jnp.concatenate([mixed_part[u, 0], mixed_cross[u]], axis=1), keep

    def send_heads(u):
        def keep(moved):
            grad_heads[u] = moved
            if swap:
                heads_cross[u] = cross(moved[:, head_dim:])
                pending.append(heads_cross[u])

        return lambda: middle[u][7].reshape(count, here * head_dim, width), keep

    def send_back(u, h):
        def keep(moved):
            returned[u, h] = moved

        return lambda: back_cross[u] if swap and h == 1 else packed_grads[u, h], keep

    def work_project(u):
        def work(token):
            run_project(u, token)
            return flats[u]

        return work

    def work(function, *args):
        return lambda token: function(*args, token)

    total = len(units)
    order = [(u, h) for u in range(total) for h in range(here)]
    if swap:
        steps = [
            (work_project(0), None),
            (work_project(1), send_packed(0, 1)),
            (work(run_forward, 0, 1), send_packed(0, 0)),
            (work(run_forward, 0, 0), send_packed(1, 1)),
            (work(run_forward, 1, 1), send_packed(1, 0)),
            (work(run_forward, 1, 0), send_mixed(0)),
            (work(run_middle, 0), send_mixed(1)),
            (work(run_middle, 1), send_heads(0)),
            (weights_work, send_heads(1)),
            (work(run_backward, 0, 0), None),
            (work(run_backward, 0, 1), send_back(0, 0)),
            (work(run_backward, 1, 0), send_back(0, 1)),
            (work(run_backward, 1, 1), send_back(1, 0)),
            (work(run_final, 0), send_back(1, 1)),
            (work(run_final, 1), None),
        ]
    else:
        steps = [(work_project(u), None) for u in range(total)]
        steps += [(None, send_packed(*at)) for at in order]
        for u in range(total):
            steps += [(work(run_forward, u, h), None) for h in range(here)]
            steps += [(None, send_mixed(u))]
        for u in range(total):
            steps += [(work(run_middle, u), None), (None, send_heads(u))]
        steps += [(weights_work, None)]
        for at in order:
            steps += [(work(run_backward, *at), None), (None, send_back(*at))]
        steps += [(work(run_final, u), None) for u in range(total)]

    late = [task for task, _ in steps[-2:]]
    token = ()
    pending = []
    for task, send in steps:
        done = ()
        moved = None
        waited = tuple(pending)
        pending.clear()
        if "streams" in holder:
            leaving = advance(token)
            token = token if task in late else token + leaving
        if send is not None:
            moved = exchange(after(send[0](), *token))
            done = (moved,)
        holder["flying"] = done
        if task is not None:
            done = done + (task(token),)
        if send is not None:
            send[1](after(moved, *done[1:]))
        token = done + waited
    acc_bias = jnp.concatenate(
        [sum(bias_terms[u, h] for u in range(total))[0:1, 0:2] for h in range(here)], axis=0
    )
    if swap:
        acc_bias = acc_bias[0:1] + acc_bias[1:2]
    bias_full = lax.dynamic_update_slice(
        jnp.zeros((heads, 2), F32), acc_bias, (first_head, jnp.int32(0))
    )
    gain_attn = sum(item[3][0] for item in finals)
    gain_ffn = sum(item[8][0] for item in middle)
    if direct:
        while holder["streams"][0][2]:
            advance(token)
        down_own, gate_own, up_own, out_own = [
            wide_sum(after(keep, *token), came) for keep, came, _ in holder["streams"]
        ]
        table = jnp.concatenate([places_of(order) for order in orders])
        attn_terms = picked_grads(
            table, [(i * devices, devices) for i in range(3)], flats,
            [item[i] for i in range(3) for item in finals], rows, True, 1, 256, "attn_grads",
        )
        flat = jnp.concatenate([gain_attn, gain_ffn, bias_full.reshape(-1)])
        tiles = -(-flat.shape[0] // 1024) * 8
        flat = jnp.pad(flat, (0, tiles * 128 - flat.shape[0])).reshape(tiles, 128)
        query_own, key_own, value_own, flat = reduce_rows(list(attn_terms), flat, orders, count)
        flat = flat.reshape(-1)
        gain_attn, gain_ffn = flat[:model], flat[model : 2 * model]
        bias_full = flat[2 * model : 2 * model + 2 * heads].reshape(heads, 2)
    else:

        def scatter(value):
            owned = lax.psum_scatter(value, ("shard", "seq"), scatter_dimension=0, tiled=True)
            return owned.astype(F32)

        gate_own, up_own, down_own, out_own = [scatter(value) for value in holder["terms"]]
        query_own, key_own, value_own = [
            scatter(
                sum(contract(flat, item[i], 1, 1) for flat, item in zip(flats, finals)).astype(BF16)
            )
            for i in range(3)
        ]
        gain_attn, gain_ffn, bias_full = lax.psum(
            (gain_attn, gain_ffn, bias_full), ("shard", "seq")
        )
    return (
        state["output"], state["grads"], gain_attn, query_own, key_own, value_own, out_own,
        bias_full, gain_ffn, gate_own, up_own, down_own,
    )


def solution(mesh):
    token_spec = P(None, "shard", "seq", None)
    row_spec = P("shard", None)
    in_specs = (
        token_spec, token_spec, P(None, "shard"), P(None, "shard", "seq"), P(None, "shard", "seq"),
        P(), row_spec, row_spec, row_spec, row_spec, P(), P(), row_spec, row_spec, row_spec,
    )
    owned = P(("shard", "seq"), None)
    out_specs = (
        token_spec, token_spec, P(), owned, owned, owned, owned, P(), P(), owned, owned, owned,
    )
    return jax.shard_map(
        on_device, mesh=mesh, in_specs=in_specs, out_specs=out_specs, check_vma=False
    )
```

```python
import functools
import math

import jax
import jax.numpy as jnp
from jax import lax
from jax.experimental import pallas as pl
from jax.experimental.pallas import tpu as pltpu
from jax.sharding import PartitionSpec as P

EPSILON = 1e-06
ROTARY_BASE = 10000.0
LOG2E = 1.4426950408889634
LN2 = 0.6931471805599453
CLASSES = 8
AUX = 16
COVER = 16
EXTRA = 32
MASKED = -1.5e9
FAR = 1e30
F32 = jnp.float32
BF16 = jnp.bfloat16


def dot(a, b):
    return jnp.dot(a, b, preferred_element_type=F32)


def contract(a, b, da, db):
    return lax.dot_general(a, b, (((da,), (db,)), ((), ())), preferred_element_type=F32)


def pieces(x):
    high = x.astype(BF16).astype(F32)
    rest = x - high
    mid = rest.astype(BF16).astype(F32)
    low = (rest - mid).astype(BF16).astype(F32)
    return high, mid, low


def one_hot(row):
    classes = lax.broadcasted_iota(jnp.int32, (CLASSES, row.shape[1]), 0).astype(F32)
    return jnp.where(classes == row, 1.0, 0.0)


def rows_of(values, width):
    index = lax.broadcasted_iota(jnp.int32, (8, width), 0)
    out = jnp.zeros((8, width), F32)
    for at, value in enumerate(values):
        out = jnp.where(index == at, value, out)
    return out


def key_extra(row, start, length, other, same):
    width = row.shape[1]
    hot = one_hot(row)
    step = pieces(jnp.full((1, width), same - other, F32))
    base = pieces(jnp.full((1, width), other, F32))
    index = start + lax.broadcasted_iota(jnp.int32, (1, width), 1)
    mask = jnp.where(index < length, 0.0, MASKED)
    tail = rows_of(base + (mask, 1.0, 1.0, 1.0), width)
    return jnp.concatenate([hot * step[0], hot * step[1], hot * step[2], tail], axis=0).astype(BF16)


def query_extra(row, shift):
    hot = one_hot(row)
    tail = rows_of((1.0, 1.0, 1.0, 1.0) + shift, row.shape[1])
    return jnp.concatenate([hot, hot, hot, tail], axis=0).astype(BF16)


def forward_kernel(
    shape, len_ref, bias_ref, x_ref, ids_ref, *rest
):
    local, head_dim, block, aliased = shape
    if aliased:
        rest = rest[1:]
    mixed_ref, lse_ref, keys, vals, query, score, peak, total = rest
    count, _, width = x_ref.shape
    sub = block // width
    step = pl.program_id(0)
    length = len_ref[0]
    other = bias_ref[local, 0] * LOG2E
    same = bias_ref[local, 1] * LOG2E

    @pl.when(step == 0)
    def _():
        for b in range(count):
            at = pl.ds(b * width, width)
            row = ids_ref[b, 0:1, :].astype(F32)
            extra = key_extra(row, b * width, length, other, same)
            full = jnp.concatenate([x_ref[b, head_dim : 2 * head_dim, :], extra], axis=0)
            keys[at, :] = full.T
            vals[0:head_dim, at] = x_ref[b, 2 * head_dim : 3 * head_dim, :]
        vals[head_dim:, :] = jnp.ones((16, vals.shape[1]), BF16)

    used = pl.cdiv(length, block)
    inside = step * block < length

    @pl.when(jnp.logical_not(inside))
    def _():
        mixed_ref[...] = jnp.zeros_like(mixed_ref)
        lse_ref[...] = jnp.full(lse_ref.shape, FAR, F32)

    @pl.when(inside)
    def _():
        for b in range(sub):
            at = slice(b * width, (b + 1) * width)
            row = ids_ref[step * sub + b, 0:1, :].astype(F32)
            query[0:head_dim, at] = x_ref[step * sub + b, 0:head_dim, :]
            query[head_dim:, at] = query_extra(row, (0.0, 0.0, 0.0))
        peak[...] = jnp.full(peak.shape, -FAR, F32)
        total[...] = jnp.zeros_like(total)

        def span(j):
            return pl.ds(pl.multiple_of(j * block, block), block)

        def scores_of(j):
            return dot(keys[span(j), :], query[...])

        def one(j, now, ahead):
            if ahead:
                score[1 - now] = scores_of(j + 1)
            current = score[now]
            before = peak[...]
            top = jnp.maximum(before, jnp.max(current, axis=0, keepdims=True))
            weight = jnp.exp2(current - top).astype(BF16)
            peak[...] = top
            total[...] = total[...] * jnp.exp2(before - top) + dot(vals[:, span(j)], weight)

        score[0] = scores_of(0)
        pairs = (used - 1) // 2

        def pair(j, carry):
            one(2 * j, 0, True)
            one(2 * j + 1, 1, True)
            return carry

        lax.fori_loop(0, pairs, pair, 0)
        last = 2 * pairs

        @pl.when(used - last == 1)
        def _():
            one(last, 0, False)

        @pl.when(used - last == 2)
        def _():
            one(last, 0, True)
            one(last + 1, 1, False)

        mass = total[head_dim : head_dim + 1, :]
        mixed = (total[0:head_dim, :] / mass).astype(BF16)
        for b in range(sub):
            mixed_ref[b] = mixed[:, b * width : (b + 1) * width]
        lse_ref[0] = peak[...] + jnp.log2(mass)


def attend_forward(x, ids, length, bias, mixed, local, heads_here, head_dim):
    count, rows, width = x.shape
    block = max(width, 512)
    seq_len = count * width
    blocks = seq_len // block
    depth = head_dim + EXTRA
    whole = pl.BlockSpec((count, rows, width), lambda i, *_: (0, 0, 0))
    operands = [length, bias, x, ids]
    in_specs = [whole, pl.BlockSpec((count, AUX, width), lambda i, *_: (0, 3 * head_dim // AUX, 0))]
    aliases = {}
    if mixed is not None:
        operands.append(mixed)
        in_specs.append(pl.BlockSpec(memory_space=pl.ANY))
        aliases = {4: 0}
    return pl.pallas_call(
        functools.partial(forward_kernel, (local, head_dim, block, mixed is not None)),
        grid_spec=pltpu.PrefetchScalarGridSpec(
            num_scalar_prefetch=2,
            grid=(blocks,),
            in_specs=in_specs,
            out_specs=[
                pl.BlockSpec((block // width, head_dim, width), lambda i, *_: (i, local, 0)),
                pl.BlockSpec((1, 1, block), lambda i, *_: (i, 0, 0)),
            ],
            scratch_shapes=[
                pltpu.VMEM((seq_len, depth), BF16),
                pltpu.VMEM((head_dim + 16, seq_len), BF16),
                pltpu.VMEM((depth, block), BF16),
                pltpu.VMEM((2, block, block), F32),
                pltpu.VMEM((1, block), F32),
                pltpu.VMEM((head_dim + 16, block), F32),
            ],
        ),
        out_shape=[
            jax.ShapeDtypeStruct((count, heads_here * head_dim, width), BF16),
            jax.ShapeDtypeStruct((blocks, 1, block), F32),
        ],
        input_output_aliases=aliases,
        compiler_params=pltpu.CompilerParams(vmem_limit_bytes=62 << 20),
        cost_estimate=pl.CostEstimate(
            flops=8 * seq_len * seq_len * 256 // COVER,
            bytes_accessed=x.size * 4,
            transcendentals=0,
        ),
        name="attend_forward",
    )(*operands)


def backward_kernel(
    shape, len_ref, bias_ref, x_ref, ids_ref, grad_ref, mixed_ref, lse_ref, out_ref, bias_out_ref,
    keys, keys_flat, vals, query, grads, query_rows, grad_rows, acc_keys, acc_vals, acc_query,
):
    local, head_dim, block = shape
    count, _, width = x_ref.shape
    sub = block // width
    step = pl.program_id(0)
    length = len_ref[0]
    other = bias_ref[local, 0] * LOG2E
    same = bias_ref[local, 1] * LOG2E

    @pl.when(step == 0)
    def _():
        ones = jnp.ones((16, width), BF16)
        for b in range(count):
            at = pl.ds(b * width, width)
            row = ids_ref[b, 0:1, :].astype(F32)
            extra = key_extra(row, b * width, length, other, same)
            here = x_ref[b, head_dim : 2 * head_dim, :]
            keys[at, :] = jnp.concatenate([here, extra], axis=0).T
            keys_flat[:, at] = here
            vals[at, :] = jnp.concatenate([x_ref[b, 2 * head_dim : 3 * head_dim, :], ones], axis=0).T
        acc_keys[...] = jnp.zeros_like(acc_keys)
        acc_vals[...] = jnp.zeros_like(acc_vals)

    used = pl.cdiv(length, block)
    inside = step * block < length

    @pl.when(jnp.logical_not(inside))
    def _():
        for b in range(sub):
            out_ref[step * sub + b, 0:head_dim, :] = jnp.zeros((head_dim, width), BF16)

    @pl.when(inside)
    def _():
        for b in range(sub):
            at = slice(b * width, (b + 1) * width)
            here = step * sub + b
            row = ids_ref[here, 0:1, :].astype(F32)
            shift = pieces(-lse_ref[step][:, at])
            grad = grad_ref[here]
            delta = jnp.sum(grad.astype(F32) * mixed_ref[here].astype(F32), axis=0, keepdims=True)
            query[0:head_dim, at] = x_ref[here, 0:head_dim, :]
            query[head_dim:, at] = query_extra(row, shift)
            grads[0:head_dim, at] = grad
            tail = rows_of(pieces(-delta), width)
            grads[head_dim:, at] = jnp.concatenate([tail, jnp.zeros_like(tail)], axis=0).astype(BF16)
        query_rows[...] = query[...].T
        grad_rows[...] = grads[...].T
        acc_query[...] = jnp.zeros_like(acc_query)

        def one(j):
            at = pl.ds(pl.multiple_of(j * block, block), block)
            probs = jnp.exp2(dot(keys[at, :], query[...]))
            grad_probs = dot(vals[at, :], grads[...])
            grad_scores = (probs * grad_probs).astype(BF16)
            acc_vals[at, :] += dot(probs.astype(BF16), grad_rows[...])
            acc_keys[at, :] += dot(grad_scores, query_rows[...])
            acc_query[...] += dot(keys_flat[:, at], grad_scores)

        def pair(j, carry):
            one(2 * j)
            one(2 * j + 1)
            return carry

        lax.fori_loop(0, used // 2, pair, 0)

        @pl.when(used % 2 == 1)
        def _():
            one(used - 1)

        grad_query = (acc_query[...] * (1.0 / math.sqrt(head_dim))).astype(BF16)
        for b in range(sub):
            out_ref[step * sub + b, 0:head_dim, :] = grad_query[:, b * width : (b + 1) * width]

    @pl.when(step == pl.num_programs(0) - 1)
    def _():
        same_total = jnp.zeros((CLASSES, width), F32)
        all_total = jnp.zeros((CLASSES, width), F32)
        for b in range(count):
            at = pl.ds(b * width, width)
            row = ids_ref[b, 0:1, :].astype(F32)
            flat = acc_keys[at, :].T
            out_ref[b, head_dim : 2 * head_dim, :] = (flat[0:head_dim] * LN2).astype(BF16)
            out_ref[b, 2 * head_dim : 3 * head_dim, :] = acc_vals[at, :].T[0:head_dim].astype(BF16)
            by_class = flat[head_dim : head_dim + CLASSES]
            all_total += by_class
            same_total += by_class * one_hot(row)
        same_sum = jnp.sum(same_total, keepdims=True)
        other_sum = jnp.sum(all_total, keepdims=True) - same_sum
        lane = lax.broadcasted_iota(jnp.int32, (8, 128), 1)
        bias_out_ref[...] = jnp.where(lane == 0, other_sum, jnp.where(lane == 1, same_sum, 0.0))


def attend_backward(x, ids, grad, mixed, lse, length, bias, local, head_dim):
    count, rows, width = x.shape
    blocks, _, block = lse.shape
    seq_len = count * width
    depth = head_dim + EXTRA

    def whole(a):
        return pl.BlockSpec(a.shape, lambda i, *_: (0,) * a.ndim)

    head_spec = pl.BlockSpec((count, head_dim, width), lambda i, *_: (0, local, 0))
    return pl.pallas_call(
        functools.partial(backward_kernel, (local, head_dim, block)),
        grid_spec=pltpu.PrefetchScalarGridSpec(
            num_scalar_prefetch=2,
            grid=(blocks,),
            in_specs=[
                whole(x),
                pl.BlockSpec((count, AUX, width), lambda i, *_: (0, 3 * head_dim // AUX, 0)),
                head_spec, head_spec, whole(lse),
            ],
            out_specs=[
                pl.BlockSpec((count, 3 * head_dim, width), lambda i, *_: (0, 0, 0)),
                pl.BlockSpec((8, 128), lambda i, *_: (0, 0)),
            ],
            scratch_shapes=[
                pltpu.VMEM((seq_len, depth), BF16),
                pltpu.VMEM((head_dim, seq_len), BF16),
                pltpu.VMEM((seq_len, head_dim + 16), BF16),
                pltpu.VMEM((depth, block), BF16),
                pltpu.VMEM((head_dim + 16, block), BF16),
                pltpu.VMEM((block, depth), BF16),
                pltpu.VMEM((block, head_dim + 16), BF16),
                pltpu.VMEM((seq_len, depth), F32),
                pltpu.VMEM((seq_len, head_dim + 16), F32),
                pltpu.VMEM((head_dim, block), F32),
            ],
        ),
        out_shape=[
            jax.ShapeDtypeStruct((count, 3 * head_dim, width), BF16),
            jax.ShapeDtypeStruct((8, 128), F32),
        ],
        compiler_params=pltpu.CompilerParams(vmem_limit_bytes=62 << 20),
        cost_estimate=pl.CostEstimate(
            flops=20 * seq_len * seq_len * 256 // COVER,
            bytes_accessed=x.size * 6,
            transcendentals=0,
        ),
        name="attend_backward",
    )(length, bias, x, ids, grad, mixed, lse)


def rotary_tables(places, half_dim):
    frequency = jnp.exp(-math.log(ROTARY_BASE) * jnp.arange(half_dim, dtype=F32) / half_dim)
    angles = places.astype(F32)[None, :] * frequency[:, None]
    return jnp.cos(angles), jnp.sin(angles)


def sigmoid_of(x):
    return 1.0 / (1.0 + jnp.exp2(x * -LOG2E))


def project_kernel(
    shape, core_ref, tokens_ref, gain_ref, query_ref, key_ref, value_ref, cos_ref, sin_ref, ids_ref, flat_ref, *rest
):
    here, head_dim, extras, swap = shape
    outs, flat_weights = rest[:-1], rest[-1]
    pair = pl.program_id(0)

    @pl.when(pair == 0)
    def _():
        inputs = tokens_ref[0, 0].astype(F32)
        inverse = lax.rsqrt(jnp.mean(inputs * inputs, axis=-1, keepdims=True) + EPSILON)
        flat_ref[...] = (inputs * inverse * gain_ref[...]).astype(BF16).T

    flat_weights[0:128, :] = query_ref[...].T
    flat_weights[128:256, :] = key_ref[...].T
    flat_weights[256:384, :] = value_ref[...].T
    made = dot(flat_weights[...], flat_ref[...])
    cosine, sine = cos_ref[...], sin_ref[...]
    half = head_dim // 2

    def turned(start, scale):
        first = made[start : start + half]
        second = made[start + half : start + head_dim]
        both = [first * cosine - second * sine, second * cosine + first * sine]
        return (jnp.concatenate(both, axis=0) * scale).astype(BF16)

    def put(at, slot, place):
        spot = at * head_dim
        target = outs[slot]
        target[place, 0:head_dim, :] = turned(spot, LOG2E / math.sqrt(head_dim))
        target[place, head_dim : 2 * head_dim, :] = turned(128 + spot, 1.0)
        target[place, 2 * head_dim : 3 * head_dim, :] = made[256 + spot : 256 + spot + head_dim].astype(BF16)
        if extras[slot]:
            target[place, 3 * head_dim :, :] = jnp.broadcast_to(ids_ref[...], (AUX, ids_ref.shape[1])).astype(BF16)

    if swap:
        for core in range(2):

            @pl.when(core_ref[0] == core)
            def _():
                put(core, 0, 0)
                put(1 - core, 1, 0)

    else:
        for at in range(128 // head_dim):
            put(at, at % here, 0 if here > 1 else at)


def project(core, tokens, unit, gain, weights, cosine, sine, ids, count, here, head_dim, swap):
    width, model = tokens.shape[2:]
    heads = count * here
    pairs = heads * head_dim // 128
    per = 128 // head_dim // here
    extras = [h == (1 if swap else 0) for h in range(here)]

    def fixed(a):
        return pl.BlockSpec(a.shape, lambda p: (0,) * a.ndim)

    weight_specs = [pl.BlockSpec((model, 128), lambda p, i=i: (0, i * pairs + p)) for i in range(3)]
    return pl.pallas_call(
        functools.partial(project_kernel, (here, head_dim, extras, swap)),
        grid=(pairs,),
        in_specs=[
            pl.BlockSpec(memory_space=pltpu.SMEM),
            pl.BlockSpec((1, 1, width, model), lambda p: unit + (0, 0)),
            fixed(gain), *weight_specs, fixed(cosine), fixed(sine), fixed(ids),
        ],
        out_specs=[pl.BlockSpec((model, width), lambda p: (0, 0))]
        + [pl.BlockSpec((per, 3 * head_dim + AUX * e, width), lambda p: (p, 0, 0)) for e in extras],
        out_shape=[jax.ShapeDtypeStruct((model, width), BF16)]
        + [jax.ShapeDtypeStruct((count, 3 * head_dim + AUX * e, width), BF16) for e in extras],
        scratch_shapes=[pltpu.VMEM((384, model), BF16)],
        compiler_params=pltpu.CompilerParams(vmem_limit_bytes=62 << 20),
        cost_estimate=pl.CostEstimate(
            flops=6 * width * model * model // COVER, bytes_accessed=12 * model * model, transcendentals=0
        ),
        name="project",
    )(core, tokens, gain, weights, weights, weights, cosine, sine, ids)


def middle_kernel(
    shape, info_ref, mixed_ref, tokens_ref, cot_ref, out_w_ref, gain_ref, gate_w_ref, up_w_ref, down_w_ref, *rest
):
    head_dim, aliased = shape
    if aliased:
        rest = rest[1:]
    (
        output_ref, ordered_ref, flat_ref, hidden_ref, grad_gate_ref, grad_up_ref, grad_ffn_ref, grad_res_ref,
        grad_attn_ref, grad_mixed_ref, gain_out_ref, normed, residual, ffn_out, grad_normed, slots,
    ) = rest
    core = info_ref[2]
    step = pl.program_id(0)
    width = normed.shape[0]

    def valid():
        index = info_ref[1] + lax.broadcasted_iota(jnp.int32, (width, 1), 0)
        return jnp.where(index < info_ref[0], 1.0, 0.0)

    def inverse_of(x):
        return lax.rsqrt(jnp.mean(x * x, axis=-1, keepdims=True) + EPSILON)

    def head_rows(pair, slot):
        head = 2 * pair + (core if slot == 0 else 1 - core)
        return pl.ds(pl.multiple_of(head * head_dim, head_dim), head_dim)

    def slot_rows(pair, slot):
        return slice((2 * pair + slot) * head_dim, (2 * pair + slot + 1) * head_dim)

    spots = [(pair, slot) for pair in range(mixed_ref.shape[0] // head_dim // 2) for slot in range(2)]

    @pl.when(step == 0)
    def _():
        for spot in spots:
            ordered_ref[head_rows(*spot), :] = mixed_ref[slot_rows(*spot), :]
        inputs = tokens_ref[0, 0].astype(F32) + dot(ordered_ref[...].T, out_w_ref[...])
        residual[...] = inputs
        made = (inputs * inverse_of(inputs) * gain_ref[...]).astype(BF16)
        normed[...] = made
        flat_ref[...] = made.T
        grad_ffn_ref[...] = (cot_ref[0, 0].astype(F32) * valid()).astype(BF16)
        ffn_out[...] = jnp.zeros_like(ffn_out)
        grad_normed[...] = jnp.zeros_like(grad_normed)

    gate = dot(normed[...], gate_w_ref[...])
    up = dot(normed[...], up_w_ref[...])
    grad_hidden = contract(grad_ffn_ref[...], down_w_ref[...], 1, 1)
    sigmoid = sigmoid_of(gate)
    silu = gate * sigmoid
    hidden = (silu * up).astype(BF16)
    grad_gate = (grad_hidden * up * (sigmoid + silu * (1.0 - sigmoid))).astype(BF16)
    grad_up = (grad_hidden * silu).astype(BF16)
    hidden_ref[...] = hidden.T
    grad_gate_ref[...] = grad_gate
    grad_up_ref[...] = grad_up
    ffn_out[...] += dot(hidden, down_w_ref[...])
    grad_normed[...] += contract(grad_gate, gate_w_ref[...], 1, 1) + contract(grad_up, up_w_ref[...], 1, 1)

    @pl.when(step == pl.num_programs(0) - 1)
    def _():
        keep = valid()
        kept = residual[...]
        output_ref[0, 0] = ((kept + ffn_out[...]) * keep).astype(BF16)
        inverse = inverse_of(kept)
        scaled = grad_normed[...] * gain_ref[...]
        mean = jnp.mean(scaled * kept, axis=-1, keepdims=True)
        grad = cot_ref[0, 0].astype(F32) * keep
        grad = grad + (inverse * scaled - kept * (inverse * inverse * inverse) * mean)
        gain_out_ref[...] = jnp.sum(grad_normed[...] * kept * inverse, axis=0, keepdims=True)
        grad_res_ref[...] = grad
        low = grad.astype(BF16)
        grad_attn_ref[...] = low
        slots[...] = contract(out_w_ref[...], low, 1, 1).astype(BF16)
        for spot in spots:
            grad_mixed_ref[slot_rows(*spot), :] = slots[head_rows(*spot), :]


def middle_part(info, mixed, tokens, cotangent, unit, weights, gain, head_dim, output):
    width, model = tokens.shape[2:]
    out_w, gate_w, up_w, down_w = weights
    ffn = gate_w.shape[1]
    block = 512

    def fixed(a):
        return pl.BlockSpec(a.shape, lambda f, *_: (0,) * a.ndim)

    def one(*shape):
        return pl.BlockSpec(shape, lambda f, *_: (0,) * len(shape))

    token_spec = pl.BlockSpec((1, 1, width, model), lambda f, *_: unit + (0, 0))
    operands = [info, mixed, tokens, cotangent, out_w, gain, gate_w, up_w, down_w]
    in_specs = [
        fixed(mixed), token_spec, token_spec, fixed(out_w), fixed(gain),
        pl.BlockSpec((model, block), lambda f, *_: (0, f)),
        pl.BlockSpec((model, block), lambda f, *_: (0, f)),
        pl.BlockSpec((block, model), lambda f, *_: (f, 0)),
    ]
    aliases = {}
    if output is not None:
        aliases = {len(operands): 0}
        operands.append(output)
        in_specs.append(pl.BlockSpec(memory_space=pl.ANY))
    struct = jax.ShapeDtypeStruct
    return pl.pallas_call(
        functools.partial(middle_kernel, (head_dim, output is not None)),
        grid_spec=pltpu.PrefetchScalarGridSpec(
            num_scalar_prefetch=1,
            grid=(ffn // block,),
            in_specs=in_specs,
            out_specs=[
                token_spec, one(model, width), one(model, width),
                pl.BlockSpec((block, width), lambda f, *_: (f, 0)),
                pl.BlockSpec((width, block), lambda f, *_: (0, f)),
                pl.BlockSpec((width, block), lambda f, *_: (0, f)),
                one(width, model), one(width, model), one(width, model), one(model, width), one(1, model),
            ],
            scratch_shapes=[
                pltpu.VMEM((width, model), BF16),
                pltpu.VMEM((width, model), F32),
                pltpu.VMEM((width, model), F32),
                pltpu.VMEM((width, model), F32),
                pltpu.VMEM((model, width), BF16),
            ],
        ),
        out_shape=[
            struct(tokens.shape, BF16), struct((model, width), BF16), struct((model, width), BF16),
            struct((ffn, width), BF16),
            struct((width, ffn), BF16), struct((width, ffn), BF16), struct((width, model), BF16),
            struct((width, model), F32), struct((width, model), BF16), struct((model, width), BF16),
            struct((1, model), F32),
        ],
        input_output_aliases=aliases,
        compiler_params=pltpu.CompilerParams(vmem_limit_bytes=62 << 20),
        cost_estimate=pl.CostEstimate(
            flops=12 * width * model * ffn // COVER, bytes_accessed=8 * model * ffn, transcendentals=0
        ),
        name="middle_part",
    )(*operands)


def final_kernel(
    shape, core_ref, tokens_ref, grad_res_ref, gain_ref, query_ref, key_ref, value_ref, cos_ref, sin_ref, *rest
):
    here, head_dim, aliased = shape
    back = rest[:here]
    rest = rest[here:]
    if aliased:
        rest = rest[1:]
    out_ref, grad_q_ref, grad_k_ref, grad_v_ref, gain_out_ref, total = rest
    step = pl.program_id(0)
    cosine, sine = cos_ref[...], sin_ref[...]
    half = head_dim // 2

    def turned(x):
        first, second = x[:half].astype(F32), x[half:].astype(F32)
        return jnp.concatenate(
            [first * cosine + second * sine, second * cosine - first * sine], axis=0
        ).astype(BF16)

    for at in range(256 // head_dim):
        head = at
        if here == 2:
            head = at // 2 * 2 + (core_ref[0] if at % 2 == 0 else 1 - core_ref[0])
        place = pl.ds(pl.multiple_of(head * head_dim, head_dim), head_dim)
        part = back[at % here]
        grad_q_ref[place, :] = turned(part[at // here, 0:head_dim, :])
        grad_k_ref[place, :] = turned(part[at // here, head_dim : 2 * head_dim, :])
        grad_v_ref[place, :] = part[at // here, 2 * head_dim : 3 * head_dim, :]
    made = (
        contract(grad_q_ref[...].T, query_ref[...], 1, 1)
        + contract(grad_k_ref[...].T, key_ref[...], 1, 1)
        + contract(grad_v_ref[...].T, value_ref[...], 1, 1)
    )

    @pl.when(step == 0)
    def _():
        total[...] = made

    @pl.when(step > 0)
    def _():
        total[...] += made

    @pl.when(step == pl.num_programs(0) - 1)
    def _():
        inputs = tokens_ref[0, 0].astype(F32)
        inverse = lax.rsqrt(jnp.mean(inputs * inputs, axis=-1, keepdims=True) + EPSILON)
        scaled = total[...] * gain_ref[...]
        mean = jnp.mean(scaled * inputs, axis=-1, keepdims=True)
        grad = inverse * scaled - inputs * (inverse * inverse * inverse) * mean
        out_ref[0, 0] = (grad_res_ref[...] + grad).astype(BF16)
        gain_out_ref[...] = jnp.sum(total[...] * inputs * inverse, axis=0, keepdims=True)


def final_part(core, tokens, unit, grad_res, gain, weights, cosine, sine, back, head_dim, output):
    width, model = tokens.shape[2:]
    here = len(back)
    steps = model // 256

    def fixed(a):
        return pl.BlockSpec(a.shape, lambda c: (0,) * a.ndim)

    token_spec = pl.BlockSpec((1, 1, width, model), lambda c: unit + (0, 0))
    weight_specs = [pl.BlockSpec((model, 256), lambda c, i=i: (0, i * steps + c)) for i in range(3)]
    row_spec = pl.BlockSpec((256, width), lambda c: (c, 0))
    operands = [core, tokens, grad_res, gain, weights, weights, weights, cosine, sine, *back]
    in_specs = [
        pl.BlockSpec(memory_space=pltpu.SMEM), token_spec, fixed(grad_res), fixed(gain), *weight_specs,
        fixed(cosine), fixed(sine),
    ] + [
        pl.BlockSpec((256 // head_dim // here, 3 * head_dim, width), lambda c: (c, 0, 0)) for _ in back
    ]
    aliases = {}
    if output is not None:
        aliases = {len(operands): 0}
        operands.append(output)
        in_specs.append(pl.BlockSpec(memory_space=pl.ANY))
    struct = jax.ShapeDtypeStruct
    return pl.pallas_call(
        functools.partial(final_kernel, (here, head_dim, output is not None)),
        grid=(steps,),
        in_specs=in_specs,
        out_specs=[token_spec, row_spec, row_spec, row_spec, pl.BlockSpec((1, model), lambda c: (0, 0))],
        out_shape=[
            struct(tokens.shape, BF16), struct((model, width), BF16), struct((model, width), BF16),
            struct((model, width), BF16), struct((1, model), F32),
        ],
        scratch_shapes=[pltpu.VMEM((width, model), F32)],
        input_output_aliases=aliases,
        compiler_params=pltpu.CompilerParams(vmem_limit_bytes=62 << 20),
        cost_estimate=pl.CostEstimate(
            flops=6 * width * model * model // COVER, bytes_accessed=12 * model * model, transcendentals=0
        ),
        name="final_part",
    )(*operands)


def picked_kernel(units, rows, places, flipped, split, table_ref, *refs):
    weights = len(places)
    lefts = refs[0:units]
    rights = refs[units : units * (1 + weights)]
    outs = refs[units * (1 + weights) : units * (1 + weights) + weights * split]
    picked = refs[units * (1 + weights) + weights * split :]

    @pl.when(pl.program_id(0) == 0)
    def _():
        for w, (start, size) in enumerate(places):
            for p in range(size):
                at = pl.ds(pl.multiple_of(table_ref[start + p] * rows, rows), rows)
                for u in range(units):
                    picked[w * units + u][p * rows : (p + 1) * rows, :] = lefts[u][at, :]

    for w in range(weights):
        total = None
        for u in range(units):
            right = rights[w * units + u][...]
            left = picked[w * units + u][...]
            made = contract(left, right, 1, 1) if flipped else dot(left, right)
            total = made if total is None else total + made
        height = total.shape[0] // split
        for i in range(split):
            outs[w * split + i][...] = total[i * height : (i + 1) * height].astype(BF16)


def picked_grads(table, places, lefts, rights, rows, flipped, split, block, name):
    units = len(lefts)
    width = lefts[0].shape[1]
    columns = rights[0].shape[0 if flipped else 1]
    in_specs = [pl.BlockSpec(a.shape, lambda n, *_: (0, 0)) for a in lefts]
    for a in rights:
        if flipped:
            in_specs.append(pl.BlockSpec((block, width), lambda n, *_: (n, 0)))
        else:
            in_specs.append(pl.BlockSpec((width, block), lambda n, *_: (0, n)))
    heights = [size * rows for _, size in places]
    return pl.pallas_call(
        functools.partial(picked_kernel, units, rows, places, flipped, split),
        grid_spec=pltpu.PrefetchScalarGridSpec(
            num_scalar_prefetch=1,
            grid=(columns // block,),
            in_specs=in_specs,
            out_specs=[
                pl.BlockSpec((height // split, block), lambda n, *_: (0, n)) for height in heights for _ in range(split)
            ],
            scratch_shapes=[pltpu.VMEM((height, width), BF16) for height in heights for _ in lefts],
        ),
        out_shape=[
            jax.ShapeDtypeStruct((height // split, columns), BF16) for height in heights for _ in range(split)
        ],
        compiler_params=pltpu.CompilerParams(vmem_limit_bytes=62 << 20),
        cost_estimate=pl.CostEstimate(
            flops=2 * units * sum(heights) * width * columns // COVER,
            bytes_accessed=4 * sum(heights) * columns,
            transcendentals=0,
        ),
        name=name,
    )(table, *lefts, *rights)


def weights_kernel(units, *refs):
    out_ref = refs[-1]
    total = dot(refs[0][...], refs[units][...])
    for u in range(1, units):
        total += dot(refs[u][...], refs[units + u][...])
    out_ref[...] = total.astype(BF16).reshape(out_ref.shape)


def weight_grad(lefts, rights, by_left, out_struct, out_spec, steps, into, name):
    units = len(lefts)

    def fixed(a):
        return pl.BlockSpec(a.shape, lambda n: (0, 0))

    def left_spec(a):
        return pl.BlockSpec((a.shape[0] // steps, a.shape[1]), lambda n: (n, 0))

    def right_spec(a):
        return pl.BlockSpec((a.shape[0], a.shape[1] // steps), lambda n: (0, n))

    operands = list(lefts) + list(rights)
    if by_left:
        in_specs = [left_spec(a) for a in lefts] + [fixed(a) for a in rights]
    else:
        in_specs = [fixed(a) for a in lefts] + [right_spec(a) for a in rights]
    aliases = {}
    if into is not None:
        aliases = {len(operands): 0}
        operands.append(into)
        in_specs.append(pl.BlockSpec(memory_space=pl.ANY))
    return pl.pallas_call(
        functools.partial(weights_kernel, units),
        grid=(steps,),
        in_specs=in_specs,
        out_specs=out_spec,
        out_shape=out_struct,
        input_output_aliases=aliases,
        compiler_params=pltpu.CompilerParams(vmem_limit_bytes=62 << 20),
        cost_estimate=pl.CostEstimate(
            flops=2 * units * lefts[0].shape[0] * lefts[0].shape[1] * rights[0].shape[1] // COVER,
            bytes_accessed=2 * lefts[0].shape[0] * rights[0].shape[1],
            transcendentals=0,
        ),
        name=name,
    )(*operands)


def reduce_kernel(orders, count, *refs):
    streams = len(orders)
    rounds = len(orders[0])
    ins, vec_ref = refs[:streams], refs[streams]
    outs, vec_out = refs[streams + 1 : 2 * streams + 1], refs[2 * streams + 1]
    rest = refs[2 * streams + 2 :]
    works, arrivals = rest[:streams], rest[streams : 2 * streams]
    vec_work, vec_arrival, send_sem, recv_sem, vec_send, vec_recv = rest[2 * streams :]
    shard, seq = lax.axis_index("shard"), lax.axis_index("seq")

    def partner(mask):
        if mask >= count:
            step = mask // count
            return (shard + step * (1 - 2 * (shard // step % 2)), seq)
        return (shard, seq + mask * (1 - 2 * (seq // mask % 2)))

    barrier = pltpu.get_barrier_semaphore()
    for mask in orders[0]:
        pl.semaphore_signal(
            barrier, inc=1, device_id=partner(mask), device_id_type=pl.DeviceIdType.MESH
        )
    pl.semaphore_wait(barrier, rounds)

    height = ins[0].shape[0]
    halves = [height >> (r + 1) for r in range(rounds)]
    starts = [sum(halves[:r]) for r in range(rounds)]

    def copy_of(s, r):
        source = ins[s] if r == 0 else works[s]
        return pltpu.make_async_remote_copy(
            src_ref=source.at[pl.ds(halves[r], halves[r])],
            dst_ref=arrivals[s].at[pl.ds(starts[r], halves[r])],
            send_sem=send_sem.at[s, r],
            recv_sem=recv_sem.at[s, r],
            device_id=partner(orders[s][r]),
            device_id_type=pl.DeviceIdType.MESH,
        )

    def vec_copy(r):
        return pltpu.make_async_remote_copy(
            src_ref=vec_ref if r == 0 else vec_work.at[r - 1],
            dst_ref=vec_arrival.at[r],
            send_sem=vec_send.at[r],
            recv_sem=vec_recv.at[r],
            device_id=partner(orders[0][r]),
            device_id_type=pl.DeviceIdType.MESH,
        )

    for s in range(streams):
        copy_of(s, 0).start()
    vec_copy(0).start()
    for r in range(rounds):
        for s in range(streams):
            copy_of(s, r).wait_recv()
            source = ins[s] if r == 0 else works[s]
            size = halves[r]

            def added(low, high):
                mine = source[low:high].astype(F32)
                return mine + arrivals[s][starts[r] + low : starts[r] + high].astype(F32)

            if r == rounds - 1:
                outs[s][...] = added(0, size)
            else:
                works[s][size // 2 : size] = added(size // 2, size).astype(BF16)
                copy_of(s, r + 1).start()
                works[s][0 : size // 2] = added(0, size // 2).astype(BF16)
        vec_copy(r).wait_recv()
        before = vec_ref[...] if r == 0 else vec_work[r - 1]
        if r == rounds - 1:
            vec_out[...] = before + vec_arrival[r]
        else:
            vec_work[r] = before + vec_arrival[r]
            vec_copy(r + 1).start()
    for r in range(rounds):
        for s in range(streams):
            copy_of(s, r).wait_send()
        vec_copy(r).wait_send()


def reduce_rows(parts, vector, orders, count):
    streams = len(parts)
    rounds = len(orders[0])
    height, columns = parts[0].shape
    rows = height >> rounds
    vmem = pl.BlockSpec(memory_space=pltpu.VMEM)
    return pl.pallas_call(
        functools.partial(reduce_kernel, orders, count),
        in_specs=[vmem] * (streams + 1),
        out_specs=[vmem] * (streams + 1),
        out_shape=[jax.ShapeDtypeStruct((rows, columns), F32)] * streams
        + [jax.ShapeDtypeStruct(vector.shape, F32)],
        scratch_shapes=[pltpu.VMEM((height // 2, columns), BF16) for _ in parts]
        + [pltpu.VMEM((height - rows, columns), BF16) for _ in parts]
        + [
            pltpu.VMEM((rounds - 1,) + vector.shape, F32),
            pltpu.VMEM((rounds,) + vector.shape, F32),
            pltpu.SemaphoreType.DMA((streams, rounds)),
            pltpu.SemaphoreType.DMA((streams, rounds)),
            pltpu.SemaphoreType.DMA((rounds,)),
            pltpu.SemaphoreType.DMA((rounds,)),
        ],
        compiler_params=pltpu.CompilerParams(
            collective_id=0, has_side_effects=True, vmem_limit_bytes=62 << 20
        ),
        name="reduce_rows",
    )(*parts, vector)


def on_device(
    tokens, cotangent, lengths, variates, positions, attn_gain, w_query, w_key, w_value, w_out,
    bias_table, ffn_gain, w_gate, w_up, w_down,
):
    micro, seqs, width, model = tokens.shape
    heads = bias_table.shape[0]
    head_dim = model // heads
    count = lax.axis_size("seq")
    here = heads // count
    ffn = w_gate.shape[1]
    devices = lax.axis_size("shard") * count
    seq_index = lax.axis_index("seq")
    units = [(m, s) for m in range(micro) for s in range(seqs)]
    swap = here == 2 and len(units) == 2 and lax.axis_size("shard") % 2 == 0
    core = (lax.axis_index("shard") % 2 if swap else jnp.int32(0)).astype(jnp.int32).reshape(1)
    heads_here = 1 if swap else here
    first_head = seq_index * here + core[0]
    bias_here = lax.dynamic_slice_in_dim(bias_table, first_head, heads_here, 0)
    attn_row, ffn_row = attn_gain[None, :], ffn_gain[None, :]

    def gather(weight):
        return lax.all_gather(weight, "shard", axis=0, tiled=True)

    def exchange(values):
        return lax.all_to_all(values, "seq", split_axis=0, concat_axis=0, tiled=True)

    def after(value, *before):
        return lax.optimization_barrier((value,) + before)[0]

    attn_joined = gather(jnp.concatenate([w_query, w_key, w_value], axis=1))
    ffn_weights = [gather(w_out), gather(w_gate), gather(w_up), gather(w_down)]

    def permute(value, mask):
        return lax.ppermute(value, ("shard", "seq"), [(i, i ^ mask) for i in range(devices)])

    def cross(value):
        return permute(value, count)

    lengths_of = [lengths, cross(lengths)] if swap else [lengths] * here
    packed_list, flats, tables = [], [], []

    def run_project(u, token):
        m, s = units[u]
        cosine, sine = rotary_tables(positions[m, s], head_dim // 2)
        ids = after(variates[m, s].astype(F32)[None, :], *token)
        flat, *packed = project(
            core, tokens, (m, s), attn_row, attn_joined, cosine, sine, ids, count, here, head_dim, swap
        )
        flats.append(flat)
        tables.append((cosine, sine))
        packed_list.append(packed)

    sent = {}
    mixed_now = [None] * len(units)
    sums = {}
    mixed_tok = {}
    crossed, mixed_part, mixed_cross, heads_cross, back_cross = {}, {}, {}, {}, {}
    middle = [None] * len(units)
    grad_heads = {}
    state = {"output": None, "grads": None}
    packed_grads = {}
    returned = {}
    bias_terms = {}
    finals = [None] * len(units)

    def length_of(u, h, token):
        m, s = units[u]
        return after(lengths_of[h][m, s].reshape(1), *token)

    def inputs_of(u, h):
        if not swap:
            return sent[u, h], sent[u, 0]
        return (sent[u, 0], sent[u, 1]) if h == 0 else (crossed[u], crossed[u])

    def run_forward(u, h, token):
        made, sums[u, h] = attend_forward(
            *inputs_of(u, h), length_of(u, h, token), bias_here, None if swap else mixed_now[u],
            0 if swap else h, heads_here, head_dim,
        )
        if swap:
            mixed_part[u, h] = made
            if h == 1:
                mixed_cross[u] = cross(made)
        else:
            mixed_now[u] = made
        return sums[u, h]

    def run_middle(u, token):
        m, s = units[u]
        info = jnp.stack([lengths[m, s], seq_index * width, core[0]]).astype(jnp.int32)
        state["output"], mixed_tok[u], *middle[u] = middle_part(
            after(info, *token), mixed_tok[u], tokens, cotangent, (m, s), ffn_weights, ffn_row, head_dim,
            state["output"],
        )
        return middle[u][8]

    def run_backward(u, h, token):
        if swap:
            grad = grad_heads[u] if h == 0 else heads_cross[u]
            mixed = mixed_part[u, h]
        else:
            grad, mixed = grad_heads[u], mixed_now[u]
        packed_grads[u, h], both = attend_backward(
            *inputs_of(u, h), grad, mixed, sums[u, h], length_of(u, h, token), bias_here,
            0 if swap else h, head_dim,
        )
        if swap and h == 1:
            back_cross[u] = cross(packed_grads[u, h])
        bias_terms[u, h] = both
        return both

    def run_final(u, token):
        m, s = units[u]
        cosine, sine = tables[u]
        state["grads"], *finals[u] = final_part(
            core, tokens, (m, s), middle[u][5], after(attn_row, *token), attn_joined, cosine, sine,
            [returned[u, h] for h in range(here)], head_dim, state["grads"],
        )
        return finals[u][3]

    rows = model // devices
    fold = ffn // model
    tall = ffn // devices
    seq_masks = [1 << i for i in range(count.bit_length() - 1)]
    shard_masks = [count << i for i in range((devices // count).bit_length() - 1)]
    spread = shard_masks[1:]
    orders = (
        shard_masks[:1] + spread + seq_masks,
        shard_masks[:1] + seq_masks[:1] + spread + seq_masks[1:],
        shard_masks[:1] + seq_masks[1:2] + seq_masks[:1] + spread + seq_masks[2:],
    )
    direct = rows % 16 == 0 and devices == 1 << len(orders[0])

    def places_of(order):
        marks = []
        for p in range(devices):
            bits = [p >> (len(order) - 1 - i) & 1 for i in range(len(order))]
            marks.append(sum(mask for bit, mask in zip(bits, order) if bit))
        me = lax.axis_index("shard") * count + seq_index
        return me.astype(jnp.int32) ^ jnp.array(marks, jnp.int32)

    def column(index):
        return [item[index] for item in middle]

    def run_weights(token):
        if not direct:
            return [
                sum(dot(left, right) for left, right in zip(lefts, rights)).astype(BF16)
                for lefts, rights in (
                    (column(0), column(2)), (column(0), column(3)), (column(1), column(4)),
                    ([mixed_tok[u] for u in range(len(units))], column(6)),
                )
            ]
        part = ffn // fold
        spare = -(-(3 * part + model // fold) // 384) * 384
        struct = jax.ShapeDtypeStruct((devices, fold, rows, spare), BF16)
        down = pl.BlockSpec((512 // tall, fold, rows, model), lambda n: (n, 0, 0, 0))
        gate = pl.BlockSpec((devices, 1, rows, part), lambda n: (0, n, 0, 1))
        up = pl.BlockSpec((devices, 1, rows, part), lambda n: (0, n, 0, 2))
        narrow = model // fold
        out = pl.BlockSpec((devices, 1, rows, narrow), lambda n: (0, n, 0, 3 * part // narrow))
        firsts = [after(middle[0][4], *token)] + [item[4] for item in middle[1:]]
        terms = weight_grad(column(1), firsts, True, struct, down, ffn // 512, None, "down_grad")
        rights = [after(middle[0][2], *holder["flying"])] + [item[2] for item in middle[1:]]
        terms = weight_grad(column(0), rights, False, struct, gate, fold, terms, "gate_grad")
        terms = weight_grad(column(0), column(3), False, struct, up, fold, terms, "up_grad")
        mixed_all = [mixed_tok[u] for u in range(len(units))]
        terms = weight_grad(mixed_all, column(6), False, struct, out, fold, terms, "out_grad")
        terms = terms.reshape(ffn, spare)
        holder["owned"] = lax.psum_scatter(terms, ("shard", "seq"), scatter_dimension=0, tiled=True)
        return terms

    holder = {}

    def weights_work(token):
        holder["terms"] = run_weights(token)
        return holder["terms"]

    def send_packed(u, h):
        def keep(moved):
            sent[u, h] = moved
            if swap and h == 1:
                crossed[u] = cross(moved)

        return lambda: packed_list[u][h], keep

    def send_mixed(u):
        def keep(moved):
            mixed_tok[u] = moved.reshape(model, width)

        if not swap:
            return lambda: mixed_now[u], keep
        return lambda: jnp.concatenate([mixed_part[u, 0], mixed_cross[u]], axis=1), keep

    def send_heads(u):
        def keep(moved):
            grad_heads[u] = moved
            if swap:
                heads_cross[u] = cross(moved[:, head_dim:])
                pending.append(heads_cross[u])

        return lambda: middle[u][7].reshape(count, here * head_dim, width), keep

    def send_back(u, h):
        def keep(moved):
            returned[u, h] = moved

        return lambda: back_cross[u] if swap and h == 1 else packed_grads[u, h], keep

    def work_project(u):
        def work(token):
            run_project(u, token)
            return flats[u]

        return work

    def work(function, *args):
        return lambda token: function(*args, token)

    total = len(units)
    order = [(u, h) for u in range(total) for h in range(here)]
    if swap:
        steps = [
            (work_project(0), None),
            (work_project(1), send_packed(0, 1)),
            (work(run_forward, 0, 1), send_packed(0, 0)),
            (work(run_forward, 0, 0), send_packed(1, 1)),
            (work(run_forward, 1, 1), send_packed(1, 0)),
            (work(run_forward, 1, 0), send_mixed(0)),
            (work(run_middle, 0), send_mixed(1)),
            (work(run_middle, 1), send_heads(0)),
            (weights_work, send_heads(1)),
            (work(run_backward, 0, 0), None),
            (work(run_backward, 0, 1), send_back(0, 0)),
            (work(run_backward, 1, 0), send_back(0, 1)),
            (work(run_backward, 1, 1), send_back(1, 0)),
            (work(run_final, 0), send_back(1, 1)),
            (work(run_final, 1), None),
        ]
    else:
        steps = [(work_project(u), None) for u in range(total)]
        steps += [(None, send_packed(*at)) for at in order]
        for u in range(total):
            steps += [(work(run_forward, u, h), None) for h in range(here)]
            steps += [(None, send_mixed(u))]
        for u in range(total):
            steps += [(work(run_middle, u), None), (None, send_heads(u))]
        steps += [(weights_work, None)]
        for at in order:
            steps += [(work(run_backward, *at), None), (None, send_back(*at))]
        steps += [(work(run_final, u), None) for u in range(total)]

    token = ()
    pending = []
    for task, send in steps:
        done = ()
        moved = None
        waited = tuple(pending)
        pending.clear()
        if send is not None:
            moved = exchange(after(send[0](), *token))
            done = (moved,)
        holder["flying"] = done
        if task is not None:
            done = done + (task(token),)
        if send is not None:
            send[1](after(moved, *done[1:]))
        token = done + waited
    acc_bias = jnp.concatenate(
        [sum(bias_terms[u, h] for u in range(total))[0:1, 0:2] for h in range(here)], axis=0
    )
    if swap:
        acc_bias = acc_bias[0:1] + acc_bias[1:2]
    bias_full = lax.dynamic_update_slice(
        jnp.zeros((heads, 2), F32), acc_bias, (first_head, jnp.int32(0))
    )
    gain_attn = sum(item[3][0] for item in finals)
    gain_ffn = sum(item[8][0] for item in middle)
    if direct:
        owned, part = holder["owned"], ffn // fold

        def joined(start, size):
            piece = owned[:, start : start + size].reshape(fold, rows, size)
            return jnp.swapaxes(piece, 0, 1).reshape(rows, fold * size).astype(F32)

        down_own = owned[:, :part].astype(F32)
        gate_own, up_own = joined(part, part), joined(2 * part, part)
        out_own = joined(3 * part, model // fold)
        table = jnp.concatenate([places_of(order) for order in orders])
        attn_terms = picked_grads(
            table, [(i * devices, devices) for i in range(3)], flats,
            [item[i] for i in range(3) for item in finals], rows, True, 1, 256, "attn_grads",
        )
        flat = jnp.concatenate([gain_attn, gain_ffn, bias_full.reshape(-1)])
        tiles = -(-flat.shape[0] // 1024) * 8
        flat = jnp.pad(flat, (0, tiles * 128 - flat.shape[0])).reshape(tiles, 128)
        query_own, key_own, value_own, flat = reduce_rows(list(attn_terms), flat, orders, count)
        flat = flat.reshape(-1)
        gain_attn, gain_ffn = flat[:model], flat[model : 2 * model]
        bias_full = flat[2 * model : 2 * model + 2 * heads].reshape(heads, 2)
    else:

        def scatter(value):
            owned = lax.psum_scatter(value, ("shard", "seq"), scatter_dimension=0, tiled=True)
            return owned.astype(F32)

        gate_own, up_own, down_own, out_own = [scatter(value) for value in holder["terms"]]
        query_own, key_own, value_own = [
            scatter(
                sum(contract(flat, item[i], 1, 1) for flat, item in zip(flats, finals)).astype(BF16)
            )
            for i in range(3)
        ]
        gain_attn, gain_ffn, bias_full = lax.psum(
            (gain_attn, gain_ffn, bias_full), ("shard", "seq")
        )
    return (
        state["output"], state["grads"], gain_attn, query_own, key_own, value_own, out_own,
        bias_full, gain_ffn, gate_own, up_own, down_own,
    )


def solution(mesh):
    token_spec = P(None, "shard", "seq", None)
    row_spec = P("shard", None)
    in_specs = (
        token_spec, token_spec, P(None, "shard"), P(None, "shard", "seq"), P(None, "shard", "seq"),
        P(), row_spec, row_spec, row_spec, row_spec, P(), P(), row_spec, row_spec, row_spec,
    )
    owned = P(("shard", "seq"), None)
    out_specs = (
        token_spec, token_spec, P(), owned, owned, owned, owned, P(), P(), owned, owned, owned,
    )
    return jax.shard_map(
        on_device, mesh=mesh, in_specs=in_specs, out_specs=out_specs, check_vma=False
    )
```

```python
import functools
import math

import jax
import jax.numpy as jnp
from jax import lax
from jax.experimental import pallas as pl
from jax.experimental.pallas import tpu as pltpu
from jax.sharding import PartitionSpec as P

EPSILON = 1e-06
ROTARY_BASE = 10000.0
LOG2E = 1.4426950408889634
LN2 = 0.6931471805599453
CLASSES = 8
AUX = 16
COVER = 16
EXTRA = 32
MASKED = -1.5e9
FAR = 1e30
F32 = jnp.float32
BF16 = jnp.bfloat16


def dot(a, b):
    return jnp.dot(a, b, preferred_element_type=F32)


def contract(a, b, da, db):
    return lax.dot_general(a, b, (((da,), (db,)), ((), ())), preferred_element_type=F32)


def pieces(x):
    high = x.astype(BF16).astype(F32)
    rest = x - high
    mid = rest.astype(BF16).astype(F32)
    low = (rest - mid).astype(BF16).astype(F32)
    return high, mid, low


def one_hot(row):
    classes = lax.broadcasted_iota(jnp.int32, (CLASSES, row.shape[1]), 0).astype(F32)
    return jnp.where(classes == row, 1.0, 0.0)


def rows_of(values, width):
    index = lax.broadcasted_iota(jnp.int32, (8, width), 0)
    out = jnp.zeros((8, width), F32)
    for at, value in enumerate(values):
        out = jnp.where(index == at, value, out)
    return out


def key_extra(row, start, length, other, same):
    width = row.shape[1]
    hot = one_hot(row)
    step = pieces(jnp.full((1, width), same - other, F32))
    base = pieces(jnp.full((1, width), other, F32))
    index = start + lax.broadcasted_iota(jnp.int32, (1, width), 1)
    mask = jnp.where(index < length, 0.0, MASKED)
    tail = rows_of(base + (mask, 1.0, 1.0, 1.0), width)
    return jnp.concatenate([hot * step[0], hot * step[1], hot * step[2], tail], axis=0).astype(BF16)


def query_extra(row, shift):
    hot = one_hot(row)
    tail = rows_of((1.0, 1.0, 1.0, 1.0) + shift, row.shape[1])
    return jnp.concatenate([hot, hot, hot, tail], axis=0).astype(BF16)


def forward_kernel(
    shape, len_ref, bias_ref, x_ref, ids_ref, *rest
):
    local, head_dim, block, aliased = shape
    if aliased:
        rest = rest[1:]
    mixed_ref, lse_ref, keys, vals, query, score, peak, total = rest
    count, _, width = x_ref.shape
    sub = block // width
    step = pl.program_id(0)
    length = len_ref[0]
    other = bias_ref[local, 0] * LOG2E
    same = bias_ref[local, 1] * LOG2E

    @pl.when(step == 0)
    def _():
        for b in range(count):
            at = pl.ds(b * width, width)
            row = ids_ref[b, 0:1, :].astype(F32)
            extra = key_extra(row, b * width, length, other, same)
            full = jnp.concatenate([x_ref[b, head_dim : 2 * head_dim, :], extra], axis=0)
            keys[at, :] = full.T
            vals[0:head_dim, at] = x_ref[b, 2 * head_dim : 3 * head_dim, :]
        vals[head_dim:, :] = jnp.ones((16, vals.shape[1]), BF16)

    used = pl.cdiv(length, block)
    inside = step * block < length

    @pl.when(jnp.logical_not(inside))
    def _():
        mixed_ref[...] = jnp.zeros_like(mixed_ref)
        lse_ref[...] = jnp.full(lse_ref.shape, FAR, F32)

    @pl.when(inside)
    def _():
        for b in range(sub):
            at = slice(b * width, (b + 1) * width)
            row = ids_ref[step * sub + b, 0:1, :].astype(F32)
            query[0:head_dim, at] = x_ref[step * sub + b, 0:head_dim, :]
            query[head_dim:, at] = query_extra(row, (0.0, 0.0, 0.0))
        peak[...] = jnp.full(peak.shape, -FAR, F32)
        total[...] = jnp.zeros_like(total)

        def span(j):
            return pl.ds(pl.multiple_of(j * block, block), block)

        def scores_of(j):
            return dot(keys[span(j), :], query[...])

        def one(j, now, ahead):
            if ahead:
                score[1 - now] = scores_of(j + 1)
            current = score[now]
            before = peak[...]
            top = jnp.maximum(before, jnp.max(current, axis=0, keepdims=True))
            weight = jnp.exp2(current - top).astype(BF16)
            peak[...] = top
            total[...] = total[...] * jnp.exp2(before - top) + dot(vals[:, span(j)], weight)

        score[0] = scores_of(0)
        pairs = (used - 1) // 2

        def pair(j, carry):
            one(2 * j, 0, True)
            one(2 * j + 1, 1, True)
            return carry

        lax.fori_loop(0, pairs, pair, 0)
        last = 2 * pairs

        @pl.when(used - last == 1)
        def _():
            one(last, 0, False)

        @pl.when(used - last == 2)
        def _():
            one(last, 0, True)
            one(last + 1, 1, False)

        mass = total[head_dim : head_dim + 1, :]
        mixed = (total[0:head_dim, :] / mass).astype(BF16)
        for b in range(sub):
            mixed_ref[b] = mixed[:, b * width : (b + 1) * width]
        lse_ref[0] = peak[...] + jnp.log2(mass)


def attend_forward(x, ids, length, bias, mixed, local, heads_here, head_dim):
    count, rows, width = x.shape
    block = max(width, 512)
    seq_len = count * width
    blocks = seq_len // block
    depth = head_dim + EXTRA
    whole = pl.BlockSpec((count, rows, width), lambda i, *_: (0, 0, 0))
    operands = [length, bias, x, ids]
    in_specs = [whole, pl.BlockSpec((count, AUX, width), lambda i, *_: (0, 3 * head_dim // AUX, 0))]
    aliases = {}
    if mixed is not None:
        operands.append(mixed)
        in_specs.append(pl.BlockSpec(memory_space=pl.ANY))
        aliases = {4: 0}
    return pl.pallas_call(
        functools.partial(forward_kernel, (local, head_dim, block, mixed is not None)),
        grid_spec=pltpu.PrefetchScalarGridSpec(
            num_scalar_prefetch=2,
            grid=(blocks,),
            in_specs=in_specs,
            out_specs=[
                pl.BlockSpec((block // width, head_dim, width), lambda i, *_: (i, local, 0)),
                pl.BlockSpec((1, 1, block), lambda i, *_: (i, 0, 0)),
            ],
            scratch_shapes=[
                pltpu.VMEM((seq_len, depth), BF16),
                pltpu.VMEM((head_dim + 16, seq_len), BF16),
                pltpu.VMEM((depth, block), BF16),
                pltpu.VMEM((2, block, block), F32),
                pltpu.VMEM((1, block), F32),
                pltpu.VMEM((head_dim + 16, block), F32),
            ],
        ),
        out_shape=[
            jax.ShapeDtypeStruct((count, heads_here * head_dim, width), BF16),
            jax.ShapeDtypeStruct((blocks, 1, block), F32),
        ],
        input_output_aliases=aliases,
        compiler_params=pltpu.CompilerParams(vmem_limit_bytes=62 << 20),
        cost_estimate=pl.CostEstimate(
            flops=8 * seq_len * seq_len * 256 // COVER,
            bytes_accessed=x.size * 4,
            transcendentals=0,
        ),
        name="attend_forward",
    )(*operands)


def backward_kernel(
    shape, len_ref, bias_ref, x_ref, ids_ref, grad_ref, mixed_ref, lse_ref, out_ref, bias_out_ref,
    keys, keys_flat, vals, query, grads, query_rows, grad_rows, acc_keys, acc_vals, acc_query,
):
    local, head_dim, block = shape
    count, _, width = x_ref.shape
    sub = block // width
    step = pl.program_id(0)
    length = len_ref[0]
    other = bias_ref[local, 0] * LOG2E
    same = bias_ref[local, 1] * LOG2E

    @pl.when(step == 0)
    def _():
        ones = jnp.ones((16, width), BF16)
        for b in range(count):
            at = pl.ds(b * width, width)
            row = ids_ref[b, 0:1, :].astype(F32)
            extra = key_extra(row, b * width, length, other, same)
            here = x_ref[b, head_dim : 2 * head_dim, :]
            keys[at, :] = jnp.concatenate([here, extra], axis=0).T
            keys_flat[:, at] = here
            vals[at, :] = jnp.concatenate([x_ref[b, 2 * head_dim : 3 * head_dim, :], ones], axis=0).T
        acc_keys[...] = jnp.zeros_like(acc_keys)
        acc_vals[...] = jnp.zeros_like(acc_vals)

    used = pl.cdiv(length, block)
    inside = step * block < length

    @pl.when(jnp.logical_not(inside))
    def _():
        for b in range(sub):
            out_ref[step * sub + b, 0:head_dim, :] = jnp.zeros((head_dim, width), BF16)

    @pl.when(inside)
    def _():
        for b in range(sub):
            at = slice(b * width, (b + 1) * width)
            here = step * sub + b
            row = ids_ref[here, 0:1, :].astype(F32)
            shift = pieces(-lse_ref[step][:, at])
            grad = grad_ref[here]
            delta = jnp.sum(grad.astype(F32) * mixed_ref[here].astype(F32), axis=0, keepdims=True)
            query[0:head_dim, at] = x_ref[here, 0:head_dim, :]
            query[head_dim:, at] = query_extra(row, shift)
            grads[0:head_dim, at] = grad
            tail = rows_of(pieces(-delta), width)
            grads[head_dim:, at] = jnp.concatenate([tail, jnp.zeros_like(tail)], axis=0).astype(BF16)
        query_rows[...] = query[...].T
        grad_rows[...] = grads[...].T
        acc_query[...] = jnp.zeros_like(acc_query)

        def one(j):
            at = pl.ds(pl.multiple_of(j * block, block), block)
            probs = jnp.exp2(dot(keys[at, :], query[...]))
            grad_probs = dot(vals[at, :], grads[...])
            grad_scores = (probs * grad_probs).astype(BF16)
            acc_vals[at, :] += dot(probs.astype(BF16), grad_rows[...])
            acc_keys[at, :] += dot(grad_scores, query_rows[...])
            acc_query[...] += dot(keys_flat[:, at], grad_scores)

        def pair(j, carry):
            one(2 * j)
            one(2 * j + 1)
            return carry

        lax.fori_loop(0, used // 2, pair, 0)

        @pl.when(used % 2 == 1)
        def _():
            one(used - 1)

        grad_query = (acc_query[...] * (1.0 / math.sqrt(head_dim))).astype(BF16)
        for b in range(sub):
            out_ref[step * sub + b, 0:head_dim, :] = grad_query[:, b * width : (b + 1) * width]

    @pl.when(step == pl.num_programs(0) - 1)
    def _():
        same_total = jnp.zeros((CLASSES, width), F32)
        all_total = jnp.zeros((CLASSES, width), F32)
        for b in range(count):
            at = pl.ds(b * width, width)
            row = ids_ref[b, 0:1, :].astype(F32)
            flat = acc_keys[at, :].T
            out_ref[b, head_dim : 2 * head_dim, :] = (flat[0:head_dim] * LN2).astype(BF16)
            out_ref[b, 2 * head_dim : 3 * head_dim, :] = acc_vals[at, :].T[0:head_dim].astype(BF16)
            by_class = flat[head_dim : head_dim + CLASSES]
            all_total += by_class
            same_total += by_class * one_hot(row)
        same_sum = jnp.sum(same_total, keepdims=True)
        other_sum = jnp.sum(all_total, keepdims=True) - same_sum
        lane = lax.broadcasted_iota(jnp.int32, (8, 128), 1)
        bias_out_ref[...] = jnp.where(lane == 0, other_sum, jnp.where(lane == 1, same_sum, 0.0))


def attend_backward(x, ids, grad, mixed, lse, length, bias, local, head_dim):
    count, rows, width = x.shape
    blocks, _, block = lse.shape
    seq_len = count * width
    depth = head_dim + EXTRA

    def whole(a):
        return pl.BlockSpec(a.shape, lambda i, *_: (0,) * a.ndim)

    head_spec = pl.BlockSpec((count, head_dim, width), lambda i, *_: (0, local, 0))
    return pl.pallas_call(
        functools.partial(backward_kernel, (local, head_dim, block)),
        grid_spec=pltpu.PrefetchScalarGridSpec(
            num_scalar_prefetch=2,
            grid=(blocks,),
            in_specs=[
                whole(x),
                pl.BlockSpec((count, AUX, width), lambda i, *_: (0, 3 * head_dim // AUX, 0)),
                head_spec, head_spec, whole(lse),
            ],
            out_specs=[
                pl.BlockSpec((count, 3 * head_dim, width), lambda i, *_: (0, 0, 0)),
                pl.BlockSpec((8, 128), lambda i, *_: (0, 0)),
            ],
            scratch_shapes=[
                pltpu.VMEM((seq_len, depth), BF16),
                pltpu.VMEM((head_dim, seq_len), BF16),
                pltpu.VMEM((seq_len, head_dim + 16), BF16),
                pltpu.VMEM((depth, block), BF16),
                pltpu.VMEM((head_dim + 16, block), BF16),
                pltpu.VMEM((block, depth), BF16),
                pltpu.VMEM((block, head_dim + 16), BF16),
                pltpu.VMEM((seq_len, depth), F32),
                pltpu.VMEM((seq_len, head_dim + 16), F32),
                pltpu.VMEM((head_dim, block), F32),
            ],
        ),
        out_shape=[
            jax.ShapeDtypeStruct((count, 3 * head_dim, width), BF16),
            jax.ShapeDtypeStruct((8, 128), F32),
        ],
        compiler_params=pltpu.CompilerParams(vmem_limit_bytes=62 << 20),
        cost_estimate=pl.CostEstimate(
            flops=20 * seq_len * seq_len * 256 // COVER,
            bytes_accessed=x.size * 6,
            transcendentals=0,
        ),
        name="attend_backward",
    )(length, bias, x, ids, grad, mixed, lse)


def rotary_tables(places, half_dim):
    frequency = jnp.exp(-math.log(ROTARY_BASE) * jnp.arange(half_dim, dtype=F32) / half_dim)
    angles = places.astype(F32)[None, :] * frequency[:, None]
    return jnp.cos(angles), jnp.sin(angles)


def sigmoid_of(x):
    return 1.0 / (1.0 + jnp.exp2(x * -LOG2E))


def project_kernel(
    shape, core_ref, tokens_ref, gain_ref, query_ref, key_ref, value_ref, cos_ref, sin_ref, ids_ref, flat_ref, *rest
):
    here, head_dim, extras, swap = shape
    outs, flat_weights = rest[:-1], rest[-1]
    pair = pl.program_id(0)

    @pl.when(pair == 0)
    def _():
        inputs = tokens_ref[0, 0].astype(F32)
        inverse = lax.rsqrt(jnp.mean(inputs * inputs, axis=-1, keepdims=True) + EPSILON)
        flat_ref[...] = (inputs * inverse * gain_ref[...]).astype(BF16).T

    flat_weights[0:128, :] = query_ref[...].T
    flat_weights[128:256, :] = key_ref[...].T
    flat_weights[256:384, :] = value_ref[...].T
    made = dot(flat_weights[...], flat_ref[...])
    cosine, sine = cos_ref[...], sin_ref[...]
    half = head_dim // 2

    def turned(start, scale):
        first = made[start : start + half]
        second = made[start + half : start + head_dim]
        both = [first * cosine - second * sine, second * cosine + first * sine]
        return (jnp.concatenate(both, axis=0) * scale).astype(BF16)

    def put(at, slot, place):
        spot = at * head_dim
        target = outs[slot]
        target[place, 0:head_dim, :] = turned(spot, LOG2E / math.sqrt(head_dim))
        target[place, head_dim : 2 * head_dim, :] = turned(128 + spot, 1.0)
        target[place, 2 * head_dim : 3 * head_dim, :] = made[256 + spot : 256 + spot + head_dim].astype(BF16)
        if extras[slot]:
            target[place, 3 * head_dim :, :] = jnp.broadcast_to(ids_ref[...], (AUX, ids_ref.shape[1])).astype(BF16)

    if swap:
        for core in range(2):

            @pl.when(core_ref[0] == core)
            def _():
                put(core, 0, 0)
                put(1 - core, 1, 0)

    else:
        for at in range(128 // head_dim):
            put(at, at % here, 0 if here > 1 else at)


def project(core, tokens, unit, gain, weights, cosine, sine, ids, count, here, head_dim, swap):
    width, model = tokens.shape[2:]
    heads = count * here
    pairs = heads * head_dim // 128
    per = 128 // head_dim // here
    extras = [h == (1 if swap else 0) for h in range(here)]

    def fixed(a):
        return pl.BlockSpec(a.shape, lambda p: (0,) * a.ndim)

    weight_specs = [pl.BlockSpec((model, 128), lambda p, i=i: (0, i * pairs + p)) for i in range(3)]
    return pl.pallas_call(
        functools.partial(project_kernel, (here, head_dim, extras, swap)),
        grid=(pairs,),
        in_specs=[
            pl.BlockSpec(memory_space=pltpu.SMEM),
            pl.BlockSpec((1, 1, width, model), lambda p: unit + (0, 0)),
            fixed(gain), *weight_specs, fixed(cosine), fixed(sine), fixed(ids),
        ],
        out_specs=[pl.BlockSpec((model, width), lambda p: (0, 0))]
        + [pl.BlockSpec((per, 3 * head_dim + AUX * e, width), lambda p: (p, 0, 0)) for e in extras],
        out_shape=[jax.ShapeDtypeStruct((model, width), BF16)]
        + [jax.ShapeDtypeStruct((count, 3 * head_dim + AUX * e, width), BF16) for e in extras],
        scratch_shapes=[pltpu.VMEM((384, model), BF16)],
        compiler_params=pltpu.CompilerParams(vmem_limit_bytes=62 << 20),
        cost_estimate=pl.CostEstimate(
            flops=6 * width * model * model // COVER, bytes_accessed=12 * model * model, transcendentals=0
        ),
        name="project",
    )(core, tokens, gain, weights, weights, weights, cosine, sine, ids)


def middle_kernel(
    shape, info_ref, mixed_ref, tokens_ref, cot_ref, out_w_ref, gain_ref, gate_w_ref, up_w_ref, down_w_ref, *rest
):
    head_dim, aliased = shape
    if aliased:
        rest = rest[1:]
    (
        output_ref, ordered_ref, flat_ref, hidden_ref, grad_gate_ref, grad_up_ref, grad_ffn_ref, grad_res_ref,
        grad_attn_ref, grad_mixed_ref, gain_out_ref, normed, residual, ffn_out, grad_normed, slots,
    ) = rest
    core = info_ref[2]
    step = pl.program_id(0)
    width = normed.shape[0]

    def valid():
        index = info_ref[1] + lax.broadcasted_iota(jnp.int32, (width, 1), 0)
        return jnp.where(index < info_ref[0], 1.0, 0.0)

    def inverse_of(x):
        return lax.rsqrt(jnp.mean(x * x, axis=-1, keepdims=True) + EPSILON)

    def head_rows(pair, slot):
        head = 2 * pair + (core if slot == 0 else 1 - core)
        return pl.ds(pl.multiple_of(head * head_dim, head_dim), head_dim)

    def slot_rows(pair, slot):
        return slice((2 * pair + slot) * head_dim, (2 * pair + slot + 1) * head_dim)

    spots = [(pair, slot) for pair in range(mixed_ref.shape[0] // head_dim // 2) for slot in range(2)]

    @pl.when(step == 0)
    def _():
        for spot in spots:
            ordered_ref[head_rows(*spot), :] = mixed_ref[slot_rows(*spot), :]
        inputs = tokens_ref[0, 0].astype(F32) + dot(ordered_ref[...].T, out_w_ref[...])
        residual[...] = inputs
        made = (inputs * inverse_of(inputs) * gain_ref[...]).astype(BF16)
        normed[...] = made
        flat_ref[...] = made.T
        grad_ffn_ref[...] = (cot_ref[0, 0].astype(F32) * valid()).astype(BF16)
        ffn_out[...] = jnp.zeros_like(ffn_out)
        grad_normed[...] = jnp.zeros_like(grad_normed)

    gate = dot(normed[...], gate_w_ref[...])
    up = dot(normed[...], up_w_ref[...])
    grad_hidden = contract(grad_ffn_ref[...], down_w_ref[...], 1, 1)
    sigmoid = sigmoid_of(gate)
    silu = gate * sigmoid
    hidden = (silu * up).astype(BF16)
    grad_gate = (grad_hidden * up * (sigmoid + silu * (1.0 - sigmoid))).astype(BF16)
    grad_up = (grad_hidden * silu).astype(BF16)
    hidden_ref[...] = hidden.T
    grad_gate_ref[...] = grad_gate
    grad_up_ref[...] = grad_up
    ffn_out[...] += dot(hidden, down_w_ref[...])
    grad_normed[...] += contract(grad_gate, gate_w_ref[...], 1, 1) + contract(grad_up, up_w_ref[...], 1, 1)

    @pl.when(step == pl.num_programs(0) - 1)
    def _():
        keep = valid()
        kept = residual[...]
        output_ref[0, 0] = ((kept + ffn_out[...]) * keep).astype(BF16)
        inverse = inverse_of(kept)
        scaled = grad_normed[...] * gain_ref[...]
        mean = jnp.mean(scaled * kept, axis=-1, keepdims=True)
        grad = cot_ref[0, 0].astype(F32) * keep
        grad = grad + (inverse * scaled - kept * (inverse * inverse * inverse) * mean)
        gain_out_ref[...] = jnp.sum(grad_normed[...] * kept * inverse, axis=0, keepdims=True)
        grad_res_ref[...] = grad
        low = grad.astype(BF16)
        grad_attn_ref[...] = low
        slots[...] = contract(out_w_ref[...], low, 1, 1).astype(BF16)
        for spot in spots:
            grad_mixed_ref[slot_rows(*spot), :] = slots[head_rows(*spot), :]


def middle_part(info, mixed, tokens, cotangent, unit, weights, gain, head_dim, output):
    width, model = tokens.shape[2:]
    out_w, gate_w, up_w, down_w = weights
    ffn = gate_w.shape[1]
    block = 1024

    def fixed(a):
        return pl.BlockSpec(a.shape, lambda f, *_: (0,) * a.ndim)

    def one(*shape):
        return pl.BlockSpec(shape, lambda f, *_: (0,) * len(shape))

    token_spec = pl.BlockSpec((1, 1, width, model), lambda f, *_: unit + (0, 0))
    operands = [info, mixed, tokens, cotangent, out_w, gain, gate_w, up_w, down_w]
    in_specs = [
        fixed(mixed), token_spec, token_spec, fixed(out_w), fixed(gain),
        pl.BlockSpec((model, block), lambda f, *_: (0, f)),
        pl.BlockSpec((model, block), lambda f, *_: (0, f)),
        pl.BlockSpec((block, model), lambda f, *_: (f, 0)),
    ]
    aliases = {}
    if output is not None:
        aliases = {len(operands): 0}
        operands.append(output)
        in_specs.append(pl.BlockSpec(memory_space=pl.ANY))
    struct = jax.ShapeDtypeStruct
    return pl.pallas_call(
        functools.partial(middle_kernel, (head_dim, output is not None)),
        grid_spec=pltpu.PrefetchScalarGridSpec(
            num_scalar_prefetch=1,
            grid=(ffn // block,),
            in_specs=in_specs,
            out_specs=[
                token_spec, one(model, width), one(model, width),
                pl.BlockSpec((block, width), lambda f, *_: (f, 0)),
                pl.BlockSpec((width, block), lambda f, *_: (0, f)),
                pl.BlockSpec((width, block), lambda f, *_: (0, f)),
                one(width, model), one(width, model), one(width, model), one(model, width), one(1, model),
            ],
            scratch_shapes=[
                pltpu.VMEM((width, model), BF16),
                pltpu.VMEM((width, model), F32),
                pltpu.VMEM((width, model), F32),
                pltpu.VMEM((width, model), F32),
                pltpu.VMEM((model, width), BF16),
            ],
        ),
        out_shape=[
            struct(tokens.shape, BF16), struct((model, width), BF16), struct((model, width), BF16),
            struct((ffn, width), BF16),
            struct((width, ffn), BF16), struct((width, ffn), BF16), struct((width, model), BF16),
            struct((width, model), F32), struct((width, model), BF16), struct((model, width), BF16),
            struct((1, model), F32),
        ],
        input_output_aliases=aliases,
        compiler_params=pltpu.CompilerParams(vmem_limit_bytes=62 << 20),
        cost_estimate=pl.CostEstimate(
            flops=12 * width * model * ffn // COVER, bytes_accessed=8 * model * ffn, transcendentals=0
        ),
        name="middle_part",
    )(*operands)


def final_kernel(
    shape, core_ref, tokens_ref, grad_res_ref, gain_ref, query_ref, key_ref, value_ref, cos_ref, sin_ref, *rest
):
    here, head_dim, aliased = shape
    back = rest[:here]
    rest = rest[here:]
    if aliased:
        rest = rest[1:]
    out_ref, grad_q_ref, grad_k_ref, grad_v_ref, gain_out_ref, total = rest
    step = pl.program_id(0)
    cosine, sine = cos_ref[...], sin_ref[...]
    half = head_dim // 2

    def turned(x):
        first, second = x[:half].astype(F32), x[half:].astype(F32)
        return jnp.concatenate(
            [first * cosine + second * sine, second * cosine - first * sine], axis=0
        ).astype(BF16)

    for at in range(256 // head_dim):
        head = at
        if here == 2:
            head = at // 2 * 2 + (core_ref[0] if at % 2 == 0 else 1 - core_ref[0])
        place = pl.ds(pl.multiple_of(head * head_dim, head_dim), head_dim)
        part = back[at % here]
        grad_q_ref[place, :] = turned(part[at // here, 0:head_dim, :])
        grad_k_ref[place, :] = turned(part[at // here, head_dim : 2 * head_dim, :])
        grad_v_ref[place, :] = part[at // here, 2 * head_dim : 3 * head_dim, :]
    made = (
        contract(grad_q_ref[...].T, query_ref[...], 1, 1)
        + contract(grad_k_ref[...].T, key_ref[...], 1, 1)
        + contract(grad_v_ref[...].T, value_ref[...], 1, 1)
    )

    @pl.when(step == 0)
    def _():
        total[...] = made

    @pl.when(step > 0)
    def _():
        total[...] += made

    @pl.when(step == pl.num_programs(0) - 1)
    def _():
        inputs = tokens_ref[0, 0].astype(F32)
        inverse = lax.rsqrt(jnp.mean(inputs * inputs, axis=-1, keepdims=True) + EPSILON)
        scaled = total[...] * gain_ref[...]
        mean = jnp.mean(scaled * inputs, axis=-1, keepdims=True)
        grad = inverse * scaled - inputs * (inverse * inverse * inverse) * mean
        out_ref[0, 0] = (grad_res_ref[...] + grad).astype(BF16)
        gain_out_ref[...] = jnp.sum(total[...] * inputs * inverse, axis=0, keepdims=True)


def final_part(core, tokens, unit, grad_res, gain, weights, cosine, sine, back, head_dim, output):
    width, model = tokens.shape[2:]
    here = len(back)
    steps = model // 256

    def fixed(a):
        return pl.BlockSpec(a.shape, lambda c: (0,) * a.ndim)

    token_spec = pl.BlockSpec((1, 1, width, model), lambda c: unit + (0, 0))
    weight_specs = [pl.BlockSpec((model, 256), lambda c, i=i: (0, i * steps + c)) for i in range(3)]
    row_spec = pl.BlockSpec((256, width), lambda c: (c, 0))
    operands = [core, tokens, grad_res, gain, weights, weights, weights, cosine, sine, *back]
    in_specs = [
        pl.BlockSpec(memory_space=pltpu.SMEM), token_spec, fixed(grad_res), fixed(gain), *weight_specs,
        fixed(cosine), fixed(sine),
    ] + [
        pl.BlockSpec((256 // head_dim // here, 3 * head_dim, width), lambda c: (c, 0, 0)) for _ in back
    ]
    aliases = {}
    if output is not None:
        aliases = {len(operands): 0}
        operands.append(output)
        in_specs.append(pl.BlockSpec(memory_space=pl.ANY))
    struct = jax.ShapeDtypeStruct
    return pl.pallas_call(
        functools.partial(final_kernel, (here, head_dim, output is not None)),
        grid=(steps,),
        in_specs=in_specs,
        out_specs=[token_spec, row_spec, row_spec, row_spec, pl.BlockSpec((1, model), lambda c: (0, 0))],
        out_shape=[
            struct(tokens.shape, BF16), struct((model, width), BF16), struct((model, width), BF16),
            struct((model, width), BF16), struct((1, model), F32),
        ],
        scratch_shapes=[pltpu.VMEM((width, model), F32)],
        input_output_aliases=aliases,
        compiler_params=pltpu.CompilerParams(vmem_limit_bytes=62 << 20),
        cost_estimate=pl.CostEstimate(
            flops=6 * width * model * model // COVER, bytes_accessed=12 * model * model, transcendentals=0
        ),
        name="final_part",
    )(*operands)


def picked_kernel(units, rows, places, flipped, split, table_ref, *refs):
    weights = len(places)
    lefts = refs[0:units]
    rights = refs[units : units * (1 + weights)]
    outs = refs[units * (1 + weights) : units * (1 + weights) + weights * split]
    picked = refs[units * (1 + weights) + weights * split :]

    @pl.when(pl.program_id(0) == 0)
    def _():
        for w, (start, size) in enumerate(places):
            for p in range(size):
                at = pl.ds(pl.multiple_of(table_ref[start + p] * rows, rows), rows)
                for u in range(units):
                    picked[w * units + u][p * rows : (p + 1) * rows, :] = lefts[u][at, :]

    for w in range(weights):
        total = None
        for u in range(units):
            right = rights[w * units + u][...]
            left = picked[w * units + u][...]
            made = contract(left, right, 1, 1) if flipped else dot(left, right)
            total = made if total is None else total + made
        height = total.shape[0] // split
        for i in range(split):
            outs[w * split + i][...] = total[i * height : (i + 1) * height].astype(BF16)


def picked_grads(table, places, lefts, rights, rows, flipped, split, block, name):
    units = len(lefts)
    width = lefts[0].shape[1]
    columns = rights[0].shape[0 if flipped else 1]
    in_specs = [pl.BlockSpec(a.shape, lambda n, *_: (0, 0)) for a in lefts]
    for a in rights:
        if flipped:
            in_specs.append(pl.BlockSpec((block, width), lambda n, *_: (n, 0)))
        else:
            in_specs.append(pl.BlockSpec((width, block), lambda n, *_: (0, n)))
    heights = [size * rows for _, size in places]
    return pl.pallas_call(
        functools.partial(picked_kernel, units, rows, places, flipped, split),
        grid_spec=pltpu.PrefetchScalarGridSpec(
            num_scalar_prefetch=1,
            grid=(columns // block,),
            in_specs=in_specs,
            out_specs=[
                pl.BlockSpec((height // split, block), lambda n, *_: (0, n)) for height in heights for _ in range(split)
            ],
            scratch_shapes=[pltpu.VMEM((height, width), BF16) for height in heights for _ in lefts],
        ),
        out_shape=[
            jax.ShapeDtypeStruct((height // split, columns), BF16) for height in heights for _ in range(split)
        ],
        compiler_params=pltpu.CompilerParams(vmem_limit_bytes=62 << 20),
        cost_estimate=pl.CostEstimate(
            flops=2 * units * sum(heights) * width * columns // COVER,
            bytes_accessed=4 * sum(heights) * columns,
            transcendentals=0,
        ),
        name=name,
    )(table, *lefts, *rights)


def weights_kernel(units, *refs):
    out_ref = refs[-1]
    total = dot(refs[0][...], refs[units][...])
    for u in range(1, units):
        total += dot(refs[u][...], refs[units + u][...])
    out_ref[...] = total.astype(BF16).reshape(out_ref.shape)


def weight_grad(lefts, rights, by_left, out_struct, out_spec, steps, into, name):
    units = len(lefts)

    def fixed(a):
        return pl.BlockSpec(a.shape, lambda n: (0, 0))

    def left_spec(a):
        return pl.BlockSpec((a.shape[0] // steps, a.shape[1]), lambda n: (n, 0))

    def right_spec(a):
        return pl.BlockSpec((a.shape[0], a.shape[1] // steps), lambda n: (0, n))

    operands = list(lefts) + list(rights)
    if by_left:
        in_specs = [left_spec(a) for a in lefts] + [fixed(a) for a in rights]
    else:
        in_specs = [fixed(a) for a in lefts] + [right_spec(a) for a in rights]
    aliases = {}
    if into is not None:
        aliases = {len(operands): 0}
        operands.append(into)
        in_specs.append(pl.BlockSpec(memory_space=pl.ANY))
    return pl.pallas_call(
        functools.partial(weights_kernel, units),
        grid=(steps,),
        in_specs=in_specs,
        out_specs=out_spec,
        out_shape=out_struct,
        input_output_aliases=aliases,
        compiler_params=pltpu.CompilerParams(vmem_limit_bytes=62 << 20),
        cost_estimate=pl.CostEstimate(
            flops=2 * units * lefts[0].shape[0] * lefts[0].shape[1] * rights[0].shape[1] // COVER,
            bytes_accessed=2 * lefts[0].shape[0] * rights[0].shape[1],
            transcendentals=0,
        ),
        name=name,
    )(*operands)


def reduce_kernel(orders, count, *refs):
    streams = len(orders)
    rounds = len(orders[0])
    ins, vec_ref = refs[:streams], refs[streams]
    outs, vec_out = refs[streams + 1 : 2 * streams + 1], refs[2 * streams + 1]
    rest = refs[2 * streams + 2 :]
    works, arrivals = rest[:streams], rest[streams : 2 * streams]
    vec_work, vec_arrival, send_sem, recv_sem, vec_send, vec_recv = rest[2 * streams :]
    shard, seq = lax.axis_index("shard"), lax.axis_index("seq")

    def partner(mask):
        if mask >= count:
            step = mask // count
            return (shard + step * (1 - 2 * (shard // step % 2)), seq)
        return (shard, seq + mask * (1 - 2 * (seq // mask % 2)))

    barrier = pltpu.get_barrier_semaphore()
    for mask in orders[0]:
        pl.semaphore_signal(
            barrier, inc=1, device_id=partner(mask), device_id_type=pl.DeviceIdType.MESH
        )
    pl.semaphore_wait(barrier, rounds)

    height = ins[0].shape[0]
    halves = [height >> (r + 1) for r in range(rounds)]
    starts = [sum(halves[:r]) for r in range(rounds)]

    def copy_of(s, r):
        source = ins[s] if r == 0 else works[s]
        return pltpu.make_async_remote_copy(
            src_ref=source.at[pl.ds(halves[r], halves[r])],
            dst_ref=arrivals[s].at[pl.ds(starts[r], halves[r])],
            send_sem=send_sem.at[s, r],
            recv_sem=recv_sem.at[s, r],
            device_id=partner(orders[s][r]),
            device_id_type=pl.DeviceIdType.MESH,
        )

    def vec_copy(r):
        return pltpu.make_async_remote_copy(
            src_ref=vec_ref if r == 0 else vec_work.at[r - 1],
            dst_ref=vec_arrival.at[r],
            send_sem=vec_send.at[r],
            recv_sem=vec_recv.at[r],
            device_id=partner(orders[0][r]),
            device_id_type=pl.DeviceIdType.MESH,
        )

    for s in range(streams):
        copy_of(s, 0).start()
    vec_copy(0).start()
    for r in range(rounds):
        for s in range(streams):
            copy_of(s, r).wait_recv()
            source = ins[s] if r == 0 else works[s]
            size = halves[r]

            def added(low, high):
                mine = source[low:high].astype(F32)
                return mine + arrivals[s][starts[r] + low : starts[r] + high].astype(F32)

            if r == rounds - 1:
                outs[s][...] = added(0, size)
            else:
                works[s][size // 2 : size] = added(size // 2, size).astype(BF16)
                copy_of(s, r + 1).start()
                works[s][0 : size // 2] = added(0, size // 2).astype(BF16)
        vec_copy(r).wait_recv()
        before = vec_ref[...] if r == 0 else vec_work[r - 1]
        if r == rounds - 1:
            vec_out[...] = before + vec_arrival[r]
        else:
            vec_work[r] = before + vec_arrival[r]
            vec_copy(r + 1).start()
    for r in range(rounds):
        for s in range(streams):
            copy_of(s, r).wait_send()
        vec_copy(r).wait_send()


def reduce_rows(parts, vector, orders, count):
    streams = len(parts)
    rounds = len(orders[0])
    height, columns = parts[0].shape
    rows = height >> rounds
    vmem = pl.BlockSpec(memory_space=pltpu.VMEM)
    return pl.pallas_call(
        functools.partial(reduce_kernel, orders, count),
        in_specs=[vmem] * (streams + 1),
        out_specs=[vmem] * (streams + 1),
        out_shape=[jax.ShapeDtypeStruct((rows, columns), F32)] * streams
        + [jax.ShapeDtypeStruct(vector.shape, F32)],
        scratch_shapes=[pltpu.VMEM((height // 2, columns), BF16) for _ in parts]
        + [pltpu.VMEM((height - rows, columns), BF16) for _ in parts]
        + [
            pltpu.VMEM((rounds - 1,) + vector.shape, F32),
            pltpu.VMEM((rounds,) + vector.shape, F32),
            pltpu.SemaphoreType.DMA((streams, rounds)),
            pltpu.SemaphoreType.DMA((streams, rounds)),
            pltpu.SemaphoreType.DMA((rounds,)),
            pltpu.SemaphoreType.DMA((rounds,)),
        ],
        compiler_params=pltpu.CompilerParams(
            collective_id=0, has_side_effects=True, vmem_limit_bytes=62 << 20
        ),
        name="reduce_rows",
    )(*parts, vector)


def on_device(
    tokens, cotangent, lengths, variates, positions, attn_gain, w_query, w_key, w_value, w_out,
    bias_table, ffn_gain, w_gate, w_up, w_down,
):
    micro, seqs, width, model = tokens.shape
    heads = bias_table.shape[0]
    head_dim = model // heads
    count = lax.axis_size("seq")
    here = heads // count
    ffn = w_gate.shape[1]
    devices = lax.axis_size("shard") * count
    seq_index = lax.axis_index("seq")
    units = [(m, s) for m in range(micro) for s in range(seqs)]
    swap = here == 2 and len(units) == 2 and lax.axis_size("shard") % 2 == 0
    core = (lax.axis_index("shard") % 2 if swap else jnp.int32(0)).astype(jnp.int32).reshape(1)
    heads_here = 1 if swap else here
    first_head = seq_index * here + core[0]
    bias_here = lax.dynamic_slice_in_dim(bias_table, first_head, heads_here, 0)
    attn_row, ffn_row = attn_gain[None, :], ffn_gain[None, :]

    def gather(weight):
        return lax.all_gather(weight, "shard", axis=0, tiled=True)

    def exchange(values):
        return lax.all_to_all(values, "seq", split_axis=0, concat_axis=0, tiled=True)

    def after(value, *before):
        return lax.optimization_barrier((value,) + before)[0]

    attn_joined = gather(jnp.concatenate([w_query, w_key, w_value], axis=1))
    ffn_weights = [gather(w_out), gather(w_gate), gather(w_up), gather(w_down)]

    def permute(value, mask):
        return lax.ppermute(value, ("shard", "seq"), [(i, i ^ mask) for i in range(devices)])

    def cross(value):
        return permute(value, count)

    lengths_of = [lengths, cross(lengths)] if swap else [lengths] * here
    packed_list, flats, tables = [], [], []

    def run_project(u, token):
        m, s = units[u]
        cosine, sine = rotary_tables(positions[m, s], head_dim // 2)
        ids = after(variates[m, s].astype(F32)[None, :], *token)
        flat, *packed = project(
            core, tokens, (m, s), attn_row, attn_joined, cosine, sine, ids, count, here, head_dim, swap
        )
        flats.append(flat)
        tables.append((cosine, sine))
        packed_list.append(packed)

    sent = {}
    mixed_now = [None] * len(units)
    sums = {}
    mixed_tok = {}
    crossed, mixed_part, mixed_cross, heads_cross, back_cross = {}, {}, {}, {}, {}
    middle = [None] * len(units)
    grad_heads = {}
    state = {"output": None, "grads": None}
    packed_grads = {}
    returned = {}
    bias_terms = {}
    finals = [None] * len(units)

    def length_of(u, h, token):
        m, s = units[u]
        return after(lengths_of[h][m, s].reshape(1), *token)

    def inputs_of(u, h):
        if not swap:
            return sent[u, h], sent[u, 0]
        return (sent[u, 0], sent[u, 1]) if h == 0 else (crossed[u], crossed[u])

    def run_forward(u, h, token):
        made, sums[u, h] = attend_forward(
            *inputs_of(u, h), length_of(u, h, token), bias_here, None if swap else mixed_now[u],
            0 if swap else h, heads_here, head_dim,
        )
        if swap:
            mixed_part[u, h] = made
            if h == 1:
                mixed_cross[u] = cross(made)
        else:
            mixed_now[u] = made
        return sums[u, h]

    def run_middle(u, token):
        m, s = units[u]
        info = jnp.stack([lengths[m, s], seq_index * width, core[0]]).astype(jnp.int32)
        state["output"], mixed_tok[u], *middle[u] = middle_part(
            after(info, *token), mixed_tok[u], tokens, cotangent, (m, s), ffn_weights, ffn_row, head_dim,
            state["output"],
        )
        return middle[u][8]

    def run_backward(u, h, token):
        if swap:
            token = token + ((heads_cross[1],) if (u, h) == (0, 1) else ())
            grad = grad_heads[u] if h == 0 else heads_cross[u]
            mixed = mixed_part[u, h]
        else:
            grad, mixed = grad_heads[u], mixed_now[u]
        packed_grads[u, h], both = attend_backward(
            *inputs_of(u, h), grad, mixed, sums[u, h], length_of(u, h, token), bias_here,
            0 if swap else h, head_dim,
        )
        if swap and h == 1:
            back_cross[u] = cross(packed_grads[u, h])
        bias_terms[u, h] = both
        return both

    def run_final(u, token):
        m, s = units[u]
        cosine, sine = tables[u]
        state["grads"], *finals[u] = final_part(
            core, tokens, (m, s), middle[u][5], after(attn_row, *token), attn_joined, cosine, sine,
            [returned[u, h] for h in range(here)], head_dim, state["grads"],
        )
        return finals[u][3]

    rows = model // devices
    fold = ffn // model
    tall = ffn // devices
    seq_masks = [1 << i for i in range(count.bit_length() - 1)]
    shard_masks = [count << i for i in range((devices // count).bit_length() - 1)]
    spread = shard_masks[1:]
    orders = (
        shard_masks[:1] + spread + seq_masks,
        shard_masks[:1] + seq_masks[:1] + spread + seq_masks[1:],
        shard_masks[:1] + seq_masks[1:2] + seq_masks[:1] + spread + seq_masks[2:],
    )
    direct = rows % 16 == 0 and devices == 1 << len(orders[0])

    def places_of(order):
        marks = []
        for p in range(devices):
            bits = [p >> (len(order) - 1 - i) & 1 for i in range(len(order))]
            marks.append(sum(mask for bit, mask in zip(bits, order) if bit))
        me = lax.axis_index("shard") * count + seq_index
        return me.astype(jnp.int32) ^ jnp.array(marks, jnp.int32)

    def column(index):
        return [item[index] for item in middle]

    def run_weights(token):
        if not direct:
            return [
                sum(dot(left, right) for left, right in zip(lefts, rights)).astype(BF16)
                for lefts, rights in (
                    (column(0), column(2)), (column(0), column(3)), (column(1), column(4)),
                    ([mixed_tok[u] for u in range(len(units))], column(6)),
                )
            ]
        part = ffn // fold
        narrow = model // fold
        spare = -(-(2 * part + narrow) // 384) * 384
        struct = jax.ShapeDtypeStruct((devices, fold, rows, spare), BF16)
        down = pl.BlockSpec((512 // tall, fold, rows, model), lambda n: (n, 0, 0, 0))
        gate = pl.BlockSpec((devices, 1, rows, part), lambda n: (0, n, 0, 1))
        out = pl.BlockSpec((devices, 1, rows, narrow), lambda n: (0, n, 0, 2 * part // narrow))
        table = after(places_of(orders[0]), *token)
        up = picked_grads(table, [(0, devices)], column(0), column(3), rows, False, 2, 1024, "up_grad")
        holder["streams"] = [[up[0], permute(up[1], orders[0][0]), orders[0][1:]]]
        firsts = [after(middle[0][4], up[0])] + [item[4] for item in middle[1:]]
        terms = weight_grad(column(1), firsts, True, struct, down, ffn // 512, None, "down_grad")
        landed = (holder["streams"][0][1],) + ((heads_cross[0],) if swap else ())
        rights = [after(middle[0][2], *holder["flying"], *landed)] + [item[2] for item in middle[1:]]
        terms = weight_grad(column(0), rights, False, struct, gate, fold, terms, "gate_grad")
        mixed_all = [mixed_tok[u] for u in range(len(units))]
        terms = weight_grad(mixed_all, column(6), False, struct, out, fold, terms, "out_grad")
        terms = terms.reshape(ffn, spare)
        holder["owned"] = lax.psum_scatter(terms, ("shard", "seq"), scatter_dimension=0, tiled=True)
        return terms

    def wide_sum(a, b):
        return a.astype(F32) + b.astype(F32)

    def advance(token):
        out = ()
        if not direct:
            return out
        for stream in holder["streams"]:
            keep, came, masks = stream
            if not masks:
                continue
            keep = after(keep, *token)
            half = keep.shape[0] // 2
            send = wide_sum(keep[half:], came[half:]).astype(BF16)
            stream[0] = wide_sum(keep[:half], came[:half]).astype(BF16)
            stream[1] = permute(send, masks[0])
            stream[2] = masks[1:]
            out = out + (send, stream[0])
        return out

    holder = {}

    def weights_work(token):
        holder["terms"] = run_weights(token)
        return holder["terms"]

    def send_packed(u, h):
        def keep(moved):
            sent[u, h] = moved
            if swap and h == 1:
                crossed[u] = cross(moved)

        return lambda: packed_list[u][h], keep

    def send_mixed(u):
        def keep(moved):
            mixed_tok[u] = moved.reshape(model, width)

        if not swap:
            return lambda: mixed_now[u], keep
        return lambda: jnp.concatenate([mixed_part[u, 0], mixed_cross[u]], axis=1), keep

    def send_heads(u):
        def keep(moved):
            grad_heads[u] = moved
            if swap:
                heads_cross[u] = cross(moved[:, head_dim:])

        return lambda: middle[u][7].reshape(count, here * head_dim, width), keep

    def send_back(u, h):
        def keep(moved):
            returned[u, h] = moved

        return lambda: back_cross[u] if swap and h == 1 else packed_grads[u, h], keep

    def work_project(u):
        def work(token):
            run_project(u, token)
            return flats[u]

        return work

    def work(function, *args):
        return lambda token: function(*args, token)

    total = len(units)
    order = [(u, h) for u in range(total) for h in range(here)]
    if swap:
        steps = [
            (work_project(0), None),
            (work_project(1), send_packed(0, 1)),
            (work(run_forward, 0, 1), send_packed(0, 0)),
            (work(run_forward, 0, 0), send_packed(1, 1)),
            (work(run_forward, 1, 1), send_packed(1, 0)),
            (work(run_forward, 1, 0), send_mixed(0)),
            (work(run_middle, 0), send_mixed(1)),
            (work(run_middle, 1), send_heads(0)),
            (weights_work, send_heads(1)),
            (work(run_backward, 0, 0), None),
            (work(run_backward, 0, 1), send_back(0, 0)),
            (work(run_backward, 1, 0), send_back(0, 1)),
            (work(run_backward, 1, 1), send_back(1, 0)),
            (work(run_final, 0), send_back(1, 1)),
            (work(run_final, 1), None),
        ]
    else:
        steps = [(work_project(u), None) for u in range(total)]
        steps += [(None, send_packed(*at)) for at in order]
        for u in range(total):
            steps += [(work(run_forward, u, h), None) for h in range(here)]
            steps += [(None, send_mixed(u))]
        for u in range(total):
            steps += [(work(run_middle, u), None), (None, send_heads(u))]
        steps += [(weights_work, None)]
        for at in order:
            steps += [(work(run_backward, *at), None), (None, send_back(*at))]
        steps += [(work(run_final, u), None) for u in range(total)]

    late = [task for task, _ in steps[-2:]]
    token = ()
    for task, send in steps:
        done = ()
        moved = None
        if "streams" in holder:
            leaving = advance(token)
            token = token if task in late else token + leaving
        if send is not None:
            moved = exchange(after(send[0](), *token))
            done = (moved,)
        holder["flying"] = done
        if task is not None:
            done = done + (task(token),)
        if send is not None:
            send[1](after(moved, *done[1:]))
        token = done
    acc_bias = jnp.concatenate(
        [sum(bias_terms[u, h] for u in range(total))[0:1, 0:2] for h in range(here)], axis=0
    )
    if swap:
        acc_bias = acc_bias[0:1] + acc_bias[1:2]
    bias_full = lax.dynamic_update_slice(
        jnp.zeros((heads, 2), F32), acc_bias, (first_head, jnp.int32(0))
    )
    gain_attn = sum(item[3][0] for item in finals)
    gain_ffn = sum(item[8][0] for item in middle)
    if direct:
        while holder["streams"][0][2]:
            advance(token)
        keep, came, _ = holder["streams"][0]
        up_own = wide_sum(after(keep, *token), came)
        owned, part = holder["owned"], ffn // fold

        def joined(start, size):
            piece = owned[:, start : start + size].reshape(fold, rows, size)
            return jnp.swapaxes(piece, 0, 1).reshape(rows, fold * size).astype(F32)

        down_own = owned[:, :part].astype(F32)
        gate_own, out_own = joined(part, part), joined(2 * part, model // fold)
        table = jnp.concatenate([places_of(order) for order in orders])
        attn_terms = picked_grads(
            table, [(i * devices, devices) for i in range(3)], flats,
            [item[i] for i in range(3) for item in finals], rows, True, 1, 256, "attn_grads",
        )
        flat = jnp.concatenate([gain_attn, gain_ffn, bias_full.reshape(-1)])
        tiles = -(-flat.shape[0] // 1024) * 8
        flat = jnp.pad(flat, (0, tiles * 128 - flat.shape[0])).reshape(tiles, 128)
        query_own, key_own, value_own, flat = reduce_rows(list(attn_terms), flat, orders, count)
        flat = flat.reshape(-1)
        gain_attn, gain_ffn = flat[:model], flat[model : 2 * model]
        bias_full = flat[2 * model : 2 * model + 2 * heads].reshape(heads, 2)
    else:

        def scatter(value):
            owned = lax.psum_scatter(value, ("shard", "seq"), scatter_dimension=0, tiled=True)
            return owned.astype(F32)

        gate_own, up_own, down_own, out_own = [scatter(value) for value in holder["terms"]]
        query_own, key_own, value_own = [
            scatter(
                sum(contract(flat, item[i], 1, 1) for flat, item in zip(flats, finals)).astype(BF16)
            )
            for i in range(3)
        ]
        gain_attn, gain_ffn, bias_full = lax.psum(
            (gain_attn, gain_ffn, bias_full), ("shard", "seq")
        )
    return (
        state["output"], state["grads"], gain_attn, query_own, key_own, value_own, out_own,
        bias_full, gain_ffn, gate_own, up_own, down_own,
    )


def solution(mesh):
    token_spec = P(None, "shard", "seq", None)
    row_spec = P("shard", None)
    in_specs = (
        token_spec, token_spec, P(None, "shard"), P(None, "shard", "seq"), P(None, "shard", "seq"),
        P(), row_spec, row_spec, row_spec, row_spec, P(), P(), row_spec, row_spec, row_spec,
    )
    owned = P(("shard", "seq"), None)
    out_specs = (
        token_spec, token_spec, P(), owned, owned, owned, owned, P(), P(), owned, owned, owned,
    )
    return jax.shard_map(
        on_device, mesh=mesh, in_specs=in_specs, out_specs=out_specs, check_vma=False
    )
```

```python
import functools
import math

import jax
import jax.numpy as jnp
from jax import lax
from jax.experimental import pallas as pl
from jax.experimental.pallas import tpu as pltpu
from jax.sharding import PartitionSpec as P

EPSILON = 1e-06
ROTARY_BASE = 10000.0
LOG2E = 1.4426950408889634
LN2 = 0.6931471805599453
CLASSES = 8
COVER = 16
EXTRA = 32
MASKED = -1.5e9
FAR = 1e30
F32 = jnp.float32
BF16 = jnp.bfloat16


def dot(a, b):
    return jnp.dot(a, b, preferred_element_type=F32)


def contract(a, b, da, db):
    return lax.dot_general(a, b, (((da,), (db,)), ((), ())), preferred_element_type=F32)


def pieces(x):
    high = x.astype(BF16).astype(F32)
    rest = x - high
    mid = rest.astype(BF16).astype(F32)
    low = (rest - mid).astype(BF16).astype(F32)
    return high, mid, low


def one_hot(row):
    classes = lax.broadcasted_iota(jnp.int32, (CLASSES, row.shape[1]), 0).astype(F32)
    return jnp.where(classes == row, 1.0, 0.0)


def rows_of(values, width):
    index = lax.broadcasted_iota(jnp.int32, (8, width), 0)
    out = jnp.zeros((8, width), F32)
    for at, value in enumerate(values):
        out = jnp.where(index == at, value, out)
    return out


def key_extra(row, start, length, other, same):
    width = row.shape[1]
    hot = one_hot(row)
    step = pieces(jnp.full((1, width), same - other, F32))
    base = pieces(jnp.full((1, width), other, F32))
    index = start + lax.broadcasted_iota(jnp.int32, (1, width), 1)
    mask = jnp.where(index < length, 0.0, MASKED)
    tail = rows_of(base + (mask, 1.0, 1.0, 1.0), width)
    return jnp.concatenate([hot * step[0], hot * step[1], hot * step[2], tail], axis=0).astype(BF16)


def query_extra(row, shift):
    hot = one_hot(row)
    tail = rows_of((1.0, 1.0, 1.0, 1.0) + shift, row.shape[1])
    return jnp.concatenate([hot, hot, hot, tail], axis=0).astype(BF16)


def forward_kernel(
    shape, len_ref, bias_ref, x_ref, ids_ref, *rest
):
    local, head_dim, block, aliased = shape
    if aliased:
        rest = rest[1:]
    mixed_ref, lse_ref, keys, vals, query, score, peak, total = rest
    count, _, width = x_ref.shape
    sub = block // width
    step = pl.program_id(0)
    length = len_ref[0]
    other = bias_ref[local, 0] * LOG2E
    same = bias_ref[local, 1] * LOG2E

    @pl.when(step == 0)
    def _():
        for b in range(count):
            at = pl.ds(b * width, width)
            row = ids_ref[b, 0:1, :].astype(F32)
            extra = key_extra(row, b * width, length, other, same)
            full = jnp.concatenate([x_ref[b, head_dim : 2 * head_dim, :], extra], axis=0)
            keys[at, :] = full.T
            vals[0:head_dim, at] = x_ref[b, 2 * head_dim : 3 * head_dim, :]
        vals[head_dim:, :] = jnp.ones((16, vals.shape[1]), BF16)

    used = pl.cdiv(length, block)
    inside = step * block < length

    @pl.when(jnp.logical_not(inside))
    def _():
        mixed_ref[...] = jnp.zeros_like(mixed_ref)
        lse_ref[...] = jnp.full(lse_ref.shape, FAR, F32)

    @pl.when(inside)
    def _():
        for b in range(sub):
            at = slice(b * width, (b + 1) * width)
            row = ids_ref[step * sub + b, 0:1, :].astype(F32)
            query[0:head_dim, at] = x_ref[step * sub + b, 0:head_dim, :]
            query[head_dim:, at] = query_extra(row, (0.0, 0.0, 0.0))
        peak[...] = jnp.full(peak.shape, -FAR, F32)
        total[...] = jnp.zeros_like(total)

        def span(j):
            return pl.ds(pl.multiple_of(j * block, block), block)

        def scores_of(j):
            return dot(keys[span(j), :], query[...])

        def one(j, now, ahead):
            if ahead:
                score[1 - now] = scores_of(j + 1)
            current = score[now]
            before = peak[...]
            top = jnp.maximum(before, jnp.max(current, axis=0, keepdims=True))
            weight = jnp.exp2(current - top).astype(BF16)
            peak[...] = top
            total[...] = total[...] * jnp.exp2(before - top) + dot(vals[:, span(j)], weight)

        score[0] = scores_of(0)
        pairs = (used - 1) // 2

        def pair(j, carry):
            one(2 * j, 0, True)
            one(2 * j + 1, 1, True)
            return carry

        lax.fori_loop(0, pairs, pair, 0)
        last = 2 * pairs

        @pl.when(used - last == 1)
        def _():
            one(last, 0, False)

        @pl.when(used - last == 2)
        def _():
            one(last, 0, True)
            one(last + 1, 1, False)

        mass = total[head_dim : head_dim + 1, :]
        mixed = (total[0:head_dim, :] / mass).astype(BF16)
        for b in range(sub):
            mixed_ref[b] = mixed[:, b * width : (b + 1) * width]
        lse_ref[0] = peak[...] + jnp.log2(mass)


def attend_forward(x, ids, length, bias, mixed, local, heads_here, head_dim):
    count, rows, width = x.shape
    block = max(width, 512)
    seq_len = count * width
    blocks = seq_len // block
    depth = head_dim + EXTRA
    whole = pl.BlockSpec((count, rows, width), lambda i, *_: (0, 0, 0))
    operands = [length, bias, x, ids]
    in_specs = [whole, pl.BlockSpec((count, 1, width), lambda i, *_: (0, 0, 0))]
    aliases = {}
    if mixed is not None:
        operands.append(mixed)
        in_specs.append(pl.BlockSpec(memory_space=pl.ANY))
        aliases = {4: 0}
    return pl.pallas_call(
        functools.partial(forward_kernel, (local, head_dim, block, mixed is not None)),
        grid_spec=pltpu.PrefetchScalarGridSpec(
            num_scalar_prefetch=2,
            grid=(blocks,),
            in_specs=in_specs,
            out_specs=[
                pl.BlockSpec((block // width, head_dim, width), lambda i, *_: (i, local, 0)),
                pl.BlockSpec((1, 1, block), lambda i, *_: (i, 0, 0)),
            ],
            scratch_shapes=[
                pltpu.VMEM((seq_len, depth), BF16),
                pltpu.VMEM((head_dim + 16, seq_len), BF16),
                pltpu.VMEM((depth, block), BF16),
                pltpu.VMEM((2, block, block), F32),
                pltpu.VMEM((1, block), F32),
                pltpu.VMEM((head_dim + 16, block), F32),
            ],
        ),
        out_shape=[
            jax.ShapeDtypeStruct((count, heads_here * head_dim, width), BF16),
            jax.ShapeDtypeStruct((blocks, 1, block), F32),
        ],
        input_output_aliases=aliases,
        compiler_params=pltpu.CompilerParams(vmem_limit_bytes=62 << 20),
        cost_estimate=pl.CostEstimate(
            flops=8 * seq_len * seq_len * 256 // COVER,
            bytes_accessed=x.size * 4,
            transcendentals=0,
        ),
        name="attend_forward",
    )(*operands)


def backward_kernel(
    shape, len_ref, bias_ref, x_ref, ids_ref, grad_ref, mixed_ref, lse_ref, out_ref, bias_out_ref,
    keys, keys_flat, vals, query, grads, query_rows, grad_rows, acc_keys, acc_vals, acc_query,
):
    local, head_dim, block = shape
    count, _, width = x_ref.shape
    sub = block // width
    step = pl.program_id(0)
    length = len_ref[0]
    other = bias_ref[local, 0] * LOG2E
    same = bias_ref[local, 1] * LOG2E

    @pl.when(step == 0)
    def _():
        ones = jnp.ones((16, width), BF16)
        for b in range(count):
            at = pl.ds(b * width, width)
            row = ids_ref[b, 0:1, :].astype(F32)
            extra = key_extra(row, b * width, length, other, same)
            here = x_ref[b, head_dim : 2 * head_dim, :]
            keys[at, :] = jnp.concatenate([here, extra], axis=0).T
            keys_flat[:, at] = here
            vals[at, :] = jnp.concatenate([x_ref[b, 2 * head_dim : 3 * head_dim, :], ones], axis=0).T
        acc_keys[...] = jnp.zeros_like(acc_keys)
        acc_vals[...] = jnp.zeros_like(acc_vals)

    used = pl.cdiv(length, block)
    inside = step * block < length

    @pl.when(jnp.logical_not(inside))
    def _():
        for b in range(sub):
            out_ref[step * sub + b, 0:head_dim, :] = jnp.zeros((head_dim, width), BF16)

    @pl.when(inside)
    def _():
        for b in range(sub):
            at = slice(b * width, (b + 1) * width)
            here = step * sub + b
            row = ids_ref[here, 0:1, :].astype(F32)
            shift = pieces(-lse_ref[step][:, at])
            grad = grad_ref[here]
            delta = jnp.sum(grad.astype(F32) * mixed_ref[here].astype(F32), axis=0, keepdims=True)
            query[0:head_dim, at] = x_ref[here, 0:head_dim, :]
            query[head_dim:, at] = query_extra(row, shift)
            grads[0:head_dim, at] = grad
            tail = rows_of(pieces(-delta), width)
            grads[head_dim:, at] = jnp.concatenate([tail, jnp.zeros_like(tail)], axis=0).astype(BF16)
        query_rows[...] = query[...].T
        grad_rows[...] = grads[...].T
        acc_query[...] = jnp.zeros_like(acc_query)

        def one(j):
            at = pl.ds(pl.multiple_of(j * block, block), block)
            probs = jnp.exp2(dot(keys[at, :], query[...]))
            grad_probs = dot(vals[at, :], grads[...])
            grad_scores = (probs * grad_probs).astype(BF16)
            acc_vals[at, :] += dot(probs.astype(BF16), grad_rows[...])
            acc_keys[at, :] += dot(grad_scores, query_rows[...])
            acc_query[...] += dot(keys_flat[:, at], grad_scores)

        def pair(j, carry):
            one(2 * j)
            one(2 * j + 1)
            return carry

        lax.fori_loop(0, used // 2, pair, 0)

        @pl.when(used % 2 == 1)
        def _():
            one(used - 1)

        grad_query = (acc_query[...] * (1.0 / math.sqrt(head_dim))).astype(BF16)
        for b in range(sub):
            out_ref[step * sub + b, 0:head_dim, :] = grad_query[:, b * width : (b + 1) * width]

    @pl.when(step == pl.num_programs(0) - 1)
    def _():
        same_total = jnp.zeros((CLASSES, width), F32)
        all_total = jnp.zeros((CLASSES, width), F32)
        for b in range(count):
            at = pl.ds(b * width, width)
            row = ids_ref[b, 0:1, :].astype(F32)
            flat = acc_keys[at, :].T
            out_ref[b, head_dim : 2 * head_dim, :] = (flat[0:head_dim] * LN2).astype(BF16)
            out_ref[b, 2 * head_dim : 3 * head_dim, :] = acc_vals[at, :].T[0:head_dim].astype(BF16)
            by_class = flat[head_dim : head_dim + CLASSES]
            all_total += by_class
            same_total += by_class * one_hot(row)
        same_sum = jnp.sum(same_total, keepdims=True)
        other_sum = jnp.sum(all_total, keepdims=True) - same_sum
        lane = lax.broadcasted_iota(jnp.int32, (8, 128), 1)
        bias_out_ref[...] = jnp.where(lane == 0, other_sum, jnp.where(lane == 1, same_sum, 0.0))


def attend_backward(x, ids, grad, mixed, lse, length, bias, local, head_dim):
    count, rows, width = x.shape
    blocks, _, block = lse.shape
    seq_len = count * width
    depth = head_dim + EXTRA

    def whole(a):
        return pl.BlockSpec(a.shape, lambda i, *_: (0,) * a.ndim)

    head_spec = pl.BlockSpec((count, head_dim, width), lambda i, *_: (0, local, 0))
    return pl.pallas_call(
        functools.partial(backward_kernel, (local, head_dim, block)),
        grid_spec=pltpu.PrefetchScalarGridSpec(
            num_scalar_prefetch=2,
            grid=(blocks,),
            in_specs=[
                whole(x),
                pl.BlockSpec((count, 1, width), lambda i, *_: (0, 0, 0)),
                head_spec, head_spec, whole(lse),
            ],
            out_specs=[
                pl.BlockSpec((count, 3 * head_dim, width), lambda i, *_: (0, 0, 0)),
                pl.BlockSpec((8, 128), lambda i, *_: (0, 0)),
            ],
            scratch_shapes=[
                pltpu.VMEM((seq_len, depth), BF16),
                pltpu.VMEM((head_dim, seq_len), BF16),
                pltpu.VMEM((seq_len, head_dim + 16), BF16),
                pltpu.VMEM((depth, block), BF16),
                pltpu.VMEM((head_dim + 16, block), BF16),
                pltpu.VMEM((block, depth), BF16),
                pltpu.VMEM((block, head_dim + 16), BF16),
                pltpu.VMEM((seq_len, depth), F32),
                pltpu.VMEM((seq_len, head_dim + 16), F32),
                pltpu.VMEM((head_dim, block), F32),
            ],
        ),
        out_shape=[
            jax.ShapeDtypeStruct((count, 3 * head_dim, width), BF16),
            jax.ShapeDtypeStruct((8, 128), F32),
        ],
        compiler_params=pltpu.CompilerParams(vmem_limit_bytes=62 << 20),
        cost_estimate=pl.CostEstimate(
            flops=20 * seq_len * seq_len * 256 // COVER,
            bytes_accessed=x.size * 6,
            transcendentals=0,
        ),
        name="attend_backward",
    )(length, bias, x, ids, grad, mixed, lse)


def rotary_tables(places, half_dim):
    frequency = jnp.exp(-math.log(ROTARY_BASE) * jnp.arange(half_dim, dtype=F32) / half_dim)
    angles = places.astype(F32)[None, :] * frequency[:, None]
    return jnp.cos(angles), jnp.sin(angles)


def sigmoid_of(x):
    return 1.0 / (1.0 + jnp.exp2(x * -LOG2E))


def turn_kernel(*refs):
    out_ref = refs[-1]
    size = refs[0].shape[1]
    for i, ref in enumerate(refs[:-1]):
        out_ref[i * size : (i + 1) * size, :] = ref[...].T


def turn_weights(*weights):
    depth, size = weights[0].shape
    vmem = pl.BlockSpec(memory_space=pltpu.VMEM)
    return pl.pallas_call(
        turn_kernel,
        in_specs=[vmem] * len(weights),
        out_specs=vmem,
        out_shape=jax.ShapeDtypeStruct((len(weights) * size, depth), BF16),
        compiler_params=pltpu.CompilerParams(vmem_limit_bytes=62 << 20),
        name="turn_weights",
    )(*weights)


def project_kernel(
    shape, core_ref, tokens_ref, gain_ref, query_ref, key_ref, value_ref, cos_ref, sin_ref, flat_ref, *rest
):
    here, head_dim, swap = shape
    outs, flat_weights = rest[:-1], rest[-1]
    pair = pl.program_id(0)

    @pl.when(pair == 0)
    def _():
        inputs = tokens_ref[0, 0].astype(F32)
        inverse = lax.rsqrt(jnp.mean(inputs * inputs, axis=-1, keepdims=True) + EPSILON)
        flat_ref[...] = (inputs * inverse * gain_ref[...]).astype(BF16).T

    made = None
    depth = query_ref.shape[2]
    for shard in range(query_ref.shape[0]):
        for at, ref in enumerate((query_ref, key_ref, value_ref)):
            flat_weights[shard, at * 128 : (at + 1) * 128, :] = ref[shard]
        term = dot(flat_weights[shard], flat_ref[shard * depth : (shard + 1) * depth, :])
        made = term if made is None else made + term
    cosine, sine = cos_ref[...], sin_ref[...]
    half = head_dim // 2

    def turned(start, scale):
        first = made[start : start + half]
        second = made[start + half : start + head_dim]
        both = [first * cosine - second * sine, second * cosine + first * sine]
        return (jnp.concatenate(both, axis=0) * scale).astype(BF16)

    def put(at, slot, place):
        spot = at * head_dim
        target = outs[slot]
        target[place, 0:head_dim, :] = turned(spot, LOG2E / math.sqrt(head_dim))
        target[place, head_dim : 2 * head_dim, :] = turned(128 + spot, 1.0)
        target[place, 2 * head_dim : 3 * head_dim, :] = made[256 + spot : 256 + spot + head_dim].astype(BF16)

    if swap:
        for core in range(2):

            @pl.when(core_ref[0] == core)
            def _():
                put(core, 0, 0)
                put(1 - core, 1, 0)

    else:
        for at in range(128 // head_dim):
            put(at, at % here, 0 if here > 1 else at)


def project(core, tokens, unit, gain, weights, cosine, sine, count, here, head_dim, swap):
    width, model = tokens.shape[2:]
    heads = count * here
    pairs = heads * head_dim // 128
    per = 128 // head_dim // here

    def fixed(a):
        return pl.BlockSpec(a.shape, lambda p: (0,) * a.ndim)

    shards, _, depth = weights.shape
    weight_specs = [
        pl.BlockSpec((shards, 128, depth), lambda p, i=i: (0, i * pairs + p, 0)) for i in range(3)
    ]
    return pl.pallas_call(
        functools.partial(project_kernel, (here, head_dim, swap)),
        grid=(pairs,),
        in_specs=[
            pl.BlockSpec(memory_space=pltpu.SMEM),
            pl.BlockSpec((1, 1, width, model), lambda p: unit + (0, 0)),
            fixed(gain), *weight_specs, fixed(cosine), fixed(sine),
        ],
        out_specs=[pl.BlockSpec((model, width), lambda p: (0, 0))]
        + [pl.BlockSpec((per, 3 * head_dim, width), lambda p: (p, 0, 0))] * here,
        out_shape=[jax.ShapeDtypeStruct((model, width), BF16)]
        + [jax.ShapeDtypeStruct((count, 3 * head_dim, width), BF16)] * here,
        scratch_shapes=[pltpu.VMEM((shards, 384, depth), BF16)],
        compiler_params=pltpu.CompilerParams(vmem_limit_bytes=62 << 20),
        cost_estimate=pl.CostEstimate(
            flops=6 * width * model * model // COVER, bytes_accessed=12 * model * model, transcendentals=0
        ),
        name="project",
    )(core, tokens, gain, weights, weights, weights, cosine, sine)


def middle_kernel(
    shape, info_ref, mixed_ref, tokens_ref, cot_ref, out_w_ref, gain_ref, gate_w_ref, up_w_ref, down_w_ref, *rest
):
    head_dim, aliased = shape
    if aliased:
        rest = rest[1:]
    (
        output_ref, ordered_ref, flat_ref, hidden_ref, grad_gate_ref, grad_up_ref, grad_ffn_ref, grad_res_ref,
        grad_attn_ref, grad_mixed_ref, gain_out_ref, normed, residual, ffn_out, grad_normed, slots,
    ) = rest
    core = info_ref[2]
    step = pl.program_id(0)
    width = normed.shape[0]

    def valid():
        index = info_ref[1] + lax.broadcasted_iota(jnp.int32, (width, 1), 0)
        return jnp.where(index < info_ref[0], 1.0, 0.0)

    def inverse_of(x):
        return lax.rsqrt(jnp.mean(x * x, axis=-1, keepdims=True) + EPSILON)

    def head_rows(pair, slot):
        head = 2 * pair + (core if slot == 0 else 1 - core)
        return pl.ds(pl.multiple_of(head * head_dim, head_dim), head_dim)

    def slot_rows(pair, slot):
        return slice((2 * pair + slot) * head_dim, (2 * pair + slot + 1) * head_dim)

    spots = [(pair, slot) for pair in range(mixed_ref.shape[0] // head_dim // 2) for slot in range(2)]

    @pl.when(step == 0)
    def _():
        for spot in spots:
            ordered_ref[head_rows(*spot), :] = mixed_ref[slot_rows(*spot), :]
        inputs = tokens_ref[0, 0].astype(F32) + dot(ordered_ref[...].T, out_w_ref[...])
        residual[...] = inputs
        made = (inputs * inverse_of(inputs) * gain_ref[...]).astype(BF16)
        normed[...] = made
        flat_ref[...] = made.T
        grad_ffn_ref[...] = (cot_ref[0, 0].astype(F32) * valid()).astype(BF16)
        ffn_out[...] = jnp.zeros_like(ffn_out)
        grad_normed[...] = jnp.zeros_like(grad_normed)

    gate = dot(normed[...], gate_w_ref[...])
    up = dot(normed[...], up_w_ref[...])
    grad_hidden = contract(grad_ffn_ref[...], down_w_ref[...], 1, 1)
    sigmoid = sigmoid_of(gate)
    silu = gate * sigmoid
    hidden = (silu * up).astype(BF16)
    grad_gate = (grad_hidden * up * (sigmoid + silu * (1.0 - sigmoid))).astype(BF16)
    grad_up = (grad_hidden * silu).astype(BF16)
    hidden_ref[...] = hidden.T
    grad_gate_ref[...] = grad_gate
    grad_up_ref[...] = grad_up
    ffn_out[...] += dot(hidden, down_w_ref[...])
    grad_normed[...] += contract(grad_gate, gate_w_ref[...], 1, 1) + contract(grad_up, up_w_ref[...], 1, 1)

    @pl.when(step == pl.num_programs(0) - 1)
    def _():
        keep = valid()
        kept = residual[...]
        output_ref[0, 0] = ((kept + ffn_out[...]) * keep).astype(BF16)
        inverse = inverse_of(kept)
        scaled = grad_normed[...] * gain_ref[...]
        mean = jnp.mean(scaled * kept, axis=-1, keepdims=True)
        grad = cot_ref[0, 0].astype(F32) * keep
        grad = grad + (inverse * scaled - kept * (inverse * inverse * inverse) * mean)
        gain_out_ref[...] = jnp.sum(grad_normed[...] * kept * inverse, axis=0, keepdims=True)
        grad_res_ref[...] = grad
        low = grad.astype(BF16)
        grad_attn_ref[...] = low
        slots[...] = contract(out_w_ref[...], low, 1, 1).astype(BF16)
        for spot in spots:
            grad_mixed_ref[slot_rows(*spot), :] = slots[head_rows(*spot), :]


def middle_part(info, mixed, tokens, cotangent, unit, weights, gain, head_dim, output):
    width, model = tokens.shape[2:]
    out_w, gate_w, up_w, down_w = weights
    ffn = gate_w.shape[1]
    block = 512

    def fixed(a):
        return pl.BlockSpec(a.shape, lambda f, *_: (0,) * a.ndim)

    def one(*shape):
        return pl.BlockSpec(shape, lambda f, *_: (0,) * len(shape))

    token_spec = pl.BlockSpec((1, 1, width, model), lambda f, *_: unit + (0, 0))
    operands = [info, mixed, tokens, cotangent, out_w, gain, gate_w, up_w, down_w]
    in_specs = [
        fixed(mixed), token_spec, token_spec, fixed(out_w), fixed(gain),
        pl.BlockSpec((model, block), lambda f, *_: (0, f)),
        pl.BlockSpec((model, block), lambda f, *_: (0, f)),
        pl.BlockSpec((block, model), lambda f, *_: (f, 0)),
    ]
    aliases = {}
    if output is not None:
        aliases = {len(operands): 0}
        operands.append(output)
        in_specs.append(pl.BlockSpec(memory_space=pl.ANY))
    struct = jax.ShapeDtypeStruct
    return pl.pallas_call(
        functools.partial(middle_kernel, (head_dim, output is not None)),
        grid_spec=pltpu.PrefetchScalarGridSpec(
            num_scalar_prefetch=1,
            grid=(ffn // block,),
            in_specs=in_specs,
            out_specs=[
                token_spec, one(model, width), one(model, width),
                pl.BlockSpec((block, width), lambda f, *_: (f, 0)),
                pl.BlockSpec((width, block), lambda f, *_: (0, f)),
                pl.BlockSpec((width, block), lambda f, *_: (0, f)),
                one(width, model), one(width, model), one(width, model), one(model, width), one(1, model),
            ],
            scratch_shapes=[
                pltpu.VMEM((width, model), BF16),
                pltpu.VMEM((width, model), F32),
                pltpu.VMEM((width, model), F32),
                pltpu.VMEM((width, model), F32),
                pltpu.VMEM((model, width), BF16),
            ],
        ),
        out_shape=[
            struct(tokens.shape, BF16), struct((model, width), BF16), struct((model, width), BF16),
            struct((ffn, width), BF16),
            struct((width, ffn), BF16), struct((width, ffn), BF16), struct((width, model), BF16),
            struct((width, model), F32), struct((width, model), BF16), struct((model, width), BF16),
            struct((1, model), F32),
        ],
        input_output_aliases=aliases,
        compiler_params=pltpu.CompilerParams(vmem_limit_bytes=62 << 20),
        cost_estimate=pl.CostEstimate(
            flops=12 * width * model * ffn // COVER, bytes_accessed=8 * model * ffn, transcendentals=0
        ),
        name="middle_part",
    )(*operands)


def final_kernel(
    shape, core_ref, tokens_ref, grad_res_ref, gain_ref, query_ref, key_ref, value_ref, cos_ref, sin_ref, *rest
):
    here, head_dim, aliased = shape
    back = rest[:here]
    rest = rest[here:]
    if aliased:
        rest = rest[1:]
    out_ref, grad_q_ref, grad_k_ref, grad_v_ref, gain_out_ref, total = rest
    step = pl.program_id(0)
    cosine, sine = cos_ref[...], sin_ref[...]
    half = head_dim // 2

    def turned(x):
        first, second = x[:half].astype(F32), x[half:].astype(F32)
        return jnp.concatenate(
            [first * cosine + second * sine, second * cosine - first * sine], axis=0
        ).astype(BF16)

    for at in range(256 // head_dim):
        head = at
        if here == 2:
            head = at // 2 * 2 + (core_ref[0] if at % 2 == 0 else 1 - core_ref[0])
        place = pl.ds(pl.multiple_of(head * head_dim, head_dim), head_dim)
        part = back[at % here]
        grad_q_ref[place, :] = turned(part[at // here, 0:head_dim, :])
        grad_k_ref[place, :] = turned(part[at // here, head_dim : 2 * head_dim, :])
        grad_v_ref[place, :] = part[at // here, 2 * head_dim : 3 * head_dim, :]
    rows = [ref[...].T for ref in (grad_q_ref, grad_k_ref, grad_v_ref)]

    @pl.when(step == 0)
    def _():
        total[...] = jnp.zeros_like(total)

    depth = query_ref.shape[2]
    for shard in range(query_ref.shape[0]):
        made = dot(rows[0], query_ref[shard]) + dot(rows[1], key_ref[shard]) + dot(rows[2], value_ref[shard])
        total[:, shard * depth : (shard + 1) * depth] += made

    @pl.when(step == pl.num_programs(0) - 1)
    def _():
        inputs = tokens_ref[0, 0].astype(F32)
        inverse = lax.rsqrt(jnp.mean(inputs * inputs, axis=-1, keepdims=True) + EPSILON)
        scaled = total[...] * gain_ref[...]
        mean = jnp.mean(scaled * inputs, axis=-1, keepdims=True)
        grad = inverse * scaled - inputs * (inverse * inverse * inverse) * mean
        out_ref[0, 0] = (grad_res_ref[...] + grad).astype(BF16)
        gain_out_ref[...] = jnp.sum(total[...] * inputs * inverse, axis=0, keepdims=True)


def final_part(core, tokens, unit, grad_res, gain, weights, cosine, sine, back, head_dim, output):
    width, model = tokens.shape[2:]
    here = len(back)
    steps = model // 256

    def fixed(a):
        return pl.BlockSpec(a.shape, lambda c: (0,) * a.ndim)

    token_spec = pl.BlockSpec((1, 1, width, model), lambda c: unit + (0, 0))
    shards, _, depth = weights.shape
    weight_specs = [
        pl.BlockSpec((shards, 256, depth), lambda c, i=i: (0, i * steps + c, 0)) for i in range(3)
    ]
    row_spec = pl.BlockSpec((256, width), lambda c: (c, 0))
    operands = [core, tokens, grad_res, gain, weights, weights, weights, cosine, sine, *back]
    in_specs = [
        pl.BlockSpec(memory_space=pltpu.SMEM), token_spec, fixed(grad_res), fixed(gain), *weight_specs,
        fixed(cosine), fixed(sine),
    ] + [
        pl.BlockSpec((256 // head_dim // here, 3 * head_dim, width), lambda c: (c, 0, 0)) for _ in back
    ]
    aliases = {}
    if output is not None:
        aliases = {len(operands): 0}
        operands.append(output)
        in_specs.append(pl.BlockSpec(memory_space=pl.ANY))
    struct = jax.ShapeDtypeStruct
    return pl.pallas_call(
        functools.partial(final_kernel, (here, head_dim, output is not None)),
        grid=(steps,),
        in_specs=in_specs,
        out_specs=[token_spec, row_spec, row_spec, row_spec, pl.BlockSpec((1, model), lambda c: (0, 0))],
        out_shape=[
            struct(tokens.shape, BF16), struct((model, width), BF16), struct((model, width), BF16),
            struct((model, width), BF16), struct((1, model), F32),
        ],
        scratch_shapes=[pltpu.VMEM((width, model), F32)],
        input_output_aliases=aliases,
        compiler_params=pltpu.CompilerParams(vmem_limit_bytes=62 << 20),
        cost_estimate=pl.CostEstimate(
            flops=6 * width * model * model // COVER, bytes_accessed=12 * model * model, transcendentals=0
        ),
        name="final_part",
    )(*operands)


def picked_kernel(units, rows, places, flipped, split, table_ref, *refs):
    weights = len(places)
    lefts = refs[0:units]
    rights = refs[units : units * (1 + weights)]
    outs = refs[units * (1 + weights) : units * (1 + weights) + weights * split]
    picked = refs[units * (1 + weights) + weights * split :]

    @pl.when(pl.program_id(0) == 0)
    def _():
        for w, (start, size) in enumerate(places):
            for p in range(size):
                at = pl.ds(pl.multiple_of(table_ref[start + p] * rows, rows), rows)
                for u in range(units):
                    picked[w * units + u][p * rows : (p + 1) * rows, :] = lefts[u][at, :]

    for w in range(weights):
        total = None
        for u in range(units):
            right = rights[w * units + u][...]
            left = picked[w * units + u][...]
            made = contract(left, right, 1, 1) if flipped else dot(left, right)
            total = made if total is None else total + made
        height = total.shape[0] // split
        for i in range(split):
            outs[w * split + i][...] = total[i * height : (i + 1) * height].astype(BF16)


def picked_grads(table, places, lefts, rights, rows, flipped, split, block, name):
    units = len(lefts)
    width = lefts[0].shape[1]
    columns = rights[0].shape[0 if flipped else 1]
    in_specs = [pl.BlockSpec(a.shape, lambda n, *_: (0, 0)) for a in lefts]
    for a in rights:
        if flipped:
            in_specs.append(pl.BlockSpec((block, width), lambda n, *_: (n, 0)))
        else:
            in_specs.append(pl.BlockSpec((width, block), lambda n, *_: (0, n)))
    heights = [size * rows for _, size in places]
    return pl.pallas_call(
        functools.partial(picked_kernel, units, rows, places, flipped, split),
        grid_spec=pltpu.PrefetchScalarGridSpec(
            num_scalar_prefetch=1,
            grid=(columns // block,),
            in_specs=in_specs,
            out_specs=[
                pl.BlockSpec((height // split, block), lambda n, *_: (0, n)) for height in heights for _ in range(split)
            ],
            scratch_shapes=[pltpu.VMEM((height, width), BF16) for height in heights for _ in lefts],
        ),
        out_shape=[
            jax.ShapeDtypeStruct((height // split, columns), BF16) for height in heights for _ in range(split)
        ],
        compiler_params=pltpu.CompilerParams(vmem_limit_bytes=62 << 20),
        cost_estimate=pl.CostEstimate(
            flops=2 * units * sum(heights) * width * columns // COVER,
            bytes_accessed=4 * sum(heights) * columns,
            transcendentals=0,
        ),
        name=name,
    )(table, *lefts, *rights)


def weights_kernel(units, *refs):
    out_ref = refs[-1]
    total = dot(refs[0][...], refs[units][...])
    for u in range(1, units):
        total += dot(refs[u][...], refs[units + u][...])
    out_ref[...] = total.astype(BF16).reshape(out_ref.shape)


def weight_grad(lefts, rights, by_left, out_struct, out_spec, steps, into, name):
    units = len(lefts)

    def fixed(a):
        return pl.BlockSpec(a.shape, lambda n: (0, 0))

    def left_spec(a):
        return pl.BlockSpec((a.shape[0] // steps, a.shape[1]), lambda n: (n, 0))

    def right_spec(a):
        return pl.BlockSpec((a.shape[0], a.shape[1] // steps), lambda n: (0, n))

    operands = list(lefts) + list(rights)
    if by_left:
        in_specs = [left_spec(a) for a in lefts] + [fixed(a) for a in rights]
    else:
        in_specs = [fixed(a) for a in lefts] + [right_spec(a) for a in rights]
    aliases = {}
    if into is not None:
        aliases = {len(operands): 0}
        operands.append(into)
        in_specs.append(pl.BlockSpec(memory_space=pl.ANY))
    return pl.pallas_call(
        functools.partial(weights_kernel, units),
        grid=(steps,),
        in_specs=in_specs,
        out_specs=out_spec,
        out_shape=out_struct,
        input_output_aliases=aliases,
        compiler_params=pltpu.CompilerParams(vmem_limit_bytes=62 << 20),
        cost_estimate=pl.CostEstimate(
            flops=2 * units * lefts[0].shape[0] * lefts[0].shape[1] * rights[0].shape[1] // COVER,
            bytes_accessed=2 * lefts[0].shape[0] * rights[0].shape[1],
            transcendentals=0,
        ),
        name=name,
    )(*operands)


def reduce_kernel(orders, count, *refs):
    streams = len(orders)
    rounds = len(orders[0])
    ins, vec_ref = refs[:streams], refs[streams]
    outs, vec_out = refs[streams + 1 : 2 * streams + 1], refs[2 * streams + 1]
    rest = refs[2 * streams + 2 :]
    works, arrivals = rest[:streams], rest[streams : 2 * streams]
    vec_work, vec_arrival, send_sem, recv_sem, vec_send, vec_recv = rest[2 * streams :]
    shard, seq = lax.axis_index("shard"), lax.axis_index("seq")

    def partner(mask):
        if mask >= count:
            step = mask // count
            return (shard + step * (1 - 2 * (shard // step % 2)), seq)
        return (shard, seq + mask * (1 - 2 * (seq // mask % 2)))

    barrier = pltpu.get_barrier_semaphore()
    for mask in orders[0]:
        pl.semaphore_signal(
            barrier, inc=1, device_id=partner(mask), device_id_type=pl.DeviceIdType.MESH
        )
    pl.semaphore_wait(barrier, rounds)

    height = ins[0].shape[0]
    halves = [height >> (r + 1) for r in range(rounds)]
    starts = [sum(halves[:r]) for r in range(rounds)]

    def copy_of(s, r):
        source = ins[s] if r == 0 else works[s]
        return pltpu.make_async_remote_copy(
            src_ref=source.at[pl.ds(halves[r], halves[r])],
            dst_ref=arrivals[s].at[pl.ds(starts[r], halves[r])],
            send_sem=send_sem.at[s, r],
            recv_sem=recv_sem.at[s, r],
            device_id=partner(orders[s][r]),
            device_id_type=pl.DeviceIdType.MESH,
        )

    def vec_copy(r):
        return pltpu.make_async_remote_copy(
            src_ref=vec_ref if r == 0 else vec_work.at[r - 1],
            dst_ref=vec_arrival.at[r],
            send_sem=vec_send.at[r],
            recv_sem=vec_recv.at[r],
            device_id=partner(orders[0][r]),
            device_id_type=pl.DeviceIdType.MESH,
        )

    for s in range(streams):
        copy_of(s, 0).start()
    vec_copy(0).start()
    for r in range(rounds):
        for s in range(streams):
            copy_of(s, r).wait_recv()
            source = ins[s] if r == 0 else works[s]
            size = halves[r]

            def added(low, high):
                mine = source[low:high].astype(F32)
                return mine + arrivals[s][starts[r] + low : starts[r] + high].astype(F32)

            if r == rounds - 1:
                outs[s][...] = added(0, size)
            else:
                works[s][size // 2 : size] = added(size // 2, size).astype(BF16)
                copy_of(s, r + 1).start()
                works[s][0 : size // 2] = added(0, size // 2).astype(BF16)
        vec_copy(r).wait_recv()
        before = vec_ref[...] if r == 0 else vec_work[r - 1]
        if r == rounds - 1:
            vec_out[...] = before + vec_arrival[r]
        else:
            vec_work[r] = before + vec_arrival[r]
            vec_copy(r + 1).start()
    for r in range(rounds):
        for s in range(streams):
            copy_of(s, r).wait_send()
        vec_copy(r).wait_send()


def reduce_rows(parts, vector, orders, count):
    streams = len(parts)
    rounds = len(orders[0])
    height, columns = parts[0].shape
    rows = height >> rounds
    vmem = pl.BlockSpec(memory_space=pltpu.VMEM)
    return pl.pallas_call(
        functools.partial(reduce_kernel, orders, count),
        in_specs=[vmem] * (streams + 1),
        out_specs=[vmem] * (streams + 1),
        out_shape=[jax.ShapeDtypeStruct((rows, columns), F32)] * streams
        + [jax.ShapeDtypeStruct(vector.shape, F32)],
        scratch_shapes=[pltpu.VMEM((height // 2, columns), BF16) for _ in parts]
        + [pltpu.VMEM((height - rows, columns), BF16) for _ in parts]
        + [
            pltpu.VMEM((rounds - 1,) + vector.shape, F32),
            pltpu.VMEM((rounds,) + vector.shape, F32),
            pltpu.SemaphoreType.DMA((streams, rounds)),
            pltpu.SemaphoreType.DMA((streams, rounds)),
            pltpu.SemaphoreType.DMA((rounds,)),
            pltpu.SemaphoreType.DMA((rounds,)),
        ],
        compiler_params=pltpu.CompilerParams(
            collective_id=0, has_side_effects=True, vmem_limit_bytes=62 << 20
        ),
        name="reduce_rows",
    )(*parts, vector)


def on_device(
    tokens, cotangent, lengths, variates, positions, attn_gain, w_query, w_key, w_value, w_out,
    bias_table, ffn_gain, w_gate, w_up, w_down,
):
    micro, seqs, width, model = tokens.shape
    heads = bias_table.shape[0]
    head_dim = model // heads
    count = lax.axis_size("seq")
    here = heads // count
    ffn = w_gate.shape[1]
    devices = lax.axis_size("shard") * count
    seq_index = lax.axis_index("seq")
    units = [(m, s) for m in range(micro) for s in range(seqs)]
    swap = here == 2 and len(units) == 2 and lax.axis_size("shard") % 2 == 0
    core = (lax.axis_index("shard") % 2 if swap else jnp.int32(0)).astype(jnp.int32).reshape(1)
    heads_here = 1 if swap else here
    first_head = seq_index * here + core[0]
    bias_here = lax.dynamic_slice_in_dim(bias_table, first_head, heads_here, 0)
    attn_row, ffn_row = attn_gain[None, :], ffn_gain[None, :]

    def gather(weight):
        return lax.all_gather(weight, "shard", axis=0, tiled=True)

    def exchange(values):
        return lax.all_to_all(values, "seq", split_axis=0, concat_axis=0, tiled=True)

    def after(value, *before):
        return lax.optimization_barrier((value,) + before)[0]

    attn_rows = turn_weights(w_query, w_key, w_value)
    attn_joined = lax.all_gather(attn_rows, "shard", axis=0, tiled=False)
    ffn_weights = [gather(w_out), gather(w_gate), gather(w_up), gather(w_down)]

    def permute(value, mask):
        return lax.ppermute(value, ("shard", "seq"), [(i, i ^ mask) for i in range(devices)])

    def cross(value):
        return permute(value, count)

    lengths_of = [lengths, cross(lengths)] if swap else [lengths] * here
    ids_own = lax.all_gather(variates, "seq", axis=0, tiled=False)
    ids_of = [ids_own, cross(ids_own)] if swap else [ids_own] * here
    attn_joined = after(attn_joined, *ids_of)

    def ids_rows(u, h):
        m, s = units[u]
        return ids_of[h][:, m, s].astype(F32)[:, None, :]

    packed_list, flats, tables = [], [], []

    def run_project(u, token):
        m, s = units[u]
        cosine, sine = rotary_tables(positions[m, s], head_dim // 2)
        flat, *packed = project(
            core, tokens, (m, s), after(attn_row, *token), attn_joined, cosine, sine, count, here, head_dim,
            swap,
        )
        flats.append(flat)
        tables.append((cosine, sine))
        packed_list.append(packed)

    sent = {}
    mixed_now = [None] * len(units)
    sums = {}
    mixed_tok = {}
    crossed, mixed_part, mixed_cross, heads_cross, back_cross = {}, {}, {}, {}, {}
    middle = [None] * len(units)
    grad_heads = {}
    state = {"output": None, "grads": None}
    packed_grads = {}
    returned = {}
    bias_terms = {}
    finals = [None] * len(units)

    def length_of(u, h, token):
        m, s = units[u]
        return after(lengths_of[h][m, s].reshape(1), *token)

    def inputs_of(u, h):
        return (crossed[u] if swap and h == 1 else sent[u, h]), ids_rows(u, h)

    def run_forward(u, h, token):
        made, sums[u, h] = attend_forward(
            *inputs_of(u, h), length_of(u, h, token), bias_here, None if swap else mixed_now[u],
            0 if swap else h, heads_here, head_dim,
        )
        if swap:
            mixed_part[u, h] = made
            if h == 1:
                mixed_cross[u] = cross(made)
        else:
            mixed_now[u] = made
        return sums[u, h]

    def run_middle(u, token):
        m, s = units[u]
        info = jnp.stack([lengths[m, s], seq_index * width, core[0]]).astype(jnp.int32)
        state["output"], mixed_tok[u], *middle[u] = middle_part(
            after(info, *token), mixed_tok[u], tokens, cotangent, (m, s), ffn_weights, ffn_row, head_dim,
            state["output"],
        )
        return middle[u][8]

    def run_backward(u, h, token):
        if swap:
            token = token + ((heads_cross[1],) if (u, h) == (0, 1) else ())
            grad = grad_heads[u] if h == 0 else heads_cross[u]
            mixed = mixed_part[u, h]
        else:
            grad, mixed = grad_heads[u], mixed_now[u]
        packed_grads[u, h], both = attend_backward(
            *inputs_of(u, h), grad, mixed, sums[u, h], length_of(u, h, token), bias_here,
            0 if swap else h, head_dim,
        )
        if swap and h == 1:
            back_cross[u] = cross(packed_grads[u, h])
        bias_terms[u, h] = both
        return both

    def run_final(u, token):
        m, s = units[u]
        cosine, sine = tables[u]
        state["grads"], *finals[u] = final_part(
            core, tokens, (m, s), middle[u][5], after(attn_row, *token), attn_joined, cosine, sine,
            [returned[u, h] for h in range(here)], head_dim, state["grads"],
        )
        return finals[u][3]

    rows = model // devices
    fold = ffn // model
    tall = ffn // devices
    seq_masks = [1 << i for i in range(count.bit_length() - 1)]
    shard_masks = [count << i for i in range((devices // count).bit_length() - 1)]
    spread = shard_masks[1:]
    orders = (
        shard_masks[:1] + spread + seq_masks,
        shard_masks[:1] + seq_masks[:1] + spread + seq_masks[1:],
        shard_masks[:1] + seq_masks[1:2] + seq_masks[:1] + spread + seq_masks[2:],
    )
    direct = rows % 16 == 0 and devices == 1 << len(orders[0])

    def places_of(order):
        marks = []
        for p in range(devices):
            bits = [p >> (len(order) - 1 - i) & 1 for i in range(len(order))]
            marks.append(sum(mask for bit, mask in zip(bits, order) if bit))
        me = lax.axis_index("shard") * count + seq_index
        return me.astype(jnp.int32) ^ jnp.array(marks, jnp.int32)

    def column(index):
        return [item[index] for item in middle]

    def run_weights(token):
        if not direct:
            return [
                sum(dot(left, right) for left, right in zip(lefts, rights)).astype(BF16)
                for lefts, rights in (
                    (column(0), column(2)), (column(0), column(3)), (column(1), column(4)),
                    ([mixed_tok[u] for u in range(len(units))], column(6)),
                )
            ]
        part = ffn // fold
        narrow = model // fold
        spare = -(-(2 * part + narrow) // 384) * 384
        struct = jax.ShapeDtypeStruct((devices, fold, rows, spare), BF16)
        down = pl.BlockSpec((512 // tall, fold, rows, model), lambda n: (n, 0, 0, 0))
        gate = pl.BlockSpec((devices, 1, rows, part), lambda n: (0, n, 0, 1))
        out = pl.BlockSpec((devices, 1, rows, narrow), lambda n: (0, n, 0, 2 * part // narrow))
        table = after(places_of(orders[0]), *token)
        up = picked_grads(table, [(0, devices)], column(0), column(3), rows, False, 2, 1024, "up_grad")
        holder["streams"] = [[up[0], permute(up[1], orders[0][0]), orders[0][1:]]]
        firsts = [after(middle[0][4], up[0])] + [item[4] for item in middle[1:]]
        terms = weight_grad(column(1), firsts, True, struct, down, ffn // 512, None, "down_grad")
        landed = (holder["streams"][0][1],) + ((heads_cross[0],) if swap else ())
        rights = [after(middle[0][2], *holder["flying"], *landed)] + [item[2] for item in middle[1:]]
        terms = weight_grad(column(0), rights, False, struct, gate, fold, terms, "gate_grad")
        mixed_all = [mixed_tok[u] for u in range(len(units))]
        terms = weight_grad(mixed_all, column(6), False, struct, out, fold, terms, "out_grad")
        terms = terms.reshape(ffn, spare)
        holder["owned"] = lax.psum_scatter(terms, ("shard", "seq"), scatter_dimension=0, tiled=True)
        return terms

    def wide_sum(a, b):
        return a.astype(F32) + b.astype(F32)

    def advance(token):
        out = ()
        if not direct:
            return out
        for stream in holder["streams"]:
            keep, came, masks = stream
            if not masks:
                continue
            keep = after(keep, *token)
            half = keep.shape[0] // 2
            send = wide_sum(keep[half:], came[half:]).astype(BF16)
            stream[0] = wide_sum(keep[:half], came[:half]).astype(BF16)
            stream[1] = permute(send, masks[0])
            stream[2] = masks[1:]
            out = out + (send, stream[0])
        return out

    holder = {}

    def weights_work(token):
        holder["terms"] = run_weights(token)
        return holder["terms"]

    def send_packed(u, h):
        def keep(moved):
            sent[u, h] = moved
            if swap and h == 1:
                crossed[u] = cross(moved)

        return lambda: packed_list[u][h], keep

    def send_mixed(u):
        def keep(moved):
            mixed_tok[u] = moved.reshape(model, width)

        if not swap:
            return lambda: mixed_now[u], keep
        return lambda: jnp.concatenate([mixed_part[u, 0], mixed_cross[u]], axis=1), keep

    def send_heads(u):
        def keep(moved):
            grad_heads[u] = moved
            if swap:
                heads_cross[u] = cross(moved[:, head_dim:])

        return lambda: middle[u][7].reshape(count, here * head_dim, width), keep

    def send_back(u, h):
        def keep(moved):
            returned[u, h] = moved

        return lambda: back_cross[u] if swap and h == 1 else packed_grads[u, h], keep

    def work_project(u):
        def work(token):
            run_project(u, token)
            return flats[u]

        return work

    def work(function, *args):
        return lambda token: function(*args, token)

    total = len(units)
    order = [(u, h) for u in range(total) for h in range(here)]
    if swap:
        steps = [
            (work_project(0), None),
            (work_project(1), send_packed(0, 1)),
            (work(run_forward, 0, 1), send_packed(0, 0)),
            (work(run_forward, 0, 0), send_packed(1, 1)),
            (work(run_forward, 1, 1), send_packed(1, 0)),
            (work(run_forward, 1, 0), send_mixed(0)),
            (work(run_middle, 0), send_mixed(1)),
            (work(run_middle, 1), send_heads(0)),
            (weights_work, send_heads(1)),
            (work(run_backward, 0, 0), None),
            (work(run_backward, 0, 1), send_back(0, 0)),
            (work(run_backward, 1, 0), send_back(0, 1)),
            (work(run_backward, 1, 1), send_back(1, 0)),
            (work(run_final, 0), send_back(1, 1)),
            (work(run_final, 1), None),
        ]
    else:
        steps = [(work_project(u), None) for u in range(total)]
        steps += [(None, send_packed(*at)) for at in order]
        for u in range(total):
            steps += [(work(run_forward, u, h), None) for h in range(here)]
            steps += [(None, send_mixed(u))]
        for u in range(total):
            steps += [(work(run_middle, u), None), (None, send_heads(u))]
        steps += [(weights_work, None)]
        for at in order:
            steps += [(work(run_backward, *at), None), (None, send_back(*at))]
        steps += [(work(run_final, u), None) for u in range(total)]

    late = [task for task, _ in steps[-2:]]
    token = ()
    for task, send in steps:
        done = ()
        moved = None
        if "streams" in holder:
            leaving = advance(token)
            token = token if task in late else token + leaving
        if send is not None:
            moved = exchange(after(send[0](), *token))
            done = (moved,)
        holder["flying"] = done
        if task is not None:
            done = done + (task(token),)
        if send is not None:
            send[1](after(moved, *done[1:]))
        token = done
    acc_bias = jnp.concatenate(
        [sum(bias_terms[u, h] for u in range(total))[0:1, 0:2] for h in range(here)], axis=0
    )
    if swap:
        acc_bias = acc_bias[0:1] + acc_bias[1:2]
    bias_full = lax.dynamic_update_slice(
        jnp.zeros((heads, 2), F32), acc_bias, (first_head, jnp.int32(0))
    )
    gain_attn = sum(item[3][0] for item in finals)
    gain_ffn = sum(item[8][0] for item in middle)
    if direct:
        while holder["streams"][0][2]:
            advance(token)
        keep, came, _ = holder["streams"][0]
        up_own = wide_sum(after(keep, *token), came)
        flats[0] = after(flats[0], up_own)
        owned, part = holder["owned"], ffn // fold

        def joined(start, size):
            piece = owned[:, start : start + size].reshape(fold, rows, size)
            return jnp.swapaxes(piece, 0, 1).reshape(rows, fold * size).astype(F32)

        down_own = owned[:, :part].astype(F32)
        gate_own, out_own = joined(part, part), joined(2 * part, model // fold)
        table = jnp.concatenate([places_of(order) for order in orders])
        attn_terms = picked_grads(
            table, [(i * devices, devices) for i in range(3)], flats,
            [item[i] for i in range(3) for item in finals], rows, True, 1, 256, "attn_grads",
        )
        flat = jnp.concatenate([gain_attn, gain_ffn, bias_full.reshape(-1)])
        tiles = -(-flat.shape[0] // 1024) * 8
        flat = jnp.pad(flat, (0, tiles * 128 - flat.shape[0])).reshape(tiles, 128)
        query_own, key_own, value_own, flat = reduce_rows(list(attn_terms), flat, orders, count)
        flat = flat.reshape(-1)
        gain_attn, gain_ffn = flat[:model], flat[model : 2 * model]
        bias_full = flat[2 * model : 2 * model + 2 * heads].reshape(heads, 2)
    else:

        def scatter(value):
            owned = lax.psum_scatter(value, ("shard", "seq"), scatter_dimension=0, tiled=True)
            return owned.astype(F32)

        gate_own, up_own, down_own, out_own = [scatter(value) for value in holder["terms"]]
        query_own, key_own, value_own = [
            scatter(
                sum(contract(flat, item[i], 1, 1) for flat, item in zip(flats, finals)).astype(BF16)
            )
            for i in range(3)
        ]
        gain_attn, gain_ffn, bias_full = lax.psum(
            (gain_attn, gain_ffn, bias_full), ("shard", "seq")
        )
    return (
        state["output"], state["grads"], gain_attn, query_own, key_own, value_own, out_own,
        bias_full, gain_ffn, gate_own, up_own, down_own,
    )


def solution(mesh):
    token_spec = P(None, "shard", "seq", None)
    row_spec = P("shard", None)
    in_specs = (
        token_spec, token_spec, P(None, "shard"), P(None, "shard", "seq"), P(None, "shard", "seq"),
        P(), row_spec, row_spec, row_spec, row_spec, P(), P(), row_spec, row_spec, row_spec,
    )
    owned = P(("shard", "seq"), None)
    out_specs = (
        token_spec, token_spec, P(), owned, owned, owned, owned, P(), P(), owned, owned, owned,
    )
    return jax.shard_map(
        on_device, mesh=mesh, in_specs=in_specs, out_specs=out_specs, check_vma=False
    )
```

```python
import functools
import math

import jax
import jax.numpy as jnp
from jax import lax
from jax.experimental import pallas as pl
from jax.experimental.pallas import tpu as pltpu
from jax.sharding import PartitionSpec as P

EPSILON = 1e-06
ROTARY_BASE = 10000.0
LOG2E = 1.4426950408889634
LN2 = 0.6931471805599453
CLASSES = 8
COVER = 16
EXTRA = 32
MASKED = -1.5e9
FAR = 1e30
F32 = jnp.float32
BF16 = jnp.bfloat16


def dot(a, b):
    return jnp.dot(a, b, preferred_element_type=F32)


def contract(a, b, da, db):
    return lax.dot_general(a, b, (((da,), (db,)), ((), ())), preferred_element_type=F32)


def pieces(x):
    high = x.astype(BF16).astype(F32)
    rest = x - high
    mid = rest.astype(BF16).astype(F32)
    low = (rest - mid).astype(BF16).astype(F32)
    return high, mid, low


def one_hot(row):
    classes = lax.broadcasted_iota(jnp.int32, (CLASSES, row.shape[1]), 0).astype(F32)
    return jnp.where(classes == row, 1.0, 0.0)


def rows_of(values, width):
    index = lax.broadcasted_iota(jnp.int32, (8, width), 0)
    out = jnp.zeros((8, width), F32)
    for at, value in enumerate(values):
        out = jnp.where(index == at, value, out)
    return out


def key_extra(row, start, length, other, same):
    width = row.shape[1]
    hot = one_hot(row)
    step = pieces(jnp.full((1, width), same - other, F32))
    base = pieces(jnp.full((1, width), other, F32))
    index = start + lax.broadcasted_iota(jnp.int32, (1, width), 1)
    mask = jnp.where(index < length, 0.0, MASKED)
    tail = rows_of(base + (mask, 1.0, 1.0, 1.0), width)
    return jnp.concatenate([hot * step[0], hot * step[1], hot * step[2], tail], axis=0).astype(BF16)


def query_extra(row, shift):
    hot = one_hot(row)
    tail = rows_of((1.0, 1.0, 1.0, 1.0) + shift, row.shape[1])
    return jnp.concatenate([hot, hot, hot, tail], axis=0).astype(BF16)


def forward_kernel(
    shape, len_ref, bias_ref, x_ref, ids_ref, *rest
):
    local, head_dim, block, aliased = shape
    if aliased:
        rest = rest[1:]
    mixed_ref, lse_ref, keys, vals, query, score, peak, total = rest
    count, _, width = x_ref.shape
    sub = block // width
    step = pl.program_id(0)
    length = len_ref[0]
    other = bias_ref[local, 0] * LOG2E
    same = bias_ref[local, 1] * LOG2E

    @pl.when(step == 0)
    def _():
        for b in range(count):
            at = pl.ds(b * width, width)
            row = ids_ref[b, 0:1, :].astype(F32)
            extra = key_extra(row, b * width, length, other, same)
            full = jnp.concatenate([x_ref[b, head_dim : 2 * head_dim, :], extra], axis=0)
            keys[at, :] = full.T
            vals[0:head_dim, at] = x_ref[b, 2 * head_dim : 3 * head_dim, :]
        vals[head_dim:, :] = jnp.ones((16, vals.shape[1]), BF16)

    used = pl.cdiv(length, block)
    inside = step * block < length

    @pl.when(jnp.logical_not(inside))
    def _():
        mixed_ref[...] = jnp.zeros_like(mixed_ref)
        lse_ref[...] = jnp.full(lse_ref.shape, FAR, F32)

    @pl.when(inside)
    def _():
        for b in range(sub):
            at = slice(b * width, (b + 1) * width)
            row = ids_ref[step * sub + b, 0:1, :].astype(F32)
            query[0:head_dim, at] = x_ref[step * sub + b, 0:head_dim, :]
            query[head_dim:, at] = query_extra(row, (0.0, 0.0, 0.0))
        peak[...] = jnp.full(peak.shape, -FAR, F32)
        total[...] = jnp.zeros_like(total)

        def span(j):
            return pl.ds(pl.multiple_of(j * block, block), block)

        def scores_of(j):
            return dot(keys[span(j), :], query[...])

        def one(j, now, ahead):
            if ahead:
                score[1 - now] = scores_of(j + 1)
            current = score[now]
            before = peak[...]
            top = jnp.maximum(before, jnp.max(current, axis=0, keepdims=True))
            weight = jnp.exp2(current - top).astype(BF16)
            peak[...] = top
            total[...] = total[...] * jnp.exp2(before - top) + dot(vals[:, span(j)], weight)

        score[0] = scores_of(0)
        pairs = (used - 1) // 2

        def pair(j, carry):
            one(2 * j, 0, True)
            one(2 * j + 1, 1, True)
            return carry

        lax.fori_loop(0, pairs, pair, 0)
        last = 2 * pairs

        @pl.when(used - last == 1)
        def _():
            one(last, 0, False)

        @pl.when(used - last == 2)
        def _():
            one(last, 0, True)
            one(last + 1, 1, False)

        mass = total[head_dim : head_dim + 1, :]
        mixed = (total[0:head_dim, :] / mass).astype(BF16)
        for b in range(sub):
            mixed_ref[b] = mixed[:, b * width : (b + 1) * width]
        lse_ref[0] = peak[...] + jnp.log2(mass)


def attend_forward(x, ids, length, bias, mixed, local, heads_here, head_dim):
    count, rows, width = x.shape
    block = max(width, 512)
    seq_len = count * width
    blocks = seq_len // block
    depth = head_dim + EXTRA
    whole = pl.BlockSpec((count, rows, width), lambda i, *_: (0, 0, 0))
    operands = [length, bias, x, ids]
    in_specs = [whole, pl.BlockSpec((count, 1, width), lambda i, *_: (0, 0, 0))]
    aliases = {}
    if mixed is not None:
        operands.append(mixed)
        in_specs.append(pl.BlockSpec(memory_space=pl.ANY))
        aliases = {4: 0}
    return pl.pallas_call(
        functools.partial(forward_kernel, (local, head_dim, block, mixed is not None)),
        grid_spec=pltpu.PrefetchScalarGridSpec(
            num_scalar_prefetch=2,
            grid=(blocks,),
            in_specs=in_specs,
            out_specs=[
                pl.BlockSpec((block // width, head_dim, width), lambda i, *_: (i, local, 0)),
                pl.BlockSpec((1, 1, block), lambda i, *_: (i, 0, 0)),
            ],
            scratch_shapes=[
                pltpu.VMEM((seq_len, depth), BF16),
                pltpu.VMEM((head_dim + 16, seq_len), BF16),
                pltpu.VMEM((depth, block), BF16),
                pltpu.VMEM((2, block, block), F32),
                pltpu.VMEM((1, block), F32),
                pltpu.VMEM((head_dim + 16, block), F32),
            ],
        ),
        out_shape=[
            jax.ShapeDtypeStruct((count, heads_here * head_dim, width), BF16),
            jax.ShapeDtypeStruct((blocks, 1, block), F32),
        ],
        input_output_aliases=aliases,
        compiler_params=pltpu.CompilerParams(vmem_limit_bytes=62 << 20),
        cost_estimate=pl.CostEstimate(
            flops=8 * seq_len * seq_len * 256 // COVER,
            bytes_accessed=x.size * 4,
            transcendentals=0,
        ),
        name="attend_forward",
    )(*operands)


def backward_kernel(
    shape, len_ref, bias_ref, x_ref, ids_ref, grad_ref, mixed_ref, lse_ref, out_ref, bias_out_ref,
    keys, keys_flat, vals, query, grads, query_rows, grad_rows, acc_keys, acc_vals, acc_query,
):
    local, head_dim, block = shape
    count, _, width = x_ref.shape
    sub = block // width
    step = pl.program_id(0)
    length = len_ref[0]
    other = bias_ref[local, 0] * LOG2E
    same = bias_ref[local, 1] * LOG2E

    @pl.when(step == 0)
    def _():
        ones = jnp.ones((16, width), BF16)
        for b in range(count):
            at = pl.ds(b * width, width)
            row = ids_ref[b, 0:1, :].astype(F32)
            extra = key_extra(row, b * width, length, other, same)
            here = x_ref[b, head_dim : 2 * head_dim, :]
            keys[at, :] = jnp.concatenate([here, extra], axis=0).T
            keys_flat[:, at] = here
            vals[at, :] = jnp.concatenate([x_ref[b, 2 * head_dim : 3 * head_dim, :], ones], axis=0).T
        acc_keys[...] = jnp.zeros_like(acc_keys)
        acc_vals[...] = jnp.zeros_like(acc_vals)

    used = pl.cdiv(length, block)
    inside = step * block < length

    @pl.when(jnp.logical_not(inside))
    def _():
        for b in range(sub):
            out_ref[step * sub + b, 0:head_dim, :] = jnp.zeros((head_dim, width), BF16)

    @pl.when(inside)
    def _():
        for b in range(sub):
            at = slice(b * width, (b + 1) * width)
            here = step * sub + b
            row = ids_ref[here, 0:1, :].astype(F32)
            shift = pieces(-lse_ref[step][:, at])
            grad = grad_ref[here]
            delta = jnp.sum(grad.astype(F32) * mixed_ref[here].astype(F32), axis=0, keepdims=True)
            query[0:head_dim, at] = x_ref[here, 0:head_dim, :]
            query[head_dim:, at] = query_extra(row, shift)
            grads[0:head_dim, at] = grad
            tail = rows_of(pieces(-delta), width)
            grads[head_dim:, at] = jnp.concatenate([tail, jnp.zeros_like(tail)], axis=0).astype(BF16)
        query_rows[...] = query[...].T
        grad_rows[...] = grads[...].T
        acc_query[...] = jnp.zeros_like(acc_query)

        def one(j):
            at = pl.ds(pl.multiple_of(j * block, block), block)
            probs = jnp.exp2(dot(keys[at, :], query[...]))
            grad_probs = dot(vals[at, :], grads[...])
            grad_scores = (probs * grad_probs).astype(BF16)
            acc_vals[at, :] += dot(probs.astype(BF16), grad_rows[...])
            acc_keys[at, :] += dot(grad_scores, query_rows[...])
            acc_query[...] += dot(keys_flat[:, at], grad_scores)

        def pair(j, carry):
            one(2 * j)
            one(2 * j + 1)
            return carry

        lax.fori_loop(0, used // 2, pair, 0)

        @pl.when(used % 2 == 1)
        def _():
            one(used - 1)

        grad_query = (acc_query[...] * (1.0 / math.sqrt(head_dim))).astype(BF16)
        for b in range(sub):
            out_ref[step * sub + b, 0:head_dim, :] = grad_query[:, b * width : (b + 1) * width]

    @pl.when(step == pl.num_programs(0) - 1)
    def _():
        same_total = jnp.zeros((CLASSES, width), F32)
        all_total = jnp.zeros((CLASSES, width), F32)
        for b in range(count):
            at = pl.ds(b * width, width)
            row = ids_ref[b, 0:1, :].astype(F32)
            flat = acc_keys[at, :].T
            out_ref[b, head_dim : 2 * head_dim, :] = (flat[0:head_dim] * LN2).astype(BF16)
            out_ref[b, 2 * head_dim : 3 * head_dim, :] = acc_vals[at, :].T[0:head_dim].astype(BF16)
            by_class = flat[head_dim : head_dim + CLASSES]
            all_total += by_class
            same_total += by_class * one_hot(row)
        same_sum = jnp.sum(same_total, keepdims=True)
        other_sum = jnp.sum(all_total, keepdims=True) - same_sum
        lane = lax.broadcasted_iota(jnp.int32, (8, 128), 1)
        bias_out_ref[...] = jnp.where(lane == 0, other_sum, jnp.where(lane == 1, same_sum, 0.0))


def attend_backward(x, ids, grad, mixed, lse, length, bias, local, head_dim):
    count, rows, width = x.shape
    blocks, _, block = lse.shape
    seq_len = count * width
    depth = head_dim + EXTRA

    def whole(a):
        return pl.BlockSpec(a.shape, lambda i, *_: (0,) * a.ndim)

    head_spec = pl.BlockSpec((count, head_dim, width), lambda i, *_: (0, local, 0))
    return pl.pallas_call(
        functools.partial(backward_kernel, (local, head_dim, block)),
        grid_spec=pltpu.PrefetchScalarGridSpec(
            num_scalar_prefetch=2,
            grid=(blocks,),
            in_specs=[
                whole(x),
                pl.BlockSpec((count, 1, width), lambda i, *_: (0, 0, 0)),
                head_spec, head_spec, whole(lse),
            ],
            out_specs=[
                pl.BlockSpec((count, 3 * head_dim, width), lambda i, *_: (0, 0, 0)),
                pl.BlockSpec((8, 128), lambda i, *_: (0, 0)),
            ],
            scratch_shapes=[
                pltpu.VMEM((seq_len, depth), BF16),
                pltpu.VMEM((head_dim, seq_len), BF16),
                pltpu.VMEM((seq_len, head_dim + 16), BF16),
                pltpu.VMEM((depth, block), BF16),
                pltpu.VMEM((head_dim + 16, block), BF16),
                pltpu.VMEM((block, depth), BF16),
                pltpu.VMEM((block, head_dim + 16), BF16),
                pltpu.VMEM((seq_len, depth), F32),
                pltpu.VMEM((seq_len, head_dim + 16), F32),
                pltpu.VMEM((head_dim, block), F32),
            ],
        ),
        out_shape=[
            jax.ShapeDtypeStruct((count, 3 * head_dim, width), BF16),
            jax.ShapeDtypeStruct((8, 128), F32),
        ],
        compiler_params=pltpu.CompilerParams(vmem_limit_bytes=62 << 20),
        cost_estimate=pl.CostEstimate(
            flops=20 * seq_len * seq_len * 256 // COVER,
            bytes_accessed=x.size * 6,
            transcendentals=0,
        ),
        name="attend_backward",
    )(length, bias, x, ids, grad, mixed, lse)


def rotary_tables(places, half_dim):
    frequency = jnp.exp(-math.log(ROTARY_BASE) * jnp.arange(half_dim, dtype=F32) / half_dim)
    angles = places.astype(F32)[None, :] * frequency[:, None]
    return jnp.cos(angles), jnp.sin(angles)


def sigmoid_of(x):
    return 1.0 / (1.0 + jnp.exp2(x * -LOG2E))


def turn_kernel(*refs):
    out_ref = refs[-1]
    size = refs[0].shape[1]
    for i, ref in enumerate(refs[:-1]):
        out_ref[i * size : (i + 1) * size, :] = ref[...].T


def turn_weights(*weights):
    depth, size = weights[0].shape
    vmem = pl.BlockSpec(memory_space=pltpu.VMEM)
    return pl.pallas_call(
        turn_kernel,
        in_specs=[vmem] * len(weights),
        out_specs=vmem,
        out_shape=jax.ShapeDtypeStruct((len(weights) * size, depth), BF16),
        compiler_params=pltpu.CompilerParams(vmem_limit_bytes=62 << 20),
        name="turn_weights",
    )(*weights)


def project_kernel(
    shape, core_ref, tokens_ref, gain_ref, query_ref, key_ref, value_ref, cos_ref, sin_ref, flat_ref, *rest
):
    here, head_dim, swap = shape
    outs, flat_weights = rest[:-1], rest[-1]
    pair = pl.program_id(0)

    @pl.when(pair == 0)
    def _():
        inputs = tokens_ref[0, 0].astype(F32)
        inverse = lax.rsqrt(jnp.mean(inputs * inputs, axis=-1, keepdims=True) + EPSILON)
        flat_ref[...] = (inputs * inverse * gain_ref[...]).astype(BF16).T

    made = None
    depth = query_ref.shape[2]
    for shard in range(query_ref.shape[0]):
        for at, ref in enumerate((query_ref, key_ref, value_ref)):
            flat_weights[shard, at * 128 : (at + 1) * 128, :] = ref[shard]
        term = dot(flat_weights[shard], flat_ref[shard * depth : (shard + 1) * depth, :])
        made = term if made is None else made + term
    cosine, sine = cos_ref[...], sin_ref[...]
    half = head_dim // 2

    def turned(start, scale):
        first = made[start : start + half]
        second = made[start + half : start + head_dim]
        both = [first * cosine - second * sine, second * cosine + first * sine]
        return (jnp.concatenate(both, axis=0) * scale).astype(BF16)

    def put(at, slot, place):
        spot = at * head_dim
        target = outs[slot]
        target[place, 0:head_dim, :] = turned(spot, LOG2E / math.sqrt(head_dim))
        target[place, head_dim : 2 * head_dim, :] = turned(128 + spot, 1.0)
        target[place, 2 * head_dim : 3 * head_dim, :] = made[256 + spot : 256 + spot + head_dim].astype(BF16)

    if swap:
        for core in range(2):

            @pl.when(core_ref[0] == core)
            def _():
                put(core, 0, 0)
                put(1 - core, 1, 0)

    else:
        for at in range(128 // head_dim):
            put(at, at % here, 0 if here > 1 else at)


def project(core, tokens, unit, gain, weights, cosine, sine, count, here, head_dim, swap):
    width, model = tokens.shape[2:]
    heads = count * here
    pairs = heads * head_dim // 128
    per = 128 // head_dim // here

    def fixed(a):
        return pl.BlockSpec(a.shape, lambda p: (0,) * a.ndim)

    shards, _, depth = weights.shape
    weight_specs = [
        pl.BlockSpec((shards, 128, depth), lambda p, i=i: (0, i * pairs + p, 0)) for i in range(3)
    ]
    return pl.pallas_call(
        functools.partial(project_kernel, (here, head_dim, swap)),
        grid=(pairs,),
        in_specs=[
            pl.BlockSpec(memory_space=pltpu.SMEM),
            pl.BlockSpec((1, 1, width, model), lambda p: unit + (0, 0)),
            fixed(gain), *weight_specs, fixed(cosine), fixed(sine),
        ],
        out_specs=[pl.BlockSpec((model, width), lambda p: (0, 0))]
        + [pl.BlockSpec((per, 3 * head_dim, width), lambda p: (p, 0, 0))] * here,
        out_shape=[jax.ShapeDtypeStruct((model, width), BF16)]
        + [jax.ShapeDtypeStruct((count, 3 * head_dim, width), BF16)] * here,
        scratch_shapes=[pltpu.VMEM((shards, 384, depth), BF16)],
        compiler_params=pltpu.CompilerParams(vmem_limit_bytes=62 << 20),
        cost_estimate=pl.CostEstimate(
            flops=6 * width * model * model // COVER, bytes_accessed=12 * model * model, transcendentals=0
        ),
        name="project",
    )(core, tokens, gain, weights, weights, weights, cosine, sine)


def middle_kernel(
    shape, info_ref, mixed_ref, tokens_ref, cot_ref, out_w_ref, gain_ref, gate_w_ref, up_w_ref, down_w_ref, *rest
):
    head_dim, aliased = shape
    if aliased:
        rest = rest[1:]
    (
        output_ref, ordered_ref, flat_ref, hidden_ref, grad_gate_ref, grad_up_ref, grad_ffn_ref, grad_res_ref,
        grad_attn_ref, grad_mixed_ref, gain_out_ref, normed, residual, ffn_out, grad_normed, slots,
    ) = rest
    core = info_ref[2]
    step = pl.program_id(0)
    width = normed.shape[0]

    def valid():
        index = info_ref[1] + lax.broadcasted_iota(jnp.int32, (width, 1), 0)
        return jnp.where(index < info_ref[0], 1.0, 0.0)

    def inverse_of(x):
        return lax.rsqrt(jnp.mean(x * x, axis=-1, keepdims=True) + EPSILON)

    def head_rows(pair, slot):
        head = 2 * pair + (core if slot == 0 else 1 - core)
        return pl.ds(pl.multiple_of(head * head_dim, head_dim), head_dim)

    def slot_rows(pair, slot):
        return slice((2 * pair + slot) * head_dim, (2 * pair + slot + 1) * head_dim)

    spots = [(pair, slot) for pair in range(mixed_ref.shape[0] // head_dim // 2) for slot in range(2)]

    @pl.when(step == 0)
    def _():
        for spot in spots:
            ordered_ref[head_rows(*spot), :] = mixed_ref[slot_rows(*spot), :]
        inputs = tokens_ref[0, 0].astype(F32) + dot(ordered_ref[...].T, out_w_ref[...])
        residual[...] = inputs
        made = (inputs * inverse_of(inputs) * gain_ref[...]).astype(BF16)
        normed[...] = made
        flat_ref[...] = made.T
        grad_ffn_ref[...] = (cot_ref[0, 0].astype(F32) * valid()).astype(BF16)
        ffn_out[...] = jnp.zeros_like(ffn_out)
        grad_normed[...] = jnp.zeros_like(grad_normed)

    gate = dot(normed[...], gate_w_ref[...])
    up = dot(normed[...], up_w_ref[...])
    grad_hidden = contract(grad_ffn_ref[...], down_w_ref[...], 1, 1)
    sigmoid = sigmoid_of(gate)
    silu = gate * sigmoid
    hidden = (silu * up).astype(BF16)
    grad_gate = (grad_hidden * up * (sigmoid + silu * (1.0 - sigmoid))).astype(BF16)
    grad_up = (grad_hidden * silu).astype(BF16)
    hidden_ref[...] = hidden.T
    grad_gate_ref[...] = grad_gate
    grad_up_ref[...] = grad_up
    ffn_out[...] += dot(hidden, down_w_ref[...])
    grad_normed[...] += contract(grad_gate, gate_w_ref[...], 1, 1) + contract(grad_up, up_w_ref[...], 1, 1)

    @pl.when(step == pl.num_programs(0) - 1)
    def _():
        keep = valid()
        kept = residual[...]
        output_ref[0, 0] = ((kept + ffn_out[...]) * keep).astype(BF16)
        inverse = inverse_of(kept)
        scaled = grad_normed[...] * gain_ref[...]
        mean = jnp.mean(scaled * kept, axis=-1, keepdims=True)
        grad = cot_ref[0, 0].astype(F32) * keep
        grad = grad + (inverse * scaled - kept * (inverse * inverse * inverse) * mean)
        gain_out_ref[...] = jnp.sum(grad_normed[...] * kept * inverse, axis=0, keepdims=True)
        grad_res_ref[...] = grad
        low = grad.astype(BF16)
        grad_attn_ref[...] = low
        slots[...] = contract(out_w_ref[...], low, 1, 1).astype(BF16)
        for spot in spots:
            grad_mixed_ref[slot_rows(*spot), :] = slots[head_rows(*spot), :]


def middle_part(info, mixed, tokens, cotangent, unit, weights, gain, head_dim, output):
    width, model = tokens.shape[2:]
    out_w, gate_w, up_w, down_w = weights
    ffn = gate_w.shape[1]
    block = 512

    def fixed(a):
        return pl.BlockSpec(a.shape, lambda f, *_: (0,) * a.ndim)

    def one(*shape):
        return pl.BlockSpec(shape, lambda f, *_: (0,) * len(shape))

    token_spec = pl.BlockSpec((1, 1, width, model), lambda f, *_: unit + (0, 0))
    operands = [info, mixed, tokens, cotangent, out_w, gain, gate_w, up_w, down_w]
    in_specs = [
        fixed(mixed), token_spec, token_spec, fixed(out_w), fixed(gain),
        pl.BlockSpec((model, block), lambda f, *_: (0, f)),
        pl.BlockSpec((model, block), lambda f, *_: (0, f)),
        pl.BlockSpec((block, model), lambda f, *_: (f, 0)),
    ]
    aliases = {}
    if output is not None:
        aliases = {len(operands): 0}
        operands.append(output)
        in_specs.append(pl.BlockSpec(memory_space=pl.ANY))
    struct = jax.ShapeDtypeStruct
    return pl.pallas_call(
        functools.partial(middle_kernel, (head_dim, output is not None)),
        grid_spec=pltpu.PrefetchScalarGridSpec(
            num_scalar_prefetch=1,
            grid=(ffn // block,),
            in_specs=in_specs,
            out_specs=[
                token_spec, one(model, width), one(model, width),
                pl.BlockSpec((block, width), lambda f, *_: (f, 0)),
                pl.BlockSpec((width, block), lambda f, *_: (0, f)),
                pl.BlockSpec((width, block), lambda f, *_: (0, f)),
                one(width, model), one(width, model), one(width, model), one(model, width), one(1, model),
            ],
            scratch_shapes=[
                pltpu.VMEM((width, model), BF16),
                pltpu.VMEM((width, model), F32),
                pltpu.VMEM((width, model), F32),
                pltpu.VMEM((width, model), F32),
                pltpu.VMEM((model, width), BF16),
            ],
        ),
        out_shape=[
            struct(tokens.shape, BF16), struct((model, width), BF16), struct((model, width), BF16),
            struct((ffn, width), BF16),
            struct((width, ffn), BF16), struct((width, ffn), BF16), struct((width, model), BF16),
            struct((width, model), F32), struct((width, model), BF16), struct((model, width), BF16),
            struct((1, model), F32),
        ],
        input_output_aliases=aliases,
        compiler_params=pltpu.CompilerParams(vmem_limit_bytes=62 << 20),
        cost_estimate=pl.CostEstimate(
            flops=12 * width * model * ffn // COVER, bytes_accessed=8 * model * ffn, transcendentals=0
        ),
        name="middle_part",
    )(*operands)


def final_kernel(
    shape, core_ref, tokens_ref, grad_res_ref, gain_ref, query_ref, key_ref, value_ref, cos_ref, sin_ref, *rest
):
    here, head_dim, aliased = shape
    back = rest[:here]
    rest = rest[here:]
    if aliased:
        rest = rest[1:]
    out_ref, grad_q_ref, grad_k_ref, grad_v_ref, gain_out_ref, total = rest
    step = pl.program_id(0)
    cosine, sine = cos_ref[...], sin_ref[...]
    half = head_dim // 2

    def turned(x):
        first, second = x[:half].astype(F32), x[half:].astype(F32)
        return jnp.concatenate(
            [first * cosine + second * sine, second * cosine - first * sine], axis=0
        ).astype(BF16)

    for at in range(256 // head_dim):
        head = at
        if here == 2:
            head = at // 2 * 2 + (core_ref[0] if at % 2 == 0 else 1 - core_ref[0])
        place = pl.ds(pl.multiple_of(head * head_dim, head_dim), head_dim)
        part = back[at % here]
        grad_q_ref[place, :] = turned(part[at // here, 0:head_dim, :])
        grad_k_ref[place, :] = turned(part[at // here, head_dim : 2 * head_dim, :])
        grad_v_ref[place, :] = part[at // here, 2 * head_dim : 3 * head_dim, :]
    rows = [ref[...].T for ref in (grad_q_ref, grad_k_ref, grad_v_ref)]

    @pl.when(step == 0)
    def _():
        total[...] = jnp.zeros_like(total)

    depth = query_ref.shape[2]
    for shard in range(query_ref.shape[0]):
        made = dot(rows[0], query_ref[shard]) + dot(rows[1], key_ref[shard]) + dot(rows[2], value_ref[shard])
        total[:, shard * depth : (shard + 1) * depth] += made

    @pl.when(step == pl.num_programs(0) - 1)
    def _():
        inputs = tokens_ref[0, 0].astype(F32)
        inverse = lax.rsqrt(jnp.mean(inputs * inputs, axis=-1, keepdims=True) + EPSILON)
        scaled = total[...] * gain_ref[...]
        mean = jnp.mean(scaled * inputs, axis=-1, keepdims=True)
        grad = inverse * scaled - inputs * (inverse * inverse * inverse) * mean
        out_ref[0, 0] = (grad_res_ref[...] + grad).astype(BF16)
        gain_out_ref[...] = jnp.sum(total[...] * inputs * inverse, axis=0, keepdims=True)


def final_part(core, tokens, unit, grad_res, gain, weights, cosine, sine, back, head_dim, output):
    width, model = tokens.shape[2:]
    here = len(back)
    steps = model // 256

    def fixed(a):
        return pl.BlockSpec(a.shape, lambda c: (0,) * a.ndim)

    token_spec = pl.BlockSpec((1, 1, width, model), lambda c: unit + (0, 0))
    shards, _, depth = weights.shape
    weight_specs = [
        pl.BlockSpec((shards, 256, depth), lambda c, i=i: (0, i * steps + c, 0)) for i in range(3)
    ]
    row_spec = pl.BlockSpec((256, width), lambda c: (c, 0))
    operands = [core, tokens, grad_res, gain, weights, weights, weights, cosine, sine, *back]
    in_specs = [
        pl.BlockSpec(memory_space=pltpu.SMEM), token_spec, fixed(grad_res), fixed(gain), *weight_specs,
        fixed(cosine), fixed(sine),
    ] + [
        pl.BlockSpec((256 // head_dim // here, 3 * head_dim, width), lambda c: (c, 0, 0)) for _ in back
    ]
    aliases = {}
    if output is not None:
        aliases = {len(operands): 0}
        operands.append(output)
        in_specs.append(pl.BlockSpec(memory_space=pl.ANY))
    struct = jax.ShapeDtypeStruct
    return pl.pallas_call(
        functools.partial(final_kernel, (here, head_dim, output is not None)),
        grid=(steps,),
        in_specs=in_specs,
        out_specs=[token_spec, row_spec, row_spec, row_spec, pl.BlockSpec((1, model), lambda c: (0, 0))],
        out_shape=[
            struct(tokens.shape, BF16), struct((model, width), BF16), struct((model, width), BF16),
            struct((model, width), BF16), struct((1, model), F32),
        ],
        scratch_shapes=[pltpu.VMEM((width, model), F32)],
        input_output_aliases=aliases,
        compiler_params=pltpu.CompilerParams(vmem_limit_bytes=62 << 20),
        cost_estimate=pl.CostEstimate(
            flops=6 * width * model * model // COVER, bytes_accessed=12 * model * model, transcendentals=0
        ),
        name="final_part",
    )(*operands)


def picked_kernel(units, rows, places, flipped, split, table_ref, *refs):
    weights = len(places)
    lefts = refs[0:units]
    rights = refs[units : units * (1 + weights)]
    outs = refs[units * (1 + weights) : units * (1 + weights) + weights * split]
    picked = refs[units * (1 + weights) + weights * split :]

    @pl.when(pl.program_id(0) == 0)
    def _():
        for w, (start, size) in enumerate(places):
            for p in range(size):
                at = pl.ds(pl.multiple_of(table_ref[start + p] * rows, rows), rows)
                for u in range(units):
                    picked[w * units + u][p * rows : (p + 1) * rows, :] = lefts[u][at, :]

    for w in range(weights):
        total = None
        for u in range(units):
            right = rights[w * units + u][...]
            left = picked[w * units + u][...]
            made = contract(left, right, 1, 1) if flipped else dot(left, right)
            total = made if total is None else total + made
        height = total.shape[0] // split
        for i in range(split):
            outs[w * split + i][...] = total[i * height : (i + 1) * height].astype(BF16)


def picked_grads(table, places, lefts, rights, rows, flipped, split, block, name):
    units = len(lefts)
    width = lefts[0].shape[1]
    columns = rights[0].shape[0 if flipped else 1]
    in_specs = [pl.BlockSpec(a.shape, lambda n, *_: (0, 0)) for a in lefts]
    for a in rights:
        if flipped:
            in_specs.append(pl.BlockSpec((block, width), lambda n, *_: (n, 0)))
        else:
            in_specs.append(pl.BlockSpec((width, block), lambda n, *_: (0, n)))
    heights = [size * rows for _, size in places]
    return pl.pallas_call(
        functools.partial(picked_kernel, units, rows, places, flipped, split),
        grid_spec=pltpu.PrefetchScalarGridSpec(
            num_scalar_prefetch=1,
            grid=(columns // block,),
            in_specs=in_specs,
            out_specs=[
                pl.BlockSpec((height // split, block), lambda n, *_: (0, n)) for height in heights for _ in range(split)
            ],
            scratch_shapes=[pltpu.VMEM((height, width), BF16) for height in heights for _ in lefts],
        ),
        out_shape=[
            jax.ShapeDtypeStruct((height // split, columns), BF16) for height in heights for _ in range(split)
        ],
        compiler_params=pltpu.CompilerParams(vmem_limit_bytes=62 << 20),
        cost_estimate=pl.CostEstimate(
            flops=2 * units * sum(heights) * width * columns // COVER,
            bytes_accessed=4 * sum(heights) * columns,
            transcendentals=0,
        ),
        name=name,
    )(table, *lefts, *rights)


def weights_kernel(units, *refs):
    out_ref = refs[-1]
    total = dot(refs[0][...], refs[units][...])
    for u in range(1, units):
        total += dot(refs[u][...], refs[units + u][...])
    out_ref[...] = total.astype(BF16).reshape(out_ref.shape)


def weight_grad(lefts, rights, by_left, out_struct, out_spec, steps, into, name):
    units = len(lefts)

    def fixed(a):
        return pl.BlockSpec(a.shape, lambda n: (0, 0))

    def left_spec(a):
        return pl.BlockSpec((a.shape[0] // steps, a.shape[1]), lambda n: (n, 0))

    def right_spec(a):
        return pl.BlockSpec((a.shape[0], a.shape[1] // steps), lambda n: (0, n))

    operands = list(lefts) + list(rights)
    if by_left:
        in_specs = [left_spec(a) for a in lefts] + [fixed(a) for a in rights]
    else:
        in_specs = [fixed(a) for a in lefts] + [right_spec(a) for a in rights]
    aliases = {}
    if into is not None:
        aliases = {len(operands): 0}
        operands.append(into)
        in_specs.append(pl.BlockSpec(memory_space=pl.ANY))
    return pl.pallas_call(
        functools.partial(weights_kernel, units),
        grid=(steps,),
        in_specs=in_specs,
        out_specs=out_spec,
        out_shape=out_struct,
        input_output_aliases=aliases,
        compiler_params=pltpu.CompilerParams(vmem_limit_bytes=62 << 20),
        cost_estimate=pl.CostEstimate(
            flops=2 * units * lefts[0].shape[0] * lefts[0].shape[1] * rights[0].shape[1] // COVER,
            bytes_accessed=2 * lefts[0].shape[0] * rights[0].shape[1],
            transcendentals=0,
        ),
        name=name,
    )(*operands)


def reduce_kernel(orders, count, *refs):
    streams = len(orders)
    rounds = len(orders[0])
    ins, vec_ref = refs[:streams], refs[streams]
    outs, vec_out = refs[streams + 1 : 2 * streams + 1], refs[2 * streams + 1]
    rest = refs[2 * streams + 2 :]
    works, arrivals = rest[:streams], rest[streams : 2 * streams]
    vec_work, vec_arrival, send_sem, recv_sem, vec_send, vec_recv = rest[2 * streams :]
    shard, seq = lax.axis_index("shard"), lax.axis_index("seq")

    def partner(mask):
        if mask >= count:
            step = mask // count
            return (shard + step * (1 - 2 * (shard // step % 2)), seq)
        return (shard, seq + mask * (1 - 2 * (seq // mask % 2)))

    barrier = pltpu.get_barrier_semaphore()
    for mask in orders[0]:
        pl.semaphore_signal(
            barrier, inc=1, device_id=partner(mask), device_id_type=pl.DeviceIdType.MESH
        )
    pl.semaphore_wait(barrier, rounds)

    height = ins[0].shape[0]
    halves = [height >> (r + 1) for r in range(rounds)]
    starts = [sum(halves[:r]) for r in range(rounds)]

    def copy_of(s, r):
        source = ins[s] if r == 0 else works[s]
        return pltpu.make_async_remote_copy(
            src_ref=source.at[pl.ds(halves[r], halves[r])],
            dst_ref=arrivals[s].at[pl.ds(starts[r], halves[r])],
            send_sem=send_sem.at[s, r],
            recv_sem=recv_sem.at[s, r],
            device_id=partner(orders[s][r]),
            device_id_type=pl.DeviceIdType.MESH,
        )

    def vec_copy(r):
        return pltpu.make_async_remote_copy(
            src_ref=vec_ref if r == 0 else vec_work.at[r - 1],
            dst_ref=vec_arrival.at[r],
            send_sem=vec_send.at[r],
            recv_sem=vec_recv.at[r],
            device_id=partner(orders[0][r]),
            device_id_type=pl.DeviceIdType.MESH,
        )

    for s in range(streams):
        copy_of(s, 0).start()
    vec_copy(0).start()
    for r in range(rounds):
        for s in range(streams):
            copy_of(s, r).wait_recv()
            source = ins[s] if r == 0 else works[s]
            size = halves[r]

            def added(low, high):
                mine = source[low:high].astype(F32)
                return mine + arrivals[s][starts[r] + low : starts[r] + high].astype(F32)

            if r == rounds - 1:
                outs[s][...] = added(0, size)
            else:
                works[s][size // 2 : size] = added(size // 2, size).astype(BF16)
                copy_of(s, r + 1).start()
                works[s][0 : size // 2] = added(0, size // 2).astype(BF16)
        vec_copy(r).wait_recv()
        before = vec_ref[...] if r == 0 else vec_work[r - 1]
        if r == rounds - 1:
            vec_out[...] = before + vec_arrival[r]
        else:
            vec_work[r] = before + vec_arrival[r]
            vec_copy(r + 1).start()
    for r in range(rounds):
        for s in range(streams):
            copy_of(s, r).wait_send()
        vec_copy(r).wait_send()


def reduce_rows(parts, vector, orders, count):
    streams = len(parts)
    rounds = len(orders[0])
    height, columns = parts[0].shape
    rows = height >> rounds
    vmem = pl.BlockSpec(memory_space=pltpu.VMEM)
    return pl.pallas_call(
        functools.partial(reduce_kernel, orders, count),
        in_specs=[vmem] * (streams + 1),
        out_specs=[vmem] * (streams + 1),
        out_shape=[jax.ShapeDtypeStruct((rows, columns), F32)] * streams
        + [jax.ShapeDtypeStruct(vector.shape, F32)],
        scratch_shapes=[pltpu.VMEM((height // 2, columns), BF16) for _ in parts]
        + [pltpu.VMEM((height - rows, columns), BF16) for _ in parts]
        + [
            pltpu.VMEM((rounds - 1,) + vector.shape, F32),
            pltpu.VMEM((rounds,) + vector.shape, F32),
            pltpu.SemaphoreType.DMA((streams, rounds)),
            pltpu.SemaphoreType.DMA((streams, rounds)),
            pltpu.SemaphoreType.DMA((rounds,)),
            pltpu.SemaphoreType.DMA((rounds,)),
        ],
        compiler_params=pltpu.CompilerParams(
            collective_id=0, has_side_effects=True, vmem_limit_bytes=62 << 20
        ),
        name="reduce_rows",
    )(*parts, vector)


def on_device(
    tokens, cotangent, lengths, variates, positions, attn_gain, w_query, w_key, w_value, w_out,
    bias_table, ffn_gain, w_gate, w_up, w_down,
):
    micro, seqs, width, model = tokens.shape
    heads = bias_table.shape[0]
    head_dim = model // heads
    count = lax.axis_size("seq")
    here = heads // count
    ffn = w_gate.shape[1]
    devices = lax.axis_size("shard") * count
    seq_index = lax.axis_index("seq")
    units = [(m, s) for m in range(micro) for s in range(seqs)]
    swap = here == 2 and len(units) == 2 and lax.axis_size("shard") % 2 == 0
    core = (lax.axis_index("shard") % 2 if swap else jnp.int32(0)).astype(jnp.int32).reshape(1)
    heads_here = 1 if swap else here
    first_head = seq_index * here + core[0]
    bias_here = lax.dynamic_slice_in_dim(bias_table, first_head, heads_here, 0)
    attn_row, ffn_row = attn_gain[None, :], ffn_gain[None, :]

    def gather(weight):
        return lax.all_gather(weight, "shard", axis=0, tiled=True)

    def exchange(values):
        return lax.all_to_all(values, "seq", split_axis=0, concat_axis=0, tiled=True)

    def after(value, *before):
        return lax.optimization_barrier((value,) + before)[0]

    attn_rows = turn_weights(w_query, w_key, w_value)
    attn_joined = lax.all_gather(attn_rows, "shard", axis=0, tiled=False)
    ffn_weights = [gather(w_out), gather(w_gate), gather(w_up), gather(w_down)]

    def permute(value, mask):
        return lax.ppermute(value, ("shard", "seq"), [(i, i ^ mask) for i in range(devices)])

    def cross(value):
        return permute(value, count)

    lengths_of = [lengths, cross(lengths)] if swap else [lengths] * here
    ids_own = lax.all_gather(variates, "seq", axis=0, tiled=False)
    ids_of = [ids_own, cross(ids_own)] if swap else [ids_own] * here
    attn_joined = after(attn_joined, *ids_of)

    def ids_rows(u, h):
        m, s = units[u]
        return ids_of[h][:, m, s].astype(F32)[:, None, :]

    packed_list, flats, tables = [], [], []

    def run_project(u, token):
        m, s = units[u]
        cosine, sine = rotary_tables(positions[m, s], head_dim // 2)
        flat, *packed = project(
            core, tokens, (m, s), after(attn_row, *token), attn_joined, cosine, sine, count, here, head_dim,
            swap,
        )
        flats.append(flat)
        tables.append((cosine, sine))
        packed_list.append(packed)

    sent = {}
    mixed_now = [None] * len(units)
    sums = {}
    mixed_tok = {}
    crossed, mixed_part, mixed_cross, heads_cross, back_cross = {}, {}, {}, {}, {}
    middle = [None] * len(units)
    grad_heads = {}
    state = {"output": None, "grads": None}
    packed_grads = {}
    returned = {}
    bias_terms = {}
    finals = [None] * len(units)

    def length_of(u, h, token):
        m, s = units[u]
        return after(lengths_of[h][m, s].reshape(1), *token)

    def inputs_of(u, h):
        return (crossed[u] if swap and h == 1 else sent[u, h]), ids_rows(u, h)

    def run_forward(u, h, token):
        made, sums[u, h] = attend_forward(
            *inputs_of(u, h), length_of(u, h, token), bias_here, None if swap else mixed_now[u],
            0 if swap else h, heads_here, head_dim,
        )
        if swap:
            mixed_part[u, h] = made
            if h == 1:
                mixed_cross[u] = cross(made)
        else:
            mixed_now[u] = made
        return sums[u, h]

    def run_middle(u, token):
        m, s = units[u]
        info = jnp.stack([lengths[m, s], seq_index * width, core[0]]).astype(jnp.int32)
        state["output"], mixed_tok[u], *middle[u] = middle_part(
            after(info, *token), mixed_tok[u], tokens, cotangent, (m, s), ffn_weights, ffn_row, head_dim,
            state["output"],
        )
        return middle[u][8]

    def run_backward(u, h, token):
        if swap:
            token = token + ((heads_cross[1],) if (u, h) == (0, 1) else ())
            grad = grad_heads[u] if h == 0 else heads_cross[u]
            mixed = mixed_part[u, h]
        else:
            grad, mixed = grad_heads[u], mixed_now[u]
        packed_grads[u, h], both = attend_backward(
            *inputs_of(u, h), grad, mixed, sums[u, h], length_of(u, h, token), bias_here,
            0 if swap else h, head_dim,
        )
        if swap and h == 1:
            back_cross[u] = cross(packed_grads[u, h])
        bias_terms[u, h] = both
        return both

    def run_final(u, token):
        m, s = units[u]
        cosine, sine = tables[u]
        state["grads"], *finals[u] = final_part(
            core, tokens, (m, s), middle[u][5], after(attn_row, *token), attn_joined, cosine, sine,
            [returned[u, h] for h in range(here)], head_dim, state["grads"],
        )
        return finals[u][3]

    rows = model // devices
    fold = ffn // model
    tall = ffn // devices
    seq_masks = [1 << i for i in range(count.bit_length() - 1)]
    shard_masks = [count << i for i in range((devices // count).bit_length() - 1)]
    spread = shard_masks[1:]
    orders = (
        shard_masks[:1] + spread + seq_masks,
        shard_masks[:1] + seq_masks[:1] + spread + seq_masks[1:],
        shard_masks[:1] + seq_masks[1:2] + seq_masks[:1] + spread + seq_masks[2:],
    )
    direct = rows % 16 == 0 and devices == 1 << len(orders[0])

    def places_of(order):
        marks = []
        for p in range(devices):
            bits = [p >> (len(order) - 1 - i) & 1 for i in range(len(order))]
            marks.append(sum(mask for bit, mask in zip(bits, order) if bit))
        me = lax.axis_index("shard") * count + seq_index
        return me.astype(jnp.int32) ^ jnp.array(marks, jnp.int32)

    def column(index):
        return [item[index] for item in middle]

    def run_weights(token):
        if not direct:
            return [
                sum(dot(left, right) for left, right in zip(lefts, rights)).astype(BF16)
                for lefts, rights in (
                    (column(0), column(2)), (column(0), column(3)), (column(1), column(4)),
                    ([mixed_tok[u] for u in range(len(units))], column(6)),
                )
            ]
        part = ffn // fold
        narrow = model // fold
        spare = -(-(2 * part + narrow) // 384) * 384
        struct = jax.ShapeDtypeStruct((devices, fold, rows, spare), BF16)
        down = pl.BlockSpec((512 // tall, fold, rows, model), lambda n: (n, 0, 0, 0))
        gate = pl.BlockSpec((devices, 1, rows, part), lambda n: (0, n, 0, 1))
        out = pl.BlockSpec((devices, 1, rows, narrow), lambda n: (0, n, 0, 2 * part // narrow))
        table = after(places_of(orders[0]), *token)
        up = picked_grads(table, [(0, devices)], column(0), column(3), rows, False, 2, 1024, "up_grad")
        holder["streams"] = [[up[0], permute(up[1], orders[0][0]), orders[0][1:]]]
        firsts = [after(middle[0][4], up[0])] + [item[4] for item in middle[1:]]
        terms = weight_grad(column(1), firsts, True, struct, down, ffn // 512, None, "down_grad")
        landed = (holder["streams"][0][1],) + ((heads_cross[0],) if swap else ())
        rights = [after(middle[0][2], *holder["flying"], *landed)] + [item[2] for item in middle[1:]]
        terms = weight_grad(column(0), rights, False, struct, gate, fold, terms, "gate_grad")
        mixed_all = [mixed_tok[u] for u in range(len(units))]
        terms = weight_grad(mixed_all, column(6), False, struct, out, fold, terms, "out_grad")
        terms = terms.reshape(ffn, spare)
        holder["owned"] = lax.psum_scatter(terms, ("shard", "seq"), scatter_dimension=0, tiled=True)
        return terms

    def wide_sum(a, b):
        return a.astype(F32) + b.astype(F32)

    def advance(token):
        out = ()
        if not direct:
            return out
        for stream in holder["streams"]:
            keep, came, masks = stream
            if not masks:
                continue
            keep = after(keep, *token)
            half = keep.shape[0] // 2
            send = wide_sum(keep[half:], came[half:]).astype(BF16)
            stream[0] = wide_sum(keep[:half], came[:half]).astype(BF16)
            stream[1] = permute(send, masks[0])
            stream[2] = masks[1:]
            out = out + (send, stream[0])
        return out

    holder = {}

    def weights_work(token):
        holder["terms"] = run_weights(token)
        return holder["terms"]

    def send_packed(u, h):
        def keep(moved):
            sent[u, h] = moved
            if swap and h == 1:
                crossed[u] = cross(moved)

        return lambda: packed_list[u][h], keep

    def send_mixed(u):
        def keep(moved):
            mixed_tok[u] = moved.reshape(model, width)

        if not swap:
            return lambda: mixed_now[u], keep
        return lambda: jnp.concatenate([mixed_part[u, 0], mixed_cross[u]], axis=1), keep

    def send_heads(u):
        def keep(moved):
            grad_heads[u] = moved
            if swap:
                heads_cross[u] = cross(moved[:, head_dim:])

        return lambda: middle[u][7].reshape(count, here * head_dim, width), keep

    def send_back(u, h):
        def keep(moved):
            returned[u, h] = moved

        return lambda: back_cross[u] if swap and h == 1 else packed_grads[u, h], keep

    def work_project(u):
        def work(token):
            run_project(u, token)
            return flats[u]

        return work

    def work(function, *args):
        return lambda token: function(*args, token)

    total = len(units)
    order = [(u, h) for u in range(total) for h in range(here)]
    if swap:
        steps = [
            (work_project(0), None),
            (work_project(1), send_packed(0, 1)),
            (work(run_forward, 0, 1), send_packed(0, 0)),
            (work(run_forward, 0, 0), send_packed(1, 1)),
            (work(run_forward, 1, 1), send_packed(1, 0)),
            (work(run_forward, 1, 0), send_mixed(0)),
            (work(run_middle, 0), send_mixed(1)),
            (work(run_middle, 1), send_heads(0)),
            (weights_work, send_heads(1)),
            (work(run_backward, 0, 0), None),
            (work(run_backward, 0, 1), send_back(0, 0)),
            (work(run_backward, 1, 0), send_back(0, 1)),
            (work(run_backward, 1, 1), send_back(1, 0)),
            (work(run_final, 0), send_back(1, 1)),
            (work(run_final, 1), None),
        ]
    else:
        steps = [(work_project(u), None) for u in range(total)]
        steps += [(None, send_packed(*at)) for at in order]
        for u in range(total):
            steps += [(work(run_forward, u, h), None) for h in range(here)]
            steps += [(None, send_mixed(u))]
        for u in range(total):
            steps += [(work(run_middle, u), None), (None, send_heads(u))]
        steps += [(weights_work, None)]
        for at in order:
            steps += [(work(run_backward, *at), None), (None, send_back(*at))]
        steps += [(work(run_final, u), None) for u in range(total)]

    late = [task for task, _ in steps[-2:]]
    token = ()
    for index, (task, send) in enumerate(steps):
        done = ()
        moved = None
        ahead = ()
        if "streams" in holder:
            leaving = advance(token[-1:])
            if index == len(steps) - 5:
                ahead = leaving
            elif task not in late:
                token = token + leaving
        if send is not None:
            moved = exchange(after(send[0](), *token))
            done = (moved,)
        holder["flying"] = done
        if task is not None:
            done = done + (task(token + ahead),)
        if send is not None:
            send[1](after(moved, *done[1:]))
        token = done
    acc_bias = jnp.concatenate(
        [sum(bias_terms[u, h] for u in range(total))[0:1, 0:2] for h in range(here)], axis=0
    )
    if swap:
        acc_bias = acc_bias[0:1] + acc_bias[1:2]
    bias_full = lax.dynamic_update_slice(
        jnp.zeros((heads, 2), F32), acc_bias, (first_head, jnp.int32(0))
    )
    gain_attn = sum(item[3][0] for item in finals)
    gain_ffn = sum(item[8][0] for item in middle)
    if direct:
        while holder["streams"][0][2]:
            advance(token)
        keep, came, _ = holder["streams"][0]
        up_own = wide_sum(after(keep, *token), came)
        flats[0] = after(flats[0], up_own)
        owned, part = holder["owned"], ffn // fold

        def joined(start, size):
            piece = owned[:, start : start + size].reshape(fold, rows, size)
            return jnp.swapaxes(piece, 0, 1).reshape(rows, fold * size).astype(F32)

        down_own = owned[:, :part].astype(F32)
        gate_own, out_own = joined(part, part), joined(2 * part, model // fold)
        table = jnp.concatenate([places_of(order) for order in orders])
        attn_terms = picked_grads(
            table, [(i * devices, devices) for i in range(3)], flats,
            [item[i] for i in range(3) for item in finals], rows, True, 1, 256, "attn_grads",
        )
        flat = jnp.concatenate([gain_attn, gain_ffn, bias_full.reshape(-1)])
        tiles = -(-flat.shape[0] // 1024) * 8
        flat = jnp.pad(flat, (0, tiles * 128 - flat.shape[0])).reshape(tiles, 128)
        query_own, key_own, value_own, flat = reduce_rows(list(attn_terms), flat, orders, count)
        flat = flat.reshape(-1)
        gain_attn, gain_ffn = flat[:model], flat[model : 2 * model]
        bias_full = flat[2 * model : 2 * model + 2 * heads].reshape(heads, 2)
    else:

        def scatter(value):
            owned = lax.psum_scatter(value, ("shard", "seq"), scatter_dimension=0, tiled=True)
            return owned.astype(F32)

        gate_own, up_own, down_own, out_own = [scatter(value) for value in holder["terms"]]
        query_own, key_own, value_own = [
            scatter(
                sum(contract(flat, item[i], 1, 1) for flat, item in zip(flats, finals)).astype(BF16)
            )
            for i in range(3)
        ]
        gain_attn, gain_ffn, bias_full = lax.psum(
            (gain_attn, gain_ffn, bias_full), ("shard", "seq")
        )
    return (
        state["output"], state["grads"], gain_attn, query_own, key_own, value_own, out_own,
        bias_full, gain_ffn, gate_own, up_own, down_own,
    )


def solution(mesh):
    token_spec = P(None, "shard", "seq", None)
    row_spec = P("shard", None)
    in_specs = (
        token_spec, token_spec, P(None, "shard"), P(None, "shard", "seq"), P(None, "shard", "seq"),
        P(), row_spec, row_spec, row_spec, row_spec, P(), P(), row_spec, row_spec, row_spec,
    )
    owned = P(("shard", "seq"), None)
    out_specs = (
        token_spec, token_spec, P(), owned, owned, owned, owned, P(), P(), owned, owned, owned,
    )
    return jax.shard_map(
        on_device, mesh=mesh, in_specs=in_specs, out_specs=out_specs, check_vma=False
    )
```

```python
import functools
import math

import jax
import jax.numpy as jnp
from jax import lax
from jax.experimental import pallas as pl
from jax.experimental.pallas import tpu as pltpu
from jax.sharding import PartitionSpec as P

EPSILON = 1e-06
ROTARY_BASE = 10000.0
LOG2E = 1.4426950408889634
LN2 = 0.6931471805599453
CLASSES = 8
COVER = 16
EXTRA = 32
MASKED = -1.5e9
FAR = 1e30
F32 = jnp.float32
BF16 = jnp.bfloat16


def dot(a, b):
    return jnp.dot(a, b, preferred_element_type=F32)


def contract(a, b, da, db):
    return lax.dot_general(a, b, (((da,), (db,)), ((), ())), preferred_element_type=F32)


def pieces(x):
    high = x.astype(BF16).astype(F32)
    rest = x - high
    mid = rest.astype(BF16).astype(F32)
    low = (rest - mid).astype(BF16).astype(F32)
    return high, mid, low


def one_hot(row):
    classes = lax.broadcasted_iota(jnp.int32, (CLASSES, row.shape[1]), 0).astype(F32)
    return jnp.where(classes == row, 1.0, 0.0)


def rows_of(values, width):
    index = lax.broadcasted_iota(jnp.int32, (8, width), 0)
    out = jnp.zeros((8, width), F32)
    for at, value in enumerate(values):
        out = jnp.where(index == at, value, out)
    return out


def key_extra(row, start, length, other, same):
    width = row.shape[1]
    hot = one_hot(row)
    step = pieces(jnp.full((1, width), same - other, F32))
    base = pieces(jnp.full((1, width), other, F32))
    index = start + lax.broadcasted_iota(jnp.int32, (1, width), 1)
    mask = jnp.where(index < length, 0.0, MASKED)
    tail = rows_of(base + (mask, 1.0, 1.0, 1.0), width)
    return jnp.concatenate([hot * step[0], hot * step[1], hot * step[2], tail], axis=0).astype(BF16)


def query_extra(row, shift):
    hot = one_hot(row)
    tail = rows_of((1.0, 1.0, 1.0, 1.0) + shift, row.shape[1])
    return jnp.concatenate([hot, hot, hot, tail], axis=0).astype(BF16)


def forward_kernel(
    shape, len_ref, bias_ref, x_ref, ids_ref, *rest
):
    local, head_dim, block, aliased = shape
    if aliased:
        rest = rest[1:]
    mixed_ref, lse_ref, keys, vals, query, score, peak, total = rest
    count, _, width = x_ref.shape
    sub = block // width
    step = pl.program_id(0)
    length = len_ref[0]
    other = bias_ref[local, 0] * LOG2E
    same = bias_ref[local, 1] * LOG2E

    @pl.when(step == 0)
    def _():
        for b in range(count):
            at = pl.ds(b * width, width)
            row = ids_ref[b, 0:1, :].astype(F32)
            extra = key_extra(row, b * width, length, other, same)
            full = jnp.concatenate([x_ref[b, head_dim : 2 * head_dim, :], extra], axis=0)
            keys[at, :] = full.T
            vals[0:head_dim, at] = x_ref[b, 2 * head_dim : 3 * head_dim, :]
        vals[head_dim:, :] = jnp.ones((16, vals.shape[1]), BF16)

    used = pl.cdiv(length, block)
    inside = step * block < length

    @pl.when(jnp.logical_not(inside))
    def _():
        mixed_ref[...] = jnp.zeros_like(mixed_ref)
        lse_ref[...] = jnp.full(lse_ref.shape, FAR, F32)

    @pl.when(inside)
    def _():
        for b in range(sub):
            at = slice(b * width, (b + 1) * width)
            row = ids_ref[step * sub + b, 0:1, :].astype(F32)
            query[0:head_dim, at] = x_ref[step * sub + b, 0:head_dim, :]
            query[head_dim:, at] = query_extra(row, (0.0, 0.0, 0.0))
        peak[...] = jnp.full(peak.shape, -FAR, F32)
        total[...] = jnp.zeros_like(total)

        def span(j):
            return pl.ds(pl.multiple_of(j * block, block), block)

        def scores_of(j):
            return dot(keys[span(j), :], query[...])

        def one(j, now, ahead):
            if ahead:
                score[1 - now] = scores_of(j + 1)
            current = score[now]
            before = peak[...]
            top = jnp.maximum(before, jnp.max(current, axis=0, keepdims=True))
            weight = jnp.exp2(current - top).astype(BF16)
            peak[...] = top
            total[...] = total[...] * jnp.exp2(before - top) + dot(vals[:, span(j)], weight)

        score[0] = scores_of(0)
        pairs = (used - 1) // 2

        def pair(j, carry):
            one(2 * j, 0, True)
            one(2 * j + 1, 1, True)
            return carry

        lax.fori_loop(0, pairs, pair, 0)
        last = 2 * pairs

        @pl.when(used - last == 1)
        def _():
            one(last, 0, False)

        @pl.when(used - last == 2)
        def _():
            one(last, 0, True)
            one(last + 1, 1, False)

        mass = total[head_dim : head_dim + 1, :]
        mixed = (total[0:head_dim, :] / mass).astype(BF16)
        for b in range(sub):
            mixed_ref[b] = mixed[:, b * width : (b + 1) * width]
        lse_ref[0] = peak[...] + jnp.log2(mass)


def attend_forward(x, ids, length, bias, mixed, local, heads_here, head_dim):
    count, rows, width = x.shape
    block = max(width, 512)
    seq_len = count * width
    blocks = seq_len // block
    depth = head_dim + EXTRA
    whole = pl.BlockSpec((count, rows, width), lambda i, *_: (0, 0, 0))
    operands = [length, bias, x, ids]
    in_specs = [whole, pl.BlockSpec((count, 1, width), lambda i, *_: (0, 0, 0))]
    aliases = {}
    if mixed is not None:
        operands.append(mixed)
        in_specs.append(pl.BlockSpec(memory_space=pl.ANY))
        aliases = {4: 0}
    return pl.pallas_call(
        functools.partial(forward_kernel, (local, head_dim, block, mixed is not None)),
        grid_spec=pltpu.PrefetchScalarGridSpec(
            num_scalar_prefetch=2,
            grid=(blocks,),
            in_specs=in_specs,
            out_specs=[
                pl.BlockSpec((block // width, head_dim, width), lambda i, *_: (i, local, 0)),
                pl.BlockSpec((1, 1, block), lambda i, *_: (i, 0, 0)),
            ],
            scratch_shapes=[
                pltpu.VMEM((seq_len, depth), BF16),
                pltpu.VMEM((head_dim + 16, seq_len), BF16),
                pltpu.VMEM((depth, block), BF16),
                pltpu.VMEM((2, block, block), F32),
                pltpu.VMEM((1, block), F32),
                pltpu.VMEM((head_dim + 16, block), F32),
            ],
        ),
        out_shape=[
            jax.ShapeDtypeStruct((count, heads_here * head_dim, width), BF16),
            jax.ShapeDtypeStruct((blocks, 1, block), F32),
        ],
        input_output_aliases=aliases,
        compiler_params=pltpu.CompilerParams(vmem_limit_bytes=62 << 20),
        cost_estimate=pl.CostEstimate(
            flops=8 * seq_len * seq_len * 256 // COVER,
            bytes_accessed=x.size * 4,
            transcendentals=0,
        ),
        name="attend_forward",
    )(*operands)


def backward_kernel(
    shape, len_ref, bias_ref, x_ref, ids_ref, grad_ref, mixed_ref, lse_ref, out_ref, bias_out_ref,
    keys, keys_flat, vals, query, grads, query_rows, grad_rows, acc_keys, acc_vals, acc_query,
):
    local, head_dim, block = shape
    count, _, width = x_ref.shape
    sub = block // width
    step = pl.program_id(0)
    length = len_ref[0]
    other = bias_ref[local, 0] * LOG2E
    same = bias_ref[local, 1] * LOG2E

    @pl.when(step == 0)
    def _():
        ones = jnp.ones((16, width), BF16)
        for b in range(count):
            at = pl.ds(b * width, width)
            row = ids_ref[b, 0:1, :].astype(F32)
            extra = key_extra(row, b * width, length, other, same)
            here = x_ref[b, head_dim : 2 * head_dim, :]
            keys[at, :] = jnp.concatenate([here, extra], axis=0).T
            keys_flat[:, at] = here
            vals[at, :] = jnp.concatenate([x_ref[b, 2 * head_dim : 3 * head_dim, :], ones], axis=0).T
        acc_keys[...] = jnp.zeros_like(acc_keys)
        acc_vals[...] = jnp.zeros_like(acc_vals)

    used = pl.cdiv(length, block)
    inside = step * block < length

    @pl.when(jnp.logical_not(inside))
    def _():
        for b in range(sub):
            out_ref[step * sub + b, 0:head_dim, :] = jnp.zeros((head_dim, width), BF16)

    @pl.when(inside)
    def _():
        for b in range(sub):
            at = slice(b * width, (b + 1) * width)
            here = step * sub + b
            row = ids_ref[here, 0:1, :].astype(F32)
            shift = pieces(-lse_ref[step][:, at])
            grad = grad_ref[here]
            delta = jnp.sum(grad.astype(F32) * mixed_ref[here].astype(F32), axis=0, keepdims=True)
            query[0:head_dim, at] = x_ref[here, 0:head_dim, :]
            query[head_dim:, at] = query_extra(row, shift)
            grads[0:head_dim, at] = grad
            tail = rows_of(pieces(-delta), width)
            grads[head_dim:, at] = jnp.concatenate([tail, jnp.zeros_like(tail)], axis=0).astype(BF16)
        query_rows[...] = query[...].T
        grad_rows[...] = grads[...].T
        acc_query[...] = jnp.zeros_like(acc_query)

        def one(j):
            at = pl.ds(pl.multiple_of(j * block, block), block)
            probs = jnp.exp2(dot(keys[at, :], query[...]))
            grad_probs = dot(vals[at, :], grads[...])
            grad_scores = (probs * grad_probs).astype(BF16)
            acc_vals[at, :] += dot(probs.astype(BF16), grad_rows[...])
            acc_keys[at, :] += dot(grad_scores, query_rows[...])
            acc_query[...] += dot(keys_flat[:, at], grad_scores)

        def pair(j, carry):
            one(2 * j)
            one(2 * j + 1)
            return carry

        lax.fori_loop(0, used // 2, pair, 0)

        @pl.when(used % 2 == 1)
        def _():
            one(used - 1)

        grad_query = (acc_query[...] * (1.0 / math.sqrt(head_dim))).astype(BF16)
        for b in range(sub):
            out_ref[step * sub + b, 0:head_dim, :] = grad_query[:, b * width : (b + 1) * width]

    @pl.when(step == pl.num_programs(0) - 1)
    def _():
        same_total = jnp.zeros((CLASSES, width), F32)
        all_total = jnp.zeros((CLASSES, width), F32)
        for b in range(count):
            at = pl.ds(b * width, width)
            row = ids_ref[b, 0:1, :].astype(F32)
            flat = acc_keys[at, :].T
            out_ref[b, head_dim : 2 * head_dim, :] = (flat[0:head_dim] * LN2).astype(BF16)
            out_ref[b, 2 * head_dim : 3 * head_dim, :] = acc_vals[at, :].T[0:head_dim].astype(BF16)
            by_class = flat[head_dim : head_dim + CLASSES]
            all_total += by_class
            same_total += by_class * one_hot(row)
        same_sum = jnp.sum(same_total, keepdims=True)
        other_sum = jnp.sum(all_total, keepdims=True) - same_sum
        lane = lax.broadcasted_iota(jnp.int32, (8, 128), 1)
        bias_out_ref[...] = jnp.where(lane == 0, other_sum, jnp.where(lane == 1, same_sum, 0.0))


def attend_backward(x, ids, grad, mixed, lse, length, bias, local, head_dim):
    count, rows, width = x.shape
    blocks, _, block = lse.shape
    seq_len = count * width
    depth = head_dim + EXTRA

    def whole(a):
        return pl.BlockSpec(a.shape, lambda i, *_: (0,) * a.ndim)

    head_spec = pl.BlockSpec((count, head_dim, width), lambda i, *_: (0, local, 0))
    return pl.pallas_call(
        functools.partial(backward_kernel, (local, head_dim, block)),
        grid_spec=pltpu.PrefetchScalarGridSpec(
            num_scalar_prefetch=2,
            grid=(blocks,),
            in_specs=[
                whole(x),
                pl.BlockSpec((count, 1, width), lambda i, *_: (0, 0, 0)),
                head_spec, head_spec, whole(lse),
            ],
            out_specs=[
                pl.BlockSpec((count, 3 * head_dim, width), lambda i, *_: (0, 0, 0)),
                pl.BlockSpec((8, 128), lambda i, *_: (0, 0)),
            ],
            scratch_shapes=[
                pltpu.VMEM((seq_len, depth), BF16),
                pltpu.VMEM((head_dim, seq_len), BF16),
                pltpu.VMEM((seq_len, head_dim + 16), BF16),
                pltpu.VMEM((depth, block), BF16),
                pltpu.VMEM((head_dim + 16, block), BF16),
                pltpu.VMEM((block, depth), BF16),
                pltpu.VMEM((block, head_dim + 16), BF16),
                pltpu.VMEM((seq_len, depth), F32),
                pltpu.VMEM((seq_len, head_dim + 16), F32),
                pltpu.VMEM((head_dim, block), F32),
            ],
        ),
        out_shape=[
            jax.ShapeDtypeStruct((count, 3 * head_dim, width), BF16),
            jax.ShapeDtypeStruct((8, 128), F32),
        ],
        compiler_params=pltpu.CompilerParams(vmem_limit_bytes=62 << 20),
        cost_estimate=pl.CostEstimate(
            flops=20 * seq_len * seq_len * 256 // COVER,
            bytes_accessed=x.size * 6,
            transcendentals=0,
        ),
        name="attend_backward",
    )(length, bias, x, ids, grad, mixed, lse)


def rotary_tables(places, half_dim):
    frequency = jnp.exp(-math.log(ROTARY_BASE) * jnp.arange(half_dim, dtype=F32) / half_dim)
    angles = places.astype(F32)[None, :] * frequency[:, None]
    return jnp.cos(angles), jnp.sin(angles)


def sigmoid_of(x):
    return 1.0 / (1.0 + jnp.exp2(x * -LOG2E))


def turn_kernel(*refs):
    out_ref = refs[-1]
    size = refs[0].shape[1]
    for i, ref in enumerate(refs[:-1]):
        out_ref[i * size : (i + 1) * size, :] = ref[...].T


def turn_weights(*weights):
    depth, size = weights[0].shape
    vmem = pl.BlockSpec(memory_space=pltpu.VMEM)
    return pl.pallas_call(
        turn_kernel,
        in_specs=[vmem] * len(weights),
        out_specs=vmem,
        out_shape=jax.ShapeDtypeStruct((len(weights) * size, depth), BF16),
        compiler_params=pltpu.CompilerParams(vmem_limit_bytes=62 << 20),
        name="turn_weights",
    )(*weights)


def project_kernel(
    shape, core_ref, tokens_ref, gain_ref, query_ref, key_ref, value_ref, cos_ref, sin_ref, flat_ref, *rest
):
    here, head_dim, swap = shape
    outs, flat_weights = rest[:-1], rest[-1]
    pair = pl.program_id(0)

    @pl.when(pair == 0)
    def _():
        inputs = tokens_ref[0, 0].astype(F32)
        inverse = lax.rsqrt(jnp.mean(inputs * inputs, axis=-1, keepdims=True) + EPSILON)
        flat_ref[...] = (inputs * inverse * gain_ref[...]).astype(BF16).T

    made = None
    depth = query_ref.shape[2]
    for shard in range(query_ref.shape[0]):
        for at, ref in enumerate((query_ref, key_ref, value_ref)):
            flat_weights[shard, at * 128 : (at + 1) * 128, :] = ref[shard]
        term = dot(flat_weights[shard], flat_ref[shard * depth : (shard + 1) * depth, :])
        made = term if made is None else made + term
    cosine, sine = cos_ref[...], sin_ref[...]
    half = head_dim // 2

    def turned(start, scale):
        first = made[start : start + half]
        second = made[start + half : start + head_dim]
        both = [first * cosine - second * sine, second * cosine + first * sine]
        return (jnp.concatenate(both, axis=0) * scale).astype(BF16)

    def put(at, slot, place):
        spot = at * head_dim
        target = outs[slot]
        target[place, 0:head_dim, :] = turned(spot, LOG2E / math.sqrt(head_dim))
        target[place, head_dim : 2 * head_dim, :] = turned(128 + spot, 1.0)
        target[place, 2 * head_dim : 3 * head_dim, :] = made[256 + spot : 256 + spot + head_dim].astype(BF16)

    if swap:
        for core in range(2):

            @pl.when(core_ref[0] == core)
            def _():
                put(core, 0, 0)
                put(1 - core, 1, 0)

    else:
        for at in range(128 // head_dim):
            put(at, at % here, 0 if here > 1 else at)


def project(core, tokens, unit, gain, weights, cosine, sine, count, here, head_dim, swap):
    width, model = tokens.shape[2:]
    heads = count * here
    pairs = heads * head_dim // 128
    per = 128 // head_dim // here

    def fixed(a):
        return pl.BlockSpec(a.shape, lambda p: (0,) * a.ndim)

    shards, _, depth = weights.shape
    weight_specs = [
        pl.BlockSpec((shards, 128, depth), lambda p, i=i: (0, i * pairs + p, 0)) for i in range(3)
    ]
    return pl.pallas_call(
        functools.partial(project_kernel, (here, head_dim, swap)),
        grid=(pairs,),
        in_specs=[
            pl.BlockSpec(memory_space=pltpu.SMEM),
            pl.BlockSpec((1, 1, width, model), lambda p: unit + (0, 0)),
            fixed(gain), *weight_specs, fixed(cosine), fixed(sine),
        ],
        out_specs=[pl.BlockSpec((model, width), lambda p: (0, 0))]
        + [pl.BlockSpec((per, 3 * head_dim, width), lambda p: (p, 0, 0))] * here,
        out_shape=[jax.ShapeDtypeStruct((model, width), BF16)]
        + [jax.ShapeDtypeStruct((count, 3 * head_dim, width), BF16)] * here,
        scratch_shapes=[pltpu.VMEM((shards, 384, depth), BF16)],
        compiler_params=pltpu.CompilerParams(vmem_limit_bytes=62 << 20),
        cost_estimate=pl.CostEstimate(
            flops=6 * width * model * model // COVER, bytes_accessed=12 * model * model, transcendentals=0
        ),
        name="project",
    )(core, tokens, gain, weights, weights, weights, cosine, sine)


def middle_kernel(
    shape, info_ref, mixed_ref, tokens_ref, cot_ref, out_w_ref, gain_ref, gate_w_ref, up_w_ref, down_w_ref, *rest
):
    head_dim, aliased = shape
    if aliased:
        rest = rest[1:]
    (
        output_ref, ordered_ref, flat_ref, hidden_ref, grad_gate_ref, grad_up_ref, grad_ffn_ref, grad_res_ref,
        grad_attn_ref, grad_mixed_ref, gain_out_ref, normed, residual, ffn_out, grad_normed, slots,
    ) = rest
    core = info_ref[2]
    step = pl.program_id(0)
    width = normed.shape[0]

    def valid():
        index = info_ref[1] + lax.broadcasted_iota(jnp.int32, (width, 1), 0)
        return jnp.where(index < info_ref[0], 1.0, 0.0)

    def inverse_of(x):
        return lax.rsqrt(jnp.mean(x * x, axis=-1, keepdims=True) + EPSILON)

    def head_rows(pair, slot):
        head = 2 * pair + (core if slot == 0 else 1 - core)
        return pl.ds(pl.multiple_of(head * head_dim, head_dim), head_dim)

    def slot_rows(pair, slot):
        return slice((2 * pair + slot) * head_dim, (2 * pair + slot + 1) * head_dim)

    spots = [(pair, slot) for pair in range(mixed_ref.shape[0] // head_dim // 2) for slot in range(2)]

    @pl.when(step == 0)
    def _():
        for spot in spots:
            ordered_ref[head_rows(*spot), :] = mixed_ref[slot_rows(*spot), :]
        inputs = tokens_ref[0, 0].astype(F32) + dot(ordered_ref[...].T, out_w_ref[...])
        residual[...] = inputs
        made = (inputs * inverse_of(inputs) * gain_ref[...]).astype(BF16)
        normed[...] = made
        flat_ref[...] = made.T
        grad_ffn_ref[...] = (cot_ref[0, 0].astype(F32) * valid()).astype(BF16)
        ffn_out[...] = jnp.zeros_like(ffn_out)
        grad_normed[...] = jnp.zeros_like(grad_normed)

    gate = dot(normed[...], gate_w_ref[...])
    up = dot(normed[...], up_w_ref[...])
    grad_hidden = contract(grad_ffn_ref[...], down_w_ref[...], 1, 1)
    sigmoid = sigmoid_of(gate)
    silu = gate * sigmoid
    hidden = (silu * up).astype(BF16)
    grad_gate = (grad_hidden * up * (sigmoid + silu * (1.0 - sigmoid))).astype(BF16)
    grad_up = (grad_hidden * silu).astype(BF16)
    hidden_ref[...] = hidden.T
    grad_gate_ref[...] = grad_gate
    grad_up_ref[...] = grad_up
    ffn_out[...] += dot(hidden, down_w_ref[...])
    grad_normed[...] += contract(grad_gate, gate_w_ref[...], 1, 1) + contract(grad_up, up_w_ref[...], 1, 1)

    @pl.when(step == pl.num_programs(0) - 1)
    def _():
        keep = valid()
        kept = residual[...]
        output_ref[0, 0] = ((kept + ffn_out[...]) * keep).astype(BF16)
        inverse = inverse_of(kept)
        scaled = grad_normed[...] * gain_ref[...]
        mean = jnp.mean(scaled * kept, axis=-1, keepdims=True)
        grad = cot_ref[0, 0].astype(F32) * keep
        grad = grad + (inverse * scaled - kept * (inverse * inverse * inverse) * mean)
        gain_out_ref[...] = jnp.sum(grad_normed[...] * kept * inverse, axis=0, keepdims=True)
        grad_res_ref[...] = grad
        low = grad.astype(BF16)
        grad_attn_ref[...] = low
        slots[...] = contract(out_w_ref[...], low, 1, 1).astype(BF16)
        for spot in spots:
            grad_mixed_ref[slot_rows(*spot), :] = slots[head_rows(*spot), :]


def middle_part(info, mixed, tokens, cotangent, unit, weights, gain, head_dim, output):
    width, model = tokens.shape[2:]
    out_w, gate_w, up_w, down_w = weights
    ffn = gate_w.shape[1]
    block = 512

    def fixed(a):
        return pl.BlockSpec(a.shape, lambda f, *_: (0,) * a.ndim)

    def one(*shape):
        return pl.BlockSpec(shape, lambda f, *_: (0,) * len(shape))

    token_spec = pl.BlockSpec((1, 1, width, model), lambda f, *_: unit + (0, 0))
    operands = [info, mixed, tokens, cotangent, out_w, gain, gate_w, up_w, down_w]
    in_specs = [
        fixed(mixed), token_spec, token_spec, fixed(out_w), fixed(gain),
        pl.BlockSpec((model, block), lambda f, *_: (0, f)),
        pl.BlockSpec((model, block), lambda f, *_: (0, f)),
        pl.BlockSpec((block, model), lambda f, *_: (f, 0)),
    ]
    aliases = {}
    if output is not None:
        aliases = {len(operands): 0}
        operands.append(output)
        in_specs.append(pl.BlockSpec(memory_space=pl.ANY))
    struct = jax.ShapeDtypeStruct
    return pl.pallas_call(
        functools.partial(middle_kernel, (head_dim, output is not None)),
        grid_spec=pltpu.PrefetchScalarGridSpec(
            num_scalar_prefetch=1,
            grid=(ffn // block,),
            in_specs=in_specs,
            out_specs=[
                token_spec, one(model, width), one(model, width),
                pl.BlockSpec((block, width), lambda f, *_: (f, 0)),
                pl.BlockSpec((width, block), lambda f, *_: (0, f)),
                pl.BlockSpec((width, block), lambda f, *_: (0, f)),
                one(width, model), one(width, model), one(width, model), one(model, width), one(1, model),
            ],
            scratch_shapes=[
                pltpu.VMEM((width, model), BF16),
                pltpu.VMEM((width, model), F32),
                pltpu.VMEM((width, model), F32),
                pltpu.VMEM((width, model), F32),
                pltpu.VMEM((model, width), BF16),
            ],
        ),
        out_shape=[
            struct(tokens.shape, BF16), struct((model, width), BF16), struct((model, width), BF16),
            struct((ffn, width), BF16),
            struct((width, ffn), BF16), struct((width, ffn), BF16), struct((width, model), BF16),
            struct((width, model), F32), struct((width, model), BF16), struct((model, width), BF16),
            struct((1, model), F32),
        ],
        input_output_aliases=aliases,
        compiler_params=pltpu.CompilerParams(vmem_limit_bytes=62 << 20),
        cost_estimate=pl.CostEstimate(
            flops=12 * width * model * ffn // COVER, bytes_accessed=8 * model * ffn, transcendentals=0
        ),
        name="middle_part",
    )(*operands)


def final_kernel(
    shape, core_ref, tokens_ref, grad_res_ref, gain_ref, query_ref, key_ref, value_ref, cos_ref, sin_ref, *rest
):
    here, head_dim, aliased = shape
    back = rest[:here]
    rest = rest[here:]
    if aliased:
        rest = rest[1:]
    out_ref, grad_q_ref, grad_k_ref, grad_v_ref, gain_out_ref, total = rest
    step = pl.program_id(0)
    cosine, sine = cos_ref[...], sin_ref[...]
    half = head_dim // 2

    def turned(x):
        first, second = x[:half].astype(F32), x[half:].astype(F32)
        return jnp.concatenate(
            [first * cosine + second * sine, second * cosine - first * sine], axis=0
        ).astype(BF16)

    for at in range(256 // head_dim):
        head = at
        if here == 2:
            head = at // 2 * 2 + (core_ref[0] if at % 2 == 0 else 1 - core_ref[0])
        place = pl.ds(pl.multiple_of(head * head_dim, head_dim), head_dim)
        part = back[at % here]
        grad_q_ref[place, :] = turned(part[at // here, 0:head_dim, :])
        grad_k_ref[place, :] = turned(part[at // here, head_dim : 2 * head_dim, :])
        grad_v_ref[place, :] = part[at // here, 2 * head_dim : 3 * head_dim, :]
    rows = [ref[...].T for ref in (grad_q_ref, grad_k_ref, grad_v_ref)]

    @pl.when(step == 0)
    def _():
        total[...] = jnp.zeros_like(total)

    depth = query_ref.shape[2]
    for shard in range(query_ref.shape[0]):
        made = dot(rows[0], query_ref[shard]) + dot(rows[1], key_ref[shard]) + dot(rows[2], value_ref[shard])
        total[:, shard * depth : (shard + 1) * depth] += made

    @pl.when(step == pl.num_programs(0) - 1)
    def _():
        inputs = tokens_ref[0, 0].astype(F32)
        inverse = lax.rsqrt(jnp.mean(inputs * inputs, axis=-1, keepdims=True) + EPSILON)
        scaled = total[...] * gain_ref[...]
        mean = jnp.mean(scaled * inputs, axis=-1, keepdims=True)
        grad = inverse * scaled - inputs * (inverse * inverse * inverse) * mean
        out_ref[0, 0] = (grad_res_ref[...] + grad).astype(BF16)
        gain_out_ref[...] = jnp.sum(total[...] * inputs * inverse, axis=0, keepdims=True)


def final_part(core, tokens, unit, grad_res, gain, weights, cosine, sine, back, head_dim, output):
    width, model = tokens.shape[2:]
    here = len(back)
    steps = model // 256

    def fixed(a):
        return pl.BlockSpec(a.shape, lambda c: (0,) * a.ndim)

    token_spec = pl.BlockSpec((1, 1, width, model), lambda c: unit + (0, 0))
    shards, _, depth = weights.shape
    weight_specs = [
        pl.BlockSpec((shards, 256, depth), lambda c, i=i: (0, i * steps + c, 0)) for i in range(3)
    ]
    row_spec = pl.BlockSpec((256, width), lambda c: (c, 0))
    operands = [core, tokens, grad_res, gain, weights, weights, weights, cosine, sine, *back]
    in_specs = [
        pl.BlockSpec(memory_space=pltpu.SMEM), token_spec, fixed(grad_res), fixed(gain), *weight_specs,
        fixed(cosine), fixed(sine),
    ] + [
        pl.BlockSpec((256 // head_dim // here, 3 * head_dim, width), lambda c: (c, 0, 0)) for _ in back
    ]
    aliases = {}
    if output is not None:
        aliases = {len(operands): 0}
        operands.append(output)
        in_specs.append(pl.BlockSpec(memory_space=pl.ANY))
    struct = jax.ShapeDtypeStruct
    return pl.pallas_call(
        functools.partial(final_kernel, (here, head_dim, output is not None)),
        grid=(steps,),
        in_specs=in_specs,
        out_specs=[token_spec, row_spec, row_spec, row_spec, pl.BlockSpec((1, model), lambda c: (0, 0))],
        out_shape=[
            struct(tokens.shape, BF16), struct((model, width), BF16), struct((model, width), BF16),
            struct((model, width), BF16), struct((1, model), F32),
        ],
        scratch_shapes=[pltpu.VMEM((width, model), F32)],
        input_output_aliases=aliases,
        compiler_params=pltpu.CompilerParams(vmem_limit_bytes=62 << 20),
        cost_estimate=pl.CostEstimate(
            flops=6 * width * model * model // COVER, bytes_accessed=12 * model * model, transcendentals=0
        ),
        name="final_part",
    )(*operands)


def picked_kernel(units, rows, places, flipped, split, table_ref, *refs):
    weights = len(places)
    lefts = refs[0:units]
    rights = refs[units : units * (1 + weights)]
    outs = refs[units * (1 + weights) : units * (1 + weights) + weights * split]
    picked = refs[units * (1 + weights) + weights * split :]

    @pl.when(pl.program_id(0) == 0)
    def _():
        for w, (start, size) in enumerate(places):
            for p in range(size):
                at = pl.ds(pl.multiple_of(table_ref[start + p] * rows, rows), rows)
                for u in range(units):
                    picked[w * units + u][p * rows : (p + 1) * rows, :] = lefts[u][at, :]

    for w in range(weights):
        total = None
        for u in range(units):
            right = rights[w * units + u][...]
            left = picked[w * units + u][...]
            made = contract(left, right, 1, 1) if flipped else dot(left, right)
            total = made if total is None else total + made
        height = total.shape[0] // split
        for i in range(split):
            outs[w * split + i][...] = total[i * height : (i + 1) * height].astype(BF16)


def picked_grads(table, places, lefts, rights, rows, flipped, split, block, name):
    units = len(lefts)
    width = lefts[0].shape[1]
    columns = rights[0].shape[0 if flipped else 1]
    in_specs = [pl.BlockSpec(a.shape, lambda n, *_: (0, 0)) for a in lefts]
    for a in rights:
        if flipped:
            in_specs.append(pl.BlockSpec((block, width), lambda n, *_: (n, 0)))
        else:
            in_specs.append(pl.BlockSpec((width, block), lambda n, *_: (0, n)))
    heights = [size * rows for _, size in places]
    return pl.pallas_call(
        functools.partial(picked_kernel, units, rows, places, flipped, split),
        grid_spec=pltpu.PrefetchScalarGridSpec(
            num_scalar_prefetch=1,
            grid=(columns // block,),
            in_specs=in_specs,
            out_specs=[
                pl.BlockSpec((height // split, block), lambda n, *_: (0, n)) for height in heights for _ in range(split)
            ],
            scratch_shapes=[pltpu.VMEM((height, width), BF16) for height in heights for _ in lefts],
        ),
        out_shape=[
            jax.ShapeDtypeStruct((height // split, columns), BF16) for height in heights for _ in range(split)
        ],
        compiler_params=pltpu.CompilerParams(vmem_limit_bytes=62 << 20),
        cost_estimate=pl.CostEstimate(
            flops=2 * units * sum(heights) * width * columns // COVER,
            bytes_accessed=4 * sum(heights) * columns,
            transcendentals=0,
        ),
        name=name,
    )(table, *lefts, *rights)


def weights_kernel(units, *refs):
    out_ref = refs[-1]
    total = dot(refs[0][...], refs[units][...])
    for u in range(1, units):
        total += dot(refs[u][...], refs[units + u][...])
    out_ref[...] = total.astype(BF16).reshape(out_ref.shape)


def weight_grad(lefts, rights, by_left, out_struct, out_spec, steps, into, name):
    units = len(lefts)

    def fixed(a):
        return pl.BlockSpec(a.shape, lambda n: (0, 0))

    def left_spec(a):
        return pl.BlockSpec((a.shape[0] // steps, a.shape[1]), lambda n: (n, 0))

    def right_spec(a):
        return pl.BlockSpec((a.shape[0], a.shape[1] // steps), lambda n: (0, n))

    operands = list(lefts) + list(rights)
    if by_left:
        in_specs = [left_spec(a) for a in lefts] + [fixed(a) for a in rights]
    else:
        in_specs = [fixed(a) for a in lefts] + [right_spec(a) for a in rights]
    aliases = {}
    if into is not None:
        aliases = {len(operands): 0}
        operands.append(into)
        in_specs.append(pl.BlockSpec(memory_space=pl.ANY))
    return pl.pallas_call(
        functools.partial(weights_kernel, units),
        grid=(steps,),
        in_specs=in_specs,
        out_specs=out_spec,
        out_shape=out_struct,
        input_output_aliases=aliases,
        compiler_params=pltpu.CompilerParams(vmem_limit_bytes=62 << 20),
        cost_estimate=pl.CostEstimate(
            flops=2 * units * lefts[0].shape[0] * lefts[0].shape[1] * rights[0].shape[1] // COVER,
            bytes_accessed=2 * lefts[0].shape[0] * rights[0].shape[1],
            transcendentals=0,
        ),
        name=name,
    )(*operands)


def reduce_kernel(orders, count, *refs):
    streams = len(orders)
    rounds = len(orders[0])
    ins, vec_ref = refs[:streams], refs[streams]
    outs, vec_out = refs[streams + 1 : 2 * streams + 1], refs[2 * streams + 1]
    rest = refs[2 * streams + 2 :]
    works, arrivals = rest[:streams], rest[streams : 2 * streams]
    vec_work, vec_arrival, send_sem, recv_sem, vec_send, vec_recv = rest[2 * streams :]
    shard, seq = lax.axis_index("shard"), lax.axis_index("seq")

    def partner(mask):
        if mask >= count:
            step = mask // count
            return (shard + step * (1 - 2 * (shard // step % 2)), seq)
        return (shard, seq + mask * (1 - 2 * (seq // mask % 2)))

    barrier = pltpu.get_barrier_semaphore()
    for mask in orders[0]:
        pl.semaphore_signal(
            barrier, inc=1, device_id=partner(mask), device_id_type=pl.DeviceIdType.MESH
        )
    pl.semaphore_wait(barrier, rounds)

    height = ins[0].shape[0]
    halves = [height >> (r + 1) for r in range(rounds)]
    starts = [sum(halves[:r]) for r in range(rounds)]

    def copy_of(s, r):
        source = ins[s] if r == 0 else works[s]
        return pltpu.make_async_remote_copy(
            src_ref=source.at[pl.ds(halves[r], halves[r])],
            dst_ref=arrivals[s].at[pl.ds(starts[r], halves[r])],
            send_sem=send_sem.at[s, r],
            recv_sem=recv_sem.at[s, r],
            device_id=partner(orders[s][r]),
            device_id_type=pl.DeviceIdType.MESH,
        )

    def vec_copy(r):
        return pltpu.make_async_remote_copy(
            src_ref=vec_ref if r == 0 else vec_work.at[r - 1],
            dst_ref=vec_arrival.at[r],
            send_sem=vec_send.at[r],
            recv_sem=vec_recv.at[r],
            device_id=partner(orders[0][r]),
            device_id_type=pl.DeviceIdType.MESH,
        )

    for s in range(streams):
        copy_of(s, 0).start()
    vec_copy(0).start()
    for r in range(rounds):
        for s in range(streams):
            copy_of(s, r).wait_recv()
            source = ins[s] if r == 0 else works[s]
            size = halves[r]

            def added(low, high):
                mine = source[low:high].astype(F32)
                return mine + arrivals[s][starts[r] + low : starts[r] + high].astype(F32)

            if r == rounds - 1:
                outs[s][...] = added(0, size)
            else:
                works[s][size // 2 : size] = added(size // 2, size).astype(BF16)
                copy_of(s, r + 1).start()
                works[s][0 : size // 2] = added(0, size // 2).astype(BF16)
        vec_copy(r).wait_recv()
        before = vec_ref[...] if r == 0 else vec_work[r - 1]
        if r == rounds - 1:
            vec_out[...] = before + vec_arrival[r]
        else:
            vec_work[r] = before + vec_arrival[r]
            vec_copy(r + 1).start()
    for r in range(rounds):
        for s in range(streams):
            copy_of(s, r).wait_send()
        vec_copy(r).wait_send()


def reduce_rows(parts, vector, orders, count):
    streams = len(parts)
    rounds = len(orders[0])
    height, columns = parts[0].shape
    rows = height >> rounds
    vmem = pl.BlockSpec(memory_space=pltpu.VMEM)
    return pl.pallas_call(
        functools.partial(reduce_kernel, orders, count),
        in_specs=[vmem] * (streams + 1),
        out_specs=[vmem] * (streams + 1),
        out_shape=[jax.ShapeDtypeStruct((rows, columns), F32)] * streams
        + [jax.ShapeDtypeStruct(vector.shape, F32)],
        scratch_shapes=[pltpu.VMEM((height // 2, columns), BF16) for _ in parts]
        + [pltpu.VMEM((height - rows, columns), BF16) for _ in parts]
        + [
            pltpu.VMEM((rounds - 1,) + vector.shape, F32),
            pltpu.VMEM((rounds,) + vector.shape, F32),
            pltpu.SemaphoreType.DMA((streams, rounds)),
            pltpu.SemaphoreType.DMA((streams, rounds)),
            pltpu.SemaphoreType.DMA((rounds,)),
            pltpu.SemaphoreType.DMA((rounds,)),
        ],
        compiler_params=pltpu.CompilerParams(
            collective_id=0, has_side_effects=True, vmem_limit_bytes=62 << 20
        ),
        name="reduce_rows",
    )(*parts, vector)


def on_device(
    tokens, cotangent, lengths, variates, positions, attn_gain, w_query, w_key, w_value, w_out,
    bias_table, ffn_gain, w_gate, w_up, w_down,
):
    micro, seqs, width, model = tokens.shape
    heads = bias_table.shape[0]
    head_dim = model // heads
    count = lax.axis_size("seq")
    here = heads // count
    ffn = w_gate.shape[1]
    devices = lax.axis_size("shard") * count
    seq_index = lax.axis_index("seq")
    units = [(m, s) for m in range(micro) for s in range(seqs)]
    swap = here == 2 and len(units) == 2 and lax.axis_size("shard") % 2 == 0
    core = (lax.axis_index("shard") % 2 if swap else jnp.int32(0)).astype(jnp.int32).reshape(1)
    heads_here = 1 if swap else here
    first_head = seq_index * here + core[0]
    bias_here = lax.dynamic_slice_in_dim(bias_table, first_head, heads_here, 0)
    attn_row, ffn_row = attn_gain[None, :], ffn_gain[None, :]

    def gather(weight):
        return lax.all_gather(weight, "shard", axis=0, tiled=True)

    def exchange(values):
        return lax.all_to_all(values, "seq", split_axis=0, concat_axis=0, tiled=True)

    def after(value, *before):
        return lax.optimization_barrier((value,) + before)[0]

    attn_rows = turn_weights(w_query, w_key, w_value)
    attn_joined = lax.all_gather(attn_rows, "shard", axis=0, tiled=False)
    ffn_weights = [gather(w_out), gather(w_gate), gather(w_up), gather(w_down)]

    def permute(value, mask):
        return lax.ppermute(value, ("shard", "seq"), [(i, i ^ mask) for i in range(devices)])

    def cross(value):
        return permute(value, count)

    lengths_of = [lengths, cross(lengths)] if swap else [lengths] * here
    ids_own = lax.all_gather(variates, "seq", axis=0, tiled=False)
    ids_of = [ids_own, cross(ids_own)] if swap else [ids_own] * here
    attn_joined = after(attn_joined, *ids_of)

    def ids_rows(u, h):
        m, s = units[u]
        return ids_of[h][:, m, s].astype(F32)[:, None, :]

    packed_list, flats, tables = [], [], []

    def run_project(u, token):
        m, s = units[u]
        cosine, sine = rotary_tables(positions[m, s], head_dim // 2)
        flat, *packed = project(
            core, tokens, (m, s), after(attn_row, *token), attn_joined, cosine, sine, count, here, head_dim,
            swap,
        )
        flats.append(flat)
        tables.append((cosine, sine))
        packed_list.append(packed)

    sent = {}
    mixed_now = [None] * len(units)
    sums = {}
    mixed_tok = {}
    crossed, mixed_part, mixed_cross, heads_cross, back_cross = {}, {}, {}, {}, {}
    middle = [None] * len(units)
    grad_heads = {}
    state = {"output": None, "grads": None}
    packed_grads = {}
    returned = {}
    bias_terms = {}
    finals = [None] * len(units)

    def length_of(u, h, token):
        m, s = units[u]
        return after(lengths_of[h][m, s].reshape(1), *token)

    def inputs_of(u, h):
        return (crossed[u] if swap and h == 1 else sent[u, h]), ids_rows(u, h)

    def run_forward(u, h, token):
        made, sums[u, h] = attend_forward(
            *inputs_of(u, h), length_of(u, h, token), bias_here, None if swap else mixed_now[u],
            0 if swap else h, heads_here, head_dim,
        )
        if swap:
            mixed_part[u, h] = made
            if h == 1:
                mixed_cross[u] = cross(made)
        else:
            mixed_now[u] = made
        return sums[u, h]

    def run_middle(u, token):
        m, s = units[u]
        info = jnp.stack([lengths[m, s], seq_index * width, core[0]]).astype(jnp.int32)
        state["output"], mixed_tok[u], *middle[u] = middle_part(
            after(info, *token), mixed_tok[u], tokens, cotangent, (m, s), ffn_weights, ffn_row, head_dim,
            state["output"],
        )
        return middle[u][8]

    def run_backward(u, h, token):
        if swap:
            token = token + ((heads_cross[1],) if (u, h) == (0, 1) else ())
            grad = grad_heads[u] if h == 0 else heads_cross[u]
            mixed = mixed_part[u, h]
        else:
            grad, mixed = grad_heads[u], mixed_now[u]
        packed_grads[u, h], both = attend_backward(
            *inputs_of(u, h), grad, mixed, sums[u, h], length_of(u, h, token), bias_here,
            0 if swap else h, head_dim,
        )
        if swap and h == 1:
            back_cross[u] = cross(packed_grads[u, h])
        bias_terms[u, h] = both
        return both

    def run_final(u, token):
        m, s = units[u]
        cosine, sine = tables[u]
        state["grads"], *finals[u] = final_part(
            core, tokens, (m, s), middle[u][5], after(attn_row, *token), attn_joined, cosine, sine,
            [returned[u, h] for h in range(here)], head_dim, state["grads"],
        )
        return finals[u][3]

    rows = model // devices
    fold = ffn // model
    tall = ffn // devices
    seq_masks = [1 << i for i in range(count.bit_length() - 1)]
    shard_masks = [count << i for i in range((devices // count).bit_length() - 1)]
    spread = shard_masks[1:]
    orders = (
        shard_masks[:1] + spread + seq_masks,
        shard_masks[:1] + seq_masks[:1] + spread + seq_masks[1:],
        shard_masks[:1] + seq_masks[1:2] + seq_masks[:1] + spread + seq_masks[2:],
    )
    direct = rows % 16 == 0 and devices == 1 << len(orders[0])

    def places_of(order):
        marks = []
        for p in range(devices):
            bits = [p >> (len(order) - 1 - i) & 1 for i in range(len(order))]
            marks.append(sum(mask for bit, mask in zip(bits, order) if bit))
        me = lax.axis_index("shard") * count + seq_index
        return me.astype(jnp.int32) ^ jnp.array(marks, jnp.int32)

    def column(index):
        return [item[index] for item in middle]

    def run_weights(token):
        if not direct:
            return [
                sum(dot(left, right) for left, right in zip(lefts, rights)).astype(BF16)
                for lefts, rights in (
                    (column(0), column(2)), (column(0), column(3)), (column(1), column(4)),
                    ([mixed_tok[u] for u in range(len(units))], column(6)),
                )
            ]
        part = ffn // fold
        narrow = model // fold
        spare = -(-(2 * part + narrow) // 384) * 384
        struct = jax.ShapeDtypeStruct((devices, fold, rows, spare), BF16)
        down = pl.BlockSpec((512 // tall, fold, rows, model), lambda n: (n, 0, 0, 0))
        gate = pl.BlockSpec((devices, 1, rows, part), lambda n: (0, n, 0, 1))
        out = pl.BlockSpec((devices, 1, rows, narrow), lambda n: (0, n, 0, 2 * part // narrow))
        table = after(places_of(orders[0]), *token)
        up = picked_grads(table, [(0, devices)], column(0), column(3), rows, False, 2, 1024, "up_grad")
        holder["streams"] = [[up[0], permute(up[1], orders[0][0]), orders[0][1:]]]
        firsts = [after(middle[0][4], up[0])] + [item[4] for item in middle[1:]]
        terms = weight_grad(column(1), firsts, True, struct, down, ffn // 512, None, "down_grad")
        landed = (holder["streams"][0][1],) + ((heads_cross[0],) if swap else ())
        rights = [after(middle[0][2], *holder["flying"], *landed)] + [item[2] for item in middle[1:]]
        terms = weight_grad(column(0), rights, False, struct, gate, fold, terms, "gate_grad")
        mixed_all = [mixed_tok[u] for u in range(len(units))]
        terms = weight_grad(mixed_all, column(6), False, struct, out, fold, terms, "out_grad")
        terms = terms.reshape(ffn, spare)
        holder["half"] = lax.psum_scatter(terms, "shard", scatter_dimension=0, tiled=True)
        return terms

    def wide_sum(a, b):
        return a.astype(F32) + b.astype(F32)

    def advance(token):
        out = ()
        if not direct:
            return out
        for stream in holder["streams"]:
            keep, came, masks = stream
            if not masks:
                continue
            keep = after(keep, *token)
            half = keep.shape[0] // 2
            send = wide_sum(keep[half:], came[half:]).astype(BF16)
            stream[0] = wide_sum(keep[:half], came[:half]).astype(BF16)
            stream[1] = permute(send, masks[0])
            stream[2] = masks[1:]
            out = out + (send, stream[0])
        return out

    holder = {}

    def weights_work(token):
        holder["terms"] = run_weights(token)
        return holder["terms"]

    def send_packed(u, h):
        def keep(moved):
            sent[u, h] = moved
            if swap and h == 1:
                crossed[u] = cross(moved)

        return lambda: packed_list[u][h], keep

    def send_mixed(u):
        def keep(moved):
            mixed_tok[u] = moved.reshape(model, width)

        if not swap:
            return lambda: mixed_now[u], keep
        return lambda: jnp.concatenate([mixed_part[u, 0], mixed_cross[u]], axis=1), keep

    def send_heads(u):
        def keep(moved):
            grad_heads[u] = moved
            if swap:
                heads_cross[u] = cross(moved[:, head_dim:])

        return lambda: middle[u][7].reshape(count, here * head_dim, width), keep

    def send_back(u, h):
        def keep(moved):
            returned[u, h] = moved

        return lambda: back_cross[u] if swap and h == 1 else packed_grads[u, h], keep

    def work_project(u):
        def work(token):
            run_project(u, token)
            return flats[u]

        return work

    def work(function, *args):
        return lambda token: function(*args, token)

    total = len(units)
    order = [(u, h) for u in range(total) for h in range(here)]
    if swap:
        steps = [
            (work_project(0), None),
            (work_project(1), send_packed(0, 1)),
            (work(run_forward, 0, 1), send_packed(0, 0)),
            (work(run_forward, 0, 0), send_packed(1, 1)),
            (work(run_forward, 1, 1), send_packed(1, 0)),
            (work(run_forward, 1, 0), send_mixed(0)),
            (work(run_middle, 0), send_mixed(1)),
            (work(run_middle, 1), send_heads(0)),
            (weights_work, send_heads(1)),
            (work(run_backward, 0, 0), None),
            (work(run_backward, 0, 1), send_back(0, 0)),
            (work(run_backward, 1, 0), send_back(0, 1)),
            (work(run_backward, 1, 1), send_back(1, 0)),
            (work(run_final, 0), send_back(1, 1)),
            (work(run_final, 1), None),
        ]
    else:
        steps = [(work_project(u), None) for u in range(total)]
        steps += [(None, send_packed(*at)) for at in order]
        for u in range(total):
            steps += [(work(run_forward, u, h), None) for h in range(here)]
            steps += [(None, send_mixed(u))]
        for u in range(total):
            steps += [(work(run_middle, u), None), (None, send_heads(u))]
        steps += [(weights_work, None)]
        for at in order:
            steps += [(work(run_backward, *at), None), (None, send_back(*at))]
        steps += [(work(run_final, u), None) for u in range(total)]

    late = [task for task, _ in steps[-2:]]
    token = ()
    for index, (task, send) in enumerate(steps):
        done = ()
        moved = None
        ahead = ()
        if "streams" in holder:
            leaving = advance(token[-1:])
            if index == len(steps) - 5:
                ahead = leaving
            elif task not in late:
                token = token + leaving
        if "half" in holder and index == len(steps) - 2:
            half = after(holder["half"], *token)
            holder["owned"] = lax.psum_scatter(half, "seq", scatter_dimension=0, tiled=True)
        if send is not None:
            moved = exchange(after(send[0](), *token))
            done = (moved,)
        holder["flying"] = done
        if task is not None:
            done = done + (task(token + ahead),)
        if send is not None:
            send[1](after(moved, *done[1:]))
        token = done
    acc_bias = jnp.concatenate(
        [sum(bias_terms[u, h] for u in range(total))[0:1, 0:2] for h in range(here)], axis=0
    )
    if swap:
        acc_bias = acc_bias[0:1] + acc_bias[1:2]
    bias_full = lax.dynamic_update_slice(
        jnp.zeros((heads, 2), F32), acc_bias, (first_head, jnp.int32(0))
    )
    gain_attn = sum(item[3][0] for item in finals)
    gain_ffn = sum(item[8][0] for item in middle)
    if direct:
        while holder["streams"][0][2]:
            advance(token)
        keep, came, _ = holder["streams"][0]
        up_own = wide_sum(after(keep, *token), came)
        flats[0] = after(flats[0], up_own)
        owned, part = holder["owned"], ffn // fold

        def joined(start, size):
            piece = owned[:, start : start + size].reshape(fold, rows, size)
            return jnp.swapaxes(piece, 0, 1).reshape(rows, fold * size).astype(F32)

        down_own = owned[:, :part].astype(F32)
        gate_own, out_own = joined(part, part), joined(2 * part, model // fold)
        table = jnp.concatenate([places_of(order) for order in orders])
        attn_terms = picked_grads(
            table, [(i * devices, devices) for i in range(3)], flats,
            [item[i] for i in range(3) for item in finals], rows, True, 1, 256, "attn_grads",
        )
        flat = jnp.concatenate([gain_attn, gain_ffn, bias_full.reshape(-1)])
        tiles = -(-flat.shape[0] // 1024) * 8
        flat = jnp.pad(flat, (0, tiles * 128 - flat.shape[0])).reshape(tiles, 128)
        query_own, key_own, value_own, flat = reduce_rows(list(attn_terms), flat, orders, count)
        flat = flat.reshape(-1)
        gain_attn, gain_ffn = flat[:model], flat[model : 2 * model]
        bias_full = flat[2 * model : 2 * model + 2 * heads].reshape(heads, 2)
    else:

        def scatter(value):
            owned = lax.psum_scatter(value, ("shard", "seq"), scatter_dimension=0, tiled=True)
            return owned.astype(F32)

        gate_own, up_own, down_own, out_own = [scatter(value) for value in holder["terms"]]
        query_own, key_own, value_own = [
            scatter(
                sum(contract(flat, item[i], 1, 1) for flat, item in zip(flats, finals)).astype(BF16)
            )
            for i in range(3)
        ]
        gain_attn, gain_ffn, bias_full = lax.psum(
            (gain_attn, gain_ffn, bias_full), ("shard", "seq")
        )
    return (
        state["output"], state["grads"], gain_attn, query_own, key_own, value_own, out_own,
        bias_full, gain_ffn, gate_own, up_own, down_own,
    )


def solution(mesh):
    token_spec = P(None, "shard", "seq", None)
    row_spec = P("shard", None)
    in_specs = (
        token_spec, token_spec, P(None, "shard"), P(None, "shard", "seq"), P(None, "shard", "seq"),
        P(), row_spec, row_spec, row_spec, row_spec, P(), P(), row_spec, row_spec, row_spec,
    )
    owned = P(("shard", "seq"), None)
    out_specs = (
        token_spec, token_spec, P(), owned, owned, owned, owned, P(), P(), owned, owned, owned,
    )
    return jax.shard_map(
        on_device, mesh=mesh, in_specs=in_specs, out_specs=out_specs, check_vma=False
    )
```

```python
import functools
import math

import jax
import jax.numpy as jnp
from jax import lax
from jax.experimental import pallas as pl
from jax.experimental.pallas import tpu as pltpu
from jax.sharding import PartitionSpec as P

EPSILON = 1e-06
ROTARY_BASE = 10000.0
LOG2E = 1.4426950408889634
LN2 = 0.6931471805599453
CLASSES = 8
COVER = 16
EXTRA = 32
MASKED = -1.5e9
FAR = 1e30
F32 = jnp.float32
BF16 = jnp.bfloat16


def dot(a, b):
    return jnp.dot(a, b, preferred_element_type=F32)


def contract(a, b, da, db):
    return lax.dot_general(a, b, (((da,), (db,)), ((), ())), preferred_element_type=F32)


def pieces(x):
    high = x.astype(BF16).astype(F32)
    rest = x - high
    mid = rest.astype(BF16).astype(F32)
    low = (rest - mid).astype(BF16).astype(F32)
    return high, mid, low


def one_hot(row):
    classes = lax.broadcasted_iota(jnp.int32, (CLASSES, row.shape[1]), 0).astype(F32)
    return jnp.where(classes == row, 1.0, 0.0)


def rows_of(values, width):
    index = lax.broadcasted_iota(jnp.int32, (8, width), 0)
    out = jnp.zeros((8, width), F32)
    for at, value in enumerate(values):
        out = jnp.where(index == at, value, out)
    return out


def key_extra(row, start, length, other, same):
    width = row.shape[1]
    hot = one_hot(row)
    step = pieces(jnp.full((1, width), same - other, F32))
    base = pieces(jnp.full((1, width), other, F32))
    index = start + lax.broadcasted_iota(jnp.int32, (1, width), 1)
    mask = jnp.where(index < length, 0.0, MASKED)
    tail = rows_of(base + (mask, 1.0, 1.0, 1.0), width)
    return jnp.concatenate([hot * step[0], hot * step[1], hot * step[2], tail], axis=0).astype(BF16)


def query_extra(row, shift):
    hot = one_hot(row)
    tail = rows_of((1.0, 1.0, 1.0, 1.0) + shift, row.shape[1])
    return jnp.concatenate([hot, hot, hot, tail], axis=0).astype(BF16)


def forward_kernel(
    shape, len_ref, bias_ref, x_ref, ids_ref, *rest
):
    local, head_dim, block, aliased = shape
    if aliased:
        rest = rest[1:]
    mixed_ref, lse_ref, keys, vals, query, score, peak, total = rest
    count, _, width = x_ref.shape
    sub = block // width
    step = pl.program_id(0)
    length = len_ref[0]
    other = bias_ref[local, 0] * LOG2E
    same = bias_ref[local, 1] * LOG2E

    @pl.when(step == 0)
    def _():
        for b in range(count):
            at = pl.ds(b * width, width)
            row = ids_ref[b, 0:1, :].astype(F32)
            extra = key_extra(row, b * width, length, other, same)
            full = jnp.concatenate([x_ref[b, head_dim : 2 * head_dim, :], extra], axis=0)
            keys[at, :] = full.T
            vals[0:head_dim, at] = x_ref[b, 2 * head_dim : 3 * head_dim, :]
        vals[head_dim:, :] = jnp.ones((16, vals.shape[1]), BF16)

    used = pl.cdiv(length, block)
    inside = step * block < length

    @pl.when(jnp.logical_not(inside))
    def _():
        mixed_ref[...] = jnp.zeros_like(mixed_ref)
        lse_ref[...] = jnp.full(lse_ref.shape, FAR, F32)

    @pl.when(inside)
    def _():
        for b in range(sub):
            at = slice(b * width, (b + 1) * width)
            row = ids_ref[step * sub + b, 0:1, :].astype(F32)
            query[0:head_dim, at] = x_ref[step * sub + b, 0:head_dim, :]
            query[head_dim:, at] = query_extra(row, (0.0, 0.0, 0.0))
        peak[...] = jnp.full(peak.shape, -FAR, F32)
        total[...] = jnp.zeros_like(total)

        def span(j):
            return pl.ds(pl.multiple_of(j * block, block), block)

        def scores_of(j):
            return dot(keys[span(j), :], query[...])

        def one(j, now, ahead):
            if ahead:
                score[1 - now] = scores_of(j + 1)
            current = score[now]
            before = peak[...]
            top = jnp.maximum(before, jnp.max(current, axis=0, keepdims=True))
            weight = jnp.exp2(current - top).astype(BF16)
            peak[...] = top
            total[...] = total[...] * jnp.exp2(before - top) + dot(vals[:, span(j)], weight)

        score[0] = scores_of(0)
        pairs = (used - 1) // 2

        def pair(j, carry):
            one(2 * j, 0, True)
            one(2 * j + 1, 1, True)
            return carry

        lax.fori_loop(0, pairs, pair, 0)
        last = 2 * pairs

        @pl.when(used - last == 1)
        def _():
            one(last, 0, False)

        @pl.when(used - last == 2)
        def _():
            one(last, 0, True)
            one(last + 1, 1, False)

        mass = total[head_dim : head_dim + 1, :]
        mixed = (total[0:head_dim, :] / mass).astype(BF16)
        for b in range(sub):
            mixed_ref[b] = mixed[:, b * width : (b + 1) * width]
        lse_ref[0] = peak[...] + jnp.log2(mass)


def attend_forward(x, ids, length, bias, mixed, local, heads_here, head_dim):
    count, rows, width = x.shape
    block = max(width, 512)
    seq_len = count * width
    blocks = seq_len // block
    depth = head_dim + EXTRA
    whole = pl.BlockSpec((count, rows, width), lambda i, *_: (0, 0, 0))
    operands = [length, bias, x, ids]
    in_specs = [whole, pl.BlockSpec((count, 1, width), lambda i, *_: (0, 0, 0))]
    aliases = {}
    if mixed is not None:
        operands.append(mixed)
        in_specs.append(pl.BlockSpec(memory_space=pl.ANY))
        aliases = {4: 0}
    return pl.pallas_call(
        functools.partial(forward_kernel, (local, head_dim, block, mixed is not None)),
        grid_spec=pltpu.PrefetchScalarGridSpec(
            num_scalar_prefetch=2,
            grid=(blocks,),
            in_specs=in_specs,
            out_specs=[
                pl.BlockSpec((block // width, head_dim, width), lambda i, *_: (i, local, 0)),
                pl.BlockSpec((1, 1, block), lambda i, *_: (i, 0, 0)),
            ],
            scratch_shapes=[
                pltpu.VMEM((seq_len, depth), BF16),
                pltpu.VMEM((head_dim + 16, seq_len), BF16),
                pltpu.VMEM((depth, block), BF16),
                pltpu.VMEM((2, block, block), F32),
                pltpu.VMEM((1, block), F32),
                pltpu.VMEM((head_dim + 16, block), F32),
            ],
        ),
        out_shape=[
            jax.ShapeDtypeStruct((count, heads_here * head_dim, width), BF16),
            jax.ShapeDtypeStruct((blocks, 1, block), F32),
        ],
        input_output_aliases=aliases,
        compiler_params=pltpu.CompilerParams(vmem_limit_bytes=62 << 20),
        cost_estimate=pl.CostEstimate(
            flops=8 * seq_len * seq_len * 256 // COVER,
            bytes_accessed=x.size * 4,
            transcendentals=0,
        ),
        name="attend_forward",
    )(*operands)


def backward_kernel(
    shape, len_ref, bias_ref, x_ref, ids_ref, grad_ref, mixed_ref, lse_ref, out_ref, bias_out_ref,
    keys, keys_flat, vals, query, grads, query_rows, grad_rows, acc_keys, acc_vals, acc_query,
):
    local, head_dim, block = shape
    count, _, width = x_ref.shape
    sub = block // width
    step = pl.program_id(0)
    length = len_ref[0]
    other = bias_ref[local, 0] * LOG2E
    same = bias_ref[local, 1] * LOG2E

    @pl.when(step == 0)
    def _():
        ones = jnp.ones((16, width), BF16)
        for b in range(count):
            at = pl.ds(b * width, width)
            row = ids_ref[b, 0:1, :].astype(F32)
            extra = key_extra(row, b * width, length, other, same)
            here = x_ref[b, head_dim : 2 * head_dim, :]
            keys[at, :] = jnp.concatenate([here, extra], axis=0).T
            keys_flat[:, at] = here
            vals[at, :] = jnp.concatenate([x_ref[b, 2 * head_dim : 3 * head_dim, :], ones], axis=0).T
        acc_keys[...] = jnp.zeros_like(acc_keys)
        acc_vals[...] = jnp.zeros_like(acc_vals)

    used = pl.cdiv(length, block)
    inside = step * block < length

    @pl.when(jnp.logical_not(inside))
    def _():
        for b in range(sub):
            out_ref[step * sub + b, 0:head_dim, :] = jnp.zeros((head_dim, width), BF16)

    @pl.when(inside)
    def _():
        for b in range(sub):
            at = slice(b * width, (b + 1) * width)
            here = step * sub + b
            row = ids_ref[here, 0:1, :].astype(F32)
            shift = pieces(-lse_ref[step][:, at])
            grad = grad_ref[here]
            delta = jnp.sum(grad.astype(F32) * mixed_ref[here].astype(F32), axis=0, keepdims=True)
            query[0:head_dim, at] = x_ref[here, 0:head_dim, :]
            query[head_dim:, at] = query_extra(row, shift)
            grads[0:head_dim, at] = grad
            tail = rows_of(pieces(-delta), width)
            grads[head_dim:, at] = jnp.concatenate([tail, jnp.zeros_like(tail)], axis=0).astype(BF16)
        query_rows[...] = query[...].T
        grad_rows[...] = grads[...].T
        acc_query[...] = jnp.zeros_like(acc_query)

        def one(j):
            at = pl.ds(pl.multiple_of(j * block, block), block)
            probs = jnp.exp2(dot(keys[at, :], query[...]))
            grad_probs = dot(vals[at, :], grads[...])
            grad_scores = (probs * grad_probs).astype(BF16)
            acc_vals[at, :] += dot(probs.astype(BF16), grad_rows[...])
            acc_keys[at, :] += dot(grad_scores, query_rows[...])
            acc_query[...] += dot(keys_flat[:, at], grad_scores)

        def pair(j, carry):
            one(2 * j)
            one(2 * j + 1)
            return carry

        lax.fori_loop(0, used // 2, pair, 0)

        @pl.when(used % 2 == 1)
        def _():
            one(used - 1)

        grad_query = (acc_query[...] * (1.0 / math.sqrt(head_dim))).astype(BF16)
        for b in range(sub):
            out_ref[step * sub + b, 0:head_dim, :] = grad_query[:, b * width : (b + 1) * width]

    @pl.when(step == pl.num_programs(0) - 1)
    def _():
        same_total = jnp.zeros((CLASSES, width), F32)
        all_total = jnp.zeros((CLASSES, width), F32)
        for b in range(count):
            at = pl.ds(b * width, width)
            row = ids_ref[b, 0:1, :].astype(F32)
            flat = acc_keys[at, :].T
            out_ref[b, head_dim : 2 * head_dim, :] = (flat[0:head_dim] * LN2).astype(BF16)
            out_ref[b, 2 * head_dim : 3 * head_dim, :] = acc_vals[at, :].T[0:head_dim].astype(BF16)
            by_class = flat[head_dim : head_dim + CLASSES]
            all_total += by_class
            same_total += by_class * one_hot(row)
        same_sum = jnp.sum(same_total, keepdims=True)
        other_sum = jnp.sum(all_total, keepdims=True) - same_sum
        lane = lax.broadcasted_iota(jnp.int32, (8, 128), 1)
        bias_out_ref[...] = jnp.where(lane == 0, other_sum, jnp.where(lane == 1, same_sum, 0.0))


def attend_backward(x, ids, grad, mixed, lse, length, bias, local, head_dim):
    count, rows, width = x.shape
    blocks, _, block = lse.shape
    seq_len = count * width
    depth = head_dim + EXTRA

    def whole(a):
        return pl.BlockSpec(a.shape, lambda i, *_: (0,) * a.ndim)

    head_spec = pl.BlockSpec((count, head_dim, width), lambda i, *_: (0, local, 0))
    return pl.pallas_call(
        functools.partial(backward_kernel, (local, head_dim, block)),
        grid_spec=pltpu.PrefetchScalarGridSpec(
            num_scalar_prefetch=2,
            grid=(blocks,),
            in_specs=[
                whole(x),
                pl.BlockSpec((count, 1, width), lambda i, *_: (0, 0, 0)),
                head_spec, head_spec, whole(lse),
            ],
            out_specs=[
                pl.BlockSpec((count, 3 * head_dim, width), lambda i, *_: (0, 0, 0)),
                pl.BlockSpec((8, 128), lambda i, *_: (0, 0)),
            ],
            scratch_shapes=[
                pltpu.VMEM((seq_len, depth), BF16),
                pltpu.VMEM((head_dim, seq_len), BF16),
                pltpu.VMEM((seq_len, head_dim + 16), BF16),
                pltpu.VMEM((depth, block), BF16),
                pltpu.VMEM((head_dim + 16, block), BF16),
                pltpu.VMEM((block, depth), BF16),
                pltpu.VMEM((block, head_dim + 16), BF16),
                pltpu.VMEM((seq_len, depth), F32),
                pltpu.VMEM((seq_len, head_dim + 16), F32),
                pltpu.VMEM((head_dim, block), F32),
            ],
        ),
        out_shape=[
            jax.ShapeDtypeStruct((count, 3 * head_dim, width), BF16),
            jax.ShapeDtypeStruct((8, 128), F32),
        ],
        compiler_params=pltpu.CompilerParams(vmem_limit_bytes=62 << 20),
        cost_estimate=pl.CostEstimate(
            flops=20 * seq_len * seq_len * 256 // COVER,
            bytes_accessed=x.size * 6,
            transcendentals=0,
        ),
        name="attend_backward",
    )(length, bias, x, ids, grad, mixed, lse)


def rotary_tables(places, half_dim):
    frequency = jnp.exp(-math.log(ROTARY_BASE) * jnp.arange(half_dim, dtype=F32) / half_dim)
    angles = places.astype(F32)[None, :] * frequency[:, None]
    return jnp.cos(angles), jnp.sin(angles)


def sigmoid_of(x):
    return 1.0 / (1.0 + jnp.exp2(x * -LOG2E))


def turn_kernel(*refs):
    out_ref = refs[-1]
    size = refs[0].shape[1]
    for i, ref in enumerate(refs[:-1]):
        out_ref[i * size : (i + 1) * size, :] = ref[...].T


def turn_weights(*weights):
    depth, size = weights[0].shape
    vmem = pl.BlockSpec(memory_space=pltpu.VMEM)
    return pl.pallas_call(
        turn_kernel,
        in_specs=[vmem] * len(weights),
        out_specs=vmem,
        out_shape=jax.ShapeDtypeStruct((len(weights) * size, depth), BF16),
        compiler_params=pltpu.CompilerParams(vmem_limit_bytes=62 << 20),
        name="turn_weights",
    )(*weights)


def project_kernel(
    shape, core_ref, tokens_ref, gain_ref, query_ref, key_ref, value_ref, cos_ref, sin_ref, flat_ref, *rest
):
    here, head_dim, swap = shape
    outs, flat_weights = rest[:-1], rest[-1]
    pair = pl.program_id(0)

    @pl.when(pair == 0)
    def _():
        inputs = tokens_ref[0, 0].astype(F32)
        inverse = lax.rsqrt(jnp.mean(inputs * inputs, axis=-1, keepdims=True) + EPSILON)
        flat_ref[...] = (inputs * inverse * gain_ref[...]).astype(BF16).T

    made = None
    depth = query_ref.shape[2]
    for shard in range(query_ref.shape[0]):
        for at, ref in enumerate((query_ref, key_ref, value_ref)):
            flat_weights[shard, at * 128 : (at + 1) * 128, :] = ref[shard]
        term = dot(flat_weights[shard], flat_ref[shard * depth : (shard + 1) * depth, :])
        made = term if made is None else made + term
    cosine, sine = cos_ref[...], sin_ref[...]
    half = head_dim // 2

    def turned(start, scale):
        first = made[start : start + half]
        second = made[start + half : start + head_dim]
        both = [first * cosine - second * sine, second * cosine + first * sine]
        return (jnp.concatenate(both, axis=0) * scale).astype(BF16)

    def put(at, slot, place):
        spot = at * head_dim
        target = outs[slot]
        target[place, 0:head_dim, :] = turned(spot, LOG2E / math.sqrt(head_dim))
        target[place, head_dim : 2 * head_dim, :] = turned(128 + spot, 1.0)
        target[place, 2 * head_dim : 3 * head_dim, :] = made[256 + spot : 256 + spot + head_dim].astype(BF16)

    if swap:
        for core in range(2):

            @pl.when(core_ref[0] == core)
            def _():
                put(core, 0, 0)
                put(1 - core, 1, 0)

    else:
        for at in range(128 // head_dim):
            put(at, at % here, 0 if here > 1 else at)


def project(core, tokens, unit, gain, weights, cosine, sine, count, here, head_dim, swap):
    width, model = tokens.shape[2:]
    heads = count * here
    pairs = heads * head_dim // 128
    per = 128 // head_dim // here

    def fixed(a):
        return pl.BlockSpec(a.shape, lambda p: (0,) * a.ndim)

    shards, _, depth = weights.shape
    weight_specs = [
        pl.BlockSpec((shards, 128, depth), lambda p, i=i: (0, i * pairs + p, 0)) for i in range(3)
    ]
    return pl.pallas_call(
        functools.partial(project_kernel, (here, head_dim, swap)),
        grid=(pairs,),
        in_specs=[
            pl.BlockSpec(memory_space=pltpu.SMEM),
            pl.BlockSpec((1, 1, width, model), lambda p: unit + (0, 0)),
            fixed(gain), *weight_specs, fixed(cosine), fixed(sine),
        ],
        out_specs=[pl.BlockSpec((model, width), lambda p: (0, 0))]
        + [pl.BlockSpec((per, 3 * head_dim, width), lambda p: (p, 0, 0))] * here,
        out_shape=[jax.ShapeDtypeStruct((model, width), BF16)]
        + [jax.ShapeDtypeStruct((count, 3 * head_dim, width), BF16)] * here,
        scratch_shapes=[pltpu.VMEM((shards, 384, depth), BF16)],
        compiler_params=pltpu.CompilerParams(vmem_limit_bytes=62 << 20),
        cost_estimate=pl.CostEstimate(
            flops=6 * width * model * model // COVER, bytes_accessed=12 * model * model, transcendentals=0
        ),
        name="project",
    )(core, tokens, gain, weights, weights, weights, cosine, sine)


def middle_kernel(
    shape, info_ref, mixed_ref, tokens_ref, cot_ref, out_w_ref, gain_ref, gate_w_ref, up_w_ref, down_w_ref, *rest
):
    head_dim, aliased = shape
    if aliased:
        rest = rest[1:]
    (
        output_ref, ordered_ref, flat_ref, hidden_ref, grad_gate_ref, grad_up_ref, grad_ffn_ref, grad_res_ref,
        grad_attn_ref, grad_mixed_ref, gain_out_ref, normed, residual, ffn_out, grad_normed, slots,
    ) = rest
    core = info_ref[2]
    step = pl.program_id(0)
    width = normed.shape[0]

    def valid():
        index = info_ref[1] + lax.broadcasted_iota(jnp.int32, (width, 1), 0)
        return jnp.where(index < info_ref[0], 1.0, 0.0)

    def inverse_of(x):
        return lax.rsqrt(jnp.mean(x * x, axis=-1, keepdims=True) + EPSILON)

    def head_rows(pair, slot):
        head = 2 * pair + (core if slot == 0 else 1 - core)
        return pl.ds(pl.multiple_of(head * head_dim, head_dim), head_dim)

    def slot_rows(pair, slot):
        return slice((2 * pair + slot) * head_dim, (2 * pair + slot + 1) * head_dim)

    spots = [(pair, slot) for pair in range(mixed_ref.shape[0] // head_dim // 2) for slot in range(2)]

    @pl.when(step == 0)
    def _():
        for spot in spots:
            ordered_ref[head_rows(*spot), :] = mixed_ref[slot_rows(*spot), :]
        inputs = tokens_ref[0, 0].astype(F32) + dot(ordered_ref[...].T, out_w_ref[...])
        residual[...] = inputs
        made = (inputs * inverse_of(inputs) * gain_ref[...]).astype(BF16)
        normed[...] = made
        flat_ref[...] = made.T
        grad_ffn_ref[...] = (cot_ref[0, 0].astype(F32) * valid()).astype(BF16)
        ffn_out[...] = jnp.zeros_like(ffn_out)
        grad_normed[...] = jnp.zeros_like(grad_normed)

    gate = dot(normed[...], gate_w_ref[...])
    up = dot(normed[...], up_w_ref[...])
    grad_hidden = contract(grad_ffn_ref[...], down_w_ref[...], 1, 1)
    sigmoid = sigmoid_of(gate)
    silu = gate * sigmoid
    hidden = (silu * up).astype(BF16)
    grad_gate = (grad_hidden * up * (sigmoid + silu * (1.0 - sigmoid))).astype(BF16)
    grad_up = (grad_hidden * silu).astype(BF16)
    hidden_ref[...] = hidden.T
    grad_gate_ref[...] = grad_gate
    grad_up_ref[...] = grad_up
    ffn_out[...] += dot(hidden, down_w_ref[...])
    grad_normed[...] += contract(grad_gate, gate_w_ref[...], 1, 1) + contract(grad_up, up_w_ref[...], 1, 1)

    @pl.when(step == pl.num_programs(0) - 1)
    def _():
        keep = valid()
        kept = residual[...]
        output_ref[0, 0] = ((kept + ffn_out[...]) * keep).astype(BF16)
        inverse = inverse_of(kept)
        scaled = grad_normed[...] * gain_ref[...]
        mean = jnp.mean(scaled * kept, axis=-1, keepdims=True)
        grad = cot_ref[0, 0].astype(F32) * keep
        grad = grad + (inverse * scaled - kept * (inverse * inverse * inverse) * mean)
        gain_out_ref[...] = jnp.sum(grad_normed[...] * kept * inverse, axis=0, keepdims=True)
        grad_res_ref[...] = grad
        low = grad.astype(BF16)
        grad_attn_ref[...] = low
        slots[...] = contract(out_w_ref[...], low, 1, 1).astype(BF16)
        for spot in spots:
            grad_mixed_ref[slot_rows(*spot), :] = slots[head_rows(*spot), :]


def middle_part(info, mixed, tokens, cotangent, unit, weights, gain, head_dim, output):
    width, model = tokens.shape[2:]
    out_w, gate_w, up_w, down_w = weights
    ffn = gate_w.shape[1]
    block = 512

    def fixed(a):
        return pl.BlockSpec(a.shape, lambda f, *_: (0,) * a.ndim)

    def one(*shape):
        return pl.BlockSpec(shape, lambda f, *_: (0,) * len(shape))

    token_spec = pl.BlockSpec((1, 1, width, model), lambda f, *_: unit + (0, 0))
    operands = [info, mixed, tokens, cotangent, out_w, gain, gate_w, up_w, down_w]
    in_specs = [
        fixed(mixed), token_spec, token_spec, fixed(out_w), fixed(gain),
        pl.BlockSpec((model, block), lambda f, *_: (0, f)),
        pl.BlockSpec((model, block), lambda f, *_: (0, f)),
        pl.BlockSpec((block, model), lambda f, *_: (f, 0)),
    ]
    aliases = {}
    if output is not None:
        aliases = {len(operands): 0}
        operands.append(output)
        in_specs.append(pl.BlockSpec(memory_space=pl.ANY))
    struct = jax.ShapeDtypeStruct
    return pl.pallas_call(
        functools.partial(middle_kernel, (head_dim, output is not None)),
        grid_spec=pltpu.PrefetchScalarGridSpec(
            num_scalar_prefetch=1,
            grid=(ffn // block,),
            in_specs=in_specs,
            out_specs=[
                token_spec, one(model, width), one(model, width),
                pl.BlockSpec((block, width), lambda f, *_: (f, 0)),
                pl.BlockSpec((width, block), lambda f, *_: (0, f)),
                pl.BlockSpec((width, block), lambda f, *_: (0, f)),
                one(width, model), one(width, model), one(width, model), one(model, width), one(1, model),
            ],
            scratch_shapes=[
                pltpu.VMEM((width, model), BF16),
                pltpu.VMEM((width, model), F32),
                pltpu.VMEM((width, model), F32),
                pltpu.VMEM((width, model), F32),
                pltpu.VMEM((model, width), BF16),
            ],
        ),
        out_shape=[
            struct(tokens.shape, BF16), struct((model, width), BF16), struct((model, width), BF16),
            struct((ffn, width), BF16),
            struct((width, ffn), BF16), struct((width, ffn), BF16), struct((width, model), BF16),
            struct((width, model), F32), struct((width, model), BF16), struct((model, width), BF16),
            struct((1, model), F32),
        ],
        input_output_aliases=aliases,
        compiler_params=pltpu.CompilerParams(vmem_limit_bytes=62 << 20),
        cost_estimate=pl.CostEstimate(
            flops=12 * width * model * ffn // COVER, bytes_accessed=8 * model * ffn, transcendentals=0
        ),
        name="middle_part",
    )(*operands)


def final_kernel(
    shape, core_ref, tokens_ref, grad_res_ref, gain_ref, query_ref, key_ref, value_ref, cos_ref, sin_ref, *rest
):
    here, head_dim, aliased = shape
    back = rest[:here]
    rest = rest[here:]
    if aliased:
        rest = rest[1:]
    out_ref, grad_q_ref, grad_k_ref, grad_v_ref, gain_out_ref, total = rest
    step = pl.program_id(0)
    cosine, sine = cos_ref[...], sin_ref[...]
    half = head_dim // 2

    def turned(x):
        first, second = x[:half].astype(F32), x[half:].astype(F32)
        return jnp.concatenate(
            [first * cosine + second * sine, second * cosine - first * sine], axis=0
        ).astype(BF16)

    for at in range(256 // head_dim):
        head = at
        if here == 2:
            head = at // 2 * 2 + (core_ref[0] if at % 2 == 0 else 1 - core_ref[0])
        place = pl.ds(pl.multiple_of(head * head_dim, head_dim), head_dim)
        part = back[at % here]
        grad_q_ref[place, :] = turned(part[at // here, 0:head_dim, :])
        grad_k_ref[place, :] = turned(part[at // here, head_dim : 2 * head_dim, :])
        grad_v_ref[place, :] = part[at // here, 2 * head_dim : 3 * head_dim, :]
    rows = [ref[...].T for ref in (grad_q_ref, grad_k_ref, grad_v_ref)]

    @pl.when(step == 0)
    def _():
        total[...] = jnp.zeros_like(total)

    depth = query_ref.shape[2]
    for shard in range(query_ref.shape[0]):
        made = dot(rows[0], query_ref[shard]) + dot(rows[1], key_ref[shard]) + dot(rows[2], value_ref[shard])
        total[:, shard * depth : (shard + 1) * depth] += made

    @pl.when(step == pl.num_programs(0) - 1)
    def _():
        inputs = tokens_ref[0, 0].astype(F32)
        inverse = lax.rsqrt(jnp.mean(inputs * inputs, axis=-1, keepdims=True) + EPSILON)
        scaled = total[...] * gain_ref[...]
        mean = jnp.mean(scaled * inputs, axis=-1, keepdims=True)
        grad = inverse * scaled - inputs * (inverse * inverse * inverse) * mean
        out_ref[0, 0] = (grad_res_ref[...] + grad).astype(BF16)
        gain_out_ref[...] = jnp.sum(total[...] * inputs * inverse, axis=0, keepdims=True)


def final_part(core, tokens, unit, grad_res, gain, weights, cosine, sine, back, head_dim, output):
    width, model = tokens.shape[2:]
    here = len(back)
    steps = model // 256

    def fixed(a):
        return pl.BlockSpec(a.shape, lambda c: (0,) * a.ndim)

    token_spec = pl.BlockSpec((1, 1, width, model), lambda c: unit + (0, 0))
    shards, _, depth = weights.shape
    weight_specs = [
        pl.BlockSpec((shards, 256, depth), lambda c, i=i: (0, i * steps + c, 0)) for i in range(3)
    ]
    row_spec = pl.BlockSpec((256, width), lambda c: (c, 0))
    operands = [core, tokens, grad_res, gain, weights, weights, weights, cosine, sine, *back]
    in_specs = [
        pl.BlockSpec(memory_space=pltpu.SMEM), token_spec, fixed(grad_res), fixed(gain), *weight_specs,
        fixed(cosine), fixed(sine),
    ] + [
        pl.BlockSpec((256 // head_dim // here, 3 * head_dim, width), lambda c: (c, 0, 0)) for _ in back
    ]
    aliases = {}
    if output is not None:
        aliases = {len(operands): 0}
        operands.append(output)
        in_specs.append(pl.BlockSpec(memory_space=pl.ANY))
    struct = jax.ShapeDtypeStruct
    return pl.pallas_call(
        functools.partial(final_kernel, (here, head_dim, output is not None)),
        grid=(steps,),
        in_specs=in_specs,
        out_specs=[token_spec, row_spec, row_spec, row_spec, pl.BlockSpec((1, model), lambda c: (0, 0))],
        out_shape=[
            struct(tokens.shape, BF16), struct((model, width), BF16), struct((model, width), BF16),
            struct((model, width), BF16), struct((1, model), F32),
        ],
        scratch_shapes=[pltpu.VMEM((width, model), F32)],
        input_output_aliases=aliases,
        compiler_params=pltpu.CompilerParams(vmem_limit_bytes=62 << 20),
        cost_estimate=pl.CostEstimate(
            flops=6 * width * model * model // COVER, bytes_accessed=12 * model * model, transcendentals=0
        ),
        name="final_part",
    )(*operands)


def picked_kernel(units, rows, places, flipped, split, table_ref, *refs):
    weights = len(places)
    lefts = refs[0:units]
    rights = refs[units : units * (1 + weights)]
    outs = refs[units * (1 + weights) : units * (1 + weights) + weights * split]
    picked = refs[units * (1 + weights) + weights * split :]

    @pl.when(pl.program_id(0) == 0)
    def _():
        for w, (start, size) in enumerate(places):
            for p in range(size):
                at = pl.ds(pl.multiple_of(table_ref[start + p] * rows, rows), rows)
                for u in range(units):
                    picked[w * units + u][p * rows : (p + 1) * rows, :] = lefts[u][at, :]

    for w in range(weights):
        total = None
        for u in range(units):
            right = rights[w * units + u][...]
            left = picked[w * units + u][...]
            made = contract(left, right, 1, 1) if flipped else dot(left, right)
            total = made if total is None else total + made
        height = total.shape[0] // split
        for i in range(split):
            outs[w * split + i][...] = total[i * height : (i + 1) * height].astype(BF16)


def picked_grads(table, places, lefts, rights, rows, flipped, split, block, name):
    units = len(lefts)
    width = lefts[0].shape[1]
    columns = rights[0].shape[0 if flipped else 1]
    in_specs = [pl.BlockSpec(a.shape, lambda n, *_: (0, 0)) for a in lefts]
    for a in rights:
        if flipped:
            in_specs.append(pl.BlockSpec((block, width), lambda n, *_: (n, 0)))
        else:
            in_specs.append(pl.BlockSpec((width, block), lambda n, *_: (0, n)))
    heights = [size * rows for _, size in places]
    return pl.pallas_call(
        functools.partial(picked_kernel, units, rows, places, flipped, split),
        grid_spec=pltpu.PrefetchScalarGridSpec(
            num_scalar_prefetch=1,
            grid=(columns // block,),
            in_specs=in_specs,
            out_specs=[
                pl.BlockSpec((height // split, block), lambda n, *_: (0, n)) for height in heights for _ in range(split)
            ],
            scratch_shapes=[pltpu.VMEM((height, width), BF16) for height in heights for _ in lefts],
        ),
        out_shape=[
            jax.ShapeDtypeStruct((height // split, columns), BF16) for height in heights for _ in range(split)
        ],
        compiler_params=pltpu.CompilerParams(vmem_limit_bytes=62 << 20),
        cost_estimate=pl.CostEstimate(
            flops=2 * units * sum(heights) * width * columns // COVER,
            bytes_accessed=4 * sum(heights) * columns,
            transcendentals=0,
        ),
        name=name,
    )(table, *lefts, *rights)


def weights_kernel(units, *refs):
    out_ref = refs[-1]
    total = dot(refs[0][...], refs[units][...])
    for u in range(1, units):
        total += dot(refs[u][...], refs[units + u][...])
    out_ref[...] = total.astype(BF16).reshape(out_ref.shape)


def weight_grad(lefts, rights, by_left, out_struct, out_spec, steps, into, name):
    units = len(lefts)

    def fixed(a):
        return pl.BlockSpec(a.shape, lambda n: (0, 0))

    def left_spec(a):
        return pl.BlockSpec((a.shape[0] // steps, a.shape[1]), lambda n: (n, 0))

    def right_spec(a):
        return pl.BlockSpec((a.shape[0], a.shape[1] // steps), lambda n: (0, n))

    operands = list(lefts) + list(rights)
    if by_left:
        in_specs = [left_spec(a) for a in lefts] + [fixed(a) for a in rights]
    else:
        in_specs = [fixed(a) for a in lefts] + [right_spec(a) for a in rights]
    aliases = {}
    if into is not None:
        aliases = {len(operands): 0}
        operands.append(into)
        in_specs.append(pl.BlockSpec(memory_space=pl.ANY))
    return pl.pallas_call(
        functools.partial(weights_kernel, units),
        grid=(steps,),
        in_specs=in_specs,
        out_specs=out_spec,
        out_shape=out_struct,
        input_output_aliases=aliases,
        compiler_params=pltpu.CompilerParams(vmem_limit_bytes=62 << 20),
        cost_estimate=pl.CostEstimate(
            flops=2 * units * lefts[0].shape[0] * lefts[0].shape[1] * rights[0].shape[1] // COVER,
            bytes_accessed=2 * lefts[0].shape[0] * rights[0].shape[1],
            transcendentals=0,
        ),
        name=name,
    )(*operands)


def reduce_kernel(orders, count, *refs):
    streams = len(orders)
    rounds = len(orders[0])
    ins, vec_ref = refs[:streams], refs[streams]
    outs, vec_out = refs[streams + 1 : 2 * streams + 1], refs[2 * streams + 1]
    rest = refs[2 * streams + 2 :]
    works, arrivals = rest[:streams], rest[streams : 2 * streams]
    vec_work, vec_arrival, send_sem, recv_sem, vec_send, vec_recv = rest[2 * streams :]
    shard, seq = lax.axis_index("shard"), lax.axis_index("seq")

    def partner(mask):
        if mask >= count:
            step = mask // count
            return (shard + step * (1 - 2 * (shard // step % 2)), seq)
        return (shard, seq + mask * (1 - 2 * (seq // mask % 2)))

    barrier = pltpu.get_barrier_semaphore()
    for mask in orders[0]:
        pl.semaphore_signal(
            barrier, inc=1, device_id=partner(mask), device_id_type=pl.DeviceIdType.MESH
        )
    pl.semaphore_wait(barrier, rounds)

    height = ins[0].shape[0]
    halves = [height >> (r + 1) for r in range(rounds)]
    starts = [sum(halves[:r]) for r in range(rounds)]

    def copy_of(s, r):
        source = ins[s] if r == 0 else works[s]
        return pltpu.make_async_remote_copy(
            src_ref=source.at[pl.ds(halves[r], halves[r])],
            dst_ref=arrivals[s].at[pl.ds(starts[r], halves[r])],
            send_sem=send_sem.at[s, r],
            recv_sem=recv_sem.at[s, r],
            device_id=partner(orders[s][r]),
            device_id_type=pl.DeviceIdType.MESH,
        )

    def vec_copy(r):
        return pltpu.make_async_remote_copy(
            src_ref=vec_ref if r == 0 else vec_work.at[r - 1],
            dst_ref=vec_arrival.at[r],
            send_sem=vec_send.at[r],
            recv_sem=vec_recv.at[r],
            device_id=partner(orders[0][r]),
            device_id_type=pl.DeviceIdType.MESH,
        )

    for s in range(streams):
        copy_of(s, 0).start()
    vec_copy(0).start()
    for r in range(rounds):
        for s in range(streams):
            copy_of(s, r).wait_recv()
            source = ins[s] if r == 0 else works[s]
            size = halves[r]

            def added(low, high):
                mine = source[low:high].astype(F32)
                return mine + arrivals[s][starts[r] + low : starts[r] + high].astype(F32)

            if r == rounds - 1:
                outs[s][...] = added(0, size)
            else:
                works[s][size // 2 : size] = added(size // 2, size).astype(BF16)
                copy_of(s, r + 1).start()
                works[s][0 : size // 2] = added(0, size // 2).astype(BF16)
        vec_copy(r).wait_recv()
        before = vec_ref[...] if r == 0 else vec_work[r - 1]
        if r == rounds - 1:
            vec_out[...] = before + vec_arrival[r]
        else:
            vec_work[r] = before + vec_arrival[r]
            vec_copy(r + 1).start()
    for r in range(rounds):
        for s in range(streams):
            copy_of(s, r).wait_send()
        vec_copy(r).wait_send()


def reduce_rows(parts, vector, orders, count):
    streams = len(parts)
    rounds = len(orders[0])
    height, columns = parts[0].shape
    rows = height >> rounds
    vmem = pl.BlockSpec(memory_space=pltpu.VMEM)
    return pl.pallas_call(
        functools.partial(reduce_kernel, orders, count),
        in_specs=[vmem] * (streams + 1),
        out_specs=[vmem] * (streams + 1),
        out_shape=[jax.ShapeDtypeStruct((rows, columns), F32)] * streams
        + [jax.ShapeDtypeStruct(vector.shape, F32)],
        scratch_shapes=[pltpu.VMEM((height // 2, columns), BF16) for _ in parts]
        + [pltpu.VMEM((height - rows, columns), BF16) for _ in parts]
        + [
            pltpu.VMEM((rounds - 1,) + vector.shape, F32),
            pltpu.VMEM((rounds,) + vector.shape, F32),
            pltpu.SemaphoreType.DMA((streams, rounds)),
            pltpu.SemaphoreType.DMA((streams, rounds)),
            pltpu.SemaphoreType.DMA((rounds,)),
            pltpu.SemaphoreType.DMA((rounds,)),
        ],
        compiler_params=pltpu.CompilerParams(
            collective_id=0, has_side_effects=True, vmem_limit_bytes=62 << 20
        ),
        name="reduce_rows",
    )(*parts, vector)


def on_device(
    tokens, cotangent, lengths, variates, positions, attn_gain, w_query, w_key, w_value, w_out,
    bias_table, ffn_gain, w_gate, w_up, w_down,
):
    micro, seqs, width, model = tokens.shape
    heads = bias_table.shape[0]
    head_dim = model // heads
    count = lax.axis_size("seq")
    here = heads // count
    ffn = w_gate.shape[1]
    devices = lax.axis_size("shard") * count
    seq_index = lax.axis_index("seq")
    units = [(m, s) for m in range(micro) for s in range(seqs)]
    swap = here == 2 and len(units) == 2 and lax.axis_size("shard") % 2 == 0
    core = (lax.axis_index("shard") % 2 if swap else jnp.int32(0)).astype(jnp.int32).reshape(1)
    heads_here = 1 if swap else here
    first_head = seq_index * here + core[0]
    bias_here = lax.dynamic_slice_in_dim(bias_table, first_head, heads_here, 0)
    attn_row, ffn_row = attn_gain[None, :], ffn_gain[None, :]

    def gather(weight):
        return lax.all_gather(weight, "shard", axis=0, tiled=True)

    def exchange(values):
        return lax.all_to_all(values, "seq", split_axis=0, concat_axis=0, tiled=True)

    def after(value, *before):
        return lax.optimization_barrier((value,) + before)[0]

    attn_rows = turn_weights(w_query, w_key, w_value)
    attn_joined = lax.all_gather(attn_rows, "shard", axis=0, tiled=False)
    ffn_weights = [gather(w_out), gather(w_gate), gather(w_up), gather(w_down)]

    def permute(value, mask):
        return lax.ppermute(value, ("shard", "seq"), [(i, i ^ mask) for i in range(devices)])

    def cross(value):
        return permute(value, count)

    lengths_of = [lengths, cross(lengths)] if swap else [lengths] * here
    ids_own = lax.all_gather(variates, "seq", axis=0, tiled=False)
    ids_of = [ids_own, cross(ids_own)] if swap else [ids_own] * here
    attn_joined = after(attn_joined, *ids_of)

    def ids_rows(u, h):
        m, s = units[u]
        return ids_of[h][:, m, s].astype(F32)[:, None, :]

    packed_list, flats, tables = [], [], []

    def run_project(u, token):
        m, s = units[u]
        cosine, sine = rotary_tables(positions[m, s], head_dim // 2)
        flat, *packed = project(
            core, tokens, (m, s), after(attn_row, *token), attn_joined, cosine, sine, count, here, head_dim,
            swap,
        )
        flats.append(flat)
        tables.append((cosine, sine))
        packed_list.append(packed)

    sent = {}
    mixed_now = [None] * len(units)
    sums = {}
    mixed_tok = {}
    crossed, mixed_part, mixed_cross, heads_cross, back_cross = {}, {}, {}, {}, {}
    middle = [None] * len(units)
    grad_heads = {}
    state = {"output": None, "grads": None}
    packed_grads = {}
    returned = {}
    bias_terms = {}
    finals = [None] * len(units)

    def length_of(u, h, token):
        m, s = units[u]
        return after(lengths_of[h][m, s].reshape(1), *token)

    def inputs_of(u, h):
        return (crossed[u] if swap and h == 1 else sent[u, h]), ids_rows(u, h)

    def run_forward(u, h, token):
        made, sums[u, h] = attend_forward(
            *inputs_of(u, h), length_of(u, h, token), bias_here, None if swap else mixed_now[u],
            0 if swap else h, heads_here, head_dim,
        )
        if swap:
            mixed_part[u, h] = made
            if h == 1:
                mixed_cross[u] = cross(made)
        else:
            mixed_now[u] = made
        return sums[u, h]

    def run_middle(u, token):
        m, s = units[u]
        info = jnp.stack([lengths[m, s], seq_index * width, core[0]]).astype(jnp.int32)
        state["output"], mixed_tok[u], *middle[u] = middle_part(
            after(info, *token), mixed_tok[u], tokens, cotangent, (m, s), ffn_weights, ffn_row, head_dim,
            state["output"],
        )
        return middle[u][8]

    def run_backward(u, h, token):
        if swap:
            token = token + ((heads_cross[1],) if (u, h) == (0, 1) else ())
            grad = grad_heads[u] if h == 0 else heads_cross[u]
            mixed = mixed_part[u, h]
        else:
            grad, mixed = grad_heads[u], mixed_now[u]
        packed_grads[u, h], both = attend_backward(
            *inputs_of(u, h), grad, mixed, sums[u, h], length_of(u, h, token), bias_here,
            0 if swap else h, head_dim,
        )
        if swap and h == 1:
            back_cross[u] = cross(packed_grads[u, h])
        bias_terms[u, h] = both
        return both

    def run_final(u, token):
        m, s = units[u]
        cosine, sine = tables[u]
        state["grads"], *finals[u] = final_part(
            core, tokens, (m, s), middle[u][5], after(attn_row, *token), attn_joined, cosine, sine,
            [returned[u, h] for h in range(here)], head_dim, state["grads"],
        )
        return finals[u][3]

    rows = model // devices
    fold = ffn // model
    tall = ffn // devices
    seq_masks = [1 << i for i in range(count.bit_length() - 1)]
    shard_masks = [count << i for i in range((devices // count).bit_length() - 1)]
    spread = shard_masks[1:]
    orders = (
        shard_masks[:1] + spread + seq_masks,
        shard_masks[:1] + seq_masks[:1] + spread + seq_masks[1:],
        shard_masks[:1] + seq_masks[1:2] + seq_masks[:1] + spread + seq_masks[2:],
    )
    direct = rows % 16 == 0 and devices == 1 << len(orders[0])

    def places_of(order):
        marks = []
        for p in range(devices):
            bits = [p >> (len(order) - 1 - i) & 1 for i in range(len(order))]
            marks.append(sum(mask for bit, mask in zip(bits, order) if bit))
        me = lax.axis_index("shard") * count + seq_index
        return me.astype(jnp.int32) ^ jnp.array(marks, jnp.int32)

    def column(index):
        return [item[index] for item in middle]

    def run_weights(token):
        if not direct:
            return [
                sum(dot(left, right) for left, right in zip(lefts, rights)).astype(BF16)
                for lefts, rights in (
                    (column(0), column(2)), (column(0), column(3)), (column(1), column(4)),
                    ([mixed_tok[u] for u in range(len(units))], column(6)),
                )
            ]
        part = ffn // fold
        narrow = model // fold
        spare = -(-(2 * part + narrow) // 384) * 384
        struct = jax.ShapeDtypeStruct((devices, fold, rows, spare), BF16)
        down = pl.BlockSpec((512 // tall, fold, rows, model), lambda n: (n, 0, 0, 0))
        gate = pl.BlockSpec((devices, 1, rows, part), lambda n: (0, n, 0, 1))
        out = pl.BlockSpec((devices, 1, rows, narrow), lambda n: (0, n, 0, 2 * part // narrow))
        table = after(places_of(orders[0]), *token)
        up = picked_grads(table, [(0, devices)], column(0), column(3), rows, False, 2, 1024, "up_grad")
        holder["streams"] = [[up[0], permute(up[1], orders[0][0]), orders[0][1:]]]
        firsts = [after(middle[0][4], up[0])] + [item[4] for item in middle[1:]]
        terms = weight_grad(column(1), firsts, True, struct, down, ffn // 512, None, "down_grad")
        landed = (holder["streams"][0][1],) + ((heads_cross[0],) if swap else ())
        rights = [after(middle[0][2], *holder["flying"], *landed)] + [item[2] for item in middle[1:]]
        terms = weight_grad(column(0), rights, False, struct, gate, fold, terms, "gate_grad")
        mixed_all = [mixed_tok[u] for u in range(len(units))]
        terms = weight_grad(mixed_all, column(6), False, struct, out, fold, terms, "out_grad")
        terms = terms.reshape(ffn, spare)
        holder["half"] = lax.psum_scatter(terms, "shard", scatter_dimension=0, tiled=True)
        return terms

    def wide_sum(a, b):
        return a.astype(F32) + b.astype(F32)

    def advance(token):
        out = ()
        if not direct:
            return out
        for stream in holder["streams"]:
            keep, came, masks = stream
            if not masks:
                continue
            keep = after(keep, *token)
            half = keep.shape[0] // 2
            send = wide_sum(keep[half:], came[half:]).astype(BF16)
            stream[0] = wide_sum(keep[:half], came[:half]).astype(BF16)
            stream[1] = permute(send, masks[0])
            stream[2] = masks[1:]
            out = out + (send, stream[0])
        return out

    holder = {}

    def weights_work(token):
        holder["terms"] = run_weights(token)
        return holder["terms"]

    def send_packed(u, h):
        def keep(moved):
            sent[u, h] = moved
            if swap and h == 1:
                crossed[u] = cross(moved)

        return lambda: packed_list[u][h], keep

    def send_mixed(u):
        def keep(moved):
            mixed_tok[u] = moved.reshape(model, width)

        if not swap:
            return lambda: mixed_now[u], keep
        return lambda: jnp.concatenate([mixed_part[u, 0], mixed_cross[u]], axis=1), keep

    def send_heads(u):
        def keep(moved):
            grad_heads[u] = moved
            if swap:
                heads_cross[u] = cross(moved[:, head_dim:])

        return lambda: middle[u][7].reshape(count, here * head_dim, width), keep

    def send_back(u, h):
        def keep(moved):
            returned[u, h] = moved

        return lambda: back_cross[u] if swap and h == 1 else packed_grads[u, h], keep

    def work_project(u):
        def work(token):
            run_project(u, token)
            return flats[u]

        return work

    def work(function, *args):
        return lambda token: function(*args, token)

    total = len(units)
    order = [(u, h) for u in range(total) for h in range(here)]
    if swap:
        steps = [
            (work_project(0), None),
            (work_project(1), send_packed(0, 1)),
            (work(run_forward, 0, 1), send_packed(0, 0)),
            (work(run_forward, 0, 0), send_packed(1, 1)),
            (work(run_forward, 1, 1), send_packed(1, 0)),
            (work(run_forward, 1, 0), send_mixed(0)),
            (work(run_middle, 0), send_mixed(1)),
            (work(run_middle, 1), send_heads(0)),
            (weights_work, send_heads(1)),
            (work(run_backward, 0, 0), None),
            (work(run_backward, 0, 1), send_back(0, 0)),
            (work(run_backward, 1, 0), send_back(0, 1)),
            (work(run_backward, 1, 1), send_back(1, 0)),
            (work(run_final, 0), send_back(1, 1)),
            (work(run_final, 1), None),
        ]
    else:
        steps = [(work_project(u), None) for u in range(total)]
        steps += [(None, send_packed(*at)) for at in order]
        for u in range(total):
            steps += [(work(run_forward, u, h), None) for h in range(here)]
            steps += [(None, send_mixed(u))]
        for u in range(total):
            steps += [(work(run_middle, u), None), (None, send_heads(u))]
        steps += [(weights_work, None)]
        for at in order:
            steps += [(work(run_backward, *at), None), (None, send_back(*at))]
        steps += [(work(run_final, u), None) for u in range(total)]

    late = [task for task, _ in steps[-2:]]
    token = ()
    for index, (task, send) in enumerate(steps):
        done = ()
        moved = None
        ahead = ()
        if "streams" in holder:
            leaving = advance(token[-1:])
            if index == len(steps) - 5:
                ahead = leaving
            elif task not in late:
                token = token + leaving
        if "half" in holder and index == len(steps) - 3:
            half = after(holder["half"], *token)
            holder["owned"] = lax.psum_scatter(half, "seq", scatter_dimension=0, tiled=True)
        if send is not None:
            moved = exchange(after(send[0](), *token))
            done = (moved,)
        holder["flying"] = done
        if task is not None:
            done = done + (task(token + ahead),)
        if send is not None:
            send[1](after(moved, *done[1:]))
        token = done
    acc_bias = jnp.concatenate(
        [sum(bias_terms[u, h] for u in range(total))[0:1, 0:2] for h in range(here)], axis=0
    )
    if swap:
        acc_bias = acc_bias[0:1] + acc_bias[1:2]
    bias_full = lax.dynamic_update_slice(
        jnp.zeros((heads, 2), F32), acc_bias, (first_head, jnp.int32(0))
    )
    gain_attn = sum(item[3][0] for item in finals)
    gain_ffn = sum(item[8][0] for item in middle)
    if direct:
        while holder["streams"][0][2]:
            advance(token)
        keep, came, _ = holder["streams"][0]
        up_own = wide_sum(after(keep, *token), came)
        flats[0] = after(flats[0], up_own)
        owned, part = holder["owned"], ffn // fold

        def joined(start, size):
            piece = owned[:, start : start + size].reshape(fold, rows, size)
            return jnp.swapaxes(piece, 0, 1).reshape(rows, fold * size).astype(F32)

        down_own = owned[:, :part].astype(F32)
        gate_own, out_own = joined(part, part), joined(2 * part, model // fold)
        table = jnp.concatenate([places_of(order) for order in orders])
        attn_terms = picked_grads(
            table, [(i * devices, devices) for i in range(3)], flats,
            [item[i] for i in range(3) for item in finals], rows, True, 1, 256, "attn_grads",
        )
        flat = jnp.concatenate([gain_attn, gain_ffn, bias_full.reshape(-1)])
        tiles = -(-flat.shape[0] // 1024) * 8
        flat = jnp.pad(flat, (0, tiles * 128 - flat.shape[0])).reshape(tiles, 128)
        query_own, key_own, value_own, flat = reduce_rows(list(attn_terms), flat, orders, count)
        flat = flat.reshape(-1)
        gain_attn, gain_ffn = flat[:model], flat[model : 2 * model]
        bias_full = flat[2 * model : 2 * model + 2 * heads].reshape(heads, 2)
    else:

        def scatter(value):
            owned = lax.psum_scatter(value, ("shard", "seq"), scatter_dimension=0, tiled=True)
            return owned.astype(F32)

        gate_own, up_own, down_own, out_own = [scatter(value) for value in holder["terms"]]
        query_own, key_own, value_own = [
            scatter(
                sum(contract(flat, item[i], 1, 1) for flat, item in zip(flats, finals)).astype(BF16)
            )
            for i in range(3)
        ]
        gain_attn, gain_ffn, bias_full = lax.psum(
            (gain_attn, gain_ffn, bias_full), ("shard", "seq")
        )
    return (
        state["output"], state["grads"], gain_attn, query_own, key_own, value_own, out_own,
        bias_full, gain_ffn, gate_own, up_own, down_own,
    )


def solution(mesh):
    token_spec = P(None, "shard", "seq", None)
    row_spec = P("shard", None)
    in_specs = (
        token_spec, token_spec, P(None, "shard"), P(None, "shard", "seq"), P(None, "shard", "seq"),
        P(), row_spec, row_spec, row_spec, row_spec, P(), P(), row_spec, row_spec, row_spec,
    )
    owned = P(("shard", "seq"), None)
    out_specs = (
        token_spec, token_spec, P(), owned, owned, owned, owned, P(), P(), owned, owned, owned,
    )
    return jax.shard_map(
        on_device, mesh=mesh, in_specs=in_specs, out_specs=out_specs, check_vma=False
    )
```
